32 devices in a mesh: site: 4 (over y, x), hap: 8 (over z, core).
Axes of the slice: x: 2, y: 2, z: 4, core: 2. Of those that a mesh axis runs over, the one named last changes fastest.
Arguments:
- features: bfloat16 [512, 8, 256], P('site', 'hap'), may hold values from -6 to 6
- link_pattern: int32 [4, 4], replicated, may hold values from 0 to 1, as said below
- row_gain: float32 [256], replicated, may hold values from 0.5 to 1.5
- row_proj: bfloat16 [256, 768], replicated, may hold values from -0.5 to 6.5
- row_out: bfloat16 [256, 256], replicated, may hold values from -0.375 to 0.375
- column_norm_gain: float32 [256], replicated, may hold values from 0.5 to 1.5
- col_proj: bfloat16 [256, 768], replicated, may hold values from -0.5 to 6.5
- col_out: bfloat16 [256, 256], replicated, may hold values from -0.375 to 0.375
- cotangent: bfloat16 [512, 8, 256], P('site', 'hap'), may hold values from -6 to 6
Outputs:
- out_features: bfloat16 [512, 8, 256], P('site', 'hap')
- grad_features: bfloat16 [512, 8, 256], P('site', 'hap')
- grad_row_proj: float32 [256, 768], replicated
- grad_row_out: float32 [256, 256], replicated
- grad_col_proj: float32 [256, 768], replicated
- grad_col_out: float32 [256, 256], replicated
The draws below stay inside these ranges and needn't reach their ends.
Inputs may be any that keep to these rules, and one draw needn't show every extreme that they name: link_pattern[b, b] = 1 for every block b.
All inputs are finite; a program needn't handle non-finite values.
Results may differ from the reference program's by a relative error of at most 0.027.
The reference program's roundings to bfloat16 on the way count: a program that leaves them out, or rounds other values in their place, can miss the bound.
Values may be sent and summed in bfloat16 or wider, within the bound.
No kernel may reach another device: no remote copies, remote signals or barrier semaphores. Data moves between devices by JAX's collectives and lax.ppermute only.
A program may use at most 64 MiB of HBM per device.

```python
import jax
import jax.numpy as jnp
from jax import lax

D = 256
HEAD_DIM = 32
BLK = 128
SITES = 512
HAPS = 8
NBLK = 4


def draw_features(key, part):
    base = jax.random.normal(jax.random.fold_in(key, 11), (SITES, HAPS, D), jnp.float32)
    return jnp.clip(base, -6.0, 6.0).astype(jnp.bfloat16)


def draw_link_pattern(key, part):
    rows = lax.broadcasted_iota(jnp.int32, (NBLK, NBLK), 0)
    cols = lax.broadcasted_iota(jnp.int32, (NBLK, NBLK), 1)
    rolls = jax.random.randint(jax.random.fold_in(key, 21), (NBLK, NBLK), 0, 16)
    density = jax.random.randint(jax.random.fold_in(key, 22), (NBLK, 1), 1, 14)
    nearby = jnp.abs(rows - cols) <= 2
    linked = rolls - jnp.where(nearby, 6, 0) < density
    return jnp.where(jnp.logical_or(linked, rows == cols), 1, 0).astype(jnp.int32)


def projection_draw(key):
    noise = jnp.clip(jax.random.normal(key, (D, 3 * D), jnp.float32), -7.0, 7.0) * D ** (-0.5)
    return jnp.clip(noise, -0.5, 6.5).astype(jnp.bfloat16)


def draw_row_proj(key, part):
    return projection_draw(jax.random.fold_in(key, 31))


def draw_col_proj(key, part):
    return projection_draw(jax.random.fold_in(key, 41))


def steps_of(stream_key, shape, pieces, low, largest):
    gain = 1.0
    for axis_at, shards_of in pieces:
        heights = jax.random.uniform(jax.random.fold_in(jax.random.fold_in(stream_key, 6), axis_at), (shards_of,), jnp.float32, low / len(pieces), largest / len(pieces))
        gain = gain * jnp.repeat(jnp.exp(heights), shape[axis_at] // shards_of).reshape((-1,) + (1,) * (len(shape) - 1 - axis_at))
    return gain


def gaussian(stream_key, extent, scale, reach, cuts=(), kind=jnp.bfloat16):
    drawn = scale * jax.random.normal(stream_key, extent, jnp.float32)
    if cuts:
        drawn = drawn * steps_of(stream_key, extent, cuts, -0.22, 0.18)
    return jnp.clip(drawn, -reach, reach).astype(kind)


def setup_inputs(seed: int = 0) -> dict:
    streams_of = jax.random.split(jax.random.key(seed), 10)
    features = draw_features(jax.random.fold_in(streams_of[9], 71), 0)
    link_pattern = draw_link_pattern(jax.random.fold_in(streams_of[9], 71), 0)
    row_gain = jnp.clip(1.0 + 0.1 * jax.random.normal(streams_of[2], (D,), jnp.float32), 0.5, 1.5)
    row_proj = draw_row_proj(jax.random.fold_in(streams_of[9], 71), 0)
    row_out = gaussian(streams_of[4], (D, D), D ** -0.5, 0.375)
    column_norm_gain = jnp.clip(1.0 + 0.1 * jax.random.normal(streams_of[5], (D,), jnp.float32), 0.5, 1.5)
    col_proj = draw_col_proj(jax.random.fold_in(streams_of[9], 71), 0)
    col_out = gaussian(streams_of[7], (D, D), D ** -0.5, 0.375)
    cotangent = gaussian(streams_of[8], (SITES, HAPS, D), 1.0, 6.0, ((0, 4), (1, 8)))
    return {"features": features, "link_pattern": link_pattern, "row_gain": row_gain, "row_proj": row_proj, "row_out": row_out, "column_norm_gain": column_norm_gain, "col_proj": col_proj, "col_out": col_out, "cotangent": cotangent}


EPSILON = 1e-05

def to_widened_form(values):
    return values.astype(jnp.float32)

def to_narrow(values):
    return lax.optimization_barrier(values.astype(jnp.bfloat16))

def norm_rows(values, norm_gain):
    widened = to_widened_form(values)
    centred = widened - lax.optimization_barrier(jnp.mean(widened, axis=-1, keepdims=True))
    spread = lax.optimization_barrier(jnp.mean(centred * centred, axis=-1, keepdims=True))
    return centred * lax.rsqrt(spread + EPSILON) * to_widened_form(norm_gain)

def norm_back(values, norm_gain, incoming_gradient):
    primal, pullback = jax.vjp(lambda inside: norm_rows(inside, norm_gain), to_widened_form(values))
    return pullback(incoming_gradient)[0]

def project(other_argument, weight_matrix):
    return jnp.einsum('puh,hz->puz', to_widened_form(other_argument), to_widened_form(weight_matrix))

def project_back(incoming_gradient, weight_matrix):
    return jnp.einsum('hcr,kr->hck', to_widened_form(incoming_gradient), to_widened_form(weight_matrix))

def weight_grad(other_argument, incoming_gradient):
    return jnp.einsum('hyo,hyp->op', to_widened_form(other_argument), to_widened_form(incoming_gradient))

def split_heads(flat):
    return flat.reshape(flat.shape[0], flat.shape[1], flat.shape[2] // HEAD_DIM, HEAD_DIM)

def column_forward(hidden, column_norm_gain, col_proj, col_out):
    width = hidden.shape[2]
    scale = HEAD_DIM ** (-0.5)
    col_normed = to_narrow(norm_rows(hidden, column_norm_gain))
    col_packed = to_narrow(project(col_normed, col_proj))
    col_query = split_heads(col_packed[..., :width])
    col_key = split_heads(col_packed[..., width:2 * width])
    col_value = split_heads(col_packed[..., 2 * width:])
    scores = jnp.einsum('sqhe,skhe->shqk', to_widened_form(col_query), to_widened_form(col_key)) * scale
    highest = lax.optimization_barrier(jnp.max(scores, axis=-1))
    exp_terms = jnp.exp(scores - highest[..., None])
    row_total = lax.optimization_barrier(jnp.sum(exp_terms, axis=-1))
    mixed = jnp.einsum('shqk,skhe->sqhe', to_widened_form(to_narrow(exp_terms)), to_widened_form(col_value))
    col_attended = to_narrow(mixed / jnp.transpose(row_total, (0, 2, 1))[..., None]).reshape(hidden.shape)
    output = to_narrow(to_widened_form(hidden) + project(col_attended, col_out))
    return (output, (col_normed, col_query, col_key, col_value, col_attended, highest, row_total))

def column_backward(hidden, column_norm_gain, col_proj, col_out, saved, grad_out):
    col_normed, col_query, col_key, col_value, col_attended, highest, row_total = saved
    scale = HEAD_DIM ** (-0.5)
    grad_col_out = weight_grad(col_attended, grad_out)
    grad_att = to_narrow(project_back(grad_out, col_out))
    grad_heads = split_heads(grad_att)
    out_heads = split_heads(col_attended)
    scores = jnp.einsum('sqhe,skhe->shqk', to_widened_form(col_query), to_widened_form(col_key)) * scale
    attention_odds = jnp.exp(scores - highest[..., None]) / row_total[..., None]
    value_gradient = jnp.einsum('shqk,sqhe->skhe', to_widened_form(to_narrow(attention_odds)), to_widened_form(grad_heads))
    grad_chances = jnp.einsum('sqhe,skhe->shqk', to_widened_form(grad_heads), to_widened_form(col_value))
    deltas = jnp.transpose(lax.optimization_barrier(jnp.sum(to_widened_form(grad_heads) * to_widened_form(out_heads), axis=-1)), (0, 2, 1))
    grad_scores = to_widened_form(to_narrow(attention_odds * (grad_chances - deltas[..., None])))
    grad_query = jnp.einsum('shqk,skhe->sqhe', grad_scores, to_widened_form(col_key)) * scale
    grad_key = jnp.einsum('shqk,sqhe->skhe', grad_scores, to_widened_form(col_query)) * scale
    grad_packed = jnp.concatenate([to_narrow(grad_query.reshape(hidden.shape)), to_narrow(grad_key.reshape(hidden.shape)), to_narrow(value_gradient.reshape(hidden.shape))], axis=-1)
    grad_col_proj = weight_grad(col_normed, grad_packed)
    grad_normed = project_back(grad_packed, col_proj)
    grad_hidden = to_narrow(to_widened_form(grad_out) + norm_back(hidden, column_norm_gain, grad_normed))
    return (grad_hidden, grad_col_proj, grad_col_out)

def row_head_forward(head_query, head_key, head_value, link_pattern):
    scale = HEAD_DIM ** (-0.5)
    query_blocks = head_query.reshape(NBLK, BLK, head_query.shape[1], HEAD_DIM)

    def one_block(inputs):
        query_blk, link_row = inputs
        allowed = jnp.repeat(link_row > 0, BLK)
        scores = jnp.einsum('qne,kne->nqk', to_widened_form(query_blk), to_widened_form(head_key)) * scale
        scores = jnp.where(allowed[None, None, :], scores, -jnp.inf)
        highest = lax.optimization_barrier(jnp.max(scores, axis=-1))
        exp_terms = jnp.exp(scores - highest[..., None])
        row_total = lax.optimization_barrier(jnp.sum(exp_terms, axis=-1))
        mixed = jnp.einsum('nqk,kne->qne', exp_terms, to_widened_form(head_value), precision=lax.Precision.HIGHEST)
        return (mixed / jnp.transpose(row_total)[..., None], highest, row_total)
    return lax.map(one_block, (query_blocks, link_pattern))

def row_head_backward(head_query, head_key, head_value, head_grad, head_out, highest, row_total, link_pattern):
    scale = HEAD_DIM ** (-0.5)
    haps = head_query.shape[1]

    def blocks_of(flat):
        return flat.reshape(NBLK, BLK, haps, HEAD_DIM)

    def one_block(carry, inputs):
        grad_key, value_gradient = carry
        query_blk, grad_blk, out_blk, high_blk, total_blk, link_row = inputs
        allowed = jnp.repeat(link_row > 0, BLK)
        scores = jnp.einsum('qne,kne->nqk', to_widened_form(query_blk), to_widened_form(head_key)) * scale
        scores = jnp.where(allowed[None, None, :], scores, -jnp.inf)
        attention_odds = jnp.exp(scores - high_blk[..., None]) / total_blk[..., None]
        value_gradient = value_gradient + jnp.einsum('nqk,qne->kne', to_widened_form(to_narrow(attention_odds)), to_widened_form(grad_blk))
        grad_chances = jnp.einsum('qne,kne->nqk', to_widened_form(grad_blk), to_widened_form(head_value))
        deltas = jnp.transpose(lax.optimization_barrier(jnp.sum(to_widened_form(grad_blk) * to_widened_form(out_blk), axis=-1)))
        grad_scores = to_widened_form(to_narrow(attention_odds * (grad_chances - deltas[..., None])))
        grad_query = jnp.einsum('nqk,kne->qne', grad_scores, to_widened_form(head_key)) * scale
        grad_key = grad_key + jnp.einsum('nqk,qne->kne', grad_scores, to_widened_form(query_blk)) * scale
        return ((grad_key, value_gradient), grad_query)
    zeros = jnp.zeros(head_key.shape, jnp.float32)
    inputs = (blocks_of(head_query), blocks_of(head_grad), blocks_of(head_out), highest, row_total, link_pattern)
    (grad_key, value_gradient), grad_query = lax.scan(one_block, (zeros, zeros), inputs)
    return (grad_query.reshape(head_query.shape), grad_key, value_gradient)

def reference(features, link_pattern, row_gain, row_proj, row_out, column_norm_gain, col_proj, col_out, cotangent):
    sites, haps, width = features.shape
    heads = width // HEAD_DIM

    def by_head(flat):
        return jnp.transpose(split_heads(flat), (2, 0, 1, 3))

    def from_heads(stack):
        return jnp.transpose(stack.reshape(heads, sites, haps, HEAD_DIM), (1, 2, 0, 3)).reshape(sites, haps, width)
    normed = to_narrow(norm_rows(features, row_gain))
    packed = to_narrow(project(normed, row_proj))
    head_query = by_head(packed[..., :width])
    head_key = by_head(packed[..., width:2 * width])
    head_value = by_head(packed[..., 2 * width:])
    mixed, highest, row_total = lax.map(lambda triple: row_head_forward(triple[0], triple[1], triple[2], link_pattern), (head_query, head_key, head_value))
    attended = to_narrow(from_heads(mixed))
    hidden = to_narrow(to_widened_form(features) + project(attended, row_out))

    def column_block(pair_in):
        hidden_blk, grad_blk = pair_in
        output, saved = column_forward(hidden_blk, column_norm_gain, col_proj, col_out)
        grad_hid, grad_proj, grad_outw = column_backward(hidden_blk, column_norm_gain, col_proj, col_out, saved, grad_blk)
        return (output, grad_hid, grad_proj, grad_outw)
    shaped = (hidden.reshape(NBLK, BLK, haps, width), cotangent.reshape(NBLK, BLK, haps, width))
    out_blocks, grad_hid_blocks, proj_parts, out_parts = lax.map(column_block, shaped)
    out_features = out_blocks.reshape(sites, haps, width)
    grad_hidden = grad_hid_blocks.reshape(sites, haps, width)
    grad_col_proj = lax.optimization_barrier(jnp.sum(proj_parts, axis=0))
    grad_col_out = lax.optimization_barrier(jnp.sum(out_parts, axis=0))
    grad_row_out = weight_grad(attended, grad_hidden)
    grad_att = to_narrow(project_back(grad_hidden, row_out))
    head_grad = by_head(grad_att)
    head_out = by_head(attended)

    def head_back(group):
        return row_head_backward(group[0], group[1], group[2], group[3], group[4], group[5], group[6], link_pattern)
    grad_query, grad_key, value_gradient = lax.map(head_back, (head_query, head_key, head_value, head_grad, head_out, highest, row_total))
    grad_packed = jnp.concatenate([to_narrow(from_heads(grad_query)), to_narrow(from_heads(grad_key)), to_narrow(from_heads(value_gradient))], axis=-1)
    grad_row_proj = weight_grad(normed, grad_packed)
    grad_normed = project_back(grad_packed, row_proj)
    grad_features = to_narrow(to_widened_form(grad_hidden) + norm_back(features, row_gain, grad_normed))
    return (out_features, grad_features, grad_row_proj, grad_row_out, grad_col_proj, grad_col_out)
```

```python
import functools

import jax
import jax.numpy as jnp
from jax import lax
from jax.experimental import pallas as pl
from jax.experimental.pallas import tpu as pltpu
from jax.sharding import PartitionSpec as P

HEAD_DIM = 32
EPSILON = 1e-05
LOG2E = 1.4426950408889634
SCALE = HEAD_DIM ** (-0.5)
F32 = jnp.float32
BF16 = jnp.bfloat16
VMEM = pl.BlockSpec(memory_space=pltpu.VMEM)
SMEM = pl.BlockSpec(memory_space=pltpu.SMEM)
PARAMS = pltpu.CompilerParams(vmem_limit_bytes=48 << 20)


def mm(a, b):
    return lax.dot_general(a, b, (((1,), (0,)), ((), ())), preferred_element_type=F32)


def mm_nt(a, b):
    return lax.dot_general(a, b, (((1,), (1,)), ((), ())), preferred_element_type=F32)


def mm_tn(a, b):
    return lax.dot_general(a, b, (((0,), (0,)), ((), ())), preferred_element_type=F32)


def norm_parts(x):
    centred = x - jnp.mean(x, axis=-1, keepdims=True)
    rstd = lax.rsqrt(jnp.mean(centred * centred, axis=-1, keepdims=True) + EPSILON)
    return centred * rstd, rstd


def norm_back(xhat, rstd, gain, grad):
    scaled = grad * gain
    first = jnp.mean(scaled, axis=-1, keepdims=True)
    second = jnp.mean(scaled * xhat, axis=-1, keepdims=True)
    return rstd * (scaled - first - xhat * second)


def head_lanes(width, head):
    return lax.broadcasted_iota(jnp.int32, (1, width), 1) // HEAD_DIM == head


def only_head(values, head):
    return jnp.where(head_lanes(values.shape[1], head), values, jnp.zeros_like(values))


def flat_rows(values, dtype=BF16):
    wide = values.astype(F32)
    return wide.reshape(wide.shape[0] * wide.shape[1], wide.shape[2]).astype(dtype)


def call(body, outs, *operands, scalars=0, scratch=()):
    return pl.pallas_call(
        body,
        out_shape=[jax.ShapeDtypeStruct(s, d) for s, d in outs],
        in_specs=[SMEM] * scalars + [VMEM] * (len(operands) - scalars),
        out_specs=[VMEM] * len(outs),
        scratch_shapes=list(scratch),
        compiler_params=PARAMS,
    )(*operands)


def row_forward(sites, haps, idx, link, *refs):
    pieces = refs[:sites]
    gain, w_t = refs[sites : sites + 2]
    att_out, p_out, q_out, v_out, kt_out, n_out = refs[sites + 2 :]
    me = idx[0]
    rows = pieces[0].shape[0]
    width = q_out.shape[1]
    for k in range(sites):
        xhat, _ = norm_parts(pieces[k][...].astype(F32))
        n_out[k * rows : (k + 1) * rows, :] = (xhat * gain[...]).astype(BF16)
    normed = n_out[...]
    q = mm_nt(normed, w_t[:width, :]).astype(BF16)
    key = mm_nt(normed, w_t[width : 2 * width, :]).astype(BF16)
    q_out[...] = q
    v_out[...] = mm_nt(normed, w_t[2 * width :, :]).astype(BF16)
    kt_out[...] = mm_nt(w_t[width : 2 * width, :], normed).astype(BF16)
    v_t = mm_nt(w_t[2 * width :, :], normed).astype(BF16)
    att_t = []
    for h in range(width // HEAD_DIM):
        key_h = only_head(key, h)
        for b in range(sites):
            here = pl.ds(b * rows, rows)
            scores = mm_nt(key_h, q[b * rows : (b + 1) * rows]) * (SCALE * LOG2E)
            parts = [
                scores[a * rows : (a + 1) * rows]
                + jnp.where(link[me ^ b, me ^ a] > 0, 0.0, -jnp.inf)
                for a in range(sites)
            ]
            high = functools.reduce(
                jnp.maximum, [jnp.max(part, axis=0, keepdims=True) for part in parts]
            )
            parts = [jnp.exp2(part - high) for part in parts]
            total = sum(jnp.sum(part, axis=0, keepdims=True) for part in parts)
            inverse = 1.0 / total
            for a in range(sites):
                p_out[h, a * rows : (a + 1) * rows, here] = (parts[a] * inverse).astype(BF16)
        att_t.append(mm(v_t[h * HEAD_DIM : (h + 1) * HEAD_DIM], p_out[h]))
    att = jnp.transpose(jnp.concatenate(att_t, axis=0))
    for b in range(sites):
        block = att[b * rows : (b + 1) * rows].reshape(haps, rows // haps, width)
        att_out[pl.ds((me ^ b) * haps, haps)] = block.astype(BF16)


def column_step(
    sites, haps, xc, at, row_out, gain, col_proj, kv_t_w, col_out, ga_out, og_out, n_out, gp_out, at_out
):
    width = row_out.shape[0]
    heads = width // HEAD_DIM
    group = width // sites
    xc_all = flat_rows(xc[...], F32)
    rows = xc_all.shape[0]
    per = rows // haps
    cot_f = xc_all[:, width:]
    cot = cot_f.astype(BF16)
    hid = xc_all[:, :width]
    for i in range(sites):
        a_i = flat_rows(at[i * haps : (i + 1) * haps])
        hid = hid + mm(a_i, row_out[i * group : (i + 1) * group, :])
    hid = hid.astype(BF16).astype(F32)
    grad_att = mm_nt(cot, col_out[...]).astype(BF16)
    xhat, rstd = norm_parts(hid)
    normed = (xhat * gain[...]).astype(BF16)
    n_out[...] = normed
    packed = mm(normed, col_proj[...]).astype(BF16)
    q = packed[:, :width]
    key = packed[:, width : 2 * width]
    val = packed[:, 2 * width :]
    kv_t = mm_nt(kv_t_w[...], normed).astype(BF16)
    key_st = jnp.concatenate([only_head(key, h) for h in range(heads)], axis=0)
    val_st = jnp.concatenate([only_head(val, h) for h in range(heads)], axis=0)
    scores = mm_nt(key_st, q) * (SCALE * LOG2E)
    dprob = mm_nt(val_st, grad_att)
    same = (
        lax.broadcasted_iota(jnp.int32, (rows, rows), 0) % per
        == lax.broadcasted_iota(jnp.int32, (rows, rows), 1) % per
    )
    att_t, dq_t, prob16, ds16 = [], [], [], []
    for h in range(heads):
        cols = slice(h * HEAD_DIM, (h + 1) * HEAD_DIM)
        s_h = jnp.where(same, scores[h * rows : (h + 1) * rows], -jnp.inf)
        e_h = jnp.exp2(s_h - jnp.max(s_h, axis=0, keepdims=True))
        inverse = 1.0 / jnp.sum(e_h, axis=0, keepdims=True)
        att_t.append(mm(kv_t[width:, :][cols], e_h.astype(BF16)) * inverse)
        p_h = e_h * inverse
        d_h = dprob[h * rows : (h + 1) * rows]
        delta = jnp.sum(p_h * d_h, axis=0, keepdims=True)
        ds_h = (p_h * (d_h - delta)).astype(BF16)
        prob16.append(p_h.astype(BF16))
        ds16.append(ds_h)
        dq_t.append(mm(kv_t[:width, :][cols], ds_h))
    att_t = jnp.concatenate(att_t, axis=0)
    at_out[...] = att_t.astype(BF16)
    att = jnp.transpose(att_t).astype(BF16)
    out = hid + mm(att, col_out[...])
    dv_all = mm(jnp.concatenate(prob16, axis=0), grad_att)
    dk_all = mm(jnp.concatenate(ds16, axis=0), q)
    dv = sum(
        jnp.where(head_lanes(width, h), dv_all[h * rows : (h + 1) * rows], 0.0) for h in range(heads)
    )
    dk = sum(
        jnp.where(head_lanes(width, h), dk_all[h * rows : (h + 1) * rows], 0.0) for h in range(heads)
    )
    dq = jnp.transpose(jnp.concatenate(dq_t, axis=0))
    packed_grad = jnp.concatenate([dq * SCALE, dk * SCALE, dv], axis=1).astype(BF16)
    gp_out[...] = packed_grad
    grad_normed = mm_nt(packed_grad, col_proj[...])
    grad_hidden = (cot_f + norm_back(xhat, rstd, gain[...], grad_normed)).astype(BF16)
    for i in range(sites):
        g_i = mm_nt(grad_hidden, row_out[i * group : (i + 1) * group, :])
        ga_out[i * haps : (i + 1) * haps] = g_i.reshape(haps, per, group).astype(BF16)
    both = jnp.concatenate([out, grad_hidden.astype(F32)], axis=1)
    og_out[...] = both.reshape(haps, per, 2 * width).astype(BF16)


def column_weights(sites, haps, xc, at, og, normed, gp, att_t, w_out):
    width = normed.shape[1]
    group = width // sites
    cot = flat_rows(xc[:, :, width:])
    grad_hidden = flat_rows(og[:, :, width:])
    w_out[:, : 3 * width] = mm_tn(normed[...], gp[...]).astype(BF16)
    w_out[:, 3 * width : 4 * width] = mm(att_t[...], cot).astype(BF16)
    for i in range(sites):
        a_i = flat_rows(at[i * haps : (i + 1) * haps])
        w_out[i * group : (i + 1) * group, 4 * width :] = mm_tn(a_i, grad_hidden).astype(BF16)


def row_backward(sites, haps, idx, g_in, prob, q, val, key_t, normed, *refs):
    gp_outs = refs[:sites]
    w_out, g_all, ds_all = refs[sites:]
    me = idx[0]
    total, width = q.shape
    rows = total // sites
    for b in range(sites):
        g_all[b * rows : (b + 1) * rows, :] = flat_rows(g_in[pl.ds((me ^ b) * haps, haps)])
    dk = jnp.zeros((total, width), F32)
    dv = jnp.zeros((total, width), F32)
    dq_t = []
    for h in range(width // HEAD_DIM):
        val_h = only_head(val[...], h)
        dv = dv + mm(prob[h], only_head(g_all[...], h))
        for b in range(sites):
            here = pl.ds(b * rows, rows)
            dprob = mm_nt(val_h, g_all[b * rows : (b + 1) * rows, :])
            p_b = prob[h, :, here].astype(F32)
            delta = jnp.sum(p_b * dprob, axis=0, keepdims=True)
            ds_all[:, here] = (p_b * (dprob - delta)).astype(BF16)
        dk = dk + mm(ds_all[...], only_head(q[...], h))
        dq_t.append(mm(key_t[h * HEAD_DIM : (h + 1) * HEAD_DIM, :], ds_all[...]))
    dq_t = jnp.concatenate(dq_t, axis=0) * SCALE
    dk16 = (dk * SCALE).astype(BF16)
    dv16 = dv.astype(BF16)
    w_out[:width, :] = mm(dq_t.astype(BF16), normed[...]).astype(BF16)
    w_out[width : 2 * width, :] = mm_tn(dk16, normed[...]).astype(BF16)
    w_out[2 * width :, :] = mm_tn(dv16, normed[...]).astype(BF16)
    dq = jnp.transpose(dq_t).astype(BF16)
    joined = jnp.concatenate([dq, dk16, dv16], axis=1)
    for b in range(sites):
        gp_outs[b][...] = joined[b * rows : (b + 1) * rows]


def row_finish(sites, idx, feats, gain, w_all, og, *refs):
    gps = refs[:sites]
    out_ref, gf_ref = refs[sites:]
    me = idx[0]
    width = feats.shape[1]
    both = flat_rows(og[...], F32)
    grad_normed = sum(mm(gps[k][...], w_all[me ^ k]) for k in range(sites))
    xhat, rstd = norm_parts(feats[...].astype(F32))
    grad = both[:, width:] + norm_back(xhat, rstd, gain[...], grad_normed)
    out_ref[...] = both[:, :width].astype(BF16)
    gf_ref[...] = grad.astype(BF16)


def sum_parts(x_ref, o_ref):
    o_ref[...] = jnp.sum(x_ref[...].astype(F32), axis=0).astype(BF16)


def weights_finish(sites, row_w, col_w, rp, ro, cp, co):
    width = ro.shape[0]
    group = width // sites
    cols = flat_rows(col_w[...], F32)
    cp[...] = cols[:, : 3 * width]
    co[...] = cols[:, 3 * width : 4 * width]
    ro[...] = cols[:, 4 * width :]
    rows = flat_rows(row_w[...], F32)
    ordered = [
        rows[(3 * i + part) * group : (3 * i + part + 1) * group]
        for part in range(3)
        for i in range(sites)
    ]
    rp[...] = jnp.transpose(jnp.concatenate(ordered, axis=0))


def exchange(value, axis):
    return lax.all_to_all(value, axis, 0, 0, tiled=True)


def swapped(value, axis, by):
    length = lax.axis_size(axis)
    return lax.ppermute(value, axis, [(i, i ^ by) for i in range(length)])


def spread(value, axis, length):
    return exchange(jnp.broadcast_to(value[None], (length,) + value.shape), axis)


def on_device(
    features,
    link_pattern,
    row_gain,
    row_proj,
    row_out,
    column_norm_gain,
    col_proj,
    col_out,
    cotangent,
):
    rows, _, width = features.shape
    sites, haps = lax.axis_size("site"), lax.axis_size("hap")
    count = sites * haps
    per = rows // haps
    group = width // sites
    heads = group // HEAD_DIM
    total = rows * sites
    both_axes = ("site", "hap")
    me = lax.axis_index("site")
    idx = me.reshape(1).astype(jnp.int32)
    feats = features.reshape(rows, width)
    cot = cotangent.reshape(rows, width)
    gain_r = row_gain.reshape(1, width)
    gain_c = column_norm_gain.reshape(1, width)

    pieces = [feats] + [swapped(feats, "site", k) for k in range(1, sites)]
    xc = exchange(jnp.concatenate([feats, cot], axis=1).reshape(haps, per, 2 * width), "hap")
    w_all = jnp.transpose(row_proj.reshape(width, 3, sites, group), (2, 1, 3, 0)).reshape(
        sites, 3 * group, width
    )
    w_t = lax.dynamic_index_in_dim(w_all, me, 0, keepdims=False)
    kv_t_w = jnp.transpose(col_proj[:, width:])

    att, prob, q, val, key_t, normed = call(
        functools.partial(row_forward, sites, haps),
        [
            ((count, per, group), BF16),
            ((heads, total, total), BF16),
            ((total, group), BF16),
            ((total, group), BF16),
            ((group, total), BF16),
            ((total, width), BF16),
        ],
        idx, link_pattern, *pieces, gain_r, w_t, scalars=2,
    )
    at = exchange(att, both_axes)
    ga, og, col_normed, col_gp, col_att_t = call(
        functools.partial(column_step, sites, haps),
        [
            ((count, per, group), BF16),
            ((haps, per, 2 * width), BF16),
            ((rows, width), BF16),
            ((rows, 3 * width), BF16),
            ((width, rows), BF16),
        ],
        xc, at, row_out, gain_c, col_proj, kv_t_w, col_out,
    )
    g_in = exchange(ga, both_axes)
    (col_w,) = call(
        functools.partial(column_weights, sites, haps),
        [((width, 5 * width), BF16)],
        xc, at, og, col_normed, col_gp, col_att_t,
    )
    og_in = exchange(og, "hap")
    *gps, row_w = call(
        functools.partial(row_backward, sites, haps),
        [((rows, 3 * group), BF16)] * sites + [((3 * group, width), BF16)],
        idx, g_in, prob, q, val, key_t, normed, scalars=1,
        scratch=[pltpu.VMEM((total, group), BF16), pltpu.VMEM((total, total), BF16)],
    )
    col_parts = exchange(col_w.reshape(count, width // count, 5 * width), both_axes)
    (col_mine,) = call(sum_parts, [((width // count, 5 * width), BF16)], col_parts)
    row_parts = exchange(row_w.reshape(haps, 3 * group // haps, width), "hap")
    (row_mine,) = call(sum_parts, [((3 * group // haps, width), BF16)], row_parts)
    gps = [gps[0]] + [swapped(gps[k], "site", k) for k in range(1, sites)]
    out, grad = call(
        functools.partial(row_finish, sites),
        [((rows, width), BF16)] * 2,
        idx, feats, gain_r, w_all, og_in, *gps, scalars=1,
    )
    col_full = spread(col_mine, both_axes, count)
    row_full = spread(row_mine, both_axes, count)
    rp, ro, cp, co = call(
        functools.partial(weights_finish, sites),
        [((width, 3 * width), F32), ((width, width), F32)] * 2,
        row_full, col_full,
    )
    shape = (rows, 1, width)
    return (out.reshape(shape), grad.reshape(shape), rp, ro, cp, co)


def solution(mesh):
    data = P("site", "hap", None)
    return jax.shard_map(
        on_device,
        mesh=mesh,
        in_specs=(data, P(), P(), P(), P(), P(), P(), P(), data),
        out_specs=(data, data, P(), P(), P(), P()),
        check_vma=False,
    )
```

```python
import functools

import jax
import jax.numpy as jnp
from jax import lax
from jax.experimental import pallas as pl
from jax.experimental.pallas import tpu as pltpu
from jax.sharding import PartitionSpec as P

HEAD_DIM = 32
EPSILON = 1e-05
LOG2E = 1.4426950408889634
SCALE = HEAD_DIM ** (-0.5)
F32 = jnp.float32
BF16 = jnp.bfloat16
VMEM = pl.BlockSpec(memory_space=pltpu.VMEM)
SMEM = pl.BlockSpec(memory_space=pltpu.SMEM)
PARAMS = pltpu.CompilerParams(vmem_limit_bytes=48 << 20)


def mm(a, b):
    return lax.dot_general(a, b, (((1,), (0,)), ((), ())), preferred_element_type=F32)


def mm_nt(a, b):
    return lax.dot_general(a, b, (((1,), (1,)), ((), ())), preferred_element_type=F32)


def mm_tn(a, b):
    return lax.dot_general(a, b, (((0,), (0,)), ((), ())), preferred_element_type=F32)


def norm_parts(x):
    centred = x - jnp.mean(x, axis=-1, keepdims=True)
    rstd = lax.rsqrt(jnp.mean(centred * centred, axis=-1, keepdims=True) + EPSILON)
    return centred * rstd, rstd


def norm_back(xhat, rstd, gain, grad):
    scaled = grad * gain
    first = jnp.mean(scaled, axis=-1, keepdims=True)
    second = jnp.mean(scaled * xhat, axis=-1, keepdims=True)
    return rstd * (scaled - first - xhat * second)


def head_lanes(width, head):
    return lax.broadcasted_iota(jnp.int32, (1, width), 1) // HEAD_DIM == head


def only_head(values, head):
    return jnp.where(head_lanes(values.shape[1], head), values, jnp.zeros_like(values))


def flat_rows(values, dtype=BF16):
    wide = values.astype(F32)
    return wide.reshape(wide.shape[0] * wide.shape[1], wide.shape[2]).astype(dtype)


def lane_factor(rows, width):
    factor = 128 // width
    return factor if (rows // factor) % 8 == 0 else 1


def pack_block(values, outer):
    rows, width = values.shape[0] // outer, values.shape[1]
    factor = lane_factor(rows, width)
    split = values.reshape(outer, factor, rows // factor, width)
    return jnp.concatenate([split[:, j] for j in range(factor)], axis=2).astype(BF16)


def unpack_block(values, width):
    wide = values.astype(F32)
    factor = wide.shape[2] // width
    split = [wide[:, None, :, j * width : (j + 1) * width] for j in range(factor)]
    joined = jnp.concatenate(split, axis=1)
    return joined.reshape(-1, width).astype(BF16)


def call(body, outs, *operands, scalars=0, scratch=()):
    return pl.pallas_call(
        body,
        out_shape=[jax.ShapeDtypeStruct(s, d) for s, d in outs],
        in_specs=[SMEM] * scalars + [VMEM] * (len(operands) - scalars),
        out_specs=[VMEM] * len(outs),
        scratch_shapes=list(scratch),
        compiler_params=PARAMS,
    )(*operands)


def row_forward(sites, haps, idx, link, *refs):
    pieces = refs[:sites]
    gain, w_t = refs[sites : sites + 2]
    att_out, p_out, q_out, v_out, kt_out, n_out = refs[sites + 2 :]
    me = idx[0]
    rows = pieces[0].shape[0]
    width = q_out.shape[1]
    for k in range(sites):
        xhat, _ = norm_parts(pieces[k][...].astype(F32))
        n_out[k * rows : (k + 1) * rows, :] = (xhat * gain[...]).astype(BF16)
    normed = n_out[...]
    q = mm_nt(normed, w_t[:width, :]).astype(BF16)
    key = mm_nt(normed, w_t[width : 2 * width, :]).astype(BF16)
    q_out[...] = q
    v_out[...] = mm_nt(normed, w_t[2 * width :, :]).astype(BF16)
    kt_out[...] = mm_nt(w_t[width : 2 * width, :], normed).astype(BF16)
    v_t = mm_nt(w_t[2 * width :, :], normed).astype(BF16)
    att_t = []
    for h in range(width // HEAD_DIM):
        key_h = only_head(key, h)
        for b in range(sites):
            here = pl.ds(b * rows, rows)
            scores = mm_nt(key_h, q[b * rows : (b + 1) * rows]) * (SCALE * LOG2E)
            parts = [
                scores[a * rows : (a + 1) * rows]
                + jnp.where(link[me ^ b, me ^ a] > 0, 0.0, -jnp.inf)
                for a in range(sites)
            ]
            high = functools.reduce(
                jnp.maximum, [jnp.max(part, axis=0, keepdims=True) for part in parts]
            )
            parts = [jnp.exp2(part - high) for part in parts]
            total = sum(jnp.sum(part, axis=0, keepdims=True) for part in parts)
            inverse = 1.0 / total
            for a in range(sites):
                p_out[h, a * rows : (a + 1) * rows, here] = (parts[a] * inverse).astype(BF16)
        att_t.append(mm(v_t[h * HEAD_DIM : (h + 1) * HEAD_DIM], p_out[h]))
    att = jnp.transpose(jnp.concatenate(att_t, axis=0))
    for b in range(sites):
        att_out[pl.ds((me ^ b) * haps, haps)] = pack_block(att[b * rows : (b + 1) * rows], haps)


def column_step(
    sites, haps, xc, at, row_out, gain, col_proj, kv_t_w, col_out, ga_out, og_out, n_out, gp_out, at_out
):
    width = row_out.shape[0]
    heads = width // HEAD_DIM
    group = width // sites
    xc_all = flat_rows(xc[...], F32)
    rows = xc_all.shape[0]
    per = rows // haps
    cot_f = xc_all[:, width:]
    cot = cot_f.astype(BF16)
    hid = xc_all[:, :width]
    for i in range(sites):
        a_i = unpack_block(at[i * haps : (i + 1) * haps], group)
        hid = hid + mm(a_i, row_out[i * group : (i + 1) * group, :])
    hid = hid.astype(BF16).astype(F32)
    grad_att = mm_nt(cot, col_out[...]).astype(BF16)
    xhat, rstd = norm_parts(hid)
    normed = (xhat * gain[...]).astype(BF16)
    n_out[...] = normed
    packed = mm(normed, col_proj[...]).astype(BF16)
    q = packed[:, :width]
    key = packed[:, width : 2 * width]
    val = packed[:, 2 * width :]
    kv_t = mm_nt(kv_t_w[...], normed).astype(BF16)
    key_st = jnp.concatenate([only_head(key, h) for h in range(heads)], axis=0)
    val_st = jnp.concatenate([only_head(val, h) for h in range(heads)], axis=0)
    scores = mm_nt(key_st, q) * (SCALE * LOG2E)
    dprob = mm_nt(val_st, grad_att)
    same = (
        lax.broadcasted_iota(jnp.int32, (rows, rows), 0) % per
        == lax.broadcasted_iota(jnp.int32, (rows, rows), 1) % per
    )
    att_t, dq_t, prob16, ds16 = [], [], [], []
    for h in range(heads):
        cols = slice(h * HEAD_DIM, (h + 1) * HEAD_DIM)
        s_h = jnp.where(same, scores[h * rows : (h + 1) * rows], -jnp.inf)
        e_h = jnp.exp2(s_h - jnp.max(s_h, axis=0, keepdims=True))
        inverse = 1.0 / jnp.sum(e_h, axis=0, keepdims=True)
        att_t.append(mm(kv_t[width:, :][cols], e_h.astype(BF16)) * inverse)
        p_h = e_h * inverse
        d_h = dprob[h * rows : (h + 1) * rows]
        delta = jnp.sum(p_h * d_h, axis=0, keepdims=True)
        ds_h = (p_h * (d_h - delta)).astype(BF16)
        prob16.append(p_h.astype(BF16))
        ds16.append(ds_h)
        dq_t.append(mm(kv_t[:width, :][cols], ds_h))
    att_t = jnp.concatenate(att_t, axis=0)
    at_out[...] = att_t.astype(BF16)
    att = jnp.transpose(att_t).astype(BF16)
    out = hid + mm(att, col_out[...])
    dv_all = mm(jnp.concatenate(prob16, axis=0), grad_att)
    dk_all = mm(jnp.concatenate(ds16, axis=0), q)
    dv = sum(
        jnp.where(head_lanes(width, h), dv_all[h * rows : (h + 1) * rows], 0.0) for h in range(heads)
    )
    dk = sum(
        jnp.where(head_lanes(width, h), dk_all[h * rows : (h + 1) * rows], 0.0) for h in range(heads)
    )
    dq = jnp.transpose(jnp.concatenate(dq_t, axis=0))
    packed_grad = jnp.concatenate([dq * SCALE, dk * SCALE, dv], axis=1).astype(BF16)
    gp_out[...] = packed_grad
    grad_normed = mm_nt(packed_grad, col_proj[...])
    grad_hidden = (cot_f + norm_back(xhat, rstd, gain[...], grad_normed)).astype(BF16)
    for i in range(sites):
        g_i = mm_nt(grad_hidden, row_out[i * group : (i + 1) * group, :])
        ga_out[i * haps : (i + 1) * haps] = pack_block(g_i, haps)
    both = jnp.concatenate([out, grad_hidden.astype(F32)], axis=1)
    og_out[...] = both.reshape(haps, per, 2 * width).astype(BF16)


def column_weights(sites, haps, core, xc, at, og, normed, gp, att_t, keep, send, both):
    width = normed.shape[1]
    group = width // sites
    half = width // 2
    cot = flat_rows(xc[:, :, width:])
    grad_hidden = flat_rows(og[:, :, width:])
    both[:, : 3 * width] = mm_tn(normed[...], gp[...]).astype(BF16)
    both[:, 3 * width : 4 * width] = mm(att_t[...], cot).astype(BF16)
    for i in range(sites):
        a_i = unpack_block(at[i * haps : (i + 1) * haps], group)
        both[i * group : (i + 1) * group, 4 * width :] = mm_tn(a_i, grad_hidden).astype(BF16)
    keep[...] = both[pl.ds(pl.multiple_of(core[0] * half, half), half), :]
    send[...] = both[pl.ds(pl.multiple_of((1 - core[0]) * half, half), half), :]


def column_split(sites, idx, keep, got, *refs):
    outs, both = refs[:sites], refs[sites]
    both[...] = (keep[...].astype(F32) + got[...].astype(F32)).astype(BF16)
    part = keep.shape[0] // sites
    for k in range(sites):
        outs[k][...] = both[pl.ds(pl.multiple_of((idx[0] ^ k) * part, part), part), :]


def row_backward(sites, haps, idx, core, g_in, prob, q, val, key_t, normed, *refs):
    gp_outs = refs[:sites]
    keep, send, g_all, ds_all, w_out = refs[sites:]
    me = idx[0]
    total, width = q.shape
    rows = total // sites
    for b in range(sites):
        g_all[b * rows : (b + 1) * rows, :] = unpack_block(
            g_in[pl.ds((me ^ b) * haps, haps)], width
        )
    dk = jnp.zeros((total, width), F32)
    dv = jnp.zeros((total, width), F32)
    dq_t = []
    for h in range(width // HEAD_DIM):
        val_h = only_head(val[...], h)
        dv = dv + mm(prob[h], only_head(g_all[...], h))
        for b in range(sites):
            here = pl.ds(b * rows, rows)
            dprob = mm_nt(val_h, g_all[b * rows : (b + 1) * rows, :])
            p_b = prob[h, :, here].astype(F32)
            delta = jnp.sum(p_b * dprob, axis=0, keepdims=True)
            ds_all[:, here] = (p_b * (dprob - delta)).astype(BF16)
        dk = dk + mm(ds_all[...], only_head(q[...], h))
        dq_t.append(mm(key_t[h * HEAD_DIM : (h + 1) * HEAD_DIM, :], ds_all[...]))
    dq_t = jnp.concatenate(dq_t, axis=0) * SCALE
    dk16 = (dk * SCALE).astype(BF16)
    dv16 = dv.astype(BF16)
    w_out[:width, :] = mm(dq_t.astype(BF16), normed[...]).astype(BF16)
    w_out[width : 2 * width, :] = mm_tn(dk16, normed[...]).astype(BF16)
    w_out[2 * width :, :] = mm_tn(dv16, normed[...]).astype(BF16)
    half = 3 * width // 2
    keep[...] = w_out[pl.ds(pl.multiple_of(core[0] * half, half), half), :]
    send[...] = w_out[pl.ds(pl.multiple_of((1 - core[0]) * half, half), half), :]
    dq = jnp.transpose(dq_t).astype(BF16)
    joined = jnp.concatenate([dq, dk16, dv16], axis=1)
    for b in range(sites):
        gp_outs[b][...] = joined[b * rows : (b + 1) * rows]


def row_finish(sites, idx, feats, gain, w_all, og, *refs):
    gps = refs[:sites]
    out_ref, gf_ref = refs[sites:]
    me = idx[0]
    width = feats.shape[1]
    both = flat_rows(og[...], F32)
    grad_normed = sum(mm(gps[k][...], w_all[me ^ k]) for k in range(sites))
    xhat, rstd = norm_parts(feats[...].astype(F32))
    grad = both[:, width:] + norm_back(xhat, rstd, gain[...], grad_normed)
    out_ref[...] = both[:, :width].astype(BF16)
    gf_ref[...] = grad.astype(BF16)


def weights_join(row_keep, row_got, *refs):
    cols, out = refs[:-1], refs[-1]
    half, width = row_keep.shape
    out[:half, :] = (row_keep[...].astype(F32) + row_got[...].astype(F32)).astype(BF16)
    total = sum(c[...].astype(F32) for c in cols)
    part = total.shape[0]
    for t in range(5):
        tile = total[:, t * width : (t + 1) * width]
        out[half + t * part : half + (t + 1) * part, :] = tile.astype(BF16)


def weights_sum(*refs):
    terms = [r[...].astype(F32) for r in refs[:-1]]
    while len(terms) > 1:
        terms = [a + b for a, b in zip(terms[::2], terms[1::2])]
    refs[-1][...] = terms[0].astype(BF16)


def weights_finish(sites, idx, core, *refs):
    pieces = refs[: 2 * sites]
    rp, ro, cp, co, rows_t = refs[2 * sites :]
    width = ro.shape[0]
    group = width // sites
    unit = group // 2
    part = width // 2 // sites
    for j in range(2 * sites):
        k = j // 2
        cc = core[0] ^ (j % 2)
        g = idx[0] ^ k
        piece = pieces[j][...].astype(F32)
        for u in range(3):
            place = 3 * cc + u
            dest = (place // 2) * width + g * group + (place % 2) * unit
            rows_t[pl.ds(pl.multiple_of(dest, unit), unit), :] = piece[u * unit : (u + 1) * unit]
        here = pl.ds(pl.multiple_of(cc * (width // 2) + g * part, part), part)
        tiles = [piece[3 * unit + t * part : 3 * unit + (t + 1) * part] for t in range(5)]
        for t in range(3):
            cp[here, t * width : (t + 1) * width] = tiles[t]
        co[here, :] = tiles[3]
        ro[here, :] = tiles[4]
    rp[...] = jnp.transpose(rows_t[...])


def exchange(value, axis):
    return lax.all_to_all(value, axis, 0, 0, tiled=True)


def swapped(value, axis, by):
    length = lax.axis_size(axis)
    return lax.ppermute(value, axis, [(i, i ^ by) for i in range(length)])


def on_device(
    features,
    link_pattern,
    row_gain,
    row_proj,
    row_out,
    column_norm_gain,
    col_proj,
    col_out,
    cotangent,
):
    rows, _, width = features.shape
    sites, haps = lax.axis_size("site"), lax.axis_size("hap")
    count = sites * haps
    per = rows // haps
    group = width // sites
    heads = group // HEAD_DIM
    total = rows * sites
    both_axes = ("site", "hap")
    me = lax.axis_index("site")
    idx = me.reshape(1).astype(jnp.int32)
    core = (lax.axis_index("hap") % 2).reshape(1).astype(jnp.int32)
    factor = lane_factor(per, group)
    block = ((count, per // factor, group * factor), BF16)
    feats = features.reshape(rows, width)
    cot = cotangent.reshape(rows, width)
    gain_r = row_gain.reshape(1, width)
    gain_c = column_norm_gain.reshape(1, width)

    pieces = [feats] + [swapped(feats, "site", k) for k in range(1, sites)]
    xc = exchange(jnp.concatenate([feats, cot], axis=1).reshape(haps, per, 2 * width), "hap")
    w_all = jnp.transpose(row_proj.reshape(width, 3, sites, group), (2, 1, 3, 0)).reshape(
        sites, 3 * group, width
    )
    w_t = lax.dynamic_index_in_dim(w_all, me, 0, keepdims=False)
    kv_t_w = jnp.transpose(col_proj[:, width:])

    att, prob, q, val, key_t, normed = call(
        functools.partial(row_forward, sites, haps),
        [
            block,
            ((heads, total, total), BF16),
            ((total, group), BF16),
            ((total, group), BF16),
            ((group, total), BF16),
            ((total, width), BF16),
        ],
        idx, link_pattern, *pieces, gain_r, w_t, scalars=2,
    )
    att, xc = lax.optimization_barrier((att, xc))
    at = exchange(att, both_axes)
    ga, og, col_normed, col_gp, col_att_t = call(
        functools.partial(column_step, sites, haps),
        [
            block,
            ((haps, per, 2 * width), BF16),
            ((rows, width), BF16),
            ((rows, 3 * width), BF16),
            ((width, rows), BF16),
        ],
        xc, at, row_out, gain_c, col_proj, kv_t_w, col_out,
    )
    g_in = exchange(ga, both_axes)
    half = width // 2
    col_keep, col_send = call(
        functools.partial(column_weights, sites, haps),
        [((half, 5 * width), BF16)] * 2,
        core, xc, at, og, col_normed, col_gp, col_att_t, scalars=1,
        scratch=[pltpu.VMEM((width, 5 * width), BF16)],
    )
    col_got = swapped(col_send, "hap", 1)
    cols = call(
        functools.partial(column_split, sites),
        [((half // sites, 5 * width), BF16)] * sites,
        idx, col_keep, col_got, scalars=1,
        scratch=[pltpu.VMEM((half, 5 * width), BF16)],
    )
    g_in, cols = lax.optimization_barrier((g_in, cols))
    cols = [cols[0]] + [swapped(cols[k], "site", k) for k in range(1, sites)]
    *gps, row_keep, row_send = call(
        functools.partial(row_backward, sites, haps),
        [((rows, 3 * group), BF16)] * sites + [((3 * group // 2, width), BF16)] * 2,
        idx, core, g_in, prob, q, val, key_t, normed, scalars=2,
        scratch=[
            pltpu.VMEM((total, group), BF16),
            pltpu.VMEM((total, total), BF16),
            pltpu.VMEM((3 * group, width), BF16),
        ],
    )
    row_got = swapped(row_send, "hap", 1)
    depth = 3 * group // 2 + 5 * half // sites
    (joined,) = call(weights_join, [((depth, width), BF16)], row_keep, row_got, *cols)
    parts = [joined] + [swapped(joined, "hap", 2 * m) for m in range(1, haps // 2)]
    (mine,) = call(weights_sum, [((depth, width), BF16)], *parts)
    og, _ = lax.optimization_barrier((og, row_keep))
    og_in = exchange(og, "hap")
    gps = [gps[0]] + [swapped(gps[k], "site", k) for k in range(1, sites)]
    out, grad = call(
        functools.partial(row_finish, sites),
        [((rows, width), BF16)] * 2,
        idx, feats, gain_r, w_all, og_in, *gps, scalars=1,
    )
    full = [mine] + [swapped(mine, "site", k) for k in range(1, sites)]
    full = [x for piece in full for x in (piece, swapped(piece, "hap", 1))]
    rp, ro, cp, co = call(
        functools.partial(weights_finish, sites),
        [((width, 3 * width), F32), ((width, width), F32)] * 2,
        idx, core, *full, scalars=2,
        scratch=[pltpu.VMEM((3 * width, width), F32)],
    )
    shape = (rows, 1, width)
    return (out.reshape(shape), grad.reshape(shape), rp, ro, cp, co)


def solution(mesh):
    data = P("site", "hap", None)
    return jax.shard_map(
        on_device,
        mesh=mesh,
        in_specs=(data, P(), P(), P(), P(), P(), P(), P(), data),
        out_specs=(data, data, P(), P(), P(), P()),
        check_vma=False,
    )
```

```python
import functools

import jax
import jax.numpy as jnp
from jax import lax
from jax.experimental import pallas as pl
from jax.experimental.pallas import tpu as pltpu
from jax.sharding import PartitionSpec as P

HEAD_DIM = 32
EPSILON = 1e-05
LOG2E = 1.4426950408889634
SCALE = HEAD_DIM ** (-0.5)
F32 = jnp.float32
BF16 = jnp.bfloat16
VMEM = pl.BlockSpec(memory_space=pltpu.VMEM)
SMEM = pl.BlockSpec(memory_space=pltpu.SMEM)
PARAMS = pltpu.CompilerParams(vmem_limit_bytes=48 << 20)


def mm(a, b):
    return lax.dot_general(a, b, (((1,), (0,)), ((), ())), preferred_element_type=F32)


def mm_nt(a, b):
    return lax.dot_general(a, b, (((1,), (1,)), ((), ())), preferred_element_type=F32)


def mm_tn(a, b):
    return lax.dot_general(a, b, (((0,), (0,)), ((), ())), preferred_element_type=F32)


def norm_parts(x):
    centred = x - jnp.mean(x, axis=-1, keepdims=True)
    rstd = lax.rsqrt(jnp.mean(centred * centred, axis=-1, keepdims=True) + EPSILON)
    return centred * rstd, rstd


def norm_back(xhat, rstd, gain, grad):
    scaled = grad * gain
    first = jnp.mean(scaled, axis=-1, keepdims=True)
    second = jnp.mean(scaled * xhat, axis=-1, keepdims=True)
    return rstd * (scaled - first - xhat * second)


def head_lanes(width, head):
    return lax.broadcasted_iota(jnp.int32, (1, width), 1) // HEAD_DIM == head


def only_head(values, head):
    return jnp.where(head_lanes(values.shape[1], head), values, jnp.zeros_like(values))


def flat_rows(values, dtype=BF16):
    wide = values.astype(F32)
    return wide.reshape(wide.shape[0] * wide.shape[1], wide.shape[2]).astype(dtype)


def lane_factor(rows, width):
    factor = 128 // width
    return factor if (rows // factor) % 8 == 0 else 1


def pack_block(values, outer):
    rows, width = values.shape[0] // outer, values.shape[1]
    factor = lane_factor(rows, width)
    split = values.reshape(outer, factor, rows // factor, width)
    return jnp.concatenate([split[:, j] for j in range(factor)], axis=2).astype(BF16)


def unpack_block(values, width):
    wide = values.astype(F32)
    factor = wide.shape[2] // width
    split = [wide[:, None, :, j * width : (j + 1) * width] for j in range(factor)]
    joined = jnp.concatenate(split, axis=1)
    return joined.reshape(-1, width).astype(BF16)


def call(body, outs, *operands, scalars=0, scratch=(), us=1):
    cost = pl.CostEstimate(flops=us * 10**9, bytes_accessed=us * 3_600_000, transcendentals=0)
    return pl.pallas_call(
        body,
        out_shape=[jax.ShapeDtypeStruct(s, d) for s, d in outs],
        in_specs=[SMEM] * scalars + [VMEM] * (len(operands) - scalars),
        out_specs=[VMEM] * len(outs),
        scratch_shapes=list(scratch),
        compiler_params=PARAMS,
        cost_estimate=cost,
    )(*operands)


def row_forward(sites, haps, idx, link, *refs):
    pieces = refs[:sites]
    gain, w_t = refs[sites : sites + 2]
    att_out, p_out, q_out, v_out, kt_out, n_out = refs[sites + 2 :]
    me = idx[0]
    rows = pieces[0].shape[0]
    width = q_out.shape[1]
    for k in range(sites):
        xhat, _ = norm_parts(pieces[k][...].astype(F32))
        n_out[k * rows : (k + 1) * rows, :] = (xhat * gain[:1, :]).astype(BF16)
    normed = n_out[...]
    q = mm_nt(normed, w_t[:width, :]).astype(BF16)
    key = mm_nt(normed, w_t[width : 2 * width, :]).astype(BF16)
    q_out[...] = q
    v_out[...] = mm_nt(normed, w_t[2 * width :, :]).astype(BF16)
    kt_out[...] = mm_nt(w_t[width : 2 * width, :], normed).astype(BF16)
    v_t = mm_nt(w_t[2 * width :, :], normed).astype(BF16)
    att_t = []
    for h in range(width // HEAD_DIM):
        key_h = only_head(key, h)
        for b in range(sites):
            here = pl.ds(b * rows, rows)
            scores = mm_nt(key_h, q[b * rows : (b + 1) * rows]) * (SCALE * LOG2E)
            parts = [
                scores[a * rows : (a + 1) * rows]
                + jnp.where(link[me ^ b, me ^ a] > 0, 0.0, -jnp.inf)
                for a in range(sites)
            ]
            high = functools.reduce(
                jnp.maximum, [jnp.max(part, axis=0, keepdims=True) for part in parts]
            )
            parts = [jnp.exp2(part - high) for part in parts]
            total = sum(jnp.sum(part, axis=0, keepdims=True) for part in parts)
            inverse = 1.0 / total
            for a in range(sites):
                p_out[h, a * rows : (a + 1) * rows, here] = (parts[a] * inverse).astype(BF16)
        att_t.append(mm(v_t[h * HEAD_DIM : (h + 1) * HEAD_DIM], p_out[h]))
    att = jnp.transpose(jnp.concatenate(att_t, axis=0))
    for b in range(sites):
        att_out[pl.ds((me ^ b) * haps, haps)] = pack_block(att[b * rows : (b + 1) * rows], haps)


def split_inputs(haps, hap, feats, cot, *outs):
    rows, width = feats.shape
    per = rows // haps
    for m in range(haps):
        here = pl.ds(pl.multiple_of((hap[0] ^ m) * per, per), per)
        outs[m][:, :width] = feats[here, :]
        outs[m][:, width:] = cot[here, :]


def column_step(sites, haps, hap, at, row_out, gain, col_proj, kv_t_w, col_out, *refs):
    ga_out, og_out, n_out, gp_out, at_out, cot_out, xc = refs[haps:]
    for m in range(haps):
        xc[hap[0] ^ m] = refs[m][...]
    width = row_out.shape[0]
    heads = width // HEAD_DIM
    group = width // sites
    xc_all = flat_rows(xc[...], F32)
    rows = xc_all.shape[0]
    per = rows // haps
    cot_f = xc_all[:, width:]
    cot = cot_f.astype(BF16)
    cot_out[...] = cot
    hid = xc_all[:, :width]
    for i in range(sites):
        a_i = unpack_block(at[i * haps : (i + 1) * haps], group)
        hid = hid + mm(a_i, row_out[i * group : (i + 1) * group, :])
    hid = hid.astype(BF16).astype(F32)
    grad_att = mm_nt(cot, col_out[...]).astype(BF16)
    xhat, rstd = norm_parts(hid)
    normed = (xhat * gain[1:2, :]).astype(BF16)
    n_out[...] = normed
    packed = mm(normed, col_proj[...]).astype(BF16)
    q = packed[:, :width]
    key = packed[:, width : 2 * width]
    val = packed[:, 2 * width :]
    kv_t = mm_nt(kv_t_w[...], normed).astype(BF16)
    key_st = jnp.concatenate([only_head(key, h) for h in range(heads)], axis=0)
    val_st = jnp.concatenate([only_head(val, h) for h in range(heads)], axis=0)
    scores = mm_nt(key_st, q) * (SCALE * LOG2E)
    dprob = mm_nt(val_st, grad_att)
    same = (
        lax.broadcasted_iota(jnp.int32, (rows, rows), 0) % per
        == lax.broadcasted_iota(jnp.int32, (rows, rows), 1) % per
    )
    att_t, dq_t, prob16, ds16 = [], [], [], []
    for h in range(heads):
        cols = slice(h * HEAD_DIM, (h + 1) * HEAD_DIM)
        s_h = jnp.where(same, scores[h * rows : (h + 1) * rows], -jnp.inf)
        e_h = jnp.exp2(s_h - jnp.max(s_h, axis=0, keepdims=True))
        inverse = 1.0 / jnp.sum(e_h, axis=0, keepdims=True)
        att_t.append(mm(kv_t[width:, :][cols], e_h.astype(BF16)) * inverse)
        p_h = e_h * inverse
        d_h = dprob[h * rows : (h + 1) * rows]
        delta = jnp.sum(p_h * d_h, axis=0, keepdims=True)
        ds_h = (p_h * (d_h - delta)).astype(BF16)
        prob16.append(p_h.astype(BF16))
        ds16.append(ds_h)
        dq_t.append(mm(kv_t[:width, :][cols], ds_h))
    att_t = jnp.concatenate(att_t, axis=0)
    at_out[...] = att_t.astype(BF16)
    att = jnp.transpose(att_t).astype(BF16)
    out = hid + mm(att, col_out[...])
    dv_all = mm(jnp.concatenate(prob16, axis=0), grad_att)
    dk_all = mm(jnp.concatenate(ds16, axis=0), q)
    dv = sum(
        jnp.where(head_lanes(width, h), dv_all[h * rows : (h + 1) * rows], 0.0) for h in range(heads)
    )
    dk = sum(
        jnp.where(head_lanes(width, h), dk_all[h * rows : (h + 1) * rows], 0.0) for h in range(heads)
    )
    dq = jnp.transpose(jnp.concatenate(dq_t, axis=0))
    packed_grad = jnp.concatenate([dq * SCALE, dk * SCALE, dv], axis=1).astype(BF16)
    gp_out[...] = packed_grad
    grad_normed = mm_nt(packed_grad, col_proj[...])
    grad_hidden = (cot_f + norm_back(xhat, rstd, gain[1:2, :], grad_normed)).astype(BF16)
    for i in range(sites):
        g_i = mm_nt(grad_hidden, row_out[i * group : (i + 1) * group, :])
        ga_out[i * haps : (i + 1) * haps] = pack_block(g_i, haps)
    both = jnp.concatenate([out, grad_hidden.astype(F32)], axis=1)
    og_out[...] = both.reshape(haps, per, 2 * width).astype(BF16)


def column_weights(sites, haps, core, cot, at, og, normed, gp, att_t, keep, send, both):
    width = normed.shape[1]
    group = width // sites
    half = width // 2
    grad_hidden = flat_rows(og[:, :, width:])
    both[:, : 3 * width] = mm_tn(normed[...], gp[...]).astype(BF16)
    both[:, 3 * width : 4 * width] = mm(att_t[...], cot[...]).astype(BF16)
    for i in range(sites):
        a_i = unpack_block(at[i * haps : (i + 1) * haps], group)
        both[i * group : (i + 1) * group, 4 * width :] = mm_tn(a_i, grad_hidden).astype(BF16)
    keep[...] = both[pl.ds(pl.multiple_of(core[0] * half, half), half), :]
    send[...] = both[pl.ds(pl.multiple_of((1 - core[0]) * half, half), half), :]


def column_split(sites, idx, keep, got, *refs):
    outs, both = refs[:sites], refs[sites]
    both[...] = (keep[...].astype(F32) + got[...].astype(F32)).astype(BF16)
    part = keep.shape[0] // sites
    for k in range(sites):
        outs[k][...] = both[pl.ds(pl.multiple_of((idx[0] ^ k) * part, part), part), :]


def row_backward(sites, haps, idx, core, g_in, prob, q, val, key_t, normed, *refs):
    gp_outs = refs[:sites]
    keep, send, g_all, ds_all, w_out = refs[sites:]
    me = idx[0]
    total, width = q.shape
    rows = total // sites
    for b in range(sites):
        g_all[b * rows : (b + 1) * rows, :] = unpack_block(
            g_in[pl.ds((me ^ b) * haps, haps)], width
        )
    dk = jnp.zeros((total, width), F32)
    dv = jnp.zeros((total, width), F32)
    dq_t = []
    for h in range(width // HEAD_DIM):
        val_h = only_head(val[...], h)
        dv = dv + mm(prob[h], only_head(g_all[...], h))
        for b in range(sites):
            here = pl.ds(b * rows, rows)
            dprob = mm_nt(val_h, g_all[b * rows : (b + 1) * rows, :])
            p_b = prob[h, :, here].astype(F32)
            delta = jnp.sum(p_b * dprob, axis=0, keepdims=True)
            ds_all[:, here] = (p_b * (dprob - delta)).astype(BF16)
        dk = dk + mm(ds_all[...], only_head(q[...], h))
        dq_t.append(mm(key_t[h * HEAD_DIM : (h + 1) * HEAD_DIM, :], ds_all[...]))
    dq_t = jnp.concatenate(dq_t, axis=0) * SCALE
    dk16 = (dk * SCALE).astype(BF16)
    dv16 = dv.astype(BF16)
    w_out[:width, :] = mm(dq_t.astype(BF16), normed[...]).astype(BF16)
    w_out[width : 2 * width, :] = mm_tn(dk16, normed[...]).astype(BF16)
    w_out[2 * width :, :] = mm_tn(dv16, normed[...]).astype(BF16)
    half = 3 * width // 2
    keep[...] = w_out[pl.ds(pl.multiple_of(core[0] * half, half), half), :]
    send[...] = w_out[pl.ds(pl.multiple_of((1 - core[0]) * half, half), half), :]
    dq = jnp.transpose(dq_t).astype(BF16)
    joined = jnp.concatenate([dq, dk16, dv16], axis=1)
    for b in range(sites):
        gp_outs[b][...] = joined[b * rows : (b + 1) * rows]


def row_finish(sites, idx, feats, gain, w_all, og, *refs):
    gps = refs[:sites]
    out_ref, gf_ref = refs[sites:]
    me = idx[0]
    width = feats.shape[1]
    both = flat_rows(og[...], F32)
    grad_normed = sum(mm(gps[k][...], w_all[me ^ k]) for k in range(sites))
    xhat, rstd = norm_parts(feats[...].astype(F32))
    grad = both[:, width:] + norm_back(xhat, rstd, gain[:1, :], grad_normed)
    out_ref[...] = both[:, :width].astype(BF16)
    gf_ref[...] = grad.astype(BF16)


def weights_join(row_keep, row_got, *refs):
    cols, out = refs[:-1], refs[-1]
    half, width = row_keep.shape
    out[:half, :] = (row_keep[...].astype(F32) + row_got[...].astype(F32)).astype(BF16)
    total = sum(c[...].astype(F32) for c in cols)
    part = total.shape[0]
    for t in range(5):
        tile = total[:, t * width : (t + 1) * width]
        out[half + t * part : half + (t + 1) * part, :] = tile.astype(BF16)


def weights_sum(*refs):
    terms = [r[...].astype(F32) for r in refs[:-1]]
    while len(terms) > 1:
        terms = [a + b for a, b in zip(terms[::2], terms[1::2])]
    refs[-1][...] = terms[0].astype(BF16)


def weights_finish(sites, idx, core, *refs):
    pieces = refs[: 2 * sites]
    rp, ro, cp, co, rows_t = refs[2 * sites :]
    width = ro.shape[0]
    group = width // sites
    unit = group // 2
    part = width // 2 // sites
    for j in range(2 * sites):
        k = j // 2
        cc = core[0] ^ (j % 2)
        g = idx[0] ^ k
        piece = pieces[j][...].astype(F32)
        for u in range(3):
            place = 3 * cc + u
            dest = (place // 2) * width + g * group + (place % 2) * unit
            rows_t[pl.ds(pl.multiple_of(dest, unit), unit), :] = piece[u * unit : (u + 1) * unit]
        here = pl.ds(pl.multiple_of(cc * (width // 2) + g * part, part), part)
        tiles = [piece[3 * unit + t * part : 3 * unit + (t + 1) * part] for t in range(5)]
        for t in range(3):
            cp[here, t * width : (t + 1) * width] = tiles[t]
        co[here, :] = tiles[3]
        ro[here, :] = tiles[4]
    rp[...] = jnp.transpose(rows_t[...])


def exchange(value, axis):
    return lax.all_to_all(value, axis, 0, 0, tiled=True)


def swapped(value, axis, by):
    length = lax.axis_size(axis)
    return lax.ppermute(value, axis, [(i, i ^ by) for i in range(length)])


def on_device(
    features,
    link_pattern,
    row_gain,
    row_proj,
    row_out,
    column_norm_gain,
    col_proj,
    col_out,
    cotangent,
):
    rows, _, width = features.shape
    sites, haps = lax.axis_size("site"), lax.axis_size("hap")
    count = sites * haps
    per = rows // haps
    group = width // sites
    heads = group // HEAD_DIM
    total = rows * sites
    both_axes = ("site", "hap")
    me = lax.axis_index("site")
    idx = me.reshape(1).astype(jnp.int32)
    hap = lax.axis_index("hap").reshape(1).astype(jnp.int32)
    core = hap % 2
    factor = lane_factor(per, group)
    block = ((count, per // factor, group * factor), BF16)
    feats = features.reshape(rows, width)
    cot = cotangent.reshape(rows, width)

    pieces = [feats] + [swapped(feats, "site", k) for k in range(1, sites)]
    gains = jnp.stack([row_gain, column_norm_gain])
    xcs = call(
        functools.partial(split_inputs, haps),
        [((per, 2 * width), BF16)] * haps,
        hap, feats, cot, scalars=1,
    )
    xcs = [xcs[0]] + [swapped(xcs[m], "hap", m) for m in range(1, haps)]
    w_all = jnp.transpose(row_proj.reshape(width, 3, sites, group), (2, 1, 3, 0)).reshape(
        sites, 3 * group, width
    )
    w_t = lax.dynamic_index_in_dim(w_all, me, 0, keepdims=False)
    kv_t_w = jnp.transpose(col_proj[:, width:])

    att, prob, q, val, key_t, normed = call(
        functools.partial(row_forward, sites, haps),
        [
            block,
            ((heads, total, total), BF16),
            ((total, group), BF16),
            ((total, group), BF16),
            ((group, total), BF16),
            ((total, width), BF16),
        ],
        idx, link_pattern, *pieces, gains, w_t, scalars=2, us=3,
    )
    at = exchange(att, both_axes)
    ga, og, col_normed, col_gp, col_att_t, cot = call(
        functools.partial(column_step, sites, haps),
        [
            block,
            ((haps, per, 2 * width), BF16),
            ((rows, width), BF16),
            ((rows, 3 * width), BF16),
            ((width, rows), BF16),
            ((rows, width), BF16),
        ],
        hap, at, row_out, gains, col_proj, kv_t_w, col_out, *xcs, scalars=1, us=3,
        scratch=[pltpu.VMEM((haps, per, 2 * width), BF16)],
    )
    g_in = exchange(ga, both_axes)
    half = width // 2
    col_keep, col_send = call(
        functools.partial(column_weights, sites, haps),
        [((half, 5 * width), BF16)] * 2,
        core, cot, at, og, col_normed, col_gp, col_att_t, scalars=1, us=2,
        scratch=[pltpu.VMEM((width, 5 * width), BF16)],
    )
    col_got = swapped(col_send, "hap", 1)
    cols = call(
        functools.partial(column_split, sites),
        [((half // sites, 5 * width), BF16)] * sites,
        idx, col_keep, col_got, scalars=1,
        scratch=[pltpu.VMEM((half, 5 * width), BF16)],
    )
    g_in, cols = lax.optimization_barrier((g_in, cols))
    cols = [cols[0]] + [swapped(cols[k], "site", k) for k in range(1, sites)]
    *gps, row_keep, row_send = call(
        functools.partial(row_backward, sites, haps),
        [((rows, 3 * group), BF16)] * sites + [((3 * group // 2, width), BF16)] * 2,
        idx, core, g_in, prob, q, val, key_t, normed, scalars=2, us=3,
        scratch=[
            pltpu.VMEM((total, group), BF16),
            pltpu.VMEM((total, total), BF16),
            pltpu.VMEM((3 * group, width), BF16),
        ],
    )
    row_got = swapped(row_send, "hap", 1)
    depth = 3 * group // 2 + 5 * half // sites
    (joined,) = call(weights_join, [((depth, width), BF16)], row_keep, row_got, *cols)
    parts = [joined] + [swapped(joined, "hap", 2 * m) for m in range(1, haps // 2)]
    gps = [gps[0]] + [swapped(gps[k], "site", k) for k in range(1, sites)]
    parts, gps = lax.optimization_barrier((parts, gps))
    (mine,) = call(weights_sum, [((depth, width), BF16)], *parts)
    og, _ = lax.optimization_barrier((og, mine))
    og_in = exchange(og, "hap")
    out, grad = call(
        functools.partial(row_finish, sites),
        [((rows, width), BF16)] * 2,
        idx, feats, gains, w_all, og_in, *gps, scalars=1,
    )
    full = [mine] + [swapped(mine, "site", k) for k in range(1, sites)]
    full = [x for piece in full for x in (piece, swapped(piece, "hap", 1))]
    rp, ro, cp, co = call(
        functools.partial(weights_finish, sites),
        [((width, 3 * width), F32), ((width, width), F32)] * 2,
        idx, core, *full, scalars=2,
        scratch=[pltpu.VMEM((3 * width, width), F32)],
    )
    shape = (rows, 1, width)
    return (out.reshape(shape), grad.reshape(shape), rp, ro, cp, co)


def solution(mesh):
    data = P("site", "hap", None)
    return jax.shard_map(
        on_device,
        mesh=mesh,
        in_specs=(data, P(), P(), P(), P(), P(), P(), P(), data),
        out_specs=(data, data, P(), P(), P(), P()),
        check_vma=False,
    )
```

```python
import functools

import jax
import jax.numpy as jnp
from jax import lax
from jax.experimental import pallas as pl
from jax.experimental.pallas import tpu as pltpu
from jax.sharding import PartitionSpec as P

HEAD_DIM = 32
EPSILON = 1e-05
LOG2E = 1.4426950408889634
SCALE = HEAD_DIM ** (-0.5)
F32 = jnp.float32
BF16 = jnp.bfloat16
VMEM = pl.BlockSpec(memory_space=pltpu.VMEM)
SMEM = pl.BlockSpec(memory_space=pltpu.SMEM)
PARAMS = pltpu.CompilerParams(vmem_limit_bytes=24 << 20)


def mm(a, b):
    return lax.dot_general(a, b, (((1,), (0,)), ((), ())), preferred_element_type=F32)


def mm_nt(a, b):
    return lax.dot_general(a, b, (((1,), (1,)), ((), ())), preferred_element_type=F32)


def mm_tn(a, b):
    return lax.dot_general(a, b, (((0,), (0,)), ((), ())), preferred_element_type=F32)


def norm_parts(x):
    centred = x - jnp.mean(x, axis=-1, keepdims=True)
    rstd = lax.rsqrt(jnp.mean(centred * centred, axis=-1, keepdims=True) + EPSILON)
    return centred * rstd, rstd


def norm_back(xhat, rstd, gain, grad):
    scaled = grad * gain
    first = jnp.mean(scaled, axis=-1, keepdims=True)
    second = jnp.mean(scaled * xhat, axis=-1, keepdims=True)
    return rstd * (scaled - first - xhat * second)


def head_lanes(width, head):
    return lax.broadcasted_iota(jnp.int32, (1, width), 1) // HEAD_DIM == head


def only_head(values, head):
    return jnp.where(head_lanes(values.shape[1], head), values, jnp.zeros_like(values))


def flat_rows(values, dtype=BF16):
    wide = values.astype(F32)
    return wide.reshape(wide.shape[0] * wide.shape[1], wide.shape[2]).astype(dtype)


def lane_factor(rows, width):
    factor = 128 // width
    return factor if (rows // factor) % 8 == 0 else 1


def pack_block(values, outer):
    rows, width = values.shape[0] // outer, values.shape[1]
    factor = lane_factor(rows, width)
    split = values.reshape(outer, factor, rows // factor, width)
    return jnp.concatenate([split[:, j] for j in range(factor)], axis=2).astype(BF16)


def unpack_block(values, width):
    wide = values.astype(F32)
    factor = wide.shape[2] // width
    split = [wide[:, None, :, j * width : (j + 1) * width] for j in range(factor)]
    joined = jnp.concatenate(split, axis=1)
    return joined.reshape(-1, width).astype(BF16)


def call(body, outs, *operands, scalars=0, scratch=(), us=0):
    cost = pl.CostEstimate(flops=us * 10**9 + 1, bytes_accessed=us * 3_600_000 + 1, transcendentals=0)
    return pl.pallas_call(
        body,
        out_shape=[jax.ShapeDtypeStruct(s, d) for s, d in outs],
        in_specs=[SMEM] * scalars + [VMEM] * (len(operands) - scalars),
        out_specs=[VMEM] * len(outs),
        scratch_shapes=list(scratch),
        compiler_params=PARAMS,
        cost_estimate=cost,
    )(*operands)


def row_forward(sites, haps, idx, link, *refs):
    pieces = refs[:sites]
    gain, w_t = refs[sites : sites + 2]
    att_out, p_out, q_out, v_out, kt_out, n_out = refs[sites + 2 :]
    me = idx[0]
    rows = pieces[0].shape[0]
    width = q_out.shape[1]
    for k in range(sites):
        xhat, _ = norm_parts(pieces[k][...].astype(F32))
        n_out[k * rows : (k + 1) * rows, :] = (xhat * gain[:1, :]).astype(BF16)
    normed = n_out[...]
    q = mm_nt(normed, w_t[:width, :]).astype(BF16)
    key = mm_nt(normed, w_t[width : 2 * width, :]).astype(BF16)
    q_out[...] = q
    v_out[...] = mm_nt(normed, w_t[2 * width :, :]).astype(BF16)
    kt_out[...] = mm_nt(w_t[width : 2 * width, :], normed).astype(BF16)
    v_t = mm_nt(w_t[2 * width :, :], normed).astype(BF16)
    att_t = []
    for h in range(width // HEAD_DIM):
        key_h = only_head(key, h)
        for b in range(sites):
            here = pl.ds(b * rows, rows)
            scores = mm_nt(key_h, q[b * rows : (b + 1) * rows]) * (SCALE * LOG2E)
            parts = [
                scores[a * rows : (a + 1) * rows]
                + jnp.where(link[me ^ b, me ^ a] > 0, 0.0, -jnp.inf)
                for a in range(sites)
            ]
            high = functools.reduce(
                jnp.maximum, [jnp.max(part, axis=0, keepdims=True) for part in parts]
            )
            parts = [jnp.exp2(part - high) for part in parts]
            total = sum(jnp.sum(part, axis=0, keepdims=True) for part in parts)
            inverse = 1.0 / total
            for a in range(sites):
                p_out[h, a * rows : (a + 1) * rows, here] = (parts[a] * inverse).astype(BF16)
        att_t.append(mm(v_t[h * HEAD_DIM : (h + 1) * HEAD_DIM], p_out[h]))
    att = jnp.transpose(jnp.concatenate(att_t, axis=0))
    for b in range(sites):
        att_out[pl.ds((me ^ b) * haps, haps)] = pack_block(att[b * rows : (b + 1) * rows], haps)


def join_inputs(feats, cot, out):
    haps, per, width = out.shape
    joined = jnp.concatenate([feats[...].astype(F32), cot[...].astype(F32)], axis=1)
    out[...] = joined.reshape(haps, per, width).astype(BF16)


def column_step(sites, haps, xc, at, row_out, gain, col_proj, kv_t_w, col_out, *refs):
    ga_out, og_out, n_out, gp_out, at_out, cot_out = refs
    width = row_out.shape[0]
    heads = width // HEAD_DIM
    group = width // sites
    xc_all = flat_rows(xc[...], F32)
    rows = xc_all.shape[0]
    per = rows // haps
    cot_f = xc_all[:, width:]
    cot = cot_f.astype(BF16)
    cot_out[...] = cot
    hid = xc_all[:, :width]
    for i in range(sites):
        a_i = unpack_block(at[i * haps : (i + 1) * haps], group)
        hid = hid + mm(a_i, row_out[i * group : (i + 1) * group, :])
    hid = hid.astype(BF16).astype(F32)
    grad_att = mm_nt(cot, col_out[...]).astype(BF16)
    xhat, rstd = norm_parts(hid)
    normed = (xhat * gain[1:2, :]).astype(BF16)
    n_out[...] = normed
    packed = mm(normed, col_proj[...]).astype(BF16)
    q = packed[:, :width]
    key = packed[:, width : 2 * width]
    val = packed[:, 2 * width :]
    kv_t = mm_nt(kv_t_w[...], normed).astype(BF16)
    key_st = jnp.concatenate([only_head(key, h) for h in range(heads)], axis=0)
    val_st = jnp.concatenate([only_head(val, h) for h in range(heads)], axis=0)
    scores = mm_nt(key_st, q) * (SCALE * LOG2E)
    dprob = mm_nt(val_st, grad_att)
    same = (
        lax.broadcasted_iota(jnp.int32, (rows, rows), 0) % per
        == lax.broadcasted_iota(jnp.int32, (rows, rows), 1) % per
    )
    att_t, dq_t, prob16, ds16 = [], [], [], []
    for h in range(heads):
        cols = slice(h * HEAD_DIM, (h + 1) * HEAD_DIM)
        s_h = jnp.where(same, scores[h * rows : (h + 1) * rows], -jnp.inf)
        e_h = jnp.exp2(s_h - jnp.max(s_h, axis=0, keepdims=True))
        inverse = 1.0 / jnp.sum(e_h, axis=0, keepdims=True)
        att_t.append(mm(kv_t[width:, :][cols], e_h.astype(BF16)) * inverse)
        p_h = e_h * inverse
        d_h = dprob[h * rows : (h + 1) * rows]
        delta = jnp.sum(p_h * d_h, axis=0, keepdims=True)
        ds_h = (p_h * (d_h - delta)).astype(BF16)
        prob16.append(p_h.astype(BF16))
        ds16.append(ds_h)
        dq_t.append(mm(kv_t[:width, :][cols], ds_h))
    att_t = jnp.concatenate(att_t, axis=0)
    at_out[...] = att_t.astype(BF16)
    att = jnp.transpose(att_t).astype(BF16)
    out = hid + mm(att, col_out[...])
    dv_all = mm(jnp.concatenate(prob16, axis=0), grad_att)
    dk_all = mm(jnp.concatenate(ds16, axis=0), q)
    dv = sum(
        jnp.where(head_lanes(width, h), dv_all[h * rows : (h + 1) * rows], 0.0) for h in range(heads)
    )
    dk = sum(
        jnp.where(head_lanes(width, h), dk_all[h * rows : (h + 1) * rows], 0.0) for h in range(heads)
    )
    dq = jnp.transpose(jnp.concatenate(dq_t, axis=0))
    packed_grad = jnp.concatenate([dq * SCALE, dk * SCALE, dv], axis=1).astype(BF16)
    gp_out[...] = packed_grad
    grad_normed = mm_nt(packed_grad, col_proj[...])
    grad_hidden = (cot_f + norm_back(xhat, rstd, gain[1:2, :], grad_normed)).astype(BF16)
    for i in range(sites):
        g_i = mm_nt(grad_hidden, row_out[i * group : (i + 1) * group, :])
        ga_out[i * haps : (i + 1) * haps] = pack_block(g_i, haps)
    both = jnp.concatenate([out, grad_hidden.astype(F32)], axis=1)
    og_out[...] = both.reshape(haps, per, 2 * width).astype(BF16)


def column_weights(sites, haps, core, cot, at, og, normed, gp, att_t, keep, send, both):
    width = normed.shape[1]
    group = width // sites
    half = width // 2
    grad_hidden = flat_rows(og[:, :, width:])
    both[:, : 3 * width] = mm_tn(normed[...], gp[...]).astype(BF16)
    both[:, 3 * width : 4 * width] = mm(att_t[...], cot[...]).astype(BF16)
    for i in range(sites):
        a_i = unpack_block(at[i * haps : (i + 1) * haps], group)
        both[i * group : (i + 1) * group, 4 * width :] = mm_tn(a_i, grad_hidden).astype(BF16)
    keep[...] = both[pl.ds(pl.multiple_of(core[0] * half, half), half), :]
    send[...] = both[pl.ds(pl.multiple_of((1 - core[0]) * half, half), half), :]


def column_split(sites, idx, keep, got, *refs):
    outs, both = refs[:sites], refs[sites]
    both[...] = (keep[...].astype(F32) + got[...].astype(F32)).astype(BF16)
    part = keep.shape[0] // sites
    for k in range(sites):
        outs[k][...] = both[pl.ds(pl.multiple_of((idx[0] ^ k) * part, part), part), :]


def row_backward(sites, haps, idx, core, g_in, prob, q, val, key_t, normed, *refs):
    gp_outs = refs[:sites]
    keep, send, g_all, ds_all, w_out = refs[sites:]
    me = idx[0]
    total, width = q.shape
    rows = total // sites
    for b in range(sites):
        g_all[b * rows : (b + 1) * rows, :] = unpack_block(
            g_in[pl.ds((me ^ b) * haps, haps)], width
        )
    dk = jnp.zeros((total, width), F32)
    dv = jnp.zeros((total, width), F32)
    dq_t = []
    for h in range(width // HEAD_DIM):
        val_h = only_head(val[...], h)
        dv = dv + mm(prob[h], only_head(g_all[...], h))
        for b in range(sites):
            here = pl.ds(b * rows, rows)
            dprob = mm_nt(val_h, g_all[b * rows : (b + 1) * rows, :])
            p_b = prob[h, :, here].astype(F32)
            delta = jnp.sum(p_b * dprob, axis=0, keepdims=True)
            ds_all[:, here] = (p_b * (dprob - delta)).astype(BF16)
        dk = dk + mm(ds_all[...], only_head(q[...], h))
        dq_t.append(mm(key_t[h * HEAD_DIM : (h + 1) * HEAD_DIM, :], ds_all[...]))
    dq_t = jnp.concatenate(dq_t, axis=0) * SCALE
    dk16 = (dk * SCALE).astype(BF16)
    dv16 = dv.astype(BF16)
    w_out[:width, :] = mm(dq_t.astype(BF16), normed[...]).astype(BF16)
    w_out[width : 2 * width, :] = mm_tn(dk16, normed[...]).astype(BF16)
    w_out[2 * width :, :] = mm_tn(dv16, normed[...]).astype(BF16)
    half = 3 * width // 2
    keep[...] = w_out[pl.ds(pl.multiple_of(core[0] * half, half), half), :]
    send[...] = w_out[pl.ds(pl.multiple_of((1 - core[0]) * half, half), half), :]
    dq = jnp.transpose(dq_t).astype(BF16)
    joined = jnp.concatenate([dq, dk16, dv16], axis=1)
    for b in range(sites):
        gp_outs[b][...] = joined[b * rows : (b + 1) * rows]


def row_finish(sites, idx, feats, gain, w_all, og, *refs):
    gps = refs[:sites]
    out_ref, gf_ref = refs[sites:]
    me = idx[0]
    width = feats.shape[1]
    both = flat_rows(og[...], F32)
    grad_normed = sum(mm(gps[k][...], w_all[me ^ k]) for k in range(sites))
    xhat, rstd = norm_parts(feats[...].astype(F32))
    grad = both[:, width:] + norm_back(xhat, rstd, gain[:1, :], grad_normed)
    out_ref[...] = both[:, :width].astype(BF16)
    gf_ref[...] = grad.astype(BF16)


def weights_join(row_keep, row_got, *refs):
    cols, out = refs[:-1], refs[-1]
    half, width = row_keep.shape
    out[:half, :] = (row_keep[...].astype(F32) + row_got[...].astype(F32)).astype(BF16)
    total = sum(c[...].astype(F32) for c in cols)
    part = total.shape[0]
    for t in range(5):
        tile = total[:, t * width : (t + 1) * width]
        out[half + t * part : half + (t + 1) * part, :] = tile.astype(BF16)


def weights_sum(*refs):
    terms = [r[...].astype(F32) for r in refs[:-1]]
    while len(terms) > 1:
        terms = [a + b for a, b in zip(terms[::2], terms[1::2])]
    refs[-1][...] = terms[0].astype(BF16)


def weights_finish(sites, idx, core, *refs):
    pieces = refs[: 2 * sites]
    rp, ro, cp, co, rows_t = refs[2 * sites :]
    width = ro.shape[0]
    group = width // sites
    unit = group // 2
    part = width // 2 // sites
    for j in range(2 * sites):
        k = j // 2
        cc = core[0] ^ (j % 2)
        g = idx[0] ^ k
        piece = pieces[j][...].astype(F32)
        for u in range(3):
            place = 3 * cc + u
            dest = (place // 2) * width + g * group + (place % 2) * unit
            rows_t[pl.ds(pl.multiple_of(dest, unit), unit), :] = piece[u * unit : (u + 1) * unit]
        here = pl.ds(pl.multiple_of(cc * (width // 2) + g * part, part), part)
        tiles = [piece[3 * unit + t * part : 3 * unit + (t + 1) * part] for t in range(5)]
        for t in range(3):
            cp[here, t * width : (t + 1) * width] = tiles[t]
        co[here, :] = tiles[3]
        ro[here, :] = tiles[4]
    rp[...] = jnp.transpose(rows_t[...])


def exchange(value, axis):
    return lax.all_to_all(value, axis, 0, 0, tiled=True)


def swapped(value, axis, by):
    length = lax.axis_size(axis)
    return lax.ppermute(value, axis, [(i, i ^ by) for i in range(length)])


def on_device(
    features,
    link_pattern,
    row_gain,
    row_proj,
    row_out,
    column_norm_gain,
    col_proj,
    col_out,
    cotangent,
):
    rows, _, width = features.shape
    sites, haps = lax.axis_size("site"), lax.axis_size("hap")
    count = sites * haps
    per = rows // haps
    group = width // sites
    heads = group // HEAD_DIM
    total = rows * sites
    both_axes = ("site", "hap")
    me = lax.axis_index("site")
    idx = me.reshape(1).astype(jnp.int32)
    hap = lax.axis_index("hap").reshape(1).astype(jnp.int32)
    core = hap % 2
    factor = lane_factor(per, group)
    block = ((count, per // factor, group * factor), BF16)
    feats = features.reshape(rows, width)
    cot = cotangent.reshape(rows, width)

    pieces = [feats] + [swapped(feats, "site", k) for k in range(1, sites)]
    gains = jnp.stack([row_gain, column_norm_gain])
    (xc,) = call(join_inputs, [((haps, per, 2 * width), BF16)], feats, cot)
    xc = exchange(xc, "hap")
    w_all = jnp.transpose(row_proj.reshape(width, 3, sites, group), (2, 1, 3, 0)).reshape(
        sites, 3 * group, width
    )
    w_t = lax.dynamic_index_in_dim(w_all, me, 0, keepdims=False)
    kv_t_w = jnp.transpose(col_proj[:, width:])

    att, prob, q, val, key_t, normed = call(
        functools.partial(row_forward, sites, haps),
        [
            block,
            ((heads, total, total), BF16),
            ((total, group), BF16),
            ((total, group), BF16),
            ((group, total), BF16),
            ((total, width), BF16),
        ],
        idx, link_pattern, *pieces, gains, w_t, scalars=2, us=20,
    )
    att, xc = lax.optimization_barrier((att, xc))
    at = exchange(att, both_axes)
    ga, og, col_normed, col_gp, col_att_t, cot = call(
        functools.partial(column_step, sites, haps),
        [
            block,
            ((haps, per, 2 * width), BF16),
            ((rows, width), BF16),
            ((rows, 3 * width), BF16),
            ((width, rows), BF16),
            ((rows, width), BF16),
        ],
        xc, at, row_out, gains, col_proj, kv_t_w, col_out,
    )
    g_in = exchange(ga, both_axes)
    half = width // 2
    col_keep, col_send = call(
        functools.partial(column_weights, sites, haps),
        [((half, 5 * width), BF16)] * 2,
        core, cot, at, og, col_normed, col_gp, col_att_t, scalars=1, us=20,
        scratch=[pltpu.VMEM((width, 5 * width), BF16)],
    )
    col_got = swapped(col_send, "hap", 1)
    cols = call(
        functools.partial(column_split, sites),
        [((half // sites, 5 * width), BF16)] * sites,
        idx, col_keep, col_got, scalars=1, us=5,
        scratch=[pltpu.VMEM((half, 5 * width), BF16)],
    )
    g_in, _ = lax.optimization_barrier((g_in, cols))
    cols = [cols[0]] + [swapped(cols[k], "site", k) for k in range(1, sites)]
    *gps, row_keep, row_send = call(
        functools.partial(row_backward, sites, haps),
        [((rows, 3 * group), BF16)] * sites + [((3 * group // 2, width), BF16)] * 2,
        idx, core, g_in, prob, q, val, key_t, normed, scalars=2,
        scratch=[
            pltpu.VMEM((total, group), BF16),
            pltpu.VMEM((total, total), BF16),
            pltpu.VMEM((3 * group, width), BF16),
        ],
    )
    row_got = swapped(row_send, "hap", 1)
    depth = 3 * group // 2 + 5 * half // sites
    (joined,) = call(weights_join, [((depth, width), BF16)], row_keep, row_got, *cols)
    parts = [joined] + [swapped(joined, "hap", 2 * m) for m in range(1, haps // 2)]
    gps = [gps[0]] + [swapped(gps[k], "site", k) for k in range(1, sites)]
    parts, gps = lax.optimization_barrier((parts, gps))
    (mine,) = call(weights_sum, [((depth, width), BF16)], *parts)
    mine_swapped = swapped(mine, "hap", 1)
    og, _ = lax.optimization_barrier((og, mine_swapped))
    og_in = exchange(og, "hap")
    out, grad = call(
        functools.partial(row_finish, sites),
        [((rows, width), BF16)] * 2,
        idx, feats, gains, w_all, og_in, *gps, scalars=1,
    )
    full = [mine] + [swapped(mine, "site", k) for k in range(1, sites)]
    full = [mine, mine_swapped] + [x for p in full[1:] for x in (p, swapped(p, "hap", 1))]
    rp, ro, cp, co = call(
        functools.partial(weights_finish, sites),
        [((width, 3 * width), F32), ((width, width), F32)] * 2,
        idx, core, *full, scalars=2,
        scratch=[pltpu.VMEM((3 * width, width), F32)],
    )
    shape = (rows, 1, width)
    return (out.reshape(shape), grad.reshape(shape), rp, ro, cp, co)


def solution(mesh):
    data = P("site", "hap", None)
    return jax.shard_map(
        on_device,
        mesh=mesh,
        in_specs=(data, P(), P(), P(), P(), P(), P(), P(), data),
        out_specs=(data, data, P(), P(), P(), P()),
        check_vma=False,
    )
```

```python
import functools

import jax
import jax.numpy as jnp
from jax import lax
from jax.experimental import pallas as pl
from jax.experimental.pallas import tpu as pltpu
from jax.sharding import PartitionSpec as P

HEAD_DIM = 32
EPSILON = 1e-05
LOG2E = 1.4426950408889634
SCALE = HEAD_DIM ** (-0.5)
F32 = jnp.float32
BF16 = jnp.bfloat16
VMEM = pl.BlockSpec(memory_space=pltpu.VMEM)
HBM = pl.BlockSpec(memory_space=pltpu.HBM)
SMEM = pl.BlockSpec(memory_space=pltpu.SMEM)
PARAMS = pltpu.CompilerParams(vmem_limit_bytes=24 << 20)


def mm(a, b):
    return lax.dot_general(a, b, (((1,), (0,)), ((), ())), preferred_element_type=F32)


def mm_nt(a, b):
    return lax.dot_general(a, b, (((1,), (1,)), ((), ())), preferred_element_type=F32)


def mm_tn(a, b):
    return lax.dot_general(a, b, (((0,), (0,)), ((), ())), preferred_element_type=F32)


def norm_parts(x):
    centred = x - jnp.mean(x, axis=-1, keepdims=True)
    rstd = lax.rsqrt(jnp.mean(centred * centred, axis=-1, keepdims=True) + EPSILON)
    return centred * rstd, rstd


def norm_back(xhat, rstd, gain, grad):
    scaled = grad * gain
    first = jnp.mean(scaled, axis=-1, keepdims=True)
    second = jnp.mean(scaled * xhat, axis=-1, keepdims=True)
    return rstd * (scaled - first - xhat * second)


def head_lanes(width, head):
    return lax.broadcasted_iota(jnp.int32, (1, width), 1) // HEAD_DIM == head


def only_head(values, head):
    return jnp.where(head_lanes(values.shape[1], head), values, jnp.zeros_like(values))


def flat_rows(values, dtype=BF16):
    wide = values.astype(F32)
    return wide.reshape(wide.shape[0] * wide.shape[1], wide.shape[2]).astype(dtype)


def lane_factor(rows, width):
    factor = 128 // width
    return factor if (rows // factor) % 8 == 0 else 1


def pack_block(values, outer):
    rows, width = values.shape[0] // outer, values.shape[1]
    factor = lane_factor(rows, width)
    split = values.reshape(outer, factor, rows // factor, width)
    return jnp.concatenate([split[:, j] for j in range(factor)], axis=2).astype(BF16)


def unpack_block(values, width):
    wide = values.astype(F32)
    factor = wide.shape[2] // width
    split = [wide[:, None, :, j * width : (j + 1) * width] for j in range(factor)]
    joined = jnp.concatenate(split, axis=1)
    return joined.reshape(-1, width).astype(BF16)


def call(body, outs, *operands, scalars=0, scratch=(), us=0, far=0):
    cost = pl.CostEstimate(flops=us * 10**9 + 1, bytes_accessed=us * 3_600_000 + 1, transcendentals=0)
    return pl.pallas_call(
        body,
        out_shape=[jax.ShapeDtypeStruct(s, d) for s, d in outs[: len(outs) - far]]
        + [pltpu.HBM(s, d) for s, d in outs[len(outs) - far :]],
        in_specs=[SMEM] * scalars + [VMEM] * (len(operands) - scalars),
        out_specs=[VMEM] * (len(outs) - far) + [HBM] * far,
        scratch_shapes=list(scratch),
        compiler_params=PARAMS,
        cost_estimate=cost,
    )(*operands)


def row_forward(sites, haps, idx, link, *refs):
    pieces = refs[:sites]
    gain, w_t = refs[sites : sites + 2]
    att_out, p_out, q_out, v_out, kt_out, n_out = refs[sites + 2 :]
    me = idx[0]
    rows = pieces[0].shape[0]
    width = q_out.shape[1]
    for k in range(sites):
        xhat, _ = norm_parts(pieces[k][...].astype(F32))
        n_out[k * rows : (k + 1) * rows, :] = (xhat * gain[:1, :]).astype(BF16)
    normed = n_out[...]
    q = mm_nt(normed, w_t[:width, :]).astype(BF16)
    key = mm_nt(normed, w_t[width : 2 * width, :]).astype(BF16)
    q_out[...] = q
    v_out[...] = mm_nt(normed, w_t[2 * width :, :]).astype(BF16)
    kt_out[...] = mm_nt(w_t[width : 2 * width, :], normed).astype(BF16)
    v_t = mm_nt(w_t[2 * width :, :], normed).astype(BF16)
    att_t = []
    for h in range(width // HEAD_DIM):
        key_h = only_head(key, h)
        for b in range(sites):
            here = pl.ds(b * rows, rows)
            scores = mm_nt(key_h, q[b * rows : (b + 1) * rows]) * (SCALE * LOG2E)
            parts = [
                scores[a * rows : (a + 1) * rows]
                + jnp.where(link[me ^ b, me ^ a] > 0, 0.0, -jnp.inf)
                for a in range(sites)
            ]
            high = functools.reduce(
                jnp.maximum, [jnp.max(part, axis=0, keepdims=True) for part in parts]
            )
            parts = [jnp.exp2(part - high) for part in parts]
            total = sum(jnp.sum(part, axis=0, keepdims=True) for part in parts)
            inverse = 1.0 / total
            for a in range(sites):
                p_out[h, a * rows : (a + 1) * rows, here] = (parts[a] * inverse).astype(BF16)
        att_t.append(mm(v_t[h * HEAD_DIM : (h + 1) * HEAD_DIM], p_out[h]))
    att = jnp.transpose(jnp.concatenate(att_t, axis=0))
    for b in range(sites):
        att_out[pl.ds((me ^ b) * haps, haps)] = pack_block(att[b * rows : (b + 1) * rows], haps)


def join_inputs(haps, hap, feats, cot, keep, send, both):
    count, per, width = both.shape
    joined = jnp.concatenate([feats[...].astype(F32), cot[...].astype(F32)], axis=1)
    both[...] = joined.reshape(count, per, width).astype(BF16)
    for m in range(haps // 2):
        keep[m] = both[hap[0] ^ (2 * m)]
        send[m] = both[hap[0] ^ (2 * m + 1)]


def relay_inputs(keep, got, *outs):
    for m, out in enumerate(outs):
        out[0] = keep[m]
        out[1] = got[m]


def column_step(sites, haps, hap, at, row_out, gain, col_proj, kv_t_w, col_out, *refs):
    ga_out, og_out, *far, xc = refs[haps // 2 : haps // 2 + 7]
    near, sems = refs[haps // 2 + 7 : -1], refs[-1]
    copies = [
        pltpu.make_async_copy(near[j], far[j], sems.at[j]) for j in range(len(near))
    ]

    def save(j, value):
        near[j][...] = value
        copies[j].start()

    for m in range(haps // 2):
        xc[hap[0] ^ (2 * m)] = refs[m][0]
        xc[hap[0] ^ (2 * m + 1)] = refs[m][1]
    width = row_out.shape[0]
    heads = width // HEAD_DIM
    group = width // sites
    xc_all = flat_rows(xc[...], F32)
    rows = xc_all.shape[0]
    per = rows // haps
    cot_f = xc_all[:, width:]
    cot = cot_f.astype(BF16)
    save(3, cot)
    hid = xc_all[:, :width]
    for i in range(sites):
        a_i = unpack_block(at[i * haps : (i + 1) * haps], group)
        hid = hid + mm(a_i, row_out[i * group : (i + 1) * group, :])
    hid = hid.astype(BF16).astype(F32)
    grad_att = mm_nt(cot, col_out[...]).astype(BF16)
    xhat, rstd = norm_parts(hid)
    normed = (xhat * gain[1:2, :]).astype(BF16)
    save(0, normed)
    packed = mm(normed, col_proj[...]).astype(BF16)
    q = packed[:, :width]
    key = packed[:, width : 2 * width]
    val = packed[:, 2 * width :]
    kv_t = mm_nt(kv_t_w[...], normed).astype(BF16)
    key_st = jnp.concatenate([only_head(key, h) for h in range(heads)], axis=0)
    val_st = jnp.concatenate([only_head(val, h) for h in range(heads)], axis=0)
    scores = mm_nt(key_st, q) * (SCALE * LOG2E)
    dprob = mm_nt(val_st, grad_att)
    same = (
        lax.broadcasted_iota(jnp.int32, (rows, rows), 0) % per
        == lax.broadcasted_iota(jnp.int32, (rows, rows), 1) % per
    )
    att_t, dq_t, prob16, ds16 = [], [], [], []
    for h in range(heads):
        cols = slice(h * HEAD_DIM, (h + 1) * HEAD_DIM)
        s_h = jnp.where(same, scores[h * rows : (h + 1) * rows], -jnp.inf)
        e_h = jnp.exp2(s_h - jnp.max(s_h, axis=0, keepdims=True))
        inverse = 1.0 / jnp.sum(e_h, axis=0, keepdims=True)
        att_t.append(mm(kv_t[width:, :][cols], e_h.astype(BF16)) * inverse)
        p_h = e_h * inverse
        d_h = dprob[h * rows : (h + 1) * rows]
        delta = jnp.sum(p_h * d_h, axis=0, keepdims=True)
        ds_h = (p_h * (d_h - delta)).astype(BF16)
        prob16.append(p_h.astype(BF16))
        ds16.append(ds_h)
        dq_t.append(mm(kv_t[:width, :][cols], ds_h))
    att_t = jnp.concatenate(att_t, axis=0)
    save(2, att_t.astype(BF16))
    att = jnp.transpose(att_t).astype(BF16)
    out = hid + mm(att, col_out[...])
    dv_all = mm(jnp.concatenate(prob16, axis=0), grad_att)
    dk_all = mm(jnp.concatenate(ds16, axis=0), q)
    dv = sum(
        jnp.where(head_lanes(width, h), dv_all[h * rows : (h + 1) * rows], 0.0) for h in range(heads)
    )
    dk = sum(
        jnp.where(head_lanes(width, h), dk_all[h * rows : (h + 1) * rows], 0.0) for h in range(heads)
    )
    dq = jnp.transpose(jnp.concatenate(dq_t, axis=0))
    packed_grad = jnp.concatenate([dq * SCALE, dk * SCALE, dv], axis=1).astype(BF16)
    save(1, packed_grad)
    grad_normed = mm_nt(packed_grad, col_proj[...])
    grad_hidden = (cot_f + norm_back(xhat, rstd, gain[1:2, :], grad_normed)).astype(BF16)
    for i in range(sites):
        g_i = mm_nt(grad_hidden, row_out[i * group : (i + 1) * group, :])
        ga_out[i * haps : (i + 1) * haps] = pack_block(g_i, haps)
    both = jnp.concatenate([out, grad_hidden.astype(F32)], axis=1)
    og_out[...] = both.reshape(haps, per, 2 * width).astype(BF16)
    for copy in copies:
        copy.wait()


def column_weights(sites, haps, core, cot, at, og, normed, gp, att_t, keep, *refs):
    sends, both = refs[:-1], refs[-1]
    width = normed.shape[1]
    group = width // sites
    half = width // 2
    grad_hidden = flat_rows(og[:, :, width:])
    both[:, : 3 * width] = mm_tn(normed[...], gp[...]).astype(BF16)
    both[:, 3 * width : 4 * width] = mm(att_t[...], cot[...]).astype(BF16)
    for i in range(sites):
        a_i = unpack_block(at[i * haps : (i + 1) * haps], group)
        both[i * group : (i + 1) * group, 4 * width :] = mm_tn(a_i, grad_hidden).astype(BF16)
    keep[...] = both[pl.ds(pl.multiple_of(core[0] * half, half), half), :]
    part = half // len(sends)
    for j, send in enumerate(sends):
        start = (1 - core[0]) * half + j * part
        send[...] = both[pl.ds(pl.multiple_of(start, part), part), :]


def column_split(sites, idx, keep, *refs):
    outs, both, gots = refs[-sites - 1 : -1], refs[-1], refs[: -sites - 1]
    got = jnp.concatenate([g[...].astype(F32) for g in gots], axis=0)
    both[...] = (keep[...].astype(F32) + got).astype(BF16)
    part = keep.shape[0] // sites
    for k in range(sites):
        outs[k][...] = both[pl.ds(pl.multiple_of((idx[0] ^ k) * part, part), part), :]


def row_backward(sites, haps, idx, core, g_in, prob, q, val, key_t, normed, *refs):
    gp_outs = refs[:sites]
    keep, send, g_all, ds_all, w_out = refs[sites:]
    me = idx[0]
    total, width = q.shape
    rows = total // sites
    for b in range(sites):
        g_all[b * rows : (b + 1) * rows, :] = unpack_block(
            g_in[pl.ds((me ^ b) * haps, haps)], width
        )
    dk = jnp.zeros((total, width), F32)
    dv = jnp.zeros((total, width), F32)
    dq_t = []
    for h in range(width // HEAD_DIM):
        val_h = only_head(val[...], h)
        dv = dv + mm(prob[h], only_head(g_all[...], h))
        for b in range(sites):
            here = pl.ds(b * rows, rows)
            dprob = mm_nt(val_h, g_all[b * rows : (b + 1) * rows, :])
            p_b = prob[h, :, here].astype(F32)
            delta = jnp.sum(p_b * dprob, axis=0, keepdims=True)
            ds_all[:, here] = (p_b * (dprob - delta)).astype(BF16)
        dk = dk + mm(ds_all[...], only_head(q[...], h))
        dq_t.append(mm(key_t[h * HEAD_DIM : (h + 1) * HEAD_DIM, :], ds_all[...]))
    dq_t = jnp.concatenate(dq_t, axis=0) * SCALE
    dk16 = (dk * SCALE).astype(BF16)
    dv16 = dv.astype(BF16)
    w_out[:width, :] = mm(dq_t.astype(BF16), normed[...]).astype(BF16)
    w_out[width : 2 * width, :] = mm_tn(dk16, normed[...]).astype(BF16)
    w_out[2 * width :, :] = mm_tn(dv16, normed[...]).astype(BF16)
    half = 3 * width // 2
    keep[...] = w_out[pl.ds(pl.multiple_of(core[0] * half, half), half), :]
    send[...] = w_out[pl.ds(pl.multiple_of((1 - core[0]) * half, half), half), :]
    dq = jnp.transpose(dq_t).astype(BF16)
    joined = jnp.concatenate([dq, dk16, dv16], axis=1)
    for b in range(sites):
        gp_outs[b][...] = joined[b * rows : (b + 1) * rows]


def row_finish(sites, idx, feats, gain, w_all, og, *refs):
    gps = refs[:sites]
    out_ref, gf_ref = refs[sites:]
    me = idx[0]
    width = feats.shape[1]
    both = flat_rows(og[...], F32)
    grad_normed = sum(mm(gps[k][...], w_all[me ^ k]) for k in range(sites))
    xhat, rstd = norm_parts(feats[...].astype(F32))
    grad = both[:, width:] + norm_back(xhat, rstd, gain[:1, :], grad_normed)
    out_ref[...] = both[:, :width].astype(BF16)
    gf_ref[...] = grad.astype(BF16)


def weights_join(row_keep, row_got, *refs):
    cols, out = refs[:-1], refs[-1]
    half, width = row_keep.shape
    out[:half, :] = (row_keep[...].astype(F32) + row_got[...].astype(F32)).astype(BF16)
    total = sum(c[...].astype(F32) for c in cols)
    part = total.shape[0]
    for t in range(5):
        tile = total[:, t * width : (t + 1) * width]
        out[half + t * part : half + (t + 1) * part, :] = tile.astype(BF16)


def weights_sum(*refs):
    terms = [r[...].astype(F32) for r in refs[:-1]]
    while len(terms) > 1:
        terms = [a + b for a, b in zip(terms[::2], terms[1::2])]
    refs[-1][...] = terms[0].astype(BF16)


def weights_finish(sites, idx, core, *refs):
    pieces = refs[: 2 * sites]
    rp, ro, cp, co, rows_t = refs[2 * sites :]
    width = ro.shape[0]
    group = width // sites
    unit = group // 2
    part = width // 2 // sites
    for j in range(2 * sites):
        k = j // 2
        cc = core[0] ^ (j % 2)
        g = idx[0] ^ k
        piece = pieces[j][...].astype(F32)
        for u in range(3):
            place = 3 * cc + u
            dest = (place // 2) * width + g * group + (place % 2) * unit
            rows_t[pl.ds(pl.multiple_of(dest, unit), unit), :] = piece[u * unit : (u + 1) * unit]
        here = pl.ds(pl.multiple_of(cc * (width // 2) + g * part, part), part)
        tiles = [piece[3 * unit + t * part : 3 * unit + (t + 1) * part] for t in range(5)]
        for t in range(3):
            cp[here, t * width : (t + 1) * width] = tiles[t]
        co[here, :] = tiles[3]
        ro[here, :] = tiles[4]
    rp[...] = jnp.transpose(rows_t[...])


def exchange(value, axis):
    return lax.all_to_all(value, axis, 0, 0, tiled=True)


def swapped(value, axis, by):
    length = lax.axis_size(axis)
    return lax.ppermute(value, axis, [(i, i ^ by) for i in range(length)])


def on_device(
    features,
    link_pattern,
    row_gain,
    row_proj,
    row_out,
    column_norm_gain,
    col_proj,
    col_out,
    cotangent,
):
    rows, _, width = features.shape
    sites, haps = lax.axis_size("site"), lax.axis_size("hap")
    count = sites * haps
    per = rows // haps
    group = width // sites
    heads = group // HEAD_DIM
    total = rows * sites
    both_axes = ("site", "hap")
    me = lax.axis_index("site")
    idx = me.reshape(1).astype(jnp.int32)
    hap = lax.axis_index("hap").reshape(1).astype(jnp.int32)
    core = hap % 2
    factor = lane_factor(per, group)
    block = ((count, per // factor, group * factor), BF16)
    feats = features.reshape(rows, width)
    cot = cotangent.reshape(rows, width)

    pieces = [feats] + [swapped(feats, "site", k) for k in range(1, sites)]
    gains = jnp.stack([row_gain, column_norm_gain])
    keep, send = call(
        functools.partial(join_inputs, haps),
        [((haps // 2, per, 2 * width), BF16)] * 2,
        hap, feats, cot, scalars=1,
        scratch=[pltpu.VMEM((haps, per, 2 * width), BF16)],
    )
    got = swapped(send, "hap", 1)
    xcs = call(relay_inputs, [((2, per, 2 * width), BF16)] * (haps // 2), keep, got)
    pieces, _ = lax.optimization_barrier((pieces, xcs))
    xcs = [xcs[0]] + [swapped(xcs[m], "hap", 2 * m) for m in range(1, haps // 2)]
    w_all = jnp.transpose(row_proj.reshape(width, 3, sites, group), (2, 1, 3, 0)).reshape(
        sites, 3 * group, width
    )
    w_t = lax.dynamic_index_in_dim(w_all, me, 0, keepdims=False)
    kv_t_w = jnp.transpose(col_proj[:, width:])

    att, prob, q, val, key_t, normed = call(
        functools.partial(row_forward, sites, haps),
        [
            block,
            ((heads, total, total), BF16),
            ((total, group), BF16),
            ((total, group), BF16),
            ((group, total), BF16),
            ((total, width), BF16),
        ],
        idx, link_pattern, *pieces, gains, w_t, scalars=2, us=3,
    )
    at = exchange(att, both_axes)
    ga, og, col_normed, col_gp, col_att_t, cot = call(
        functools.partial(column_step, sites, haps),
        [
            block,
            ((haps, per, 2 * width), BF16),
            ((rows, width), BF16),
            ((rows, 3 * width), BF16),
            ((width, rows), BF16),
            ((rows, width), BF16),
        ],
        hap, at, row_out, gains, col_proj, kv_t_w, col_out, *xcs, scalars=1, far=4,
        scratch=[
            pltpu.VMEM((haps, per, 2 * width), BF16),
            pltpu.VMEM((rows, width), BF16),
            pltpu.VMEM((rows, 3 * width), BF16),
            pltpu.VMEM((width, rows), BF16),
            pltpu.VMEM((rows, width), BF16),
            pltpu.SemaphoreType.DMA((4,)),
        ],
    )
    g_in = exchange(ga, both_axes)
    half = width // 2
    col_keep, *col_sends = call(
        functools.partial(column_weights, sites, haps),
        [((half, 5 * width), BF16)] + [((half // 4, 5 * width), BF16)] * 4,
        core, cot, at, og, col_normed, col_gp, col_att_t, scalars=1, us=20,
        scratch=[pltpu.VMEM((width, 5 * width), BF16)],
    )
    col_got = [swapped(send, "hap", 1) for send in col_sends]
    cols = call(
        functools.partial(column_split, sites),
        [((half // sites, 5 * width), BF16)] * sites,
        idx, col_keep, *col_got, scalars=1, us=0,
        scratch=[pltpu.VMEM((half, 5 * width), BF16)],
    )
    g_in, _ = lax.optimization_barrier((g_in, cols))
    cols = [cols[0]] + [swapped(cols[k], "site", k) for k in range(1, sites)]
    *gps, row_keep, row_send = call(
        functools.partial(row_backward, sites, haps),
        [((rows, 3 * group), BF16)] * sites + [((3 * group // 2, width), BF16)] * 2,
        idx, core, g_in, prob, q, val, key_t, normed, scalars=2,
        scratch=[
            pltpu.VMEM((total, group), BF16),
            pltpu.VMEM((total, total), BF16),
            pltpu.VMEM((3 * group, width), BF16),
        ],
    )
    row_got = swapped(row_send, "hap", 1)
    depth = 3 * group // 2 + 5 * half // sites
    (joined,) = call(weights_join, [((depth, width), BF16)], row_keep, row_got, *cols)
    parts = [joined] + [swapped(joined, "hap", 2 * m) for m in range(1, haps // 2)]
    gps = [gps[0]] + [swapped(gps[k], "site", k) for k in range(1, sites)]
    og, _ = lax.optimization_barrier((og, gps[1]))
    og_in = exchange(og, "hap")
    parts, gps = lax.optimization_barrier((parts, gps))
    (mine,) = call(weights_sum, [((depth, width), BF16)], *parts)
    mine_swapped = swapped(mine, "hap", 1)
    out, grad = call(
        functools.partial(row_finish, sites),
        [((rows, width), BF16)] * 2,
        idx, feats, gains, w_all, og_in, *gps, scalars=1,
    )
    full = [mine] + [swapped(mine, "site", k) for k in range(1, sites)]
    full = [mine, mine_swapped] + [x for p in full[1:] for x in (p, swapped(p, "hap", 1))]
    rp, ro, cp, co = call(
        functools.partial(weights_finish, sites),
        [((width, 3 * width), F32), ((width, width), F32)] * 2,
        idx, core, *full, scalars=2,
        scratch=[pltpu.VMEM((3 * width, width), F32)],
    )
    shape = (rows, 1, width)
    return (out.reshape(shape), grad.reshape(shape), rp, ro, cp, co)


def solution(mesh):
    data = P("site", "hap", None)
    return jax.shard_map(
        on_device,
        mesh=mesh,
        in_specs=(data, P(), P(), P(), P(), P(), P(), P(), data),
        out_specs=(data, data, P(), P(), P(), P()),
        check_vma=False,
    )
```

```python
import functools

import jax
import jax.numpy as jnp
from jax import lax
from jax.experimental import pallas as pl
from jax.experimental.pallas import tpu as pltpu
from jax.sharding import PartitionSpec as P

HEAD_DIM = 32
EPSILON = 1e-05
LOG2E = 1.4426950408889634
SCALE = HEAD_DIM ** (-0.5)
F32 = jnp.float32
BF16 = jnp.bfloat16
VMEM = pl.BlockSpec(memory_space=pltpu.VMEM)
HBM = pl.BlockSpec(memory_space=pltpu.HBM)
SMEM = pl.BlockSpec(memory_space=pltpu.SMEM)
PARAMS = pltpu.CompilerParams(vmem_limit_bytes=24 << 20)


def mm(a, b):
    return lax.dot_general(a, b, (((1,), (0,)), ((), ())), preferred_element_type=F32)


def mm_nt(a, b):
    return lax.dot_general(a, b, (((1,), (1,)), ((), ())), preferred_element_type=F32)


def mm_tn(a, b):
    return lax.dot_general(a, b, (((0,), (0,)), ((), ())), preferred_element_type=F32)


def norm_parts(x):
    centred = x - jnp.mean(x, axis=-1, keepdims=True)
    rstd = lax.rsqrt(jnp.mean(centred * centred, axis=-1, keepdims=True) + EPSILON)
    return centred * rstd, rstd


def norm_back(xhat, rstd, gain, grad):
    scaled = grad * gain
    first = jnp.mean(scaled, axis=-1, keepdims=True)
    second = jnp.mean(scaled * xhat, axis=-1, keepdims=True)
    return rstd * (scaled - first - xhat * second)


def head_lanes(width, head):
    return lax.broadcasted_iota(jnp.int32, (1, width), 1) // HEAD_DIM == head


def only_head(values, head):
    return jnp.where(head_lanes(values.shape[1], head), values, jnp.zeros_like(values))


def flat_rows(values, dtype=BF16):
    wide = values.astype(F32)
    return wide.reshape(wide.shape[0] * wide.shape[1], wide.shape[2]).astype(dtype)


def lane_factor(rows, width):
    factor = 128 // width
    return factor if (rows // factor) % 8 == 0 else 1


def pack_block(values, outer):
    rows, width = values.shape[0] // outer, values.shape[1]
    factor = lane_factor(rows, width)
    split = values.reshape(outer, factor, rows // factor, width)
    return jnp.concatenate([split[:, j] for j in range(factor)], axis=2).astype(BF16)


def unpack_block(values, width):
    wide = values.astype(F32)
    factor = wide.shape[2] // width
    split = [wide[:, None, :, j * width : (j + 1) * width] for j in range(factor)]
    joined = jnp.concatenate(split, axis=1)
    return joined.reshape(-1, width).astype(BF16)


def call(body, outs, *operands, scalars=0, scratch=(), us=0, far=0):
    cost = pl.CostEstimate(flops=us * 10**9 + 1, bytes_accessed=us * 3_600_000 + 1, transcendentals=0)
    return pl.pallas_call(
        body,
        out_shape=[jax.ShapeDtypeStruct(s, d) for s, d in outs[: len(outs) - far]]
        + [pltpu.HBM(s, d) for s, d in outs[len(outs) - far :]],
        in_specs=[SMEM] * scalars + [VMEM] * (len(operands) - scalars),
        out_specs=[VMEM] * (len(outs) - far) + [HBM] * far,
        scratch_shapes=list(scratch),
        compiler_params=PARAMS,
        cost_estimate=cost,
    )(*operands)


def row_forward(sites, haps, idx, link, *refs):
    pieces = refs[:sites]
    gain, w_t = refs[sites : sites + 2]
    att_out, p_out, q_out, v_out, kt_out, n_out = refs[sites + 2 :]
    me = idx[0]
    rows = pieces[0].shape[0]
    width = q_out.shape[1]
    for k in range(sites):
        xhat, _ = norm_parts(pieces[k][...].astype(F32))
        n_out[k * rows : (k + 1) * rows, :] = (xhat * gain[:1, :]).astype(BF16)
    normed = n_out[...]
    q = mm_nt(normed, w_t[:width, :]).astype(BF16)
    key = mm_nt(normed, w_t[width : 2 * width, :]).astype(BF16)
    q_out[...] = q
    v_out[...] = mm_nt(normed, w_t[2 * width :, :]).astype(BF16)
    kt_out[...] = mm_nt(w_t[width : 2 * width, :], normed).astype(BF16)
    v_t = mm_nt(w_t[2 * width :, :], normed).astype(BF16)
    att_t = []
    for h in range(width // HEAD_DIM):
        key_h = only_head(key, h)
        for b in range(sites):
            here = pl.ds(b * rows, rows)
            scores = mm_nt(key_h, q[b * rows : (b + 1) * rows]) * (SCALE * LOG2E)
            parts = [
                scores[a * rows : (a + 1) * rows]
                + jnp.where(link[me ^ b, me ^ a] > 0, 0.0, -jnp.inf)
                for a in range(sites)
            ]
            high = functools.reduce(
                jnp.maximum, [jnp.max(part, axis=0, keepdims=True) for part in parts]
            )
            parts = [jnp.exp2(part - high) for part in parts]
            total = sum(jnp.sum(part, axis=0, keepdims=True) for part in parts)
            inverse = 1.0 / total
            for a in range(sites):
                p_out[h, a * rows : (a + 1) * rows, here] = (parts[a] * inverse).astype(BF16)
        att_t.append(mm(v_t[h * HEAD_DIM : (h + 1) * HEAD_DIM], p_out[h]))
    att = jnp.transpose(jnp.concatenate(att_t, axis=0))
    for b in range(sites):
        att_out[pl.ds((me ^ b) * haps, haps)] = pack_block(att[b * rows : (b + 1) * rows], haps)


def join_inputs(haps, hap, feats, cot, keep, send, both):
    count, per, width = both.shape
    joined = jnp.concatenate([feats[...].astype(F32), cot[...].astype(F32)], axis=1)
    both[...] = joined.reshape(count, per, width).astype(BF16)
    for m in range(haps // 2):
        keep[m] = both[hap[0] ^ (2 * m)]
        send[m] = both[hap[0] ^ (2 * m + 1)]


def relay_inputs(keep, got, *outs):
    for m, out in enumerate(outs):
        out[0] = keep[m]
        out[1] = got[m]


def column_step(sites, haps, hap, at, row_out, gain, col_proj, kv_t_w, col_out, *refs):
    ga_out, send, keep, og_out, xc, og, w_all, sems = refs[haps // 2 :]
    core = hap[0] % 2
    half = row_out.shape[0] // 2
    mine = pl.ds(pl.multiple_of(core * half, half), half)
    other = pl.ds(pl.multiple_of((1 - core) * half, half), half)

    def save(j, cols):
        return pltpu.make_async_copy(w_all.at[mine, cols], keep.at[:, cols], sems.at[j])

    for m in range(haps // 2):
        xc[hap[0] ^ (2 * m)] = refs[m][0]
        xc[hap[0] ^ (2 * m + 1)] = refs[m][1]
    width = row_out.shape[0]
    heads = width // HEAD_DIM
    group = width // sites
    xc_all = flat_rows(xc[...], F32)
    rows = xc_all.shape[0]
    per = rows // haps
    cot_f = xc_all[:, width:]
    cot = cot_f.astype(BF16)
    hid = xc_all[:, :width]
    a_blocks = [unpack_block(at[i * haps : (i + 1) * haps], group) for i in range(sites)]
    for i in range(sites):
        hid = hid + mm(a_blocks[i], row_out[i * group : (i + 1) * group, :])
    hid = hid.astype(BF16).astype(F32)
    grad_att = mm_nt(cot, col_out[...]).astype(BF16)
    xhat, rstd = norm_parts(hid)
    normed = (xhat * gain[1:2, :]).astype(BF16)
    packed = mm(normed, col_proj[...]).astype(BF16)
    q = packed[:, :width]
    key = packed[:, width : 2 * width]
    val = packed[:, 2 * width :]
    kv_t = mm_nt(kv_t_w[...], normed).astype(BF16)
    key_st = jnp.concatenate([only_head(key, h) for h in range(heads)], axis=0)
    val_st = jnp.concatenate([only_head(val, h) for h in range(heads)], axis=0)
    scores = mm_nt(key_st, q) * (SCALE * LOG2E)
    dprob = mm_nt(val_st, grad_att)
    same = (
        lax.broadcasted_iota(jnp.int32, (rows, rows), 0) % per
        == lax.broadcasted_iota(jnp.int32, (rows, rows), 1) % per
    )
    att_t, dq_t, prob16, ds16 = [], [], [], []
    for h in range(heads):
        cols = slice(h * HEAD_DIM, (h + 1) * HEAD_DIM)
        s_h = jnp.where(same, scores[h * rows : (h + 1) * rows], -jnp.inf)
        e_h = jnp.exp2(s_h - jnp.max(s_h, axis=0, keepdims=True))
        inverse = 1.0 / jnp.sum(e_h, axis=0, keepdims=True)
        att_t.append(mm(kv_t[width:, :][cols], e_h.astype(BF16)) * inverse)
        p_h = e_h * inverse
        d_h = dprob[h * rows : (h + 1) * rows]
        delta = jnp.sum(p_h * d_h, axis=0, keepdims=True)
        ds_h = (p_h * (d_h - delta)).astype(BF16)
        prob16.append(p_h.astype(BF16))
        ds16.append(ds_h)
        dq_t.append(mm(kv_t[:width, :][cols], ds_h))
    att_t = jnp.concatenate(att_t, axis=0)
    w_all[:, 3 * width : 4 * width] = mm(att_t.astype(BF16), cot).astype(BF16)
    att = jnp.transpose(att_t).astype(BF16)
    out = hid + mm(att, col_out[...])
    dv_all = mm(jnp.concatenate(prob16, axis=0), grad_att)
    dk_all = mm(jnp.concatenate(ds16, axis=0), q)
    dv = sum(
        jnp.where(head_lanes(width, h), dv_all[h * rows : (h + 1) * rows], 0.0) for h in range(heads)
    )
    dk = sum(
        jnp.where(head_lanes(width, h), dk_all[h * rows : (h + 1) * rows], 0.0) for h in range(heads)
    )
    dq = jnp.transpose(jnp.concatenate(dq_t, axis=0))
    packed_grad = jnp.concatenate([dq * SCALE, dk * SCALE, dv], axis=1).astype(BF16)
    w_all[:, : 3 * width] = mm_tn(normed, packed_grad).astype(BF16)
    first = save(0, slice(0, 4 * width))
    first.start()
    grad_normed = mm_nt(packed_grad, col_proj[...])
    grad_hidden = (cot_f + norm_back(xhat, rstd, gain[1:2, :], grad_normed)).astype(BF16)
    for i in range(sites):
        g_i = mm_nt(grad_hidden, row_out[i * group : (i + 1) * group, :])
        ga_out[i * haps : (i + 1) * haps] = pack_block(g_i, haps)
    for i in range(sites):
        w_all[i * group : (i + 1) * group, 4 * width :] = mm_tn(a_blocks[i], grad_hidden).astype(BF16)
    second = save(1, slice(4 * width, 5 * width))
    second.start()
    both = jnp.concatenate([out, grad_hidden.astype(F32)], axis=1)
    og[...] = both.reshape(haps, per, 2 * width).astype(BF16)
    third = pltpu.make_async_copy(og, og_out, sems.at[2])
    third.start()
    send[...] = w_all[other, :]
    first.wait()
    second.wait()
    third.wait()


def split_outputs(hap, og, keep, send):
    for m in range(keep.shape[0]):
        keep[m] = og[hap[0] ^ (2 * m)]
        send[m] = og[hap[0] ^ (2 * m + 1)]


def column_split(sites, idx, keep, *refs):
    outs, both, gots = refs[-sites - 1 : -1], refs[-1], refs[: -sites - 1]
    got = jnp.concatenate([g[...].astype(F32) for g in gots], axis=0)
    both[...] = (keep[...].astype(F32) + got).astype(BF16)
    part = keep.shape[0] // sites
    for k in range(sites):
        outs[k][...] = both[pl.ds(pl.multiple_of((idx[0] ^ k) * part, part), part), :]


def row_backward(sites, haps, idx, core, g_in, prob, q, val, key_t, normed, *refs):
    gp_outs = refs[:sites]
    keep, send, g_all, ds_all, w_out = refs[sites:]
    me = idx[0]
    total, width = q.shape
    rows = total // sites
    for b in range(sites):
        g_all[b * rows : (b + 1) * rows, :] = unpack_block(
            g_in[pl.ds((me ^ b) * haps, haps)], width
        )
    dk = jnp.zeros((total, width), F32)
    dv = jnp.zeros((total, width), F32)
    dq_t = []
    for h in range(width // HEAD_DIM):
        val_h = only_head(val[...], h)
        dv = dv + mm(prob[h], only_head(g_all[...], h))
        for b in range(sites):
            here = pl.ds(b * rows, rows)
            dprob = mm_nt(val_h, g_all[b * rows : (b + 1) * rows, :])
            p_b = prob[h, :, here].astype(F32)
            delta = jnp.sum(p_b * dprob, axis=0, keepdims=True)
            ds_all[:, here] = (p_b * (dprob - delta)).astype(BF16)
        dk = dk + mm(ds_all[...], only_head(q[...], h))
        dq_t.append(mm(key_t[h * HEAD_DIM : (h + 1) * HEAD_DIM, :], ds_all[...]))
    dq_t = jnp.concatenate(dq_t, axis=0) * SCALE
    dk16 = (dk * SCALE).astype(BF16)
    dv16 = dv.astype(BF16)
    w_out[:width, :] = mm(dq_t.astype(BF16), normed[...]).astype(BF16)
    w_out[width : 2 * width, :] = mm_tn(dk16, normed[...]).astype(BF16)
    w_out[2 * width :, :] = mm_tn(dv16, normed[...]).astype(BF16)
    half = 3 * width // 2
    keep[...] = w_out[pl.ds(pl.multiple_of(core[0] * half, half), half), :]
    send[...] = w_out[pl.ds(pl.multiple_of((1 - core[0]) * half, half), half), :]
    dq = jnp.transpose(dq_t).astype(BF16)
    joined = jnp.concatenate([dq, dk16, dv16], axis=1)
    for b in range(sites):
        gp_outs[b][...] = joined[b * rows : (b + 1) * rows]


def row_finish(sites, haps, idx, hap, feats, gain, w_all, *refs):
    gps, ogs = refs[:sites], refs[sites : sites + haps // 2]
    out_ref, gf_ref, og = refs[sites + haps // 2 :]
    me = idx[0]
    width = feats.shape[1]
    for m in range(haps // 2):
        og[hap[0] ^ (2 * m)] = ogs[m][0]
        og[hap[0] ^ (2 * m + 1)] = ogs[m][1]
    both = flat_rows(og[...], F32)
    grad_normed = sum(mm(gps[k][...], w_all[me ^ k]) for k in range(sites))
    xhat, rstd = norm_parts(feats[...].astype(F32))
    grad = both[:, width:] + norm_back(xhat, rstd, gain[:1, :], grad_normed)
    out_ref[...] = both[:, :width].astype(BF16)
    gf_ref[...] = grad.astype(BF16)


def weights_join(row_keep, row_got, *refs):
    cols, out = refs[:-1], refs[-1]
    half, width = row_keep.shape
    out[:half, :] = (row_keep[...].astype(F32) + row_got[...].astype(F32)).astype(BF16)
    total = sum(c[...].astype(F32) for c in cols)
    part = total.shape[0]
    for t in range(5):
        tile = total[:, t * width : (t + 1) * width]
        out[half + t * part : half + (t + 1) * part, :] = tile.astype(BF16)


def weights_sum(*refs):
    terms = [r[...].astype(F32) for r in refs[:-1]]
    while len(terms) > 1:
        terms = [a + b for a, b in zip(terms[::2], terms[1::2])]
    refs[-1][...] = terms[0].astype(BF16)


def weights_finish(sites, idx, core, *refs):
    pieces = refs[: 2 * sites]
    rp, ro, cp, co, rows_t = refs[2 * sites :]
    width = ro.shape[0]
    group = width // sites
    unit = group // 2
    part = width // 2 // sites
    for j in range(2 * sites):
        k = j // 2
        cc = core[0] ^ (j % 2)
        g = idx[0] ^ k
        piece = pieces[j][...].astype(F32)
        for u in range(3):
            place = 3 * cc + u
            dest = (place // 2) * width + g * group + (place % 2) * unit
            rows_t[pl.ds(pl.multiple_of(dest, unit), unit), :] = piece[u * unit : (u + 1) * unit]
        here = pl.ds(pl.multiple_of(cc * (width // 2) + g * part, part), part)
        tiles = [piece[3 * unit + t * part : 3 * unit + (t + 1) * part] for t in range(5)]
        for t in range(3):
            cp[here, t * width : (t + 1) * width] = tiles[t]
        co[here, :] = tiles[3]
        ro[here, :] = tiles[4]
    rp[...] = jnp.transpose(rows_t[...])


def exchange(value, axis):
    return lax.all_to_all(value, axis, 0, 0, tiled=True)


def swapped(value, axis, by):
    length = lax.axis_size(axis)
    return lax.ppermute(value, axis, [(i, i ^ by) for i in range(length)])


def on_device(
    features,
    link_pattern,
    row_gain,
    row_proj,
    row_out,
    column_norm_gain,
    col_proj,
    col_out,
    cotangent,
):
    rows, _, width = features.shape
    sites, haps = lax.axis_size("site"), lax.axis_size("hap")
    count = sites * haps
    per = rows // haps
    group = width // sites
    heads = group // HEAD_DIM
    total = rows * sites
    both_axes = ("site", "hap")
    me = lax.axis_index("site")
    idx = me.reshape(1).astype(jnp.int32)
    hap = lax.axis_index("hap").reshape(1).astype(jnp.int32)
    core = hap % 2
    factor = lane_factor(per, group)
    block = ((count, per // factor, group * factor), BF16)
    feats = features.reshape(rows, width)
    cot = cotangent.reshape(rows, width)

    pieces = [feats] + [swapped(feats, "site", k) for k in range(1, sites)]
    gains = jnp.stack([row_gain, column_norm_gain])
    keep, send = call(
        functools.partial(join_inputs, haps),
        [((haps // 2, per, 2 * width), BF16)] * 2,
        hap, feats, cot, scalars=1,
        scratch=[pltpu.VMEM((haps, per, 2 * width), BF16)],
    )
    got = swapped(send, "hap", 1)
    xcs = call(relay_inputs, [((2, per, 2 * width), BF16)] * (haps // 2), keep, got)
    xcs = [xcs[0]] + [swapped(xcs[m], "hap", 2 * m) for m in range(1, haps // 2)]
    w_all = jnp.transpose(row_proj.reshape(width, 3, sites, group), (2, 1, 3, 0)).reshape(
        sites, 3 * group, width
    )
    w_t = lax.dynamic_index_in_dim(w_all, me, 0, keepdims=False)
    kv_t_w = jnp.transpose(col_proj[:, width:])

    att, prob, q, val, key_t, normed = call(
        functools.partial(row_forward, sites, haps),
        [
            block,
            ((heads, total, total), BF16),
            ((total, group), BF16),
            ((total, group), BF16),
            ((group, total), BF16),
            ((total, width), BF16),
        ],
        idx, link_pattern, *pieces, gains, w_t, scalars=2, us=20,
    )
    att, xcs = lax.optimization_barrier((att, xcs))
    at = exchange(att, both_axes)
    half = width // 2
    ga, col_send, col_keep, og = call(
        functools.partial(column_step, sites, haps),
        [
            block,
            ((half, 5 * width), BF16),
            ((half, 5 * width), BF16),
            ((haps, per, 2 * width), BF16),
        ],
        hap, at, row_out, gains, col_proj, kv_t_w, col_out, *xcs, scalars=1, far=2,
        scratch=[
            pltpu.VMEM((haps, per, 2 * width), BF16),
            pltpu.VMEM((haps, per, 2 * width), BF16),
            pltpu.VMEM((width, 5 * width), BF16),
            pltpu.SemaphoreType.DMA((3,)),
        ],
    )
    g_in = exchange(ga, both_axes)
    col_got = [swapped(col_send, "hap", 1)]
    cols = call(
        functools.partial(column_split, sites),
        [((half // sites, 5 * width), BF16)] * sites,
        idx, col_keep, *col_got, scalars=1, us=0,
        scratch=[pltpu.VMEM((half, 5 * width), BF16)],
    )
    g_in, _ = lax.optimization_barrier((g_in, cols))
    cols = [cols[0]] + [swapped(cols[k], "site", k) for k in range(1, sites)]
    *gps, row_keep, row_send = call(
        functools.partial(row_backward, sites, haps),
        [((rows, 3 * group), BF16)] * sites + [((3 * group // 2, width), BF16)] * 2,
        idx, core, g_in, prob, q, val, key_t, normed, scalars=2,
        scratch=[
            pltpu.VMEM((total, group), BF16),
            pltpu.VMEM((total, total), BF16),
            pltpu.VMEM((3 * group, width), BF16),
        ],
    )
    row_got = swapped(row_send, "hap", 1)
    depth = 3 * group // 2 + 5 * half // sites
    (joined,) = call(weights_join, [((depth, width), BF16)], row_keep, row_got, *cols)
    parts = [joined] + [swapped(joined, "hap", 2 * m) for m in range(1, haps // 2)]
    gps = [gps[0]] + [swapped(gps[k], "site", k) for k in range(1, sites)]
    og, _ = lax.optimization_barrier((og, joined))
    og_keep, og_send = call(
        split_outputs, [((haps // 2, per, 2 * width), BF16)] * 2, hap, og, scalars=1
    )
    og_got = swapped(og_send, "hap", 1)
    ogs = call(relay_inputs, [((2, per, 2 * width), BF16)] * (haps // 2), og_keep, og_got)
    parts, gps, ogs = lax.optimization_barrier((parts, gps, ogs))
    (mine,) = call(weights_sum, [((depth, width), BF16)], *parts)
    mine_swapped = swapped(mine, "hap", 1)
    ogs, _ = lax.optimization_barrier((ogs, mine))
    ogs = [ogs[0]] + [swapped(ogs[m], "hap", 2 * m) for m in range(1, haps // 2)]
    full = [swapped(mine, "site", k) for k in range(1, sites)]
    full, ogs = lax.optimization_barrier((full, ogs))
    full = [mine, mine_swapped] + [x for p in full for x in (p, swapped(p, "hap", 1))]
    out, grad = call(
        functools.partial(row_finish, sites, haps),
        [((rows, width), BF16)] * 2,
        idx, hap, feats, gains, w_all, *gps, *ogs, scalars=2,
        scratch=[pltpu.VMEM((haps, per, 2 * width), BF16)],
    )
    rp, ro, cp, co = call(
        functools.partial(weights_finish, sites),
        [((width, 3 * width), F32), ((width, width), F32)] * 2,
        idx, core, *full, scalars=2,
        scratch=[pltpu.VMEM((3 * width, width), F32)],
    )
    shape = (rows, 1, width)
    return (out.reshape(shape), grad.reshape(shape), rp, ro, cp, co)


def solution(mesh):
    data = P("site", "hap", None)
    return jax.shard_map(
        on_device,
        mesh=mesh,
        in_specs=(data, P(), P(), P(), P(), P(), P(), P(), data),
        out_specs=(data, data, P(), P(), P(), P()),
        check_vma=False,
    )
```

```python
import functools

import jax
import jax.numpy as jnp
from jax import lax
from jax.experimental import pallas as pl
from jax.experimental.pallas import tpu as pltpu
from jax.sharding import PartitionSpec as P

HEAD_DIM = 32
EPSILON = 1e-05
LOG2E = 1.4426950408889634
SCALE = HEAD_DIM ** (-0.5)
F32 = jnp.float32
BF16 = jnp.bfloat16
VMEM = pl.BlockSpec(memory_space=pltpu.VMEM)
HBM = pl.BlockSpec(memory_space=pltpu.HBM)
SMEM = pl.BlockSpec(memory_space=pltpu.SMEM)
PARAMS = pltpu.CompilerParams(vmem_limit_bytes=24 << 20)


def mm(a, b):
    return lax.dot_general(a, b, (((1,), (0,)), ((), ())), preferred_element_type=F32)


def mm_nt(a, b):
    return lax.dot_general(a, b, (((1,), (1,)), ((), ())), preferred_element_type=F32)


def mm_tn(a, b):
    return lax.dot_general(a, b, (((0,), (0,)), ((), ())), preferred_element_type=F32)


def norm_parts(x):
    centred = x - jnp.mean(x, axis=-1, keepdims=True)
    rstd = lax.rsqrt(jnp.mean(centred * centred, axis=-1, keepdims=True) + EPSILON)
    return centred * rstd, rstd


def norm_back(xhat, rstd, gain, grad):
    scaled = grad * gain
    first = jnp.mean(scaled, axis=-1, keepdims=True)
    second = jnp.mean(scaled * xhat, axis=-1, keepdims=True)
    return rstd * (scaled - first - xhat * second)


def head_lanes(width, head):
    return lax.broadcasted_iota(jnp.int32, (1, width), 1) // HEAD_DIM == head


def only_head(values, head):
    return jnp.where(head_lanes(values.shape[1], head), values, jnp.zeros_like(values))


def flat_rows(values, dtype=BF16):
    wide = values.astype(F32)
    return wide.reshape(wide.shape[0] * wide.shape[1], wide.shape[2]).astype(dtype)


def lane_factor(rows, width):
    factor = 128 // width
    return factor if (rows // factor) % 8 == 0 else 1


def pack_block(values, outer):
    rows, width = values.shape[0] // outer, values.shape[1]
    factor = lane_factor(rows, width)
    split = values.reshape(outer, factor, rows // factor, width)
    return jnp.concatenate([split[:, j] for j in range(factor)], axis=2).astype(BF16)


def unpack_block(values, width):
    wide = values.astype(F32)
    factor = wide.shape[2] // width
    split = [wide[:, None, :, j * width : (j + 1) * width] for j in range(factor)]
    joined = jnp.concatenate(split, axis=1)
    return joined.reshape(-1, width).astype(BF16)


def call(body, outs, *operands, scalars=0, scratch=(), us=0, far=0):
    cost = pl.CostEstimate(flops=us * 10**9 + 1, bytes_accessed=us * 3_600_000 + 1, transcendentals=0)
    return pl.pallas_call(
        body,
        out_shape=[jax.ShapeDtypeStruct(s, d) for s, d in outs[: len(outs) - far]]
        + [pltpu.HBM(s, d) for s, d in outs[len(outs) - far :]],
        in_specs=[SMEM] * scalars + [VMEM] * (len(operands) - scalars),
        out_specs=[VMEM] * (len(outs) - far) + [HBM] * far,
        scratch_shapes=list(scratch),
        compiler_params=PARAMS,
        cost_estimate=cost,
    )(*operands)


def linked_scores(scores, rows, sites, me, b, link):
    return [
        scores[a * rows : (a + 1) * rows] + jnp.where(link[me ^ b, me ^ a] > 0, 0.0, -jnp.inf)
        for a in range(sites)
    ]


def exp_parts(parts):
    high = functools.reduce(jnp.maximum, [jnp.max(part, axis=0, keepdims=True) for part in parts])
    parts = [jnp.exp2(part - high) for part in parts]
    total = sum(jnp.sum(part, axis=0, keepdims=True) for part in parts)
    return parts, 1.0 / total


def row_forward(sites, haps, idx, link, *refs):
    pieces = refs[:sites]
    cot, gain, w_t, row_out, x_out, n_out = refs[sites:]
    me = idx[0]
    rows, width = cot.shape
    heads = width // HEAD_DIM
    for k in range(sites):
        xhat, _ = norm_parts(pieces[k][...].astype(F32))
        n_out[k * rows : (k + 1) * rows, :] = (xhat * gain[:1, :]).astype(BF16)
    normed = n_out[...]
    q = mm_nt(normed[:rows], w_t[:width, :]).astype(BF16)
    key = mm_nt(normed, w_t[width : 2 * width, :]).astype(BF16)
    v_t = mm_nt(w_t[2 * width :, :], normed).astype(BF16)
    q_st = jnp.concatenate([only_head(q, h) for h in range(heads)], axis=0)
    att_t = []
    for h in range(heads):
        scores = mm_nt(key, q_st[h * rows : (h + 1) * rows]) * (SCALE * LOG2E)
        parts, inverse = exp_parts(linked_scores(scores, rows, sites, me, 0, link))
        e_h = jnp.concatenate([part.astype(BF16) for part in parts], axis=0)
        att_t.append(mm(v_t[h * HEAD_DIM : (h + 1) * HEAD_DIM], e_h) * inverse)
    att = jnp.transpose(jnp.concatenate(att_t, axis=0)).astype(BF16)
    hid = pieces[0][...].astype(F32) + mm(att, row_out[...])
    joined = jnp.concatenate([hid, cot[...].astype(F32), att.astype(F32)], axis=1)
    x_out[...] = joined.reshape(haps, rows // haps, 3 * width).astype(BF16)


def row_probs(sites, idx, link, normed_ref, w_t, p_out, q_out, v_out, kt_out):
    me = idx[0]
    normed = normed_ref[...]
    total, width = q_out.shape
    full = normed.shape[1]
    rows = total // sites

    def weights(part):
        return w_t[pl.ds(pl.multiple_of(part * full + me * width, width), width), :]

    q = mm_nt(normed, weights(0)).astype(BF16)
    key = mm_nt(normed, weights(1)).astype(BF16)
    q_out[...] = q
    v_out[...] = mm_nt(normed, weights(2)).astype(BF16)
    kt_out[...] = mm_nt(weights(1), normed).astype(BF16)
    for h in range(width // HEAD_DIM):
        key_h = only_head(key, h)
        for b in range(sites):
            here = pl.ds(b * rows, rows)
            scores = mm_nt(key_h, q[b * rows : (b + 1) * rows]) * (SCALE * LOG2E)
            parts, inverse = exp_parts(linked_scores(scores, rows, sites, me, b, link))
            for a in range(sites):
                p_out[h, a * rows : (a + 1) * rows, here] = (parts[a] * inverse).astype(BF16)


def column_step(sites, haps, hap, x_in, row_out, gain, col_proj, kv_t_w, col_out, *refs):
    ga_out, send, keep, og_out, og, w_all, sems = refs
    core = hap[0] % 2
    half = row_out.shape[0] // 2
    mine = pl.ds(pl.multiple_of(core * half, half), half)
    other = pl.ds(pl.multiple_of((1 - core) * half, half), half)

    def save(j, cols):
        return pltpu.make_async_copy(w_all.at[mine, cols], keep.at[:, cols], sems.at[j])

    width = row_out.shape[0]
    heads = width // HEAD_DIM
    group = width // sites
    x_all = flat_rows(x_in[...], F32)
    rows = x_all.shape[0]
    per = rows // haps
    hid = x_all[:, :width]
    cot_f = x_all[:, width : 2 * width]
    cot = cot_f.astype(BF16)
    row_att = x_all[:, 2 * width :].astype(BF16)
    grad_att = mm_nt(cot, col_out[...]).astype(BF16)
    xhat, rstd = norm_parts(hid)
    normed = (xhat * gain[1:2, :]).astype(BF16)
    packed = mm(normed, col_proj[...]).astype(BF16)
    q = packed[:, :width]
    key = packed[:, width : 2 * width]
    val = packed[:, 2 * width :]
    kv_t = mm_nt(kv_t_w[...], normed).astype(BF16)
    key_st = jnp.concatenate([only_head(key, h) for h in range(heads)], axis=0)
    val_st = jnp.concatenate([only_head(val, h) for h in range(heads)], axis=0)
    scores = mm_nt(key_st, q) * (SCALE * LOG2E)
    dprob = mm_nt(val_st, grad_att)
    same = (
        lax.broadcasted_iota(jnp.int32, (rows, rows), 0) % per
        == lax.broadcasted_iota(jnp.int32, (rows, rows), 1) % per
    )
    att_t, dq_t, prob16, ds16 = [], [], [], []
    for h in range(heads):
        cols = slice(h * HEAD_DIM, (h + 1) * HEAD_DIM)
        s_h = jnp.where(same, scores[h * rows : (h + 1) * rows], -jnp.inf)
        e_h = jnp.exp2(s_h - jnp.max(s_h, axis=0, keepdims=True))
        inverse = 1.0 / jnp.sum(e_h, axis=0, keepdims=True)
        att_t.append(mm(kv_t[width:, :][cols], e_h.astype(BF16)) * inverse)
        p_h = e_h * inverse
        d_h = dprob[h * rows : (h + 1) * rows]
        delta = jnp.sum(p_h * d_h, axis=0, keepdims=True)
        ds_h = (p_h * (d_h - delta)).astype(BF16)
        prob16.append(p_h.astype(BF16))
        ds16.append(ds_h)
        dq_t.append(mm(kv_t[:width, :][cols], ds_h))
    att_t = jnp.concatenate(att_t, axis=0)
    w_all[:, 3 * width : 4 * width] = mm(att_t.astype(BF16), cot).astype(BF16)
    att = jnp.transpose(att_t).astype(BF16)
    out = hid + mm(att, col_out[...])
    dv_all = mm(jnp.concatenate(prob16, axis=0), grad_att)
    dk_all = mm(jnp.concatenate(ds16, axis=0), q)
    dv = sum(
        jnp.where(head_lanes(width, h), dv_all[h * rows : (h + 1) * rows], 0.0) for h in range(heads)
    )
    dk = sum(
        jnp.where(head_lanes(width, h), dk_all[h * rows : (h + 1) * rows], 0.0) for h in range(heads)
    )
    dq = jnp.transpose(jnp.concatenate(dq_t, axis=0))
    packed_grad = jnp.concatenate([dq * SCALE, dk * SCALE, dv], axis=1).astype(BF16)
    w_all[:, : 3 * width] = mm_tn(normed, packed_grad).astype(BF16)
    first = save(0, slice(0, 4 * width))
    first.start()
    grad_normed = mm_nt(packed_grad, col_proj[...])
    grad_hidden = (cot_f + norm_back(xhat, rstd, gain[1:2, :], grad_normed)).astype(BF16)
    for i in range(sites):
        g_i = mm_nt(grad_hidden, row_out[i * group : (i + 1) * group, :])
        ga_out[i * haps : (i + 1) * haps] = pack_block(g_i, haps)
    w_all[:, 4 * width :] = mm_tn(row_att, grad_hidden).astype(BF16)
    second = save(1, slice(4 * width, 5 * width))
    second.start()
    both = jnp.concatenate([out, grad_hidden.astype(F32)], axis=1)
    og[...] = both.reshape(haps, per, 2 * width).astype(BF16)
    third = pltpu.make_async_copy(og, og_out, sems.at[2])
    third.start()
    send[...] = w_all[other, :]
    first.wait()
    second.wait()
    third.wait()


def split_outputs(hap, og, keep, send):
    for m in range(keep.shape[0]):
        keep[m] = og[hap[0] ^ (2 * m)]
        send[m] = og[hap[0] ^ (2 * m + 1)]


def column_split(sites, idx, keep, *refs):
    outs, both, gots = refs[-sites - 1 : -1], refs[-1], refs[: -sites - 1]
    got = jnp.concatenate([g[...].astype(F32) for g in gots], axis=0)
    both[...] = (keep[...].astype(F32) + got).astype(BF16)
    part = keep.shape[0] // sites
    for k in range(sites):
        outs[k][...] = both[pl.ds(pl.multiple_of((idx[0] ^ k) * part, part), part), :]


def row_backward(sites, haps, idx, core, g_in, prob, q, val, key_t, normed, *refs):
    gp_outs = refs[:sites]
    keep, send, g_all, ds_all, w_out = refs[sites:]
    me = idx[0]
    total, width = q.shape
    rows = total // sites
    for b in range(sites):
        g_all[b * rows : (b + 1) * rows, :] = unpack_block(
            g_in[pl.ds((me ^ b) * haps, haps)], width
        )
    dk = jnp.zeros((total, width), F32)
    dv = jnp.zeros((total, width), F32)
    dq_t = []
    for h in range(width // HEAD_DIM):
        val_h = only_head(val[...], h)
        dv = dv + mm(prob[h], only_head(g_all[...], h))
        for b in range(sites):
            here = pl.ds(b * rows, rows)
            dprob = mm_nt(val_h, g_all[b * rows : (b + 1) * rows, :])
            p_b = prob[h, :, here].astype(F32)
            delta = jnp.sum(p_b * dprob, axis=0, keepdims=True)
            ds_all[:, here] = (p_b * (dprob - delta)).astype(BF16)
        dk = dk + mm(ds_all[...], only_head(q[...], h))
        dq_t.append(mm(key_t[h * HEAD_DIM : (h + 1) * HEAD_DIM, :], ds_all[...]))
    dq_t = jnp.concatenate(dq_t, axis=0) * SCALE
    dk16 = (dk * SCALE).astype(BF16)
    dv16 = dv.astype(BF16)
    w_out[:width, :] = mm(dq_t.astype(BF16), normed[...]).astype(BF16)
    w_out[width : 2 * width, :] = mm_tn(dk16, normed[...]).astype(BF16)
    w_out[2 * width :, :] = mm_tn(dv16, normed[...]).astype(BF16)
    half = 3 * width // 2
    keep[...] = w_out[pl.ds(pl.multiple_of(core[0] * half, half), half), :]
    send[...] = w_out[pl.ds(pl.multiple_of((1 - core[0]) * half, half), half), :]
    dq = jnp.transpose(dq_t).astype(BF16)
    joined = jnp.concatenate([dq, dk16, dv16], axis=1)
    for b in range(sites):
        gp_outs[b][...] = joined[b * rows : (b + 1) * rows]


def row_finish(sites, haps, idx, hap, feats, gain, w_t, gp, *refs):
    gps, parts = refs[: sites - 1], refs[sites - 1 : sites - 1 + haps // 2]
    out_ref, gf_ref, og = refs[sites - 1 + haps // 2 :]
    me = idx[0]
    rows, width = feats.shape
    group = width // sites
    per = rows // haps
    for m in range(haps // 2):
        base = parts[m].shape[0] - 4 * per
        for j in range(2):
            for side in range(2):
                start = base + (2 * j + side) * per
                og[side, hap[0] ^ (2 * m + j)] = parts[m][start : start + per, :].astype(F32)
    grads = [gp[...]] + [g[g.shape[0] - rows :, : 3 * group] for g in gps]
    grad_normed = 0.0
    for k in range(sites):
        place = [pl.multiple_of(p * width + (me ^ k) * group, group) for p in range(3)]
        weights = jnp.concatenate([w_t[pl.ds(p, group), :] for p in place], axis=0)
        grad_normed = grad_normed + mm(grads[k], weights)
    xhat, rstd = norm_parts(feats[...].astype(F32))
    grad = og[1].reshape(rows, width) + norm_back(xhat, rstd, gain[:1, :], grad_normed)
    out_ref[...] = og[0].reshape(rows, width).astype(BF16)
    gf_ref[...] = grad.astype(BF16)


def weights_join(sites, row_keep, row_got, og_keep, og_got, *refs):
    cols, outs = refs[:sites], refs[sites:]
    half, width = row_keep.shape
    depth = half + 5 * cols[0].shape[0]
    per = og_keep.shape[1]
    total = sum(c[...].astype(F32) for c in cols)
    tiles = [total[:, t * width : (t + 1) * width] for t in range(5)]
    rows = row_keep[...].astype(F32) + row_got[...].astype(F32)
    joined = jnp.concatenate([rows] + tiles, axis=0).astype(BF16)
    for m, out in enumerate(outs):
        out[:depth, :] = joined
        both = [og_keep[m].astype(F32), og_got[m].astype(F32)]
        both = [x[:, j * width : (j + 1) * width] for x in both for j in range(2)]
        out[depth:, :] = jnp.concatenate(both, axis=0).astype(BF16)


def weights_sum(haps, sites, *refs):
    parts, gps = refs[: haps // 2], refs[haps // 2 : haps // 2 + sites - 1]
    mine, outs = refs[haps // 2 + sites - 1], refs[haps // 2 + sites :]
    depth, width = mine.shape
    terms = [r[:depth, :].astype(F32) for r in parts]
    while len(terms) > 1:
        terms = [a + b for a, b in zip(terms[::2], terms[1::2])]
    mine[...] = terms[0].astype(BF16)
    for gp, out in zip(gps, outs):
        out[:depth, :] = mine[...]
        out[depth:, : gp.shape[1]] = gp[...]
        out[depth:, gp.shape[1] :] = jnp.zeros((gp.shape[0], width - gp.shape[1]), BF16)


def weights_finish(sites, idx, core, *refs):
    pieces = refs[: 2 * sites]
    rp, ro, cp, co, rows_t = refs[2 * sites :]
    width = ro.shape[0]
    group = width // sites
    unit = group // 2
    part = width // 2 // sites
    for j in range(2 * sites):
        k = j // 2
        cc = core[0] ^ (j % 2)
        g = idx[0] ^ k
        piece = pieces[j][...].astype(F32)
        for u in range(3):
            place = 3 * cc + u
            dest = (place // 2) * width + g * group + (place % 2) * unit
            rows_t[pl.ds(pl.multiple_of(dest, unit), unit), :] = piece[u * unit : (u + 1) * unit]
        here = pl.ds(pl.multiple_of(cc * (width // 2) + g * part, part), part)
        tiles = [piece[3 * unit + t * part : 3 * unit + (t + 1) * part] for t in range(5)]
        for t in range(3):
            cp[here, t * width : (t + 1) * width] = tiles[t]
        co[here, :] = tiles[3]
        ro[here, :] = tiles[4]
    rp[...] = jnp.transpose(rows_t[...])


def exchange(value, axis):
    return lax.all_to_all(value, axis, 0, 0, tiled=True)


def swapped(value, axis, by):
    length = lax.axis_size(axis)
    return lax.ppermute(value, axis, [(i, i ^ by) for i in range(length)])


def on_device(
    features,
    link_pattern,
    row_gain,
    row_proj,
    row_out,
    column_norm_gain,
    col_proj,
    col_out,
    cotangent,
):
    rows, _, width = features.shape
    sites, haps = lax.axis_size("site"), lax.axis_size("hap")
    count = sites * haps
    per = rows // haps
    group = width // sites
    heads = group // HEAD_DIM
    total = rows * sites
    both_axes = ("site", "hap")
    me = lax.axis_index("site")
    idx = me.reshape(1).astype(jnp.int32)
    hap = lax.axis_index("hap").reshape(1).astype(jnp.int32)
    core = hap % 2
    factor = lane_factor(per, group)
    block = ((count, per // factor, group * factor), BF16)
    feats = features.reshape(rows, width)
    cot = cotangent.reshape(rows, width)

    pieces = [feats] + [swapped(feats, "site", k) for k in range(1, sites)]
    gains = jnp.stack([row_gain, column_norm_gain])
    w_t = jnp.transpose(row_proj)
    kv_t_w = jnp.transpose(col_proj[:, width:])

    x_out, normed = call(
        functools.partial(row_forward, sites, haps),
        [((haps, per, 3 * width), BF16), ((total, width), BF16)],
        idx, link_pattern, *pieces, cot, gains, w_t, row_out, scalars=2,
    )
    x_in = exchange(x_out, "hap")
    prob, q, val, key_t = call(
        functools.partial(row_probs, sites),
        [
            ((heads, total, total), BF16),
            ((total, group), BF16),
            ((total, group), BF16),
            ((group, total), BF16),
        ],
        idx, link_pattern, normed, w_t, scalars=2, us=20,
    )
    x_in, _ = lax.optimization_barrier((x_in, prob))
    half = width // 2
    ga, col_send, col_keep, og = call(
        functools.partial(column_step, sites, haps),
        [
            block,
            ((half, 5 * width), BF16),
            ((half, 5 * width), BF16),
            ((haps, per, 2 * width), BF16),
        ],
        hap, x_in, row_out, gains, col_proj, kv_t_w, col_out, scalars=1, far=2,
        scratch=[
            pltpu.VMEM((haps, per, 2 * width), BF16),
            pltpu.VMEM((width, 5 * width), BF16),
            pltpu.SemaphoreType.DMA((3,)),
        ],
    )
    g_in = exchange(ga, both_axes)
    col_got = [swapped(col_send, "hap", 1)]
    cols = call(
        functools.partial(column_split, sites),
        [((half // sites, 5 * width), BF16)] * sites,
        idx, col_keep, *col_got, scalars=1, us=0,
        scratch=[pltpu.VMEM((half, 5 * width), BF16)],
    )
    og_keep, og_send = call(
        split_outputs, [((haps // 2, per, 2 * width), BF16)] * 2, hap, og, scalars=1
    )
    og_got = swapped(og_send, "hap", 1)
    g_in, _ = lax.optimization_barrier((g_in, (cols, og_got)))
    cols = [cols[0]] + [swapped(cols[k], "site", k) for k in range(1, sites)]
    *gps, row_keep, row_send = call(
        functools.partial(row_backward, sites, haps),
        [((rows, 3 * group), BF16)] * sites + [((3 * group // 2, width), BF16)] * 2,
        idx, core, g_in, prob, q, val, key_t, normed, scalars=2,
        scratch=[
            pltpu.VMEM((total, group), BF16),
            pltpu.VMEM((total, total), BF16),
            pltpu.VMEM((3 * group, width), BF16),
        ],
    )
    row_got = swapped(row_send, "hap", 1)
    depth = 3 * group // 2 + 5 * half // sites
    parts = call(
        functools.partial(weights_join, sites),
        [((depth + 4 * per, width), BF16)] * (haps // 2),
        row_keep, row_got, og_keep, og_got, *cols,
    )
    parts = [parts[0]] + [swapped(parts[m], "hap", 2 * m) for m in range(1, haps // 2)]
    mine, *sends = call(
        functools.partial(weights_sum, haps, sites),
        [((depth, width), BF16)] + [((depth + rows, width), BF16)] * (sites - 1),
        *parts, *gps[1:],
    )
    got = [swapped(sends[k - 1], "site", k) for k in range(1, sites)]
    full = [x for p in [mine] + got for x in (p, swapped(p, "hap", 1))]
    out, grad = call(
        functools.partial(row_finish, sites, haps),
        [((rows, width), BF16)] * 2,
        idx, hap, feats, gains, w_t, gps[0], *got, *parts, scalars=2,
        scratch=[pltpu.VMEM((2, haps, per, width), F32)],
    )
    rp, ro, cp, co = call(
        functools.partial(weights_finish, sites),
        [((width, 3 * width), F32), ((width, width), F32)] * 2,
        idx, core, *full, scalars=2,
        scratch=[pltpu.VMEM((3 * width, width), F32)],
    )
    shape = (rows, 1, width)
    return (out.reshape(shape), grad.reshape(shape), rp, ro, cp, co)


def solution(mesh):
    data = P("site", "hap", None)
    return jax.shard_map(
        on_device,
        mesh=mesh,
        in_specs=(data, P(), P(), P(), P(), P(), P(), P(), data),
        out_specs=(data, data, P(), P(), P(), P()),
        check_vma=False,
    )
```

```python
import functools

import jax
import jax.numpy as jnp
from jax import lax
from jax.experimental import pallas as pl
from jax.experimental.pallas import tpu as pltpu
from jax.sharding import PartitionSpec as P

HEAD_DIM = 32
EPSILON = 1e-05
LOG2E = 1.4426950408889634
SCALE = HEAD_DIM ** (-0.5)
F32 = jnp.float32
BF16 = jnp.bfloat16
VMEM = pl.BlockSpec(memory_space=pltpu.VMEM)
HBM = pl.BlockSpec(memory_space=pltpu.HBM)
SMEM = pl.BlockSpec(memory_space=pltpu.SMEM)
PARAMS = pltpu.CompilerParams(vmem_limit_bytes=24 << 20)


def mm(a, b):
    return lax.dot_general(a, b, (((1,), (0,)), ((), ())), preferred_element_type=F32)


def mm_nt(a, b):
    return lax.dot_general(a, b, (((1,), (1,)), ((), ())), preferred_element_type=F32)


def mm_tn(a, b):
    return lax.dot_general(a, b, (((0,), (0,)), ((), ())), preferred_element_type=F32)


def norm_parts(x):
    centred = x - jnp.mean(x, axis=-1, keepdims=True)
    rstd = lax.rsqrt(jnp.mean(centred * centred, axis=-1, keepdims=True) + EPSILON)
    return centred * rstd, rstd


def norm_back(xhat, rstd, gain, grad):
    scaled = grad * gain
    first = jnp.mean(scaled, axis=-1, keepdims=True)
    second = jnp.mean(scaled * xhat, axis=-1, keepdims=True)
    return rstd * (scaled - first - xhat * second)


def head_lanes(width, head):
    return lax.broadcasted_iota(jnp.int32, (1, width), 1) // HEAD_DIM == head


def only_head(values, head):
    return jnp.where(head_lanes(values.shape[1], head), values, jnp.zeros_like(values))


def flat_rows(values, dtype=BF16):
    wide = values.astype(F32)
    return wide.reshape(wide.shape[0] * wide.shape[1], wide.shape[2]).astype(dtype)


def lane_factor(rows, width):
    factor = 128 // width
    return factor if (rows // factor) % 8 == 0 else 1


def pack_block(values, outer):
    rows, width = values.shape[0] // outer, values.shape[1]
    factor = lane_factor(rows, width)
    split = values.reshape(outer, factor, rows // factor, width)
    return jnp.concatenate([split[:, j] for j in range(factor)], axis=2).astype(BF16)


def unpack_block(values, width):
    wide = values.astype(F32)
    factor = wide.shape[2] // width
    split = [wide[:, None, :, j * width : (j + 1) * width] for j in range(factor)]
    joined = jnp.concatenate(split, axis=1)
    return joined.reshape(-1, width).astype(BF16)


def call(body, outs, *operands, scalars=0, scratch=(), us=0, far=0):
    cost = pl.CostEstimate(flops=us * 10**9 + 1, bytes_accessed=us * 3_600_000 + 1, transcendentals=0)
    return pl.pallas_call(
        body,
        out_shape=[jax.ShapeDtypeStruct(s, d) for s, d in outs[: len(outs) - far]]
        + [pltpu.HBM(s, d) for s, d in outs[len(outs) - far :]],
        in_specs=[SMEM] * scalars + [VMEM] * (len(operands) - scalars),
        out_specs=[VMEM] * (len(outs) - far) + [HBM] * far,
        scratch_shapes=list(scratch),
        compiler_params=PARAMS,
        cost_estimate=cost,
    )(*operands)


def linked_scores(scores, rows, sites, me, b, link):
    return [
        scores[a * rows : (a + 1) * rows] + jnp.where(link[me ^ b, me ^ a] > 0, 0.0, -jnp.inf)
        for a in range(sites)
    ]


def exp_parts(parts):
    high = functools.reduce(jnp.maximum, [jnp.max(part, axis=0, keepdims=True) for part in parts])
    parts = [jnp.exp2(part - high) for part in parts]
    total = sum(jnp.sum(part, axis=0, keepdims=True) for part in parts)
    return parts, 1.0 / total


def row_forward(sites, haps, idx, link, *refs):
    pieces = refs[:sites]
    cot, gain, w_t, row_out, x_out, n_out = refs[sites:]
    me = idx[0]
    rows, width = cot.shape
    heads = width // HEAD_DIM
    for k in range(sites):
        xhat, _ = norm_parts(pieces[k][...].astype(F32))
        n_out[k * rows : (k + 1) * rows, :] = (xhat * gain[:1, :]).astype(BF16)
    normed = n_out[...]
    q = mm_nt(normed[:rows], w_t[:width, :]).astype(BF16)
    key = mm_nt(normed, w_t[width : 2 * width, :]).astype(BF16)
    v_t = mm_nt(w_t[2 * width :, :], normed).astype(BF16)
    q_st = jnp.concatenate([only_head(q, h) for h in range(heads)], axis=0)
    att_t = []
    for h in range(heads):
        scores = mm_nt(key, q_st[h * rows : (h + 1) * rows]) * (SCALE * LOG2E)
        parts, inverse = exp_parts(linked_scores(scores, rows, sites, me, 0, link))
        e_h = jnp.concatenate([part.astype(BF16) for part in parts], axis=0)
        att_t.append(mm(v_t[h * HEAD_DIM : (h + 1) * HEAD_DIM], e_h) * inverse)
    att = jnp.transpose(jnp.concatenate(att_t, axis=0)).astype(BF16)
    hid = pieces[0][...].astype(F32) + mm(att, row_out[...])
    joined = jnp.concatenate([hid, cot[...].astype(F32), att.astype(F32)], axis=1)
    x_out[...] = joined.reshape(haps, rows // haps, 3 * width).astype(BF16)


def row_probs(sites, idx, link, normed_ref, w_t, p_out, q_out, v_out, kt_out):
    me = idx[0]
    normed = normed_ref[...]
    total, width = q_out.shape
    full = normed.shape[1]
    rows = total // sites

    def weights(part):
        return w_t[pl.ds(pl.multiple_of(part * full + me * width, width), width), :]

    q = mm_nt(normed, weights(0)).astype(BF16)
    key = mm_nt(normed, weights(1)).astype(BF16)
    q_out[...] = q
    v_out[...] = mm_nt(normed, weights(2)).astype(BF16)
    kt_out[...] = mm_nt(weights(1), normed).astype(BF16)
    for h in range(width // HEAD_DIM):
        key_h = only_head(key, h)
        for b in range(sites):
            here = pl.ds(b * rows, rows)
            scores = mm_nt(key_h, q[b * rows : (b + 1) * rows]) * (SCALE * LOG2E)
            parts, inverse = exp_parts(linked_scores(scores, rows, sites, me, b, link))
            for a in range(sites):
                p_out[h, a * rows : (a + 1) * rows, here] = (parts[a] * inverse).astype(BF16)


def column_step(sites, haps, hap, x_in, row_out, gain, col_proj, kv_t_w, col_out, *refs):
    ga_out, send, keep, og_out, og, w_all, sems = refs
    core = hap[0] % 2
    half = row_out.shape[0] // 2
    mine = pl.ds(pl.multiple_of(core * half, half), half)
    other = pl.ds(pl.multiple_of((1 - core) * half, half), half)

    def save(j, cols):
        return pltpu.make_async_copy(w_all.at[mine, cols], keep.at[:, cols], sems.at[j])

    width = row_out.shape[0]
    heads = width // HEAD_DIM
    group = width // sites
    x_all = flat_rows(x_in[...], F32)
    rows = x_all.shape[0]
    per = rows // haps
    hid = x_all[:, :width]
    cot_f = x_all[:, width : 2 * width]
    cot = cot_f.astype(BF16)
    row_att = x_all[:, 2 * width :].astype(BF16)
    grad_att = mm_nt(cot, col_out[...]).astype(BF16)
    xhat, rstd = norm_parts(hid)
    normed = (xhat * gain[1:2, :]).astype(BF16)
    packed = mm(normed, col_proj[...]).astype(BF16)
    q = packed[:, :width]
    key = packed[:, width : 2 * width]
    val = packed[:, 2 * width :]
    kv_t = mm_nt(kv_t_w[...], normed).astype(BF16)
    key_st = jnp.concatenate([only_head(key, h) for h in range(heads)], axis=0)
    val_st = jnp.concatenate([only_head(val, h) for h in range(heads)], axis=0)
    scores = mm_nt(key_st, q) * (SCALE * LOG2E)
    dprob = mm_nt(val_st, grad_att)
    same = (
        lax.broadcasted_iota(jnp.int32, (rows, rows), 0) % per
        == lax.broadcasted_iota(jnp.int32, (rows, rows), 1) % per
    )
    att_t, dq_t, prob16, ds16 = [], [], [], []
    for h in range(heads):
        cols = slice(h * HEAD_DIM, (h + 1) * HEAD_DIM)
        s_h = jnp.where(same, scores[h * rows : (h + 1) * rows], -jnp.inf)
        e_h = jnp.exp2(s_h - jnp.max(s_h, axis=0, keepdims=True))
        inverse = 1.0 / jnp.sum(e_h, axis=0, keepdims=True)
        att_t.append(mm(kv_t[width:, :][cols], e_h.astype(BF16)) * inverse)
        p_h = e_h * inverse
        d_h = dprob[h * rows : (h + 1) * rows]
        delta = jnp.sum(p_h * d_h, axis=0, keepdims=True)
        ds_h = (p_h * (d_h - delta)).astype(BF16)
        prob16.append(p_h.astype(BF16))
        ds16.append(ds_h)
        dq_t.append(mm(kv_t[:width, :][cols], ds_h))
    att_t = jnp.concatenate(att_t, axis=0)
    w_all[:, 3 * width : 4 * width] = mm(att_t.astype(BF16), cot).astype(BF16)
    att = jnp.transpose(att_t).astype(BF16)
    out = hid + mm(att, col_out[...])
    dv_all = mm(jnp.concatenate(prob16, axis=0), grad_att)
    dk_all = mm(jnp.concatenate(ds16, axis=0), q)
    dv = sum(
        jnp.where(head_lanes(width, h), dv_all[h * rows : (h + 1) * rows], 0.0) for h in range(heads)
    )
    dk = sum(
        jnp.where(head_lanes(width, h), dk_all[h * rows : (h + 1) * rows], 0.0) for h in range(heads)
    )
    dq = jnp.transpose(jnp.concatenate(dq_t, axis=0))
    packed_grad = jnp.concatenate([dq * SCALE, dk * SCALE, dv], axis=1).astype(BF16)
    w_all[:, : 3 * width] = mm_tn(normed, packed_grad).astype(BF16)
    first = save(0, slice(0, 4 * width))
    first.start()
    grad_normed = mm_nt(packed_grad, col_proj[...])
    grad_hidden = (cot_f + norm_back(xhat, rstd, gain[1:2, :], grad_normed)).astype(BF16)
    for i in range(sites):
        g_i = mm_nt(grad_hidden, row_out[i * group : (i + 1) * group, :])
        ga_out[i * haps : (i + 1) * haps] = pack_block(g_i, haps)
    w_all[:, 4 * width :] = mm_tn(row_att, grad_hidden).astype(BF16)
    second = save(1, slice(4 * width, 5 * width))
    second.start()
    both = jnp.concatenate([out, grad_hidden.astype(F32)], axis=1)
    og[...] = both.reshape(haps, per, 2 * width).astype(BF16)
    third = pltpu.make_async_copy(og, og_out, sems.at[2])
    third.start()
    send[...] = w_all[other, :]
    first.wait()
    second.wait()
    third.wait()


def split_outputs(hap, og, keep, send):
    for m in range(keep.shape[0]):
        keep[m] = og[hap[0] ^ (2 * m)]
        send[m] = og[hap[0] ^ (2 * m + 1)]


def column_split(depth, hap, keep, got, *refs):
    outs, both = refs[:depth], refs[depth]
    both[...] = (keep[...].astype(F32) + got[...].astype(F32)).astype(BF16)
    part = keep.shape[0] // depth
    for m in range(depth):
        start = ((hap[0] // 2) ^ m) * part
        outs[m][...] = both[pl.ds(pl.multiple_of(start, part), part), :]


def row_backward(sites, haps, idx, core, g_in, prob, q, val, key_t, normed, *refs):
    gp_outs = refs[:sites]
    keep, send, g_all, ds_all, w_out = refs[sites:]
    me = idx[0]
    total, width = q.shape
    rows = total // sites
    for b in range(sites):
        g_all[b * rows : (b + 1) * rows, :] = unpack_block(
            g_in[pl.ds((me ^ b) * haps, haps)], width
        )
    dk = jnp.zeros((total, width), F32)
    dv = jnp.zeros((total, width), F32)
    dq_t = []
    for h in range(width // HEAD_DIM):
        val_h = only_head(val[...], h)
        dv = dv + mm(prob[h], only_head(g_all[...], h))
        for b in range(sites):
            here = pl.ds(b * rows, rows)
            dprob = mm_nt(val_h, g_all[b * rows : (b + 1) * rows, :])
            p_b = prob[h, :, here].astype(F32)
            delta = jnp.sum(p_b * dprob, axis=0, keepdims=True)
            ds_all[:, here] = (p_b * (dprob - delta)).astype(BF16)
        dk = dk + mm(ds_all[...], only_head(q[...], h))
        dq_t.append(mm(key_t[h * HEAD_DIM : (h + 1) * HEAD_DIM, :], ds_all[...]))
    dq_t = jnp.concatenate(dq_t, axis=0) * SCALE
    dk16 = (dk * SCALE).astype(BF16)
    dv16 = dv.astype(BF16)
    w_out[:width, :] = mm(dq_t.astype(BF16), normed[...]).astype(BF16)
    w_out[width : 2 * width, :] = mm_tn(dk16, normed[...]).astype(BF16)
    w_out[2 * width :, :] = mm_tn(dv16, normed[...]).astype(BF16)
    half = 3 * width // 2
    keep[...] = w_out[pl.ds(pl.multiple_of(core[0] * half, half), half), :]
    send[...] = w_out[pl.ds(pl.multiple_of((1 - core[0]) * half, half), half), :]
    dq = jnp.transpose(dq_t).astype(BF16)
    joined = jnp.concatenate([dq, dk16, dv16], axis=1)
    for b in range(sites):
        gp_outs[b][...] = joined[b * rows : (b + 1) * rows]


def tree_sum(terms):
    while len(terms) > 1:
        terms = [a + b for a, b in zip(terms[::2], terms[1::2])]
    return terms[0]


def row_join(row_keep, row_got, og_keep, og_got, *outs):
    half, width = row_keep.shape
    joined = (row_keep[...].astype(F32) + row_got[...].astype(F32)).astype(BF16)
    for m, out in enumerate(outs):
        out[:half, :] = joined
        both = [og_keep[m].astype(F32), og_got[m].astype(F32)]
        both = [x[:, j * width : (j + 1) * width] for x in both for j in range(2)]
        out[half:, :] = jnp.concatenate(both, axis=0).astype(BF16)


def column_join(depth, sites, idx, *refs):
    cols, gps, out = refs[:depth], refs[depth : depth + sites], refs[depth + sites]
    width = out.shape[2]
    total = tree_sum([c[...].astype(F32) for c in cols])
    tiles = [total[:, t * width : (t + 1) * width] for t in range(5)]
    joined = jnp.concatenate(tiles, axis=0).astype(BF16)
    top = joined.shape[0]
    rows, used = gps[0].shape
    for k in range(sites):
        place = idx[0] ^ k
        out[place, :top, :] = joined
        out[place, top:, :used] = gps[k][...]
        out[place, top:, used:] = jnp.zeros((rows, width - used), BF16)


def row_sum(*refs):
    out = refs[-1]
    total = tree_sum([r[: out.shape[1], :].astype(F32) for r in refs[:-1]]).astype(BF16)
    for i in range(out.shape[0]):
        out[i] = total


def column_sum(got, out):
    total = sum(got[i, : out.shape[0], :].astype(F32) for i in range(got.shape[0]))
    out[...] = total.astype(BF16)


def row_finish(sites, haps, hap, feats, gain, w_t, gps, *refs):
    parts = refs[: haps // 2]
    out_ref, gf_ref, og = refs[haps // 2 :]
    rows, width = feats.shape
    group = width // sites
    per = rows // haps
    for m in range(haps // 2):
        base = parts[m].shape[0] - 4 * per
        for j in range(2):
            for side in range(2):
                start = base + (2 * j + side) * per
                og[side, hap[0] ^ (2 * m + j)] = parts[m][start : start + per, :].astype(F32)
    top = gps.shape[1] - rows
    grad_normed = 0.0
    for i in range(sites):
        place = [p * width + i * group for p in range(3)]
        weights = jnp.concatenate([w_t[p : p + group, :] for p in place], axis=0)
        grad_normed = grad_normed + mm(gps[i, top:, : 3 * group], weights)
    xhat, rstd = norm_parts(feats[...].astype(F32))
    grad = og[1].reshape(rows, width) + norm_back(xhat, rstd, gain[:1, :], grad_normed)
    out_ref[...] = og[0].reshape(rows, width).astype(BF16)
    gf_ref[...] = grad.astype(BF16)


def weights_finish(depth, hap, row_own, row_other, *refs):
    pieces = refs[: 2 * depth]
    rp, ro, cp, co, rows_t = refs[2 * depth :]
    width = ro.shape[0]
    sites = row_own.shape[0]
    group = width // sites
    unit = group // 2
    part = width // 2 // depth
    core = hap[0] % 2
    for j, rows in enumerate((row_own, row_other)):
        cc = core ^ j
        for i in range(sites):
            piece = rows[i].astype(F32)
            for u in range(3):
                place = 3 * cc + u
                dest = (place // 2) * width + i * group + (place % 2) * unit
                rows_t[pl.ds(pl.multiple_of(dest, unit), unit), :] = piece[u * unit : (u + 1) * unit]
    for j in range(2 * depth):
        cc = core ^ (j % 2)
        zz = (hap[0] // 2) ^ (j // 2)
        piece = pieces[j][...].astype(F32)
        here = pl.ds(pl.multiple_of(cc * (width // 2) + zz * part, part), part)
        tiles = [piece[t * part : (t + 1) * part] for t in range(5)]
        for t in range(3):
            cp[here, t * width : (t + 1) * width] = tiles[t]
        co[here, :] = tiles[3]
        ro[here, :] = tiles[4]
    rp[...] = jnp.transpose(rows_t[...])


def exchange(value, axis):
    return lax.all_to_all(value, axis, 0, 0, tiled=True)


def swapped(value, axis, by):
    length = lax.axis_size(axis)
    return lax.ppermute(value, axis, [(i, i ^ by) for i in range(length)])


def on_device(
    features,
    link_pattern,
    row_gain,
    row_proj,
    row_out,
    column_norm_gain,
    col_proj,
    col_out,
    cotangent,
):
    rows, _, width = features.shape
    sites, haps = lax.axis_size("site"), lax.axis_size("hap")
    count = sites * haps
    per = rows // haps
    group = width // sites
    heads = group // HEAD_DIM
    total = rows * sites
    both_axes = ("site", "hap")
    me = lax.axis_index("site")
    idx = me.reshape(1).astype(jnp.int32)
    hap = lax.axis_index("hap").reshape(1).astype(jnp.int32)
    core = hap % 2
    factor = lane_factor(per, group)
    block = ((count, per // factor, group * factor), BF16)
    feats = features.reshape(rows, width)
    cot = cotangent.reshape(rows, width)

    pieces = [feats] + [swapped(feats, "site", k) for k in range(1, sites)]
    gains = jnp.stack([row_gain, column_norm_gain])
    w_t = jnp.transpose(row_proj)
    kv_t_w = jnp.transpose(col_proj[:, width:])

    x_out, normed = call(
        functools.partial(row_forward, sites, haps),
        [((haps, per, 3 * width), BF16), ((total, width), BF16)],
        idx, link_pattern, *pieces, cot, gains, w_t, row_out, scalars=2,
    )
    x_in = exchange(x_out, "hap")
    prob, q, val, key_t = call(
        functools.partial(row_probs, sites),
        [
            ((heads, total, total), BF16),
            ((total, group), BF16),
            ((total, group), BF16),
            ((group, total), BF16),
        ],
        idx, link_pattern, normed, w_t, scalars=2, us=20,
    )
    x_in, _ = lax.optimization_barrier((x_in, prob))
    half = width // 2
    ga, col_send, col_keep, og = call(
        functools.partial(column_step, sites, haps),
        [
            block,
            ((half, 5 * width), BF16),
            ((half, 5 * width), BF16),
            ((haps, per, 2 * width), BF16),
        ],
        hap, x_in, row_out, gains, col_proj, kv_t_w, col_out, scalars=1, far=2,
        scratch=[
            pltpu.VMEM((haps, per, 2 * width), BF16),
            pltpu.VMEM((width, 5 * width), BF16),
            pltpu.SemaphoreType.DMA((3,)),
        ],
    )
    g_in = exchange(ga, both_axes)
    col_got = swapped(col_send, "hap", 1)
    depth = haps // 2
    cols = call(
        functools.partial(column_split, depth),
        [((half // depth, 5 * width), BF16)] * depth,
        hap, col_keep, col_got, scalars=1,
        scratch=[pltpu.VMEM((half, 5 * width), BF16)],
    )
    og_keep, og_send = call(
        split_outputs, [((haps // 2, per, 2 * width), BF16)] * 2, hap, og, scalars=1
    )
    og_got = swapped(og_send, "hap", 1)
    g_in, _ = lax.optimization_barrier((g_in, (cols, og_got)))
    cols = [cols[0]] + [swapped(cols[m], "hap", 2 * m) for m in range(1, depth)]
    *gps, row_keep, row_send = call(
        functools.partial(row_backward, sites, haps),
        [((rows, 3 * group), BF16)] * sites + [((3 * group // 2, width), BF16)] * 2,
        idx, core, g_in, prob, q, val, key_t, normed, scalars=2,
        scratch=[
            pltpu.VMEM((total, group), BF16),
            pltpu.VMEM((total, total), BF16),
            pltpu.VMEM((3 * group, width), BF16),
        ],
    )
    row_got = swapped(row_send, "hap", 1)
    tall = 5 * half // depth
    (col_out_parts,) = call(
        functools.partial(column_join, depth, sites),
        [((sites, tall + rows, width), BF16)],
        idx, *cols, *gps, scalars=1,
    )
    parts = call(
        row_join,
        [((3 * group // 2 + 4 * per, width), BF16)] * depth,
        row_keep, row_got, og_keep, og_got,
    )
    parts, col_out_parts = lax.optimization_barrier((parts, col_out_parts))
    col_in_parts = exchange(col_out_parts, "site")
    parts = [parts[0]] + [swapped(parts[m], "hap", 2 * m) for m in range(1, depth)]
    (row_mine,) = call(row_sum, [((sites, 3 * group // 2, width), BF16)], *parts)
    (col_mine,) = call(column_sum, [((tall, width), BF16)], col_in_parts)
    row_mine, col_mine = lax.optimization_barrier((row_mine, col_mine))
    row_full = exchange(row_mine, "site")
    col_full = [col_mine] + [swapped(col_mine, "hap", 2 * m) for m in range(1, depth)]
    row_full, col_full = lax.optimization_barrier((row_full, col_full))
    col_full = [x for p in col_full for x in (p, swapped(p, "hap", 1))]
    row_other = swapped(row_full, "hap", 1)
    out, grad = call(
        functools.partial(row_finish, sites, haps),
        [((rows, width), BF16)] * 2,
        hap, feats, gains, w_t, col_in_parts, *parts, scalars=1,
        scratch=[pltpu.VMEM((2, haps, per, width), F32)],
    )
    rp, ro, cp, co = call(
        functools.partial(weights_finish, depth),
        [((width, 3 * width), F32), ((width, width), F32)] * 2,
        hap, row_full, row_other, *col_full, scalars=1,
        scratch=[pltpu.VMEM((3 * width, width), F32)],
    )
    shape = (rows, 1, width)
    return (out.reshape(shape), grad.reshape(shape), rp, ro, cp, co)


def solution(mesh):
    data = P("site", "hap", None)
    return jax.shard_map(
        on_device,
        mesh=mesh,
        in_specs=(data, P(), P(), P(), P(), P(), P(), P(), data),
        out_specs=(data, data, P(), P(), P(), P()),
        check_vma=False,
    )
```

```python
import functools

import jax
import jax.numpy as jnp
from jax import lax
from jax.experimental import pallas as pl
from jax.experimental.pallas import tpu as pltpu
from jax.sharding import PartitionSpec as P

HEAD_DIM = 32
EPSILON = 1e-05
LOG2E = 1.4426950408889634
SCALE = HEAD_DIM ** (-0.5)
F32 = jnp.float32
BF16 = jnp.bfloat16
VMEM = pl.BlockSpec(memory_space=pltpu.VMEM)
HBM = pl.BlockSpec(memory_space=pltpu.HBM)
SMEM = pl.BlockSpec(memory_space=pltpu.SMEM)
PARAMS = pltpu.CompilerParams(vmem_limit_bytes=24 << 20)


def mm(a, b):
    return lax.dot_general(a, b, (((1,), (0,)), ((), ())), preferred_element_type=F32)


def mm_nt(a, b):
    return lax.dot_general(a, b, (((1,), (1,)), ((), ())), preferred_element_type=F32)


def mm_tn(a, b):
    return lax.dot_general(a, b, (((0,), (0,)), ((), ())), preferred_element_type=F32)


def norm_parts(x):
    centred = x - jnp.mean(x, axis=-1, keepdims=True)
    rstd = lax.rsqrt(jnp.mean(centred * centred, axis=-1, keepdims=True) + EPSILON)
    return centred * rstd, rstd


def norm_back(xhat, rstd, gain, grad):
    scaled = grad * gain
    first = jnp.mean(scaled, axis=-1, keepdims=True)
    second = jnp.mean(scaled * xhat, axis=-1, keepdims=True)
    return rstd * (scaled - first - xhat * second)


def head_lanes(width, head):
    return lax.broadcasted_iota(jnp.int32, (1, width), 1) // HEAD_DIM == head


def only_head(values, head):
    return jnp.where(head_lanes(values.shape[1], head), values, jnp.zeros_like(values))


def flat_rows(values, dtype=BF16):
    wide = values.astype(F32)
    return wide.reshape(wide.shape[0] * wide.shape[1], wide.shape[2]).astype(dtype)


def lane_factor(rows, width):
    factor = 128 // width
    return factor if (rows // factor) % 8 == 0 else 1


def pack_block(values, outer):
    rows, width = values.shape[0] // outer, values.shape[1]
    factor = lane_factor(rows, width)
    split = values.reshape(outer, factor, rows // factor, width)
    return jnp.concatenate([split[:, j] for j in range(factor)], axis=2).astype(BF16)


def unpack_block(values, width):
    wide = values.astype(F32)
    factor = wide.shape[2] // width
    split = [wide[:, None, :, j * width : (j + 1) * width] for j in range(factor)]
    joined = jnp.concatenate(split, axis=1)
    return joined.reshape(-1, width).astype(BF16)


def call(body, outs, *operands, scalars=0, scratch=(), us=0, far=0):
    cost = pl.CostEstimate(flops=us * 10**9 + 1, bytes_accessed=us * 3_600_000 + 1, transcendentals=0)
    return pl.pallas_call(
        body,
        out_shape=[jax.ShapeDtypeStruct(s, d) for s, d in outs[: len(outs) - far]]
        + [pltpu.HBM(s, d) for s, d in outs[len(outs) - far :]],
        in_specs=[SMEM] * scalars + [VMEM] * (len(operands) - scalars),
        out_specs=[VMEM] * (len(outs) - far) + [HBM] * far,
        scratch_shapes=list(scratch),
        compiler_params=PARAMS,
        cost_estimate=cost,
    )(*operands)


def linked_scores(scores, rows, sites, me, b, link):
    return [
        scores[a * rows : (a + 1) * rows] + jnp.where(link[me ^ b, me ^ a] > 0, 0.0, -jnp.inf)
        for a in range(sites)
    ]


def exp_parts(parts):
    high = functools.reduce(jnp.maximum, [jnp.max(part, axis=0, keepdims=True) for part in parts])
    parts = [jnp.exp2(part - high) for part in parts]
    total = sum(jnp.sum(part, axis=0, keepdims=True) for part in parts)
    return parts, 1.0 / total


def row_forward(sites, haps, idx, link, *refs):
    pieces = refs[:sites]
    cot, gain, w_t, row_out, x_out, n_out = refs[sites:]
    me = idx[0]
    rows, width = cot.shape
    heads = width // HEAD_DIM
    for k in range(sites):
        xhat, _ = norm_parts(pieces[k][...].astype(F32))
        n_out[k * rows : (k + 1) * rows, :] = (xhat * gain[:1, :]).astype(BF16)
    normed = n_out[...]
    q = mm_nt(normed[:rows], w_t[:width, :]).astype(BF16)
    key = mm_nt(normed, w_t[width : 2 * width, :]).astype(BF16)
    v_t = mm_nt(w_t[2 * width :, :], normed).astype(BF16)
    q_st = jnp.concatenate([only_head(q, h) for h in range(heads)], axis=0)
    bias = [jnp.where(link[me, me ^ a] > 0, 0.0, -jnp.inf) for a in range(sites)]
    ones = jnp.ones((16, sites * rows), BF16)
    att_t = []
    for h in range(heads):
        scores = mm_nt(key, q_st[h * rows : (h + 1) * rows]) * (SCALE * LOG2E)
        parts = [scores[a * rows : (a + 1) * rows] for a in range(sites)]
        highs = [jnp.max(parts[a], axis=0, keepdims=True) + bias[a] for a in range(sites)]
        high = functools.reduce(jnp.maximum, highs)
        e_h = [jnp.exp2(parts[a] - (high - bias[a])).astype(BF16) for a in range(sites)]
        e_h = jnp.concatenate(e_h, axis=0)
        with_ones = jnp.concatenate([v_t[h * HEAD_DIM : (h + 1) * HEAD_DIM], ones], axis=0)
        mixed = mm(with_ones, e_h)
        att_t.append(mixed[:HEAD_DIM] / mixed[HEAD_DIM : HEAD_DIM + 1])
    att = jnp.transpose(jnp.concatenate(att_t, axis=0)).astype(BF16)
    hid = pieces[0][...].astype(F32) + mm(att, row_out[...])
    joined = jnp.concatenate([hid, cot[...].astype(F32), att.astype(F32)], axis=1)
    x_out[...] = joined.reshape(haps, rows // haps, 3 * width).astype(BF16)


def row_probs(sites, idx, link, normed_ref, w_t, p_out, q_out, v_out, kt_out):
    me = idx[0]
    normed = normed_ref[...]
    total, width = q_out.shape
    full = normed.shape[1]
    rows = total // sites

    def weights(part):
        return w_t[pl.ds(pl.multiple_of(part * full + me * width, width), width), :]

    q = mm_nt(normed, weights(0)).astype(BF16)
    key = mm_nt(normed, weights(1)).astype(BF16)
    q_out[...] = q
    v_out[...] = mm_nt(normed, weights(2)).astype(BF16)
    kt_out[...] = mm_nt(weights(1), normed).astype(BF16)
    for h in range(width // HEAD_DIM):
        key_h = only_head(key, h)
        for b in range(sites):
            here = pl.ds(b * rows, rows)
            scores = mm_nt(key_h, q[b * rows : (b + 1) * rows]) * (SCALE * LOG2E)
            parts, inverse = exp_parts(linked_scores(scores, rows, sites, me, b, link))
            for a in range(sites):
                p_out[h, a * rows : (a + 1) * rows, here] = (parts[a] * inverse).astype(BF16)


def column_step(sites, haps, hap, x_in, row_out, gain, col_proj, kv_t_w, col_out, *refs):
    ga_out, send, keep, og_out, og, w_all, sems = refs
    core = hap[0] % 2
    half = row_out.shape[0] // 2
    mine = pl.ds(pl.multiple_of(core * half, half), half)
    other = pl.ds(pl.multiple_of((1 - core) * half, half), half)

    def save(j, cols):
        return pltpu.make_async_copy(w_all.at[mine, cols], keep.at[:, cols], sems.at[j])

    width = row_out.shape[0]
    heads = width // HEAD_DIM
    group = width // sites
    x_all = flat_rows(x_in[...], F32)
    rows = x_all.shape[0]
    per = rows // haps
    hid = x_all[:, :width]
    cot_f = x_all[:, width : 2 * width]
    cot = cot_f.astype(BF16)
    row_att = x_all[:, 2 * width :].astype(BF16)
    grad_att = mm_nt(cot, col_out[...]).astype(BF16)
    xhat, rstd = norm_parts(hid)
    normed = (xhat * gain[1:2, :]).astype(BF16)
    packed = mm(normed, col_proj[...]).astype(BF16)
    q = packed[:, :width]
    key = packed[:, width : 2 * width]
    val = packed[:, 2 * width :]
    kv_t = mm_nt(kv_t_w[...], normed).astype(BF16)
    key_st = jnp.concatenate([only_head(key, h) for h in range(heads)], axis=0)
    val_st = jnp.concatenate([only_head(val, h) for h in range(heads)], axis=0)
    scores = mm_nt(key_st, q) * (SCALE * LOG2E)
    dprob = mm_nt(val_st, grad_att)
    same = (
        lax.broadcasted_iota(jnp.int32, (rows, rows), 0) % per
        == lax.broadcasted_iota(jnp.int32, (rows, rows), 1) % per
    )
    att_t, dq_t, prob16, ds16 = [], [], [], []
    for h in range(heads):
        cols = slice(h * HEAD_DIM, (h + 1) * HEAD_DIM)
        s_h = jnp.where(same, scores[h * rows : (h + 1) * rows], -jnp.inf)
        e_h = jnp.exp2(s_h - jnp.max(s_h, axis=0, keepdims=True))
        inverse = 1.0 / jnp.sum(e_h, axis=0, keepdims=True)
        att_t.append(mm(kv_t[width:, :][cols], e_h.astype(BF16)) * inverse)
        p_h = e_h * inverse
        d_h = dprob[h * rows : (h + 1) * rows]
        delta = jnp.sum(p_h * d_h, axis=0, keepdims=True)
        ds_h = (p_h * (d_h - delta)).astype(BF16)
        prob16.append(p_h.astype(BF16))
        ds16.append(ds_h)
        dq_t.append(mm(kv_t[:width, :][cols], ds_h))
    att_t = jnp.concatenate(att_t, axis=0)
    w_all[:, 3 * width : 4 * width] = mm(att_t.astype(BF16), cot).astype(BF16)
    att = jnp.transpose(att_t).astype(BF16)
    out = hid + mm(att, col_out[...])
    dv_all = mm(jnp.concatenate(prob16, axis=0), grad_att)
    dk_all = mm(jnp.concatenate(ds16, axis=0), q)
    dv = sum(
        jnp.where(head_lanes(width, h), dv_all[h * rows : (h + 1) * rows], 0.0) for h in range(heads)
    )
    dk = sum(
        jnp.where(head_lanes(width, h), dk_all[h * rows : (h + 1) * rows], 0.0) for h in range(heads)
    )
    dq = jnp.transpose(jnp.concatenate(dq_t, axis=0))
    packed_grad = jnp.concatenate([dq * SCALE, dk * SCALE, dv], axis=1).astype(BF16)
    w_all[:, : 3 * width] = mm_tn(normed, packed_grad).astype(BF16)
    first = save(0, slice(0, 4 * width))
    first.start()
    grad_normed = mm_nt(packed_grad, col_proj[...])
    grad_hidden = (cot_f + norm_back(xhat, rstd, gain[1:2, :], grad_normed)).astype(BF16)
    for i in range(sites):
        g_i = mm_nt(grad_hidden, row_out[i * group : (i + 1) * group, :])
        ga_out[i * haps : (i + 1) * haps] = pack_block(g_i, haps)
    w_all[:, 4 * width :] = mm_tn(row_att, grad_hidden).astype(BF16)
    second = save(1, slice(4 * width, 5 * width))
    second.start()
    both = jnp.concatenate([out, grad_hidden.astype(F32)], axis=1)
    og[...] = both.reshape(haps, per, 2 * width).astype(BF16)
    third = pltpu.make_async_copy(og, og_out, sems.at[2])
    third.start()
    send[...] = w_all[other, :]
    first.wait()
    second.wait()
    third.wait()


def split_outputs(hap, og, keep, send):
    for m in range(keep.shape[0]):
        keep[m] = og[hap[0] ^ (2 * m)]
        send[m] = og[hap[0] ^ (2 * m + 1)]


def column_split(sites, idx, keep, *refs):
    outs, both, gots = refs[-sites - 1 : -1], refs[-1], refs[: -sites - 1]
    got = jnp.concatenate([g[...].astype(F32) for g in gots], axis=0)
    both[...] = (keep[...].astype(F32) + got).astype(BF16)
    part = keep.shape[0] // sites
    for k in range(sites):
        outs[k][...] = both[pl.ds(pl.multiple_of((idx[0] ^ k) * part, part), part), :]


def row_backward(sites, haps, idx, core, g_in, prob, q, val, key_t, normed, *refs):
    gp_out, keep, send, g_all, ds_all, w_out = refs
    me = idx[0]
    total, width = q.shape
    rows = total // sites
    for b in range(sites):
        g_all[b * rows : (b + 1) * rows, :] = unpack_block(
            g_in[pl.ds((me ^ b) * haps, haps)], width
        )
    dk = jnp.zeros((total, width), F32)
    dv = jnp.zeros((total, width), F32)
    dq_t = []
    for h in range(width // HEAD_DIM):
        val_h = only_head(val[...], h)
        dv = dv + mm(prob[h], only_head(g_all[...], h))
        for b in range(sites):
            here = pl.ds(b * rows, rows)
            dprob = mm_nt(val_h, g_all[b * rows : (b + 1) * rows, :])
            p_b = prob[h, :, here].astype(F32)
            delta = jnp.sum(p_b * dprob, axis=0, keepdims=True)
            ds_all[:, here] = (p_b * (dprob - delta)).astype(BF16)
        dk = dk + mm(ds_all[...], only_head(q[...], h))
        dq_t.append(mm(key_t[h * HEAD_DIM : (h + 1) * HEAD_DIM, :], ds_all[...]))
    dq_t = jnp.concatenate(dq_t, axis=0) * SCALE
    dk16 = (dk * SCALE).astype(BF16)
    dv16 = dv.astype(BF16)
    w_out[:width, :] = mm(dq_t.astype(BF16), normed[...]).astype(BF16)
    w_out[width : 2 * width, :] = mm_tn(dk16, normed[...]).astype(BF16)
    w_out[2 * width :, :] = mm_tn(dv16, normed[...]).astype(BF16)
    half = 3 * width // 2
    keep[...] = w_out[pl.ds(pl.multiple_of(core[0] * half, half), half), :]
    send[...] = w_out[pl.ds(pl.multiple_of((1 - core[0]) * half, half), half), :]
    dq = jnp.transpose(dq_t).astype(BF16)
    joined = jnp.concatenate([dq, dk16, dv16], axis=1)
    for b in range(sites):
        gp_out[me ^ b, :, : 3 * width] = joined[b * rows : (b + 1) * rows]
        gp_out[me ^ b, :, 3 * width :] = jnp.zeros((rows, gp_out.shape[2] - 3 * width), BF16)


def row_finish(sites, haps, hap, feats, gain, w_t, gps, *refs):
    parts = refs[: haps // 2]
    out_ref, gf_ref, og = refs[haps // 2 :]
    rows, width = feats.shape
    group = width // sites
    per = rows // haps
    for m in range(haps // 2):
        base = parts[m].shape[0] - 4 * per
        for j in range(2):
            for side in range(2):
                start = base + (2 * j + side) * per
                og[side, hap[0] ^ (2 * m + j)] = parts[m][start : start + per, :].astype(F32)
    grad_normed = 0.0
    for i in range(sites):
        place = [p * width + i * group for p in range(3)]
        weights = jnp.concatenate([w_t[p : p + group, :] for p in place], axis=0)
        grad_normed = grad_normed + mm(gps[i, :, : 3 * group], weights)
    xhat, rstd = norm_parts(feats[...].astype(F32))
    grad = og[1].reshape(rows, width) + norm_back(xhat, rstd, gain[:1, :], grad_normed)
    out_ref[...] = og[0].reshape(rows, width).astype(BF16)
    gf_ref[...] = grad.astype(BF16)


def weights_join(sites, row_keep, row_got, og_keep, og_got, *refs):
    cols, outs = refs[:sites], refs[sites:]
    half, width = row_keep.shape
    depth = half + 5 * cols[0].shape[0]
    per = og_keep.shape[1]
    total = sum(c[...].astype(F32) for c in cols)
    tiles = [total[:, t * width : (t + 1) * width] for t in range(5)]
    rows = row_keep[...].astype(F32) + row_got[...].astype(F32)
    joined = jnp.concatenate([rows] + tiles, axis=0).astype(BF16)
    for m, out in enumerate(outs):
        out[:depth, :] = joined
        both = [og_keep[m].astype(F32), og_got[m].astype(F32)]
        both = [x[:, j * width : (j + 1) * width] for x in both for j in range(2)]
        out[depth:, :] = jnp.concatenate(both, axis=0).astype(BF16)


def weights_sum(*refs):
    terms = [r[: refs[-1].shape[0], :].astype(F32) for r in refs[:-1]]
    while len(terms) > 1:
        terms = [a + b for a, b in zip(terms[::2], terms[1::2])]
    refs[-1][...] = terms[0].astype(BF16)


def weights_finish(sites, idx, core, *refs):
    pieces = refs[: 2 * sites]
    rp, ro, cp, co, rows_t = refs[2 * sites :]
    width = ro.shape[0]
    group = width // sites
    unit = group // 2
    part = width // 2 // sites
    for j in range(2 * sites):
        k = j // 2
        cc = core[0] ^ (j % 2)
        g = idx[0] ^ k
        piece = pieces[j][...].astype(F32)
        for u in range(3):
            place = 3 * cc + u
            dest = (place // 2) * width + g * group + (place % 2) * unit
            rows_t[pl.ds(pl.multiple_of(dest, unit), unit), :] = piece[u * unit : (u + 1) * unit]
        here = pl.ds(pl.multiple_of(cc * (width // 2) + g * part, part), part)
        tiles = [piece[3 * unit + t * part : 3 * unit + (t + 1) * part] for t in range(5)]
        for t in range(3):
            cp[here, t * width : (t + 1) * width] = tiles[t]
        co[here, :] = tiles[3]
        ro[here, :] = tiles[4]
    rp[...] = jnp.transpose(rows_t[...])


def exchange(value, axis):
    return lax.all_to_all(value, axis, 0, 0, tiled=True)


def swapped(value, axis, by):
    length = lax.axis_size(axis)
    return lax.ppermute(value, axis, [(i, i ^ by) for i in range(length)])


def on_device(
    features,
    link_pattern,
    row_gain,
    row_proj,
    row_out,
    column_norm_gain,
    col_proj,
    col_out,
    cotangent,
):
    rows, _, width = features.shape
    sites, haps = lax.axis_size("site"), lax.axis_size("hap")
    count = sites * haps
    per = rows // haps
    group = width // sites
    heads = group // HEAD_DIM
    total = rows * sites
    both_axes = ("site", "hap")
    me = lax.axis_index("site")
    idx = me.reshape(1).astype(jnp.int32)
    hap = lax.axis_index("hap").reshape(1).astype(jnp.int32)
    core = hap % 2
    factor = lane_factor(per, group)
    block = ((count, per // factor, group * factor), BF16)
    feats = features.reshape(rows, width)
    cot = cotangent.reshape(rows, width)

    pieces = [feats] + [swapped(feats, "site", k) for k in range(1, sites)]
    link_pattern = jnp.where(link_pattern > 0, 1, 0)
    gains = jnp.stack([row_gain, column_norm_gain])
    w_t = jnp.transpose(row_proj)
    kv_t_w = jnp.transpose(col_proj[:, width:])

    x_out, normed = call(
        functools.partial(row_forward, sites, haps),
        [((haps, per, 3 * width), BF16), ((total, width), BF16)],
        idx, link_pattern, *pieces, cot, gains, w_t, row_out, scalars=2,
    )
    x_in = exchange(x_out, "hap")
    prob, q, val, key_t = call(
        functools.partial(row_probs, sites),
        [
            ((heads, total, total), BF16),
            ((total, group), BF16),
            ((total, group), BF16),
            ((group, total), BF16),
        ],
        idx, link_pattern, normed, w_t, scalars=2, us=20,
    )
    x_in, _ = lax.optimization_barrier((x_in, prob))
    half = width // 2
    ga, col_send, col_keep, og = call(
        functools.partial(column_step, sites, haps),
        [
            block,
            ((half, 5 * width), BF16),
            ((half, 5 * width), BF16),
            ((haps, per, 2 * width), BF16),
        ],
        hap, x_in, row_out, gains, col_proj, kv_t_w, col_out, scalars=1, far=2,
        scratch=[
            pltpu.VMEM((haps, per, 2 * width), BF16),
            pltpu.VMEM((width, 5 * width), BF16),
            pltpu.SemaphoreType.DMA((3,)),
        ],
    )
    g_in = exchange(ga, both_axes)
    col_got = [swapped(col_send, "hap", 1)]
    cols = call(
        functools.partial(column_split, sites),
        [((half // sites, 5 * width), BF16)] * sites,
        idx, col_keep, *col_got, scalars=1, us=0,
        scratch=[pltpu.VMEM((half, 5 * width), BF16)],
    )
    og_keep, og_send = call(
        split_outputs, [((haps // 2, per, 2 * width), BF16)] * 2, hap, og, scalars=1
    )
    og_got = swapped(og_send, "hap", 1)
    g_in, _ = lax.optimization_barrier((g_in, (cols, og_got)))
    cols = [cols[0]] + [swapped(cols[k], "site", k) for k in range(1, sites)]
    gps, row_keep, row_send = call(
        functools.partial(row_backward, sites, haps),
        [((sites, rows, width), BF16)] + [((3 * group // 2, width), BF16)] * 2,
        idx, core, g_in, prob, q, val, key_t, normed, scalars=2,
        scratch=[
            pltpu.VMEM((total, group), BF16),
            pltpu.VMEM((total, total), BF16),
            pltpu.VMEM((3 * group, width), BF16),
        ],
    )
    row_got = swapped(row_send, "hap", 1)
    depth = 3 * group // 2 + 5 * half // sites
    parts = call(
        functools.partial(weights_join, sites),
        [((depth + 4 * per, width), BF16)] * (haps // 2),
        row_keep, row_got, og_keep, og_got, *cols,
    )
    parts = [parts[0]] + [swapped(parts[m], "hap", 2 * m) for m in range(1, haps // 2)]
    gps, _ = lax.optimization_barrier((gps, parts[1]))
    gps = exchange(gps, "site")
    parts, gps = lax.optimization_barrier((parts, gps))
    (mine,) = call(weights_sum, [((depth, width), BF16)], *parts)
    got = [swapped(mine, "site", k) for k in range(1, sites)]
    full = [x for p in [mine] + got for x in (p, swapped(p, "hap", 1))]
    out, grad = call(
        functools.partial(row_finish, sites, haps),
        [((rows, width), BF16)] * 2,
        hap, feats, gains, w_t, gps, *parts, scalars=1,
        scratch=[pltpu.VMEM((2, haps, per, width), F32)],
    )
    rp, ro, cp, co = call(
        functools.partial(weights_finish, sites),
        [((width, 3 * width), F32), ((width, width), F32)] * 2,
        idx, core, *full, scalars=2,
        scratch=[pltpu.VMEM((3 * width, width), F32)],
    )
    shape = (rows, 1, width)
    return (out.reshape(shape), grad.reshape(shape), rp, ro, cp, co)


def solution(mesh):
    data = P("site", "hap", None)
    return jax.shard_map(
        on_device,
        mesh=mesh,
        in_specs=(data, P(), P(), P(), P(), P(), P(), P(), data),
        out_specs=(data, data, P(), P(), P(), P()),
        check_vma=False,
    )
```

```python
import functools

import jax
import jax.numpy as jnp
from jax import lax
from jax.experimental import pallas as pl
from jax.experimental.pallas import tpu as pltpu
from jax.sharding import PartitionSpec as P

HEAD_DIM = 32
EPSILON = 1e-05
LOG2E = 1.4426950408889634
SCALE = HEAD_DIM ** (-0.5)
F32 = jnp.float32
BF16 = jnp.bfloat16
VMEM = pl.BlockSpec(memory_space=pltpu.VMEM)
HBM = pl.BlockSpec(memory_space=pltpu.HBM)
SMEM = pl.BlockSpec(memory_space=pltpu.SMEM)
PARAMS = pltpu.CompilerParams(vmem_limit_bytes=24 << 20)


def mm(a, b):
    return lax.dot_general(a, b, (((1,), (0,)), ((), ())), preferred_element_type=F32)


def mm_nt(a, b):
    return lax.dot_general(a, b, (((1,), (1,)), ((), ())), preferred_element_type=F32)


def mm_tn(a, b):
    return lax.dot_general(a, b, (((0,), (0,)), ((), ())), preferred_element_type=F32)


def norm_parts(x):
    centred = x - jnp.mean(x, axis=-1, keepdims=True)
    rstd = lax.rsqrt(jnp.mean(centred * centred, axis=-1, keepdims=True) + EPSILON)
    return centred * rstd, rstd


def norm_back(xhat, rstd, gain, grad):
    scaled = grad * gain
    first = jnp.mean(scaled, axis=-1, keepdims=True)
    second = jnp.mean(scaled * xhat, axis=-1, keepdims=True)
    return rstd * (scaled - first - xhat * second)


def head_lanes(width, head):
    return lax.broadcasted_iota(jnp.int32, (1, width), 1) // HEAD_DIM == head


def only_head(values, head):
    return jnp.where(head_lanes(values.shape[1], head), values, jnp.zeros_like(values))


def flat_rows(values, dtype=BF16):
    wide = values.astype(F32)
    return wide.reshape(wide.shape[0] * wide.shape[1], wide.shape[2]).astype(dtype)


def lane_factor(rows, width):
    factor = 128 // width
    return factor if (rows // factor) % 8 == 0 else 1


def pack_block(values, outer):
    rows, width = values.shape[0] // outer, values.shape[1]
    factor = lane_factor(rows, width)
    split = values.reshape(outer, factor, rows // factor, width)
    return jnp.concatenate([split[:, j] for j in range(factor)], axis=2).astype(BF16)


def unpack_block(values, width):
    wide = values.astype(F32)
    factor = wide.shape[2] // width
    split = [wide[:, None, :, j * width : (j + 1) * width] for j in range(factor)]
    joined = jnp.concatenate(split, axis=1)
    return joined.reshape(-1, width).astype(BF16)


def call(body, outs, *operands, scalars=0, scratch=(), us=0, far=0):
    cost = pl.CostEstimate(flops=us * 10**9 + 1, bytes_accessed=us * 3_600_000 + 1, transcendentals=0)
    return pl.pallas_call(
        body,
        out_shape=[jax.ShapeDtypeStruct(s, d) for s, d in outs[: len(outs) - far]]
        + [pltpu.HBM(s, d) for s, d in outs[len(outs) - far :]],
        in_specs=[SMEM] * scalars + [VMEM] * (len(operands) - scalars),
        out_specs=[VMEM] * (len(outs) - far) + [HBM] * far,
        scratch_shapes=list(scratch),
        compiler_params=PARAMS,
        cost_estimate=cost,
    )(*operands)


def head_stack(values):
    heads = values.shape[1] // HEAD_DIM
    return jnp.concatenate([only_head(values, h) for h in range(heads)], axis=0)


def head_blocks(values):
    heads = values.shape[0] // HEAD_DIM
    wide = values.shape[1] // heads
    return jnp.concatenate(
        [
            values[h * HEAD_DIM : (h + 1) * HEAD_DIM, h * wide : (h + 1) * wide]
            for h in range(heads)
        ],
        axis=0,
    )


def exp_parts(parts):
    high = functools.reduce(jnp.maximum, [jnp.max(part, axis=0, keepdims=True) for part in parts])
    parts = [jnp.exp2(part - high) for part in parts]
    total = sum(jnp.sum(part, axis=0, keepdims=True) for part in parts)
    return parts, 1.0 / total


def row_forward(sites, haps, idx, link, *refs):
    pieces = refs[:sites]
    cot, gain, w_t, row_out, x_out, n_out = refs[sites:]
    me = idx[0]
    rows, width = cot.shape
    for k in range(sites):
        xhat, _ = norm_parts(pieces[k][...].astype(F32))
        n_out[k * rows : (k + 1) * rows, :] = (xhat * gain[:1, :]).astype(BF16)
    normed = n_out[...]
    q = mm_nt(normed[:rows], w_t[:width, :]).astype(BF16)
    key = mm_nt(normed, w_t[width : 2 * width, :]).astype(BF16)
    v_t = mm_nt(w_t[2 * width :, :], normed).astype(BF16)
    scores = mm_nt(key, head_stack(q)) * (SCALE * LOG2E)
    bias = [jnp.where(link[me, me ^ a] > 0, 0.0, -jnp.inf) for a in range(sites)]
    parts = [scores[a * rows : (a + 1) * rows] + bias[a] for a in range(sites)]
    parts, inverse = exp_parts(parts)
    exps = jnp.concatenate([part.astype(BF16) for part in parts], axis=0)
    att_t = head_blocks(mm(v_t, exps) * inverse)
    att = jnp.transpose(att_t).astype(BF16)
    hid = pieces[0][...].astype(F32) + mm(att, row_out[...])
    joined = jnp.concatenate([hid, cot[...].astype(F32), att.astype(F32)], axis=1)
    x_out[...] = joined.reshape(haps, rows // haps, 3 * width).astype(BF16)


def row_probs(sites, idx, link, normed_ref, w_t, p_out, q_out, v_out, kt_out):
    me = idx[0]
    normed = normed_ref[...]
    total, width = q_out.shape
    full = normed.shape[1]
    rows = total // sites

    def weights(part):
        return w_t[pl.ds(pl.multiple_of(part * full + me * width, width), width), :]

    q = mm_nt(normed, weights(0)).astype(BF16)
    key = mm_nt(normed, weights(1)).astype(BF16)
    q_out[...] = q
    v_out[...] = mm_nt(normed, weights(2)).astype(BF16)
    kt_out[...] = mm_nt(weights(1), normed).astype(BF16)
    scores = mm_nt(key, head_stack(q)) * (SCALE * LOG2E)
    parts = []
    for a in range(sites):
        bias = [
            jnp.full((1, rows), jnp.where(link[me ^ b, me ^ a] > 0, 0.0, -jnp.inf), F32)
            for b in range(sites)
        ]
        bias = jnp.concatenate(bias * (width // HEAD_DIM), axis=1)
        parts.append(scores[a * rows : (a + 1) * rows] + bias)
    parts, inverse = exp_parts(parts)
    for a in range(sites):
        p_out[a * rows : (a + 1) * rows, :] = (parts[a] * inverse).astype(BF16)


def column_step(sites, haps, hap, x_in, row_out, gain, col_proj, kv_t_w, col_out, *refs):
    ga_out, send, keep, og_out, og, w_all, sems = refs
    core = hap[0] % 2
    half = row_out.shape[0] // 2
    mine = pl.ds(pl.multiple_of(core * half, half), half)
    other = pl.ds(pl.multiple_of((1 - core) * half, half), half)

    def save(j, cols):
        return pltpu.make_async_copy(w_all.at[mine, cols], keep.at[:, cols], sems.at[j])

    width = row_out.shape[0]
    heads = width // HEAD_DIM
    group = width // sites
    x_all = flat_rows(x_in[...], F32)
    rows = x_all.shape[0]
    per = rows // haps
    hid = x_all[:, :width]
    cot_f = x_all[:, width : 2 * width]
    cot = cot_f.astype(BF16)
    row_att = x_all[:, 2 * width :].astype(BF16)
    grad_att = mm_nt(cot, col_out[...]).astype(BF16)
    xhat, rstd = norm_parts(hid)
    normed = (xhat * gain[1:2, :]).astype(BF16)
    packed = mm(normed, col_proj[...]).astype(BF16)
    q = packed[:, :width]
    key = packed[:, width : 2 * width]
    val = packed[:, 2 * width :]
    kv_t = mm_nt(kv_t_w[...], normed).astype(BF16)
    q_st = head_stack(q)
    g_st = head_stack(grad_att)
    scores = mm_nt(key, q_st) * (SCALE * LOG2E)
    dprob = mm_nt(val, g_st)
    same = (
        lax.broadcasted_iota(jnp.int32, scores.shape, 0) % per
        == lax.broadcasted_iota(jnp.int32, scores.shape, 1) % per
    )
    scores = jnp.where(same, scores, -jnp.inf)
    exps = jnp.exp2(scores - jnp.max(scores, axis=0, keepdims=True))
    inverse = 1.0 / jnp.sum(exps, axis=0, keepdims=True)
    att_t = head_blocks(mm(kv_t[width:, :], exps.astype(BF16)) * inverse)
    probs = exps * inverse
    delta = jnp.sum(probs * dprob, axis=0, keepdims=True)
    dscore = (probs * (dprob - delta)).astype(BF16)
    dv = mm(probs.astype(BF16), g_st)
    dk = mm(dscore, q_st)
    dq = jnp.transpose(head_blocks(mm(kv_t[:width, :], dscore)))
    w_all[:, 3 * width : 4 * width] = mm(att_t.astype(BF16), cot).astype(BF16)
    att = jnp.transpose(att_t).astype(BF16)
    out = hid + mm(att, col_out[...])
    packed_grad = jnp.concatenate([dq * SCALE, dk * SCALE, dv], axis=1).astype(BF16)
    w_all[:, : 3 * width] = mm_tn(normed, packed_grad).astype(BF16)
    first = save(0, slice(0, 4 * width))
    first.start()
    grad_normed = mm_nt(packed_grad, col_proj[...])
    grad_hidden = (cot_f + norm_back(xhat, rstd, gain[1:2, :], grad_normed)).astype(BF16)
    for i in range(sites):
        g_i = mm_nt(grad_hidden, row_out[i * group : (i + 1) * group, :])
        ga_out[i * haps : (i + 1) * haps] = pack_block(g_i, haps)
    w_all[:, 4 * width :] = mm_tn(row_att, grad_hidden).astype(BF16)
    second = save(1, slice(4 * width, 5 * width))
    second.start()
    both = jnp.concatenate([out, grad_hidden.astype(F32)], axis=1)
    og[...] = both.reshape(haps, per, 2 * width).astype(BF16)
    third = pltpu.make_async_copy(og, og_out, sems.at[2])
    third.start()
    send[...] = w_all[other, :]
    first.wait()
    second.wait()
    third.wait()


def split_outputs(hap, og, keep, send):
    for m in range(keep.shape[0]):
        keep[m] = og[hap[0] ^ (2 * m)]
        send[m] = og[hap[0] ^ (2 * m + 1)]


def column_split(sites, idx, keep, *refs):
    outs, both, gots = refs[-sites - 1 : -1], refs[-1], refs[: -sites - 1]
    got = jnp.concatenate([g[...].astype(F32) for g in gots], axis=0)
    both[...] = (keep[...].astype(F32) + got).astype(BF16)
    part = keep.shape[0] // sites
    for k in range(sites):
        outs[k][...] = both[pl.ds(pl.multiple_of((idx[0] ^ k) * part, part), part), :]


def row_backward(sites, haps, idx, core, g_in, prob, q, val, key_t, normed, *refs):
    gp_outs = refs[:sites]
    keep, send, g_all, w_out = refs[sites:]
    me = idx[0]
    total, width = q.shape
    rows = total // sites
    for b in range(sites):
        g_all[b * rows : (b + 1) * rows, :] = unpack_block(
            g_in[pl.ds((me ^ b) * haps, haps)], width
        )
    g_st = head_stack(g_all[...])
    p_all = prob[...].astype(F32)
    dprob = mm_nt(val[...], g_st)
    delta = jnp.sum(p_all * dprob, axis=0, keepdims=True)
    dscore = (p_all * (dprob - delta)).astype(BF16)
    dv = mm(prob[...], g_st)
    dk = mm(dscore, head_stack(q[...]))
    dq_t = head_blocks(mm(key_t[...], dscore)) * SCALE
    dk16 = (dk * SCALE).astype(BF16)
    dv16 = dv.astype(BF16)
    w_out[:width, :] = mm(dq_t.astype(BF16), normed[...]).astype(BF16)
    w_out[width : 2 * width, :] = mm_tn(dk16, normed[...]).astype(BF16)
    w_out[2 * width :, :] = mm_tn(dv16, normed[...]).astype(BF16)
    half = 3 * width // 2
    keep[...] = w_out[pl.ds(pl.multiple_of(core[0] * half, half), half), :]
    send[...] = w_out[pl.ds(pl.multiple_of((1 - core[0]) * half, half), half), :]
    dq = jnp.transpose(dq_t).astype(BF16)
    joined = jnp.concatenate([dq, dk16, dv16], axis=1)
    for b in range(sites):
        gp_outs[b][...] = joined[b * rows : (b + 1) * rows]


def row_finish(sites, haps, idx, hap, feats, gain, w_t, gp, *refs):
    gps, parts = refs[: sites - 1], refs[sites - 1 : sites - 1 + haps // 2]
    out_ref, gf_ref, og = refs[sites - 1 + haps // 2 :]
    me = idx[0]
    rows, width = feats.shape
    group = width // sites
    per = rows // haps
    for m in range(haps // 2):
        base = parts[m].shape[0] - 4 * per
        for j in range(2):
            for side in range(2):
                start = base + (2 * j + side) * per
                og[side, hap[0] ^ (2 * m + j)] = parts[m][start : start + per, :].astype(F32)
    grads = [gp[...]] + [g[g.shape[0] - rows :, : 3 * group] for g in gps]
    grad_normed = 0.0
    for k in range(sites):
        place = [pl.multiple_of(p * width + (me ^ k) * group, group) for p in range(3)]
        weights = jnp.concatenate([w_t[pl.ds(p, group), :] for p in place], axis=0)
        grad_normed = grad_normed + mm(grads[k], weights)
    xhat, rstd = norm_parts(feats[...].astype(F32))
    grad = og[1].reshape(rows, width) + norm_back(xhat, rstd, gain[:1, :], grad_normed)
    out_ref[...] = og[0].reshape(rows, width).astype(BF16)
    gf_ref[...] = grad.astype(BF16)


def weights_join(sites, row_keep, row_got, og_keep, og_got, *refs):
    cols, outs = refs[:sites], refs[sites:]
    half, width = row_keep.shape
    depth = half + 5 * cols[0].shape[0]
    per = og_keep.shape[1]
    total = sum(c[...].astype(F32) for c in cols)
    tiles = [total[:, t * width : (t + 1) * width] for t in range(5)]
    rows = row_keep[...].astype(F32) + row_got[...].astype(F32)
    joined = jnp.concatenate([rows] + tiles, axis=0).astype(BF16)
    for m, out in enumerate(outs):
        out[:depth, :] = joined
        both = [og_keep[m].astype(F32), og_got[m].astype(F32)]
        both = [x[:, j * width : (j + 1) * width] for x in both for j in range(2)]
        out[depth:, :] = jnp.concatenate(both, axis=0).astype(BF16)


def weights_sum(haps, sites, *refs):
    parts, gps = refs[: haps // 2], refs[haps // 2 : haps // 2 + sites - 1]
    mine, outs = refs[haps // 2 + sites - 1], refs[haps // 2 + sites :]
    depth, width = mine.shape
    terms = [r[:depth, :].astype(F32) for r in parts]
    while len(terms) > 1:
        terms = [a + b for a, b in zip(terms[::2], terms[1::2])]
    mine[...] = terms[0].astype(BF16)
    for gp, out in zip(gps, outs):
        out[:depth, :] = mine[...]
        out[depth:, : gp.shape[1]] = gp[...]
        out[depth:, gp.shape[1] :] = jnp.zeros((gp.shape[0], width - gp.shape[1]), BF16)


def weights_finish(sites, idx, core, *refs):
    pieces = refs[: 2 * sites]
    rp, ro, cp, co, rows_t = refs[2 * sites :]
    width = ro.shape[0]
    group = width // sites
    unit = group // 2
    part = width // 2 // sites
    for j in range(2 * sites):
        k = j // 2
        cc = core[0] ^ (j % 2)
        g = idx[0] ^ k
        piece = pieces[j][...].astype(F32)
        for u in range(3):
            place = 3 * cc + u
            dest = (place // 2) * width + g * group + (place % 2) * unit
            rows_t[pl.ds(pl.multiple_of(dest, unit), unit), :] = piece[u * unit : (u + 1) * unit]
        here = pl.ds(pl.multiple_of(cc * (width // 2) + g * part, part), part)
        tiles = [piece[3 * unit + t * part : 3 * unit + (t + 1) * part] for t in range(5)]
        for t in range(3):
            cp[here, t * width : (t + 1) * width] = tiles[t]
        co[here, :] = tiles[3]
        ro[here, :] = tiles[4]
    rp[...] = jnp.transpose(rows_t[...])


def exchange(value, axis):
    return lax.all_to_all(value, axis, 0, 0, tiled=True)


def swapped(value, axis, by):
    length = lax.axis_size(axis)
    return lax.ppermute(value, axis, [(i, i ^ by) for i in range(length)])


def on_device(
    features,
    link_pattern,
    row_gain,
    row_proj,
    row_out,
    column_norm_gain,
    col_proj,
    col_out,
    cotangent,
):
    rows, _, width = features.shape
    sites, haps = lax.axis_size("site"), lax.axis_size("hap")
    count = sites * haps
    per = rows // haps
    group = width // sites
    heads = group // HEAD_DIM
    total = rows * sites
    both_axes = ("site", "hap")
    me = lax.axis_index("site")
    idx = me.reshape(1).astype(jnp.int32)
    hap = lax.axis_index("hap").reshape(1).astype(jnp.int32)
    core = hap % 2
    factor = lane_factor(per, group)
    block = ((count, per // factor, group * factor), BF16)
    feats = features.reshape(rows, width)
    cot = cotangent.reshape(rows, width)

    pieces = [feats] + [swapped(feats, "site", k) for k in range(1, sites)]
    link_pattern = jnp.where(link_pattern > 0, 1, 0)
    gains = jnp.stack([row_gain, column_norm_gain])
    w_t = jnp.transpose(row_proj)
    kv_t_w = jnp.transpose(col_proj[:, width:])

    x_out, normed = call(
        functools.partial(row_forward, sites, haps),
        [((haps, per, 3 * width), BF16), ((total, width), BF16)],
        idx, link_pattern, *pieces, cot, gains, w_t, row_out, scalars=2,
    )
    x_in = exchange(x_out, "hap")
    prob, q, val, key_t = call(
        functools.partial(row_probs, sites),
        [
            ((total, heads * total), BF16),
            ((total, group), BF16),
            ((total, group), BF16),
            ((group, total), BF16),
        ],
        idx, link_pattern, normed, w_t, scalars=2, us=20,
    )
    x_in, _ = lax.optimization_barrier((x_in, prob))
    half = width // 2
    ga, col_send, col_keep, og = call(
        functools.partial(column_step, sites, haps),
        [
            block,
            ((half, 5 * width), BF16),
            ((half, 5 * width), BF16),
            ((haps, per, 2 * width), BF16),
        ],
        hap, x_in, row_out, gains, col_proj, kv_t_w, col_out, scalars=1, far=2,
        scratch=[
            pltpu.VMEM((haps, per, 2 * width), BF16),
            pltpu.VMEM((width, 5 * width), BF16),
            pltpu.SemaphoreType.DMA((3,)),
        ],
    )
    g_in = exchange(ga, both_axes)
    col_got = [swapped(col_send, "hap", 1)]
    cols = call(
        functools.partial(column_split, sites),
        [((half // sites, 5 * width), BF16)] * sites,
        idx, col_keep, *col_got, scalars=1, us=0,
        scratch=[pltpu.VMEM((half, 5 * width), BF16)],
    )
    og_keep, og_send = call(
        split_outputs, [((haps // 2, per, 2 * width), BF16)] * 2, hap, og, scalars=1
    )
    og_got = swapped(og_send, "hap", 1)
    g_in, _ = lax.optimization_barrier((g_in, (cols, og_got)))
    cols = [cols[0]] + [swapped(cols[k], "site", k) for k in range(1, sites)]
    *gps, row_keep, row_send = call(
        functools.partial(row_backward, sites, haps),
        [((rows, 3 * group), BF16)] * sites + [((3 * group // 2, width), BF16)] * 2,
        idx, core, g_in, prob, q, val, key_t, normed, scalars=2,
        scratch=[
            pltpu.VMEM((total, group), BF16),
            pltpu.VMEM((3 * group, width), BF16),
        ],
    )
    row_got = swapped(row_send, "hap", 1)
    depth = 3 * group // 2 + 5 * half // sites
    parts = call(
        functools.partial(weights_join, sites),
        [((depth + 4 * per, width), BF16)] * (haps // 2),
        row_keep, row_got, og_keep, og_got, *cols,
    )
    parts = [parts[0]] + [swapped(parts[m], "hap", 2 * m) for m in range(1, haps // 2)]
    mine, *sends = call(
        functools.partial(weights_sum, haps, sites),
        [((depth, width), BF16)] + [((depth + rows, width), BF16)] * (sites - 1),
        *parts, *gps[1:],
    )
    got = [swapped(sends[k - 1], "site", k) for k in range(1, sites)]
    full = [x for p in [mine] + got for x in (p, swapped(p, "hap", 1))]
    out, grad = call(
        functools.partial(row_finish, sites, haps),
        [((rows, width), BF16)] * 2,
        idx, hap, feats, gains, w_t, gps[0], *got, *parts, scalars=2,
        scratch=[pltpu.VMEM((2, haps, per, width), F32)],
    )
    rp, ro, cp, co = call(
        functools.partial(weights_finish, sites),
        [((width, 3 * width), F32), ((width, width), F32)] * 2,
        idx, core, *full, scalars=2,
        scratch=[pltpu.VMEM((3 * width, width), F32)],
    )
    shape = (rows, 1, width)
    return (out.reshape(shape), grad.reshape(shape), rp, ro, cp, co)


def solution(mesh):
    data = P("site", "hap", None)
    return jax.shard_map(
        on_device,
        mesh=mesh,
        in_specs=(data, P(), P(), P(), P(), P(), P(), P(), data),
        out_specs=(data, data, P(), P(), P(), P()),
        check_vma=False,
    )
```

```python
import functools

import jax
import jax.numpy as jnp
from jax import lax
from jax.experimental import pallas as pl
from jax.experimental.pallas import tpu as pltpu
from jax.sharding import PartitionSpec as P

HEAD_DIM = 32
EPSILON = 1e-05
LOG2E = 1.4426950408889634
SCALE = HEAD_DIM ** (-0.5)
F32 = jnp.float32
BF16 = jnp.bfloat16
VMEM = pl.BlockSpec(memory_space=pltpu.VMEM)
HBM = pl.BlockSpec(memory_space=pltpu.HBM)
SMEM = pl.BlockSpec(memory_space=pltpu.SMEM)
PARAMS = pltpu.CompilerParams(vmem_limit_bytes=24 << 20)


def mm(a, b):
    return lax.dot_general(a, b, (((1,), (0,)), ((), ())), preferred_element_type=F32)


def mm_nt(a, b):
    return lax.dot_general(a, b, (((1,), (1,)), ((), ())), preferred_element_type=F32)


def mm_tn(a, b):
    return lax.dot_general(a, b, (((0,), (0,)), ((), ())), preferred_element_type=F32)


def norm_parts(x):
    centred = x - jnp.mean(x, axis=-1, keepdims=True)
    rstd = lax.rsqrt(jnp.mean(centred * centred, axis=-1, keepdims=True) + EPSILON)
    return centred * rstd, rstd


def norm_back(xhat, rstd, gain, grad):
    scaled = grad * gain
    first = jnp.mean(scaled, axis=-1, keepdims=True)
    second = jnp.mean(scaled * xhat, axis=-1, keepdims=True)
    return rstd * (scaled - first - xhat * second)


def head_lanes(width, head):
    return lax.broadcasted_iota(jnp.int32, (1, width), 1) // HEAD_DIM == head


def only_head(values, head):
    return jnp.where(head_lanes(values.shape[1], head), values, jnp.zeros_like(values))


def flat_rows(values, dtype=BF16):
    wide = values.astype(F32)
    return wide.reshape(wide.shape[0] * wide.shape[1], wide.shape[2]).astype(dtype)


def lane_factor(rows, width):
    factor = 128 // width
    return factor if (rows // factor) % 8 == 0 else 1


def pack_block(values, outer):
    rows, width = values.shape[0] // outer, values.shape[1]
    factor = lane_factor(rows, width)
    split = values.reshape(outer, factor, rows // factor, width)
    return jnp.concatenate([split[:, j] for j in range(factor)], axis=2).astype(BF16)


def unpack_block(values, width):
    wide = values.astype(F32)
    factor = wide.shape[2] // width
    split = [wide[:, None, :, j * width : (j + 1) * width] for j in range(factor)]
    joined = jnp.concatenate(split, axis=1)
    return joined.reshape(-1, width).astype(BF16)


def call(body, outs, *operands, scalars=0, scratch=(), us=0, far=0):
    cost = pl.CostEstimate(flops=us * 10**9 + 1, bytes_accessed=us * 3_600_000 + 1, transcendentals=0)
    return pl.pallas_call(
        body,
        out_shape=[jax.ShapeDtypeStruct(s, d) for s, d in outs[: len(outs) - far]]
        + [pltpu.HBM(s, d) for s, d in outs[len(outs) - far :]],
        in_specs=[SMEM] * scalars + [VMEM] * (len(operands) - scalars),
        out_specs=[VMEM] * (len(outs) - far) + [HBM] * far,
        scratch_shapes=list(scratch),
        compiler_params=PARAMS,
        cost_estimate=cost,
    )(*operands)


def head_stack(values):
    heads = values.shape[1] // HEAD_DIM
    return jnp.concatenate([only_head(values, h) for h in range(heads)], axis=0)


def head_blocks(values):
    heads = values.shape[0] // HEAD_DIM
    wide = values.shape[1] // heads
    return jnp.concatenate(
        [
            values[h * HEAD_DIM : (h + 1) * HEAD_DIM, h * wide : (h + 1) * wide]
            for h in range(heads)
        ],
        axis=0,
    )


def exp_parts(parts):
    high = functools.reduce(jnp.maximum, [jnp.max(part, axis=0, keepdims=True) for part in parts])
    parts = [jnp.exp2(part - high) for part in parts]
    total = sum(jnp.sum(part, axis=0, keepdims=True) for part in parts)
    return parts, 1.0 / total


def row_forward(sites, haps, idx, link, *refs):
    pieces = refs[:sites]
    cot, gain, w_t, row_out, x_out, n_out = refs[sites:]
    me = idx[0]
    rows, width = cot.shape
    for k in range(sites):
        xhat, _ = norm_parts(pieces[k][...].astype(F32))
        n_out[k * rows : (k + 1) * rows, :] = (xhat * gain[:1, :]).astype(BF16)
    normed = n_out[...]
    q = mm_nt(normed[:rows], w_t[:width, :]).astype(BF16)
    key = mm_nt(normed, w_t[width : 2 * width, :]).astype(BF16)
    v_t = mm_nt(w_t[2 * width :, :], normed).astype(BF16)
    scores = mm_nt(key, head_stack(q)) * (SCALE * LOG2E)
    bias = [jnp.where(link[me, me ^ a] > 0, 0.0, -jnp.inf) for a in range(sites)]
    parts = [scores[a * rows : (a + 1) * rows] + bias[a] for a in range(sites)]
    parts, inverse = exp_parts(parts)
    exps = jnp.concatenate([part.astype(BF16) for part in parts], axis=0)
    att_t = head_blocks(mm(v_t, exps) * inverse)
    att = jnp.transpose(att_t).astype(BF16)
    hid = pieces[0][...].astype(F32) + mm(att, row_out[...])
    joined = jnp.concatenate([hid, cot[...].astype(F32), att.astype(F32)], axis=1)
    x_out[...] = joined.reshape(haps, rows // haps, 3 * width).astype(BF16)


def row_probs(sites, idx, link, normed_ref, w_t, p_out, q_out, v_out, kt_out):
    me = idx[0]
    normed = normed_ref[...]
    total, width = q_out.shape
    full = normed.shape[1]
    rows = total // sites

    def weights(part):
        return w_t[pl.ds(pl.multiple_of(part * full + me * width, width), width), :]

    q = mm_nt(normed, weights(0)).astype(BF16)
    key = mm_nt(normed, weights(1)).astype(BF16)
    q_out[...] = q
    v_out[...] = mm_nt(normed, weights(2)).astype(BF16)
    kt_out[...] = mm_nt(weights(1), normed).astype(BF16)
    scores = mm_nt(key, head_stack(q)) * (SCALE * LOG2E)
    parts = []
    for a in range(sites):
        bias = [
            jnp.full((1, rows), jnp.where(link[me ^ b, me ^ a] > 0, 0.0, -jnp.inf), F32)
            for b in range(sites)
        ]
        bias = jnp.concatenate(bias * (width // HEAD_DIM), axis=1)
        parts.append(scores[a * rows : (a + 1) * rows] + bias)
    parts, inverse = exp_parts(parts)
    for a in range(sites):
        p_out[a * rows : (a + 1) * rows, :] = (parts[a] * inverse).astype(BF16)


def column_step(sites, haps, hap, x_in, row_out, gain, col_proj, kv_t_w, col_out, *refs):
    ga_out, send, keep, og_out, og, w_all, sems = refs
    core = hap[0] % 2
    half = row_out.shape[0] // 2
    mine = pl.ds(pl.multiple_of(core * half, half), half)
    other = pl.ds(pl.multiple_of((1 - core) * half, half), half)

    def save(j, cols):
        return pltpu.make_async_copy(w_all.at[mine, cols], keep.at[:, cols], sems.at[j])

    width = row_out.shape[0]
    heads = width // HEAD_DIM
    group = width // sites
    x_all = flat_rows(x_in[...], F32)
    rows = x_all.shape[0]
    per = rows // haps
    hid = x_all[:, :width]
    cot_f = x_all[:, width : 2 * width]
    cot = cot_f.astype(BF16)
    row_att = x_all[:, 2 * width :].astype(BF16)
    grad_att = mm_nt(cot, col_out[...]).astype(BF16)
    xhat, rstd = norm_parts(hid)
    normed = (xhat * gain[1:2, :]).astype(BF16)
    packed = mm(normed, col_proj[...]).astype(BF16)
    q = packed[:, :width]
    key = packed[:, width : 2 * width]
    val = packed[:, 2 * width :]
    kv_t = mm_nt(kv_t_w[...], normed).astype(BF16)
    q_st = head_stack(q)
    g_st = head_stack(grad_att)
    scores = mm_nt(key, q_st) * (SCALE * LOG2E)
    dprob = mm_nt(val, g_st)
    same = (
        lax.broadcasted_iota(jnp.int32, scores.shape, 0) % per
        == lax.broadcasted_iota(jnp.int32, scores.shape, 1) % per
    )
    scores = jnp.where(same, scores, -jnp.inf)
    exps = jnp.exp2(scores - jnp.max(scores, axis=0, keepdims=True))
    inverse = 1.0 / jnp.sum(exps, axis=0, keepdims=True)
    att_t = head_blocks(mm(kv_t[width:, :], exps.astype(BF16)) * inverse)
    probs = exps * inverse
    delta = jnp.sum(probs * dprob, axis=0, keepdims=True)
    dscore = (probs * (dprob - delta)).astype(BF16)
    dv = mm(probs.astype(BF16), g_st)
    dk = mm(dscore, q_st)
    dq = jnp.transpose(head_blocks(mm(kv_t[:width, :], dscore)))
    w_all[:, 3 * width : 4 * width] = mm(att_t.astype(BF16), cot).astype(BF16)
    att = jnp.transpose(att_t).astype(BF16)
    out = hid + mm(att, col_out[...])
    packed_grad = jnp.concatenate([dq * SCALE, dk * SCALE, dv], axis=1).astype(BF16)
    w_all[:, : 3 * width] = mm_tn(normed, packed_grad).astype(BF16)
    first = save(0, slice(0, 4 * width))
    first.start()
    grad_normed = mm_nt(packed_grad, col_proj[...])
    grad_hidden = (cot_f + norm_back(xhat, rstd, gain[1:2, :], grad_normed)).astype(BF16)
    for i in range(sites):
        g_i = mm_nt(grad_hidden, row_out[i * group : (i + 1) * group, :])
        ga_out[i * haps : (i + 1) * haps] = pack_block(g_i, haps)
    w_all[:, 4 * width :] = mm_tn(row_att, grad_hidden).astype(BF16)
    second = save(1, slice(4 * width, 5 * width))
    second.start()
    both = jnp.concatenate([out, grad_hidden.astype(F32)], axis=1)
    og[...] = both.reshape(haps, per, 2 * width).astype(BF16)
    third = pltpu.make_async_copy(og, og_out, sems.at[2])
    third.start()
    send[...] = w_all[other, :]
    first.wait()
    second.wait()
    third.wait()


def split_outputs(hap, og, keep, send):
    for m in range(keep.shape[0]):
        keep[m] = og[hap[0] ^ (2 * m)]
        send[m] = og[hap[0] ^ (2 * m + 1)]


def column_split(sites, idx, keep, *refs):
    outs, both, gots = refs[-sites - 1 : -1], refs[-1], refs[: -sites - 1]
    got = jnp.concatenate([g[...].astype(F32) for g in gots], axis=0)
    both[...] = (keep[...].astype(F32) + got).astype(BF16)
    part = keep.shape[0] // sites
    for k in range(sites):
        outs[k][...] = both[pl.ds(pl.multiple_of((idx[0] ^ k) * part, part), part), :]


def row_backward(sites, haps, idx, core, g_in, prob, q, val, key_t, normed, *refs):
    gp_outs = refs[:sites]
    keep, send, g_all, w_out = refs[sites:]
    me = idx[0]
    total, width = q.shape
    rows = total // sites
    for b in range(sites):
        g_all[b * rows : (b + 1) * rows, :] = unpack_block(
            g_in[pl.ds((me ^ b) * haps, haps)], width
        )
    g_st = head_stack(g_all[...])
    p_all = prob[...].astype(F32)
    dprob = mm_nt(val[...], g_st)
    delta = jnp.sum(p_all * dprob, axis=0, keepdims=True)
    dscore = (p_all * (dprob - delta)).astype(BF16)
    dv = mm(prob[...], g_st)
    dk = mm(dscore, head_stack(q[...]))
    dq_t = head_blocks(mm(key_t[...], dscore)) * SCALE
    dk16 = (dk * SCALE).astype(BF16)
    dv16 = dv.astype(BF16)
    w_out[:width, :] = mm(dq_t.astype(BF16), normed[...]).astype(BF16)
    w_out[width : 2 * width, :] = mm_tn(dk16, normed[...]).astype(BF16)
    w_out[2 * width :, :] = mm_tn(dv16, normed[...]).astype(BF16)
    half = 3 * width // 2
    keep[...] = w_out[pl.ds(pl.multiple_of(core[0] * half, half), half), :]
    send[...] = w_out[pl.ds(pl.multiple_of((1 - core[0]) * half, half), half), :]
    dq = jnp.transpose(dq_t).astype(BF16)
    joined = jnp.concatenate([dq, dk16, dv16], axis=1)
    for b in range(sites):
        gp_outs[b][...] = joined[b * rows : (b + 1) * rows]


def row_finish(sites, haps, idx, hap, feats, gain, w_t, gp, *refs):
    gps, parts = refs[: sites - 1], refs[sites - 1 : sites - 1 + haps // 2]
    out_ref, gf_ref, og = refs[sites - 1 + haps // 2 :]
    me = idx[0]
    rows, width = feats.shape
    group = width // sites
    per = rows // haps
    for m in range(haps // 2):
        base = parts[m].shape[0] - 4 * per
        for j in range(2):
            for side in range(2):
                start = base + (2 * j + side) * per
                og[side, hap[0] ^ (2 * m + j)] = parts[m][start : start + per, :].astype(F32)
    grads = [gp[...]] + [g[g.shape[0] - rows :, : 3 * group] for g in gps[::-1]]
    grad_normed = 0.0
    for k in range(sites):
        place = [pl.multiple_of(p * width + (me ^ k) * group, group) for p in range(3)]
        weights = jnp.concatenate([w_t[pl.ds(p, group), :] for p in place], axis=0)
        grad_normed = grad_normed + mm(grads[k], weights)
    xhat, rstd = norm_parts(feats[...].astype(F32))
    grad = og[1].reshape(rows, width) + norm_back(xhat, rstd, gain[:1, :], grad_normed)
    out_ref[...] = og[0].reshape(rows, width).astype(BF16)
    gf_ref[...] = grad.astype(BF16)


def weights_join(sites, row_keep, row_got, og_keep, og_got, *refs):
    cols, outs = refs[:sites], refs[sites:]
    half, width = row_keep.shape
    depth = half + 5 * cols[0].shape[0]
    per = og_keep.shape[1]
    total = sum(c[...].astype(F32) for c in cols)
    tiles = [total[:, t * width : (t + 1) * width] for t in range(5)]
    rows = row_keep[...].astype(F32) + row_got[...].astype(F32)
    joined = jnp.concatenate([rows] + tiles, axis=0).astype(BF16)
    for m, out in enumerate(outs[:1] + outs[:0:-1]):
        out[:depth, :] = joined
        both = [og_keep[m].astype(F32), og_got[m].astype(F32)]
        both = [x[:, j * width : (j + 1) * width] for x in both for j in range(2)]
        out[depth:, :] = jnp.concatenate(both, axis=0).astype(BF16)


def weights_sum(haps, sites, *refs):
    parts, gps = refs[: haps // 2], refs[haps // 2 : haps // 2 + sites - 1]
    mine, outs = refs[haps // 2 + sites - 1], refs[haps // 2 + sites :]
    depth, width = mine.shape
    terms = [r[:depth, :].astype(F32) for r in parts]
    while len(terms) > 1:
        terms = [a + b for a, b in zip(terms[::2], terms[1::2])]
    mine[...] = terms[0].astype(BF16)
    for gp, out in zip(gps, outs[::-1]):
        out[:depth, :] = mine[...]
        out[depth:, : gp.shape[1]] = gp[...]
        out[depth:, gp.shape[1] :] = jnp.zeros((gp.shape[0], width - gp.shape[1]), BF16)


def weights_finish(sites, idx, core, *refs):
    pieces = refs[: 2 * sites]
    rp, ro_out, cp_out, co_out, rows_t, ro, cp, co, sems = refs[2 * sites :]
    width = ro.shape[0]
    group = width // sites
    unit = group // 2
    part = width // 2 // sites
    for j in range(2 * sites):
        cc = core[0] ^ (j % 2)
        g = idx[0] ^ (j // 2)
        piece = pieces[j][3 * unit : 3 * unit + 5 * part, :].astype(F32)
        here = pl.ds(pl.multiple_of(cc * (width // 2) + g * part, part), part)
        tiles = [piece[t * part : (t + 1) * part] for t in range(5)]
        for t in range(3):
            cp[here, t * width : (t + 1) * width] = tiles[t]
        co[here, :] = tiles[3]
        ro[here, :] = tiles[4]
    copies = [
        pltpu.make_async_copy(cp, cp_out, sems.at[0]),
        pltpu.make_async_copy(co, co_out, sems.at[1]),
        pltpu.make_async_copy(ro, ro_out, sems.at[2]),
    ]
    for copy in copies:
        copy.start()
    for j in range(2 * sites):
        k = j // 2
        cc = core[0] ^ (j % 2)
        g = idx[0] ^ k
        piece = pieces[j][: 3 * unit, :].astype(F32)
        for u in range(3):
            place = 3 * cc + u
            dest = (place // 2) * width + g * group + (place % 2) * unit
            rows_t[pl.ds(pl.multiple_of(dest, unit), unit), :] = piece[u * unit : (u + 1) * unit]
    rp[...] = jnp.transpose(rows_t[...])
    for copy in copies:
        copy.wait()


def exchange(value, axis):
    return lax.all_to_all(value, axis, 0, 0, tiled=True)


def swapped(value, axis, by):
    length = lax.axis_size(axis)
    return lax.ppermute(value, axis, [(i, i ^ by) for i in range(length)])


def on_device(
    features,
    link_pattern,
    row_gain,
    row_proj,
    row_out,
    column_norm_gain,
    col_proj,
    col_out,
    cotangent,
):
    rows, _, width = features.shape
    sites, haps = lax.axis_size("site"), lax.axis_size("hap")
    count = sites * haps
    per = rows // haps
    group = width // sites
    heads = group // HEAD_DIM
    total = rows * sites
    both_axes = ("site", "hap")
    me = lax.axis_index("site")
    idx = me.reshape(1).astype(jnp.int32)
    hap = lax.axis_index("hap").reshape(1).astype(jnp.int32)
    core = hap % 2
    factor = lane_factor(per, group)
    block = ((count, per // factor, group * factor), BF16)
    feats = features.reshape(rows, width)
    cot = cotangent.reshape(rows, width)

    pieces = [feats] + [swapped(feats, "site", k) for k in range(1, sites)]
    link_pattern = jnp.where(link_pattern > 0, 1, 0)
    gains = jnp.stack([row_gain, column_norm_gain])
    w_t = jnp.transpose(row_proj)
    kv_t_w = jnp.transpose(col_proj[:, width:])

    x_out, normed = call(
        functools.partial(row_forward, sites, haps),
        [((haps, per, 3 * width), BF16), ((total, width), BF16)],
        idx, link_pattern, *pieces, cot, gains, w_t, row_out, scalars=2,
    )
    x_in = exchange(x_out, "hap")
    prob, q, val, key_t = call(
        functools.partial(row_probs, sites),
        [
            ((total, heads * total), BF16),
            ((total, group), BF16),
            ((total, group), BF16),
            ((group, total), BF16),
        ],
        idx, link_pattern, normed, w_t, scalars=2, us=20,
    )
    x_in, _ = lax.optimization_barrier((x_in, prob))
    half = width // 2
    ga, col_send, col_keep, og = call(
        functools.partial(column_step, sites, haps),
        [
            block,
            ((half, 5 * width), BF16),
            ((half, 5 * width), BF16),
            ((haps, per, 2 * width), BF16),
        ],
        hap, x_in, row_out, gains, col_proj, kv_t_w, col_out, scalars=1, far=2,
        scratch=[
            pltpu.VMEM((haps, per, 2 * width), BF16),
            pltpu.VMEM((width, 5 * width), BF16),
            pltpu.SemaphoreType.DMA((3,)),
        ],
    )
    g_in = exchange(ga, both_axes)
    col_got = [swapped(col_send, "hap", 1)]
    cols = call(
        functools.partial(column_split, sites),
        [((half // sites, 5 * width), BF16)] * sites,
        idx, col_keep, *col_got, scalars=1, us=0,
        scratch=[pltpu.VMEM((half, 5 * width), BF16)],
    )
    og_keep, og_send = call(
        split_outputs, [((haps // 2, per, 2 * width), BF16)] * 2, hap, og, scalars=1
    )
    og_got = swapped(og_send, "hap", 1)
    g_in, _ = lax.optimization_barrier((g_in, (cols, og_got)))
    cols = [cols[0]] + [swapped(cols[k], "site", k) for k in range(1, sites)]
    *gps, row_keep, row_send = call(
        functools.partial(row_backward, sites, haps),
        [((rows, 3 * group), BF16)] * sites + [((3 * group // 2, width), BF16)] * 2,
        idx, core, g_in, prob, q, val, key_t, normed, scalars=2,
        scratch=[
            pltpu.VMEM((total, group), BF16),
            pltpu.VMEM((3 * group, width), BF16),
        ],
    )
    row_got = swapped(row_send, "hap", 1)
    depth = 3 * group // 2 + 5 * half // sites
    parts = call(
        functools.partial(weights_join, sites),
        [((depth + 4 * per, width), BF16)] * (haps // 2),
        row_keep, row_got, og_keep, og_got, *cols,
    )
    parts = [parts[0]] + list(parts[:0:-1])
    parts = [parts[0]] + [swapped(parts[m], "hap", 2 * m) for m in range(1, haps // 2)]
    mine, *sends = call(
        functools.partial(weights_sum, haps, sites),
        [((depth, width), BF16)] + [((depth + rows, width), BF16)] * (sites - 1),
        *parts[::-1], *gps[1:],
    )
    sends = sends[::-1]
    got = [swapped(sends[k - 1], "site", k) for k in range(1, sites)]
    full = [x for p in [mine] + got for x in (p, swapped(p, "hap", 1))]
    out, grad = call(
        functools.partial(row_finish, sites, haps),
        [((rows, width), BF16)] * 2,
        idx, hap, feats, gains, w_t, gps[0], *got[::-1], *parts, scalars=2,
        scratch=[pltpu.VMEM((2, haps, per, width), F32)],
    )
    rp, ro, cp, co = call(
        functools.partial(weights_finish, sites),
        [((width, 3 * width), F32), ((width, width), F32)] * 2,
        idx, core, *full, scalars=2, far=3,
        scratch=[
            pltpu.VMEM((3 * width, width), F32),
            pltpu.VMEM((width, width), F32),
            pltpu.VMEM((width, 3 * width), F32),
            pltpu.VMEM((width, width), F32),
            pltpu.SemaphoreType.DMA((3,)),
        ],
    )
    shape = (rows, 1, width)
    return (out.reshape(shape), grad.reshape(shape), rp, ro, cp, co)


def solution(mesh):
    data = P("site", "hap", None)
    return jax.shard_map(
        on_device,
        mesh=mesh,
        in_specs=(data, P(), P(), P(), P(), P(), P(), P(), data),
        out_specs=(data, data, P(), P(), P(), P()),
        check_vma=False,
    )
```

```python
import functools

import jax
import jax.numpy as jnp
from jax import lax
from jax.experimental import pallas as pl
from jax.experimental.pallas import tpu as pltpu
from jax.sharding import PartitionSpec as P

HEAD_DIM = 32
EPSILON = 1e-05
LOG2E = 1.4426950408889634
SCALE = HEAD_DIM ** (-0.5)
F32 = jnp.float32
BF16 = jnp.bfloat16
VMEM = pl.BlockSpec(memory_space=pltpu.VMEM)
HBM = pl.BlockSpec(memory_space=pltpu.HBM)
SMEM = pl.BlockSpec(memory_space=pltpu.SMEM)
PARAMS = pltpu.CompilerParams(vmem_limit_bytes=24 << 20)


def mm(a, b):
    return lax.dot_general(a, b, (((1,), (0,)), ((), ())), preferred_element_type=F32)


def mm_nt(a, b):
    return lax.dot_general(a, b, (((1,), (1,)), ((), ())), preferred_element_type=F32)


def mm_tn(a, b):
    return lax.dot_general(a, b, (((0,), (0,)), ((), ())), preferred_element_type=F32)


def norm_parts(x):
    centred = x - jnp.mean(x, axis=-1, keepdims=True)
    rstd = lax.rsqrt(jnp.mean(centred * centred, axis=-1, keepdims=True) + EPSILON)
    return centred * rstd, rstd


def norm_back(xhat, rstd, gain, grad):
    scaled = grad * gain
    first = jnp.mean(scaled, axis=-1, keepdims=True)
    second = jnp.mean(scaled * xhat, axis=-1, keepdims=True)
    return rstd * (scaled - first - xhat * second)


def head_lanes(width, head):
    return lax.broadcasted_iota(jnp.int32, (1, width), 1) // HEAD_DIM == head


def only_head(values, head):
    return jnp.where(head_lanes(values.shape[1], head), values, jnp.zeros_like(values))


def flat_rows(values, dtype=BF16):
    wide = values.astype(F32)
    return wide.reshape(wide.shape[0] * wide.shape[1], wide.shape[2]).astype(dtype)


def lane_factor(rows, width):
    factor = 128 // width
    return factor if (rows // factor) % 8 == 0 else 1


def pack_block(values, outer):
    rows, width = values.shape[0] // outer, values.shape[1]
    factor = lane_factor(rows, width)
    split = values.reshape(outer, factor, rows // factor, width)
    return jnp.concatenate([split[:, j] for j in range(factor)], axis=2).astype(BF16)


def unpack_block(values, width):
    wide = values.astype(F32)
    factor = wide.shape[2] // width
    split = [wide[:, None, :, j * width : (j + 1) * width] for j in range(factor)]
    joined = jnp.concatenate(split, axis=1)
    return joined.reshape(-1, width).astype(BF16)


def call(body, outs, *operands, scalars=0, scratch=(), us=0, far=0):
    cost = pl.CostEstimate(flops=us * 10**9 + 1, bytes_accessed=us * 3_600_000 + 1, transcendentals=0)
    return pl.pallas_call(
        body,
        out_shape=[jax.ShapeDtypeStruct(s, d) for s, d in outs[: len(outs) - far]]
        + [pltpu.HBM(s, d) for s, d in outs[len(outs) - far :]],
        in_specs=[SMEM] * scalars + [VMEM] * (len(operands) - scalars),
        out_specs=[VMEM] * (len(outs) - far) + [HBM] * far,
        scratch_shapes=list(scratch),
        compiler_params=PARAMS,
        cost_estimate=cost,
    )(*operands)


def head_stack(values):
    heads = values.shape[1] // HEAD_DIM
    return jnp.concatenate([only_head(values, h) for h in range(heads)], axis=0)


def head_blocks(values):
    heads = values.shape[0] // HEAD_DIM
    wide = values.shape[1] // heads
    return jnp.concatenate(
        [
            values[h * HEAD_DIM : (h + 1) * HEAD_DIM, h * wide : (h + 1) * wide]
            for h in range(heads)
        ],
        axis=0,
    )


def exp_parts(parts):
    high = functools.reduce(jnp.maximum, [jnp.max(part, axis=0, keepdims=True) for part in parts])
    parts = [jnp.exp2(part - high) for part in parts]
    total = sum(jnp.sum(part, axis=0, keepdims=True) for part in parts)
    return parts, 1.0 / total


def row_forward(sites, haps, idx, link, *refs):
    pieces = refs[:sites]
    cot, gain, w_t, row_out, x_out, n_out = refs[sites:]
    me = idx[0]
    rows, width = cot.shape
    for k in range(sites):
        xhat, _ = norm_parts(pieces[k][...].astype(F32))
        n_out[k * rows : (k + 1) * rows, :] = (xhat * gain[:1, :]).astype(BF16)
    normed = n_out[...]
    q = mm_nt(normed[:rows], w_t[:width, :]).astype(BF16)
    key = mm_nt(normed, w_t[width : 2 * width, :]).astype(BF16)
    v_t = mm_nt(w_t[2 * width :, :], normed).astype(BF16)
    scores = mm_nt(key, head_stack(q)) * (SCALE * LOG2E)
    bias = [jnp.where(link[me, me ^ a] > 0, 0.0, -jnp.inf) for a in range(sites)]
    parts = [scores[a * rows : (a + 1) * rows] + bias[a] for a in range(sites)]
    parts, inverse = exp_parts(parts)
    exps = jnp.concatenate([part.astype(BF16) for part in parts], axis=0)
    att_t = head_blocks(mm(v_t, exps) * inverse)
    att = jnp.transpose(att_t).astype(BF16)
    hid = pieces[0][...].astype(F32) + mm(att, row_out[...])
    joined = jnp.concatenate([hid, cot[...].astype(F32), att.astype(F32)], axis=1)
    x_out[...] = joined.reshape(haps, rows // haps, 3 * width).astype(BF16)


def row_probs(sites, idx, link, normed_ref, w_t, p_out, q_out, v_out, kt_out):
    me = idx[0]
    normed = normed_ref[...]
    total, width = q_out.shape
    full = normed.shape[1]
    rows = total // sites

    def weights(part):
        return w_t[pl.ds(pl.multiple_of(part * full + me * width, width), width), :]

    q = mm_nt(normed, weights(0)).astype(BF16)
    key = mm_nt(normed, weights(1)).astype(BF16)
    q_out[...] = q
    v_out[...] = mm_nt(normed, weights(2)).astype(BF16)
    kt_out[...] = mm_nt(weights(1), normed).astype(BF16)
    scores = mm_nt(key, head_stack(q)) * (SCALE * LOG2E)
    parts = []
    for a in range(sites):
        bias = [
            jnp.full((1, rows), jnp.where(link[me ^ b, me ^ a] > 0, 0.0, -jnp.inf), F32)
            for b in range(sites)
        ]
        bias = jnp.concatenate(bias * (width // HEAD_DIM), axis=1)
        parts.append(scores[a * rows : (a + 1) * rows] + bias)
    parts, inverse = exp_parts(parts)
    for a in range(sites):
        p_out[a * rows : (a + 1) * rows, :] = (parts[a] * inverse).astype(BF16)


def column_step(sites, haps, hap, x_in, row_out, gain, col_proj, kv_t_w, col_out, *refs):
    ga_out, send, keep, og_out, og, w_all, sems = refs
    core = hap[0] % 2
    half = row_out.shape[0] // 2
    mine = pl.ds(pl.multiple_of(core * half, half), half)
    other = pl.ds(pl.multiple_of((1 - core) * half, half), half)

    def save(j, cols):
        return pltpu.make_async_copy(w_all.at[mine, cols], keep.at[:, cols], sems.at[j])

    def save_outputs(j, cols):
        return pltpu.make_async_copy(og.at[:, :, cols], og_out.at[:, :, cols], sems.at[j])

    width = row_out.shape[0]
    group = width // sites
    x_all = flat_rows(x_in[...], F32)
    rows = x_all.shape[0]
    per = rows // haps
    hid = x_all[:, :width]
    cot_f = x_all[:, width : 2 * width]
    cot = cot_f.astype(BF16)
    row_att = x_all[:, 2 * width :].astype(BF16)
    grad_att = mm_nt(cot, col_out[...]).astype(BF16)
    xhat, rstd = norm_parts(hid)
    normed = (xhat * gain[1:2, :]).astype(BF16)
    packed = mm(normed, col_proj[...]).astype(BF16)
    q = packed[:, :width]
    key = packed[:, width : 2 * width]
    val = packed[:, 2 * width :]
    kv_t = mm_nt(kv_t_w[...], normed).astype(BF16)
    q_st = head_stack(q)
    g_st = head_stack(grad_att)
    scores = mm_nt(key, q_st) * (SCALE * LOG2E)
    dprob = mm_nt(val, g_st)
    same = (
        lax.broadcasted_iota(jnp.int32, scores.shape, 0) % per
        == lax.broadcasted_iota(jnp.int32, scores.shape, 1) % per
    )
    scores = jnp.where(same, scores, -jnp.inf)
    exps = jnp.exp2(scores - jnp.max(scores, axis=0, keepdims=True))
    inverse = 1.0 / jnp.sum(exps, axis=0, keepdims=True)
    att_t = head_blocks(mm(kv_t[width:, :], exps.astype(BF16)) * inverse)
    probs = exps * inverse
    delta = jnp.sum(probs * dprob, axis=0, keepdims=True)
    dscore = (probs * (dprob - delta)).astype(BF16)
    dv = mm(probs.astype(BF16), g_st)
    dk = mm(dscore, q_st)
    dq = jnp.transpose(head_blocks(mm(kv_t[:width, :], dscore)))
    w_all[:, 3 * width : 4 * width] = mm(att_t.astype(BF16), cot).astype(BF16)
    att = jnp.transpose(att_t).astype(BF16)
    out = hid + mm(att, col_out[...])
    og[:, :, :width] = out.reshape(haps, per, width).astype(BF16)
    third = save_outputs(2, slice(0, width))
    third.start()
    packed_grad = jnp.concatenate([dq * SCALE, dk * SCALE, dv], axis=1).astype(BF16)
    w_all[:, : 3 * width] = mm_tn(normed, packed_grad).astype(BF16)
    first = save(0, slice(0, 4 * width))
    first.start()
    grad_normed = mm_nt(packed_grad, col_proj[...])
    grad_hidden = (cot_f + norm_back(xhat, rstd, gain[1:2, :], grad_normed)).astype(BF16)
    og[:, :, width:] = grad_hidden.astype(F32).reshape(haps, per, width).astype(BF16)
    fourth = save_outputs(3, slice(width, 2 * width))
    fourth.start()
    w_all[:, 4 * width :] = mm_tn(row_att, grad_hidden).astype(BF16)
    second = save(1, slice(4 * width, 5 * width))
    second.start()
    for i in range(sites):
        g_i = mm_nt(grad_hidden, row_out[i * group : (i + 1) * group, :])
        ga_out[i * haps : (i + 1) * haps] = pack_block(g_i, haps)
    send[...] = w_all[other, :]
    for copy in (first, second, third, fourth):
        copy.wait()


def split_outputs(hap, og, keep, send):
    for m in range(keep.shape[0]):
        keep[m] = og[hap[0] ^ (2 * m)]
        send[m] = og[hap[0] ^ (2 * m + 1)]


def column_split(sites, idx, keep, *refs):
    outs, both, gots = refs[-sites - 1 : -1], refs[-1], refs[: -sites - 1]
    got = jnp.concatenate([g[...].astype(F32) for g in gots], axis=0)
    both[...] = (keep[...].astype(F32) + got).astype(BF16)
    part = keep.shape[0] // sites
    for k in range(sites):
        outs[k][...] = both[pl.ds(pl.multiple_of((idx[0] ^ k) * part, part), part), :]


def row_backward(sites, haps, idx, core, g_in, prob, q, val, key_t, normed, *refs):
    gp_outs = refs[:sites]
    keep, send, g_all, w_out = refs[sites:]
    me = idx[0]
    total, width = q.shape
    rows = total // sites
    for b in range(sites):
        g_all[b * rows : (b + 1) * rows, :] = unpack_block(
            g_in[pl.ds((me ^ b) * haps, haps)], width
        )
    g_st = head_stack(g_all[...])
    p_all = prob[...].astype(F32)
    dprob = mm_nt(val[...], g_st)
    delta = jnp.sum(p_all * dprob, axis=0, keepdims=True)
    dscore = (p_all * (dprob - delta)).astype(BF16)
    dv = mm(prob[...], g_st)
    dk = mm(dscore, head_stack(q[...]))
    dq_t = head_blocks(mm(key_t[...], dscore)) * SCALE
    dk16 = (dk * SCALE).astype(BF16)
    dv16 = dv.astype(BF16)
    w_out[:width, :] = mm(dq_t.astype(BF16), normed[...]).astype(BF16)
    w_out[width : 2 * width, :] = mm_tn(dk16, normed[...]).astype(BF16)
    w_out[2 * width :, :] = mm_tn(dv16, normed[...]).astype(BF16)
    half = 3 * width // 2
    keep[...] = w_out[pl.ds(pl.multiple_of(core[0] * half, half), half), :]
    send[...] = w_out[pl.ds(pl.multiple_of((1 - core[0]) * half, half), half), :]
    dq = jnp.transpose(dq_t).astype(BF16)
    joined = jnp.concatenate([dq, dk16, dv16], axis=1)
    for b in range(sites):
        gp_outs[b][...] = joined[b * rows : (b + 1) * rows]


def row_finish(sites, haps, idx, hap, feats, gain, w_t, gp, *refs):
    gps, parts = refs[: sites - 1], refs[sites - 1 : sites - 1 + haps // 2]
    out_ref, gf_ref, og = refs[sites - 1 + haps // 2 :]
    me = idx[0]
    rows, width = feats.shape
    group = width // sites
    per = rows // haps
    for m in range(haps // 2):
        base = parts[m].shape[0] - 4 * per
        for j in range(2):
            for side in range(2):
                start = base + (2 * j + side) * per
                og[side, hap[0] ^ (2 * m + j)] = parts[m][start : start + per, :].astype(F32)
    grads = [gp[...]] + [g[g.shape[0] - rows :, : 3 * group] for g in gps]
    grad_normed = 0.0
    for k in range(sites):
        place = [pl.multiple_of(p * width + (me ^ k) * group, group) for p in range(3)]
        weights = jnp.concatenate([w_t[pl.ds(p, group), :] for p in place], axis=0)
        grad_normed = grad_normed + mm(grads[k], weights)
    xhat, rstd = norm_parts(feats[...].astype(F32))
    grad = og[1].reshape(rows, width) + norm_back(xhat, rstd, gain[:1, :], grad_normed)
    out_ref[...] = og[0].reshape(rows, width).astype(BF16)
    gf_ref[...] = grad.astype(BF16)


def weights_join(sites, row_keep, row_got, og_keep, og_got, *refs):
    cols, outs = refs[:sites], refs[sites:]
    half, width = row_keep.shape
    depth = half + 5 * cols[0].shape[0]
    per = og_keep.shape[1]
    total = sum(c[...].astype(F32) for c in cols)
    tiles = [total[:, t * width : (t + 1) * width] for t in range(5)]
    rows = row_keep[...].astype(F32) + row_got[...].astype(F32)
    joined = jnp.concatenate([rows] + tiles, axis=0).astype(BF16)
    for m, out in enumerate(outs):
        out[:depth, :] = joined
        both = [og_keep[m].astype(F32), og_got[m].astype(F32)]
        both = [x[:, j * width : (j + 1) * width] for x in both for j in range(2)]
        out[depth:, :] = jnp.concatenate(both, axis=0).astype(BF16)


def weights_sum(haps, sites, *refs):
    parts, gps = refs[: haps // 2], refs[haps // 2 : haps // 2 + sites - 1]
    mine, outs = refs[haps // 2 + sites - 1], refs[haps // 2 + sites :]
    depth, width = mine.shape
    terms = [r[:depth, :].astype(F32) for r in parts]
    while len(terms) > 1:
        terms = [a + b for a, b in zip(terms[::2], terms[1::2])]
    mine[...] = terms[0].astype(BF16)
    for gp, out in zip(gps, outs):
        out[:depth, :] = mine[...]
        out[depth:, : gp.shape[1]] = gp[...]
        out[depth:, gp.shape[1] :] = jnp.zeros((gp.shape[0], width - gp.shape[1]), BF16)


def weights_finish(sites, idx, core, *refs):
    pieces = refs[: 2 * sites]
    rp, ro, cp, co, rows_t = refs[2 * sites :]
    width = ro.shape[0]
    group = width // sites
    unit = group // 2
    part = width // 2 // sites
    for j in range(2 * sites):
        k = j // 2
        cc = core[0] ^ (j % 2)
        g = idx[0] ^ k
        piece = pieces[j][...].astype(F32)
        for u in range(3):
            place = 3 * cc + u
            dest = (place // 2) * width + g * group + (place % 2) * unit
            rows_t[pl.ds(pl.multiple_of(dest, unit), unit), :] = piece[u * unit : (u + 1) * unit]
        here = pl.ds(pl.multiple_of(cc * (width // 2) + g * part, part), part)
        tiles = [piece[3 * unit + t * part : 3 * unit + (t + 1) * part] for t in range(5)]
        for t in range(3):
            cp[here, t * width : (t + 1) * width] = tiles[t]
        co[here, :] = tiles[3]
        ro[here, :] = tiles[4]
    rp[...] = jnp.transpose(rows_t[...])


def exchange(value, axis):
    return lax.all_to_all(value, axis, 0, 0, tiled=True)


def swapped(value, axis, by):
    length = lax.axis_size(axis)
    return lax.ppermute(value, axis, [(i, i ^ by) for i in range(length)])


def on_device(
    features,
    link_pattern,
    row_gain,
    row_proj,
    row_out,
    column_norm_gain,
    col_proj,
    col_out,
    cotangent,
):
    rows, _, width = features.shape
    sites, haps = lax.axis_size("site"), lax.axis_size("hap")
    count = sites * haps
    per = rows // haps
    group = width // sites
    heads = group // HEAD_DIM
    total = rows * sites
    both_axes = ("site", "hap")
    me = lax.axis_index("site")
    idx = me.reshape(1).astype(jnp.int32)
    hap = lax.axis_index("hap").reshape(1).astype(jnp.int32)
    core = hap % 2
    factor = lane_factor(per, group)
    block = ((count, per // factor, group * factor), BF16)
    feats = features.reshape(rows, width)
    cot = cotangent.reshape(rows, width)

    pieces = [feats] + [swapped(feats, "site", k) for k in range(1, sites)]
    link_pattern = jnp.where(link_pattern > 0, 1, 0)
    gains = jnp.stack([row_gain, column_norm_gain])
    w_t = jnp.transpose(row_proj)
    kv_t_w = jnp.transpose(col_proj[:, width:])

    x_out, normed = call(
        functools.partial(row_forward, sites, haps),
        [((haps, per, 3 * width), BF16), ((total, width), BF16)],
        idx, link_pattern, *pieces, cot, gains, w_t, row_out, scalars=2,
    )
    x_in = exchange(x_out, "hap")
    prob, q, val, key_t = call(
        functools.partial(row_probs, sites),
        [
            ((total, heads * total), BF16),
            ((total, group), BF16),
            ((total, group), BF16),
            ((group, total), BF16),
        ],
        idx, link_pattern, normed, w_t, scalars=2, us=20,
    )
    x_in, _ = lax.optimization_barrier((x_in, prob))
    half = width // 2
    ga, col_send, col_keep, og = call(
        functools.partial(column_step, sites, haps),
        [
            block,
            ((half, 5 * width), BF16),
            ((half, 5 * width), BF16),
            ((haps, per, 2 * width), BF16),
        ],
        hap, x_in, row_out, gains, col_proj, kv_t_w, col_out, scalars=1, far=2,
        scratch=[
            pltpu.VMEM((haps, per, 2 * width), BF16),
            pltpu.VMEM((width, 5 * width), BF16),
            pltpu.SemaphoreType.DMA((4,)),
        ],
    )
    g_in = exchange(ga, both_axes)
    col_got = [swapped(col_send, "hap", 1)]
    cols = call(
        functools.partial(column_split, sites),
        [((half // sites, 5 * width), BF16)] * sites,
        idx, col_keep, *col_got, scalars=1, us=0,
        scratch=[pltpu.VMEM((half, 5 * width), BF16)],
    )
    og_keep, og_send = call(
        split_outputs, [((haps // 2, per, 2 * width), BF16)] * 2, hap, og, scalars=1
    )
    og_got = swapped(og_send, "hap", 1)
    g_in, _ = lax.optimization_barrier((g_in, (cols, og_got)))
    cols = [cols[0]] + [swapped(cols[k], "site", k) for k in range(1, sites)]
    *gps, row_keep, row_send = call(
        functools.partial(row_backward, sites, haps),
        [((rows, 3 * group), BF16)] * sites + [((3 * group // 2, width), BF16)] * 2,
        idx, core, g_in, prob, q, val, key_t, normed, scalars=2,
        scratch=[
            pltpu.VMEM((total, group), BF16),
            pltpu.VMEM((3 * group, width), BF16),
        ],
    )
    row_got = swapped(row_send, "hap", 1)
    depth = 3 * group // 2 + 5 * half // sites
    parts = call(
        functools.partial(weights_join, sites),
        [((depth + 4 * per, width), BF16)] * (haps // 2),
        row_keep, row_got, og_keep, og_got, *cols,
    )
    parts = [parts[0]] + [swapped(parts[m], "hap", 2 * m) for m in range(1, haps // 2)]
    mine, *sends = call(
        functools.partial(weights_sum, haps, sites),
        [((depth, width), BF16)] + [((depth + rows, width), BF16)] * (sites - 1),
        *parts, *gps[1:],
    )
    got = [swapped(sends[k - 1], "site", k) for k in range(1, sites)]
    mine_swapped = swapped(mine, "hap", 1)
    got[0], mine_swapped = lax.optimization_barrier((got[0], mine_swapped))
    full = [mine, mine_swapped] + [x for p in got for x in (p, swapped(p, "hap", 1))]
    out, grad = call(
        functools.partial(row_finish, sites, haps),
        [((rows, width), BF16)] * 2,
        idx, hap, feats, gains, w_t, gps[0], *got, *parts, scalars=2,
        scratch=[pltpu.VMEM((2, haps, per, width), F32)],
    )
    rp, ro, cp, co = call(
        functools.partial(weights_finish, sites),
        [((width, 3 * width), F32), ((width, width), F32)] * 2,
        idx, core, *full, scalars=2,
        scratch=[pltpu.VMEM((3 * width, width), F32)],
    )
    shape = (rows, 1, width)
    return (out.reshape(shape), grad.reshape(shape), rp, ro, cp, co)


def solution(mesh):
    data = P("site", "hap", None)
    return jax.shard_map(
        on_device,
        mesh=mesh,
        in_specs=(data, P(), P(), P(), P(), P(), P(), P(), data),
        out_specs=(data, data, P(), P(), P(), P()),
        check_vma=False,
    )
```

```python
import functools

import jax
import jax.numpy as jnp
from jax import lax
from jax.experimental import pallas as pl
from jax.experimental.pallas import tpu as pltpu
from jax.sharding import PartitionSpec as P

HEAD_DIM = 32
EPSILON = 1e-05
LOG2E = 1.4426950408889634
SCALE = HEAD_DIM ** (-0.5)
F32 = jnp.float32
BF16 = jnp.bfloat16
VMEM = pl.BlockSpec(memory_space=pltpu.VMEM)
HBM = pl.BlockSpec(memory_space=pltpu.HBM)
SMEM = pl.BlockSpec(memory_space=pltpu.SMEM)
PARAMS = pltpu.CompilerParams(vmem_limit_bytes=24 << 20)


def mm(a, b):
    return lax.dot_general(a, b, (((1,), (0,)), ((), ())), preferred_element_type=F32)


def mm_nt(a, b):
    return lax.dot_general(a, b, (((1,), (1,)), ((), ())), preferred_element_type=F32)


def mm_tn(a, b):
    return lax.dot_general(a, b, (((0,), (0,)), ((), ())), preferred_element_type=F32)


def norm_parts(x):
    centred = x - jnp.mean(x, axis=-1, keepdims=True)
    rstd = lax.rsqrt(jnp.mean(centred * centred, axis=-1, keepdims=True) + EPSILON)
    return centred * rstd, rstd


def norm_back(xhat, rstd, gain, grad):
    scaled = grad * gain
    first = jnp.mean(scaled, axis=-1, keepdims=True)
    second = jnp.mean(scaled * xhat, axis=-1, keepdims=True)
    return rstd * (scaled - first - xhat * second)


def head_lanes(width, head):
    return lax.broadcasted_iota(jnp.int32, (1, width), 1) // HEAD_DIM == head


def only_head(values, head):
    return jnp.where(head_lanes(values.shape[1], head), values, jnp.zeros_like(values))


def flat_rows(values, dtype=BF16):
    wide = values.astype(F32)
    return wide.reshape(wide.shape[0] * wide.shape[1], wide.shape[2]).astype(dtype)


def lane_factor(rows, width):
    factor = 128 // width
    return factor if (rows // factor) % 8 == 0 else 1


def pack_block(values, outer):
    rows, width = values.shape[0] // outer, values.shape[1]
    factor = lane_factor(rows, width)
    split = values.reshape(outer, factor, rows // factor, width)
    return jnp.concatenate([split[:, j] for j in range(factor)], axis=2).astype(BF16)


def unpack_block(values, width):
    wide = values.astype(F32)
    factor = wide.shape[2] // width
    split = [wide[:, None, :, j * width : (j + 1) * width] for j in range(factor)]
    joined = jnp.concatenate(split, axis=1)
    return joined.reshape(-1, width).astype(BF16)


def call(body, outs, *operands, scalars=0, scratch=(), us=0, far=0):
    cost = pl.CostEstimate(flops=us * 10**9 + 1, bytes_accessed=us * 3_600_000 + 1, transcendentals=0)
    return pl.pallas_call(
        body,
        out_shape=[jax.ShapeDtypeStruct(s, d) for s, d in outs[: len(outs) - far]]
        + [pltpu.HBM(s, d) for s, d in outs[len(outs) - far :]],
        in_specs=[SMEM] * scalars + [VMEM] * (len(operands) - scalars),
        out_specs=[VMEM] * (len(outs) - far) + [HBM] * far,
        scratch_shapes=list(scratch),
        compiler_params=PARAMS,
        cost_estimate=cost,
    )(*operands)


def head_stack(values):
    heads = values.shape[1] // HEAD_DIM
    return jnp.concatenate([only_head(values, h) for h in range(heads)], axis=0)


def head_blocks(values):
    heads = values.shape[0] // HEAD_DIM
    wide = values.shape[1] // heads
    return jnp.concatenate(
        [
            values[h * HEAD_DIM : (h + 1) * HEAD_DIM, h * wide : (h + 1) * wide]
            for h in range(heads)
        ],
        axis=0,
    )


def exp_parts(parts):
    high = functools.reduce(jnp.maximum, [jnp.max(part, axis=0, keepdims=True) for part in parts])
    parts = [jnp.exp2(part - high) for part in parts]
    total = sum(jnp.sum(part, axis=0, keepdims=True) for part in parts)
    return parts, 1.0 / total


def row_forward(sites, haps, idx, link, *refs):
    pieces = refs[:sites]
    cot, gain, w_t, row_out, x_out, n_out = refs[sites:]
    me = idx[0]
    rows, width = cot.shape
    for k in range(sites):
        xhat, _ = norm_parts(pieces[k][...].astype(F32))
        n_out[k * rows : (k + 1) * rows, :] = (xhat * gain[:1, :]).astype(BF16)
    normed = n_out[...]
    q = mm_nt(normed[:rows], w_t[:width, :]).astype(BF16)
    key = mm_nt(normed, w_t[width : 2 * width, :]).astype(BF16)
    v_t = mm_nt(w_t[2 * width :, :], normed).astype(BF16)
    scores = mm_nt(key, head_stack(q)) * (SCALE * LOG2E)
    bias = [jnp.where(link[me, me ^ a] > 0, 0.0, -jnp.inf) for a in range(sites)]
    parts = [scores[a * rows : (a + 1) * rows] + bias[a] for a in range(sites)]
    parts, inverse = exp_parts(parts)
    exps = jnp.concatenate([part.astype(BF16) for part in parts], axis=0)
    att_t = head_blocks(mm(v_t, exps) * inverse)
    att = jnp.transpose(att_t).astype(BF16)
    hid = pieces[0][...].astype(F32) + mm(att, row_out[...])
    joined = jnp.concatenate([hid, cot[...].astype(F32), att.astype(F32)], axis=1)
    x_out[...] = joined.reshape(haps, rows // haps, 3 * width).astype(BF16)


def row_probs(sites, idx, link, normed_ref, w_t, p_out, q_out, v_out, kt_out):
    me = idx[0]
    normed = normed_ref[...]
    total, width = q_out.shape
    full = normed.shape[1]
    rows = total // sites

    def weights(part):
        return w_t[pl.ds(pl.multiple_of(part * full + me * width, width), width), :]

    q = mm_nt(normed, weights(0)).astype(BF16)
    key = mm_nt(normed, weights(1)).astype(BF16)
    q_out[...] = q
    v_out[...] = mm_nt(normed, weights(2)).astype(BF16)
    kt_out[...] = mm_nt(weights(1), normed).astype(BF16)
    scores = mm_nt(key, head_stack(q)) * (SCALE * LOG2E)
    parts = []
    for a in range(sites):
        bias = [
            jnp.full((1, rows), jnp.where(link[me ^ b, me ^ a] > 0, 0.0, -jnp.inf), F32)
            for b in range(sites)
        ]
        bias = jnp.concatenate(bias * (width // HEAD_DIM), axis=1)
        parts.append(scores[a * rows : (a + 1) * rows] + bias)
    parts, inverse = exp_parts(parts)
    for a in range(sites):
        p_out[a * rows : (a + 1) * rows, :] = (parts[a] * inverse).astype(BF16)


def column_step(sites, haps, hap, x_in, row_out, gain, col_proj, kv_t_w, col_out, *refs):
    ga_out, send, keep, og_out, og, w_all, sems = refs
    core = hap[0] % 2
    half = row_out.shape[0] // 2
    mine = pl.ds(pl.multiple_of(core * half, half), half)
    other = pl.ds(pl.multiple_of((1 - core) * half, half), half)

    def save(j, cols):
        return pltpu.make_async_copy(w_all.at[mine, cols], keep.at[:, cols], sems.at[j])

    def save_outputs(j, cols):
        return pltpu.make_async_copy(og.at[:, :, cols], og_out.at[:, :, cols], sems.at[j])

    width = row_out.shape[0]
    group = width // sites
    x_all = flat_rows(x_in[...], F32)
    rows = x_all.shape[0]
    per = rows // haps
    hid = x_all[:, :width]
    cot_f = x_all[:, width : 2 * width]
    cot = cot_f.astype(BF16)
    row_att = x_all[:, 2 * width :].astype(BF16)
    grad_att = mm_nt(cot, col_out[...]).astype(BF16)
    xhat, rstd = norm_parts(hid)
    normed = (xhat * gain[1:2, :]).astype(BF16)
    packed = mm(normed, col_proj[...]).astype(BF16)
    q = packed[:, :width]
    key = packed[:, width : 2 * width]
    val = packed[:, 2 * width :]
    kv_t = mm_nt(kv_t_w[...], normed).astype(BF16)
    q_st = head_stack(q)
    g_st = head_stack(grad_att)
    scores = mm_nt(key, q_st) * (SCALE * LOG2E)
    dprob = mm_nt(val, g_st)
    same = (
        lax.broadcasted_iota(jnp.int32, scores.shape, 0) % per
        == lax.broadcasted_iota(jnp.int32, scores.shape, 1) % per
    )
    scores = jnp.where(same, scores, -jnp.inf)
    exps = jnp.exp2(scores - jnp.max(scores, axis=0, keepdims=True))
    inverse = 1.0 / jnp.sum(exps, axis=0, keepdims=True)
    att_t = head_blocks(mm(kv_t[width:, :], exps.astype(BF16)) * inverse)
    probs = exps * inverse
    delta = jnp.sum(probs * dprob, axis=0, keepdims=True)
    dscore = (probs * (dprob - delta)).astype(BF16)
    dv = mm(probs.astype(BF16), g_st)
    dk = mm(dscore, q_st)
    dq = jnp.transpose(head_blocks(mm(kv_t[:width, :], dscore)))
    w_all[:, 3 * width : 4 * width] = mm(att_t.astype(BF16), cot).astype(BF16)
    att = jnp.transpose(att_t).astype(BF16)
    out = hid + mm(att, col_out[...])
    og[:, :, :width] = out.reshape(haps, per, width).astype(BF16)
    third = save_outputs(2, slice(0, width))
    third.start()
    packed_grad = jnp.concatenate([dq * SCALE, dk * SCALE, dv], axis=1).astype(BF16)
    w_all[:, : 3 * width] = mm_tn(normed, packed_grad).astype(BF16)
    first = save(0, slice(0, 4 * width))
    first.start()
    grad_normed = mm_nt(packed_grad, col_proj[...])
    grad_hidden = (cot_f + norm_back(xhat, rstd, gain[1:2, :], grad_normed)).astype(BF16)
    og[:, :, width:] = grad_hidden.astype(F32).reshape(haps, per, width).astype(BF16)
    fourth = save_outputs(3, slice(width, 2 * width))
    fourth.start()
    w_all[:, 4 * width :] = mm_tn(row_att, grad_hidden).astype(BF16)
    second = save(1, slice(4 * width, 5 * width))
    second.start()
    for i in range(sites):
        g_i = mm_nt(grad_hidden, row_out[i * group : (i + 1) * group, :])
        ga_out[i * haps : (i + 1) * haps] = pack_block(g_i, haps)
    send[...] = w_all[other, :]
    for copy in (first, second, third, fourth):
        copy.wait()


def split_outputs(hap, og, keep, send):
    for m in range(keep.shape[0]):
        keep[m] = og[hap[0] ^ (2 * m)]
        send[m] = og[hap[0] ^ (2 * m + 1)]


def column_split(sites, idx, keep, *refs):
    outs, both, gots = refs[-sites - 1 : -1], refs[-1], refs[: -sites - 1]
    got = jnp.concatenate([g[...].astype(F32) for g in gots], axis=0)
    both[...] = (keep[...].astype(F32) + got).astype(BF16)
    part = keep.shape[0] // sites
    for k in range(sites):
        outs[k][...] = both[pl.ds(pl.multiple_of((idx[0] ^ k) * part, part), part), :]


def row_backward(sites, haps, idx, core, g_in, prob, q, val, key_t, normed, *refs):
    gp_outs = refs[:sites]
    keep, send, g_all, w_out = refs[sites:]
    me = idx[0]
    total, width = q.shape
    rows = total // sites
    for b in range(sites):
        g_all[b * rows : (b + 1) * rows, :] = unpack_block(
            g_in[pl.ds((me ^ b) * haps, haps)], width
        )
    g_st = head_stack(g_all[...])
    p_all = prob[...].astype(F32)
    dprob = mm_nt(val[...], g_st)
    delta = jnp.sum(p_all * dprob, axis=0, keepdims=True)
    dscore = (p_all * (dprob - delta)).astype(BF16)
    dv = mm(prob[...], g_st)
    dk = mm(dscore, head_stack(q[...]))
    dq_t = head_blocks(mm(key_t[...], dscore)) * SCALE
    dk16 = (dk * SCALE).astype(BF16)
    dv16 = dv.astype(BF16)
    w_out[:width, :] = mm(dq_t.astype(BF16), normed[...]).astype(BF16)
    w_out[width : 2 * width, :] = mm_tn(dk16, normed[...]).astype(BF16)
    w_out[2 * width :, :] = mm_tn(dv16, normed[...]).astype(BF16)
    half = 3 * width // 2
    keep[...] = w_out[pl.ds(pl.multiple_of(core[0] * half, half), half), :]
    send[...] = w_out[pl.ds(pl.multiple_of((1 - core[0]) * half, half), half), :]
    dq = jnp.transpose(dq_t).astype(BF16)
    joined = jnp.concatenate([dq, dk16, dv16], axis=1)
    for b in range(sites):
        gp_outs[b][...] = joined[b * rows : (b + 1) * rows]


def row_finish(sites, haps, idx, hap, feats, gain, w_t, gp, *refs):
    gps, parts = refs[: sites - 1], refs[sites - 1 : sites - 1 + haps // 2]
    out_ref, gf_ref, og = refs[sites - 1 + haps // 2 :]
    me = idx[0]
    rows, width = feats.shape
    group = width // sites
    per = rows // haps
    for m in range(haps // 2):
        base = parts[m].shape[0] - 4 * per
        for j in range(2):
            for side in range(2):
                start = base + (2 * j + side) * per
                og[side, hap[0] ^ (2 * m + j)] = parts[m][start : start + per, :].astype(F32)
    grads = [gp[...]] + [g[g.shape[0] - rows :, : 3 * group] for g in gps]
    grad_normed = 0.0
    for k in range(sites):
        place = [pl.multiple_of(p * width + (me ^ k) * group, group) for p in range(3)]
        weights = jnp.concatenate([w_t[pl.ds(p, group), :] for p in place], axis=0)
        grad_normed = grad_normed + mm(grads[k], weights)
    xhat, rstd = norm_parts(feats[...].astype(F32))
    grad = og[1].reshape(rows, width) + norm_back(xhat, rstd, gain[:1, :], grad_normed)
    out_ref[...] = og[0].reshape(rows, width).astype(BF16)
    gf_ref[...] = grad.astype(BF16)


def outputs_pair(keep, got, m, width):
    both = [keep[m].astype(F32), got[m].astype(F32)]
    both = [x[:, j * width : (j + 1) * width] for x in both for j in range(2)]
    return jnp.concatenate(both, axis=0).astype(BF16)


def weights_join(sites, row_keep, row_got, og_keep, og_got, *refs):
    cols, (near, own, *far) = refs[:sites], refs[sites:]
    half, width = row_keep.shape
    depth = half + 5 * cols[0].shape[0]
    total = sum(c[...].astype(F32) for c in cols)
    tiles = [total[:, t * width : (t + 1) * width] for t in range(5)]
    rows = row_keep[...].astype(F32) + row_got[...].astype(F32)
    near[:depth, :] = jnp.concatenate([rows] + tiles, axis=0).astype(BF16)
    near[depth:, :] = outputs_pair(og_keep, og_got, 1, width)
    own[...] = outputs_pair(og_keep, og_got, 0, width)
    for j, out in enumerate(far):
        out[...] = outputs_pair(og_keep, og_got, j + 2, width)


def weights_add(mine, got, out):
    depth = out.shape[0]
    out[...] = (mine[:depth, :].astype(F32) + got[:depth, :].astype(F32)).astype(BF16)


def weights_last(left, right, *refs):
    gps, mine, outs = refs[: len(refs) // 2], refs[len(refs) // 2], refs[len(refs) // 2 + 1 :]
    depth, width = mine.shape
    weights_add(left, right, mine)
    for gp, out in zip(gps, outs):
        out[:depth, :] = mine[...]
        out[depth:, : gp.shape[1]] = gp[...]
        out[depth:, gp.shape[1] :] = jnp.zeros((gp.shape[0], width - gp.shape[1]), BF16)


def weights_finish(sites, idx, core, *refs):
    pieces = refs[: 2 * sites]
    rp, ro, cp, co, rows_t = refs[2 * sites :]
    width = ro.shape[0]
    group = width // sites
    unit = group // 2
    part = width // 2 // sites
    for j in range(2 * sites):
        k = j // 2
        cc = core[0] ^ (j % 2)
        g = idx[0] ^ k
        piece = pieces[j][...].astype(F32)
        for u in range(3):
            place = 3 * cc + u
            dest = (place // 2) * width + g * group + (place % 2) * unit
            rows_t[pl.ds(pl.multiple_of(dest, unit), unit), :] = piece[u * unit : (u + 1) * unit]
        here = pl.ds(pl.multiple_of(cc * (width // 2) + g * part, part), part)
        tiles = [piece[3 * unit + t * part : 3 * unit + (t + 1) * part] for t in range(5)]
        for t in range(3):
            cp[here, t * width : (t + 1) * width] = tiles[t]
        co[here, :] = tiles[3]
        ro[here, :] = tiles[4]
    rp[...] = jnp.transpose(rows_t[...])


def exchange(value, axis):
    return lax.all_to_all(value, axis, 0, 0, tiled=True)


def swapped(value, axis, by):
    length = lax.axis_size(axis)
    return lax.ppermute(value, axis, [(i, i ^ by) for i in range(length)])


def on_device(
    features,
    link_pattern,
    row_gain,
    row_proj,
    row_out,
    column_norm_gain,
    col_proj,
    col_out,
    cotangent,
):
    rows, _, width = features.shape
    sites, haps = lax.axis_size("site"), lax.axis_size("hap")
    count = sites * haps
    per = rows // haps
    group = width // sites
    heads = group // HEAD_DIM
    total = rows * sites
    both_axes = ("site", "hap")
    me = lax.axis_index("site")
    idx = me.reshape(1).astype(jnp.int32)
    hap = lax.axis_index("hap").reshape(1).astype(jnp.int32)
    core = hap % 2
    factor = lane_factor(per, group)
    block = ((count, per // factor, group * factor), BF16)
    feats = features.reshape(rows, width)
    cot = cotangent.reshape(rows, width)

    pieces = [feats] + [swapped(feats, "site", k) for k in range(1, sites)]
    link_pattern = jnp.where(link_pattern > 0, 1, 0)
    gains = jnp.stack([row_gain, column_norm_gain])
    w_t = jnp.transpose(row_proj)
    kv_t_w = jnp.transpose(col_proj[:, width:])

    x_out, normed = call(
        functools.partial(row_forward, sites, haps),
        [((haps, per, 3 * width), BF16), ((total, width), BF16)],
        idx, link_pattern, *pieces, cot, gains, w_t, row_out, scalars=2,
    )
    x_in = exchange(x_out, "hap")
    prob, q, val, key_t = call(
        functools.partial(row_probs, sites),
        [
            ((total, heads * total), BF16),
            ((total, group), BF16),
            ((total, group), BF16),
            ((group, total), BF16),
        ],
        idx, link_pattern, normed, w_t, scalars=2, us=20,
    )
    x_in, _ = lax.optimization_barrier((x_in, prob))
    half = width // 2
    ga, col_send, col_keep, og = call(
        functools.partial(column_step, sites, haps),
        [
            block,
            ((half, 5 * width), BF16),
            ((half, 5 * width), BF16),
            ((haps, per, 2 * width), BF16),
        ],
        hap, x_in, row_out, gains, col_proj, kv_t_w, col_out, scalars=1, far=2,
        scratch=[
            pltpu.VMEM((haps, per, 2 * width), BF16),
            pltpu.VMEM((width, 5 * width), BF16),
            pltpu.SemaphoreType.DMA((4,)),
        ],
    )
    g_in = exchange(ga, both_axes)
    col_got = [swapped(col_send, "hap", 1)]
    cols = call(
        functools.partial(column_split, sites),
        [((half // sites, 5 * width), BF16)] * sites,
        idx, col_keep, *col_got, scalars=1, us=0,
        scratch=[pltpu.VMEM((half, 5 * width), BF16)],
    )
    og_keep, og_send = call(
        split_outputs, [((haps // 2, per, 2 * width), BF16)] * 2, hap, og, scalars=1
    )
    og_got = swapped(og_send, "hap", 1)
    g_in, _ = lax.optimization_barrier((g_in, (cols, og_got)))
    cols = [cols[0]] + [swapped(cols[k], "site", k) for k in range(1, sites)]
    *gps, row_keep, row_send = call(
        functools.partial(row_backward, sites, haps),
        [((rows, 3 * group), BF16)] * sites + [((3 * group // 2, width), BF16)] * 2,
        idx, core, g_in, prob, q, val, key_t, normed, scalars=2,
        scratch=[
            pltpu.VMEM((total, group), BF16),
            pltpu.VMEM((3 * group, width), BF16),
        ],
    )
    row_got = swapped(row_send, "hap", 1)
    depth = 3 * group // 2 + 5 * half // sites
    near, own, *far = call(
        functools.partial(weights_join, sites),
        [((depth + 4 * per, width), BF16)] + [((4 * per, width), BF16)] * (haps // 2 - 1),
        row_keep, row_got, og_keep, og_got, *cols,
    )
    near_got = swapped(near, "hap", 2)
    far = [swapped(x, "hap", 2 * (j + 2)) for j, x in enumerate(far)]
    near_got, far = lax.optimization_barrier((near_got, far))
    parts = [own, near_got] + list(far)
    left, right, step = near, near_got, 2
    while 2 * step < haps:
        (left,) = call(weights_add, [((depth, width), BF16)], left, right)
        right, step = swapped(left, "hap", 2 * step), 2 * step
    mine, *sends = call(
        weights_last,
        [((depth, width), BF16)] + [((depth + rows, width), BF16)] * (sites - 1),
        left, right, *gps[1:],
    )
    got = [swapped(sends[k - 1], "site", k) for k in range(1, sites)]
    mine_swapped = swapped(mine, "hap", 1)
    got[0], mine_swapped = lax.optimization_barrier((got[0], mine_swapped))
    full = [mine, mine_swapped] + [x for p in got for x in (p, swapped(p, "hap", 1))]
    out, grad = call(
        functools.partial(row_finish, sites, haps),
        [((rows, width), BF16)] * 2,
        idx, hap, feats, gains, w_t, gps[0], *got, *parts, scalars=2,
        scratch=[pltpu.VMEM((2, haps, per, width), F32)],
    )
    rp, ro, cp, co = call(
        functools.partial(weights_finish, sites),
        [((width, 3 * width), F32), ((width, width), F32)] * 2,
        idx, core, *full, scalars=2,
        scratch=[pltpu.VMEM((3 * width, width), F32)],
    )
    shape = (rows, 1, width)
    return (out.reshape(shape), grad.reshape(shape), rp, ro, cp, co)


def solution(mesh):
    data = P("site", "hap", None)
    return jax.shard_map(
        on_device,
        mesh=mesh,
        in_specs=(data, P(), P(), P(), P(), P(), P(), P(), data),
        out_specs=(data, data, P(), P(), P(), P()),
        check_vma=False,
    )
```

```python
import functools

import jax
import jax.numpy as jnp
from jax import lax
from jax.experimental import pallas as pl
from jax.experimental.pallas import tpu as pltpu
from jax.sharding import PartitionSpec as P

HEAD_DIM = 32
EPSILON = 1e-05
LOG2E = 1.4426950408889634
SCALE = HEAD_DIM ** (-0.5)
F32 = jnp.float32
BF16 = jnp.bfloat16
VMEM = pl.BlockSpec(memory_space=pltpu.VMEM)
HBM = pl.BlockSpec(memory_space=pltpu.HBM)
SMEM = pl.BlockSpec(memory_space=pltpu.SMEM)
PARAMS = pltpu.CompilerParams(vmem_limit_bytes=24 << 20)


def mm(a, b):
    return lax.dot_general(a, b, (((1,), (0,)), ((), ())), preferred_element_type=F32)


def mm_nt(a, b):
    return lax.dot_general(a, b, (((1,), (1,)), ((), ())), preferred_element_type=F32)


def mm_tn(a, b):
    return lax.dot_general(a, b, (((0,), (0,)), ((), ())), preferred_element_type=F32)


def norm_parts(x):
    centred = x - jnp.mean(x, axis=-1, keepdims=True)
    rstd = lax.rsqrt(jnp.mean(centred * centred, axis=-1, keepdims=True) + EPSILON)
    return centred * rstd, rstd


def norm_back(xhat, rstd, gain, grad):
    scaled = grad * gain
    first = jnp.mean(scaled, axis=-1, keepdims=True)
    second = jnp.mean(scaled * xhat, axis=-1, keepdims=True)
    return rstd * (scaled - first - xhat * second)


def head_lanes(width, head):
    return lax.broadcasted_iota(jnp.int32, (1, width), 1) // HEAD_DIM == head


def only_head(values, head):
    return jnp.where(head_lanes(values.shape[1], head), values, jnp.zeros_like(values))


def flat_rows(values, dtype=BF16):
    wide = values.astype(F32)
    return wide.reshape(wide.shape[0] * wide.shape[1], wide.shape[2]).astype(dtype)


def lane_factor(rows, width):
    factor = 128 // width
    return factor if (rows // factor) % 8 == 0 else 1


def pack_block(values, outer):
    rows, width = values.shape[0] // outer, values.shape[1]
    factor = lane_factor(rows, width)
    split = values.reshape(outer, factor, rows // factor, width)
    return jnp.concatenate([split[:, j] for j in range(factor)], axis=2).astype(BF16)


def unpack_block(values, width):
    wide = values.astype(F32)
    factor = wide.shape[2] // width
    split = [wide[:, None, :, j * width : (j + 1) * width] for j in range(factor)]
    joined = jnp.concatenate(split, axis=1)
    return joined.reshape(-1, width).astype(BF16)


def call(body, outs, *operands, scalars=0, scratch=(), us=0, far=0):
    cost = pl.CostEstimate(flops=us * 10**9 + 1, bytes_accessed=us * 3_600_000 + 1, transcendentals=0)
    return pl.pallas_call(
        body,
        out_shape=[jax.ShapeDtypeStruct(s, d) for s, d in outs[: len(outs) - far]]
        + [pltpu.HBM(s, d) for s, d in outs[len(outs) - far :]],
        in_specs=[SMEM] * scalars + [VMEM] * (len(operands) - scalars),
        out_specs=[VMEM] * (len(outs) - far) + [HBM] * far,
        scratch_shapes=list(scratch),
        compiler_params=PARAMS,
        cost_estimate=cost,
    )(*operands)


def head_stack(values):
    heads = values.shape[1] // HEAD_DIM
    return jnp.concatenate([only_head(values, h) for h in range(heads)], axis=0)


def head_blocks(values):
    heads = values.shape[0] // HEAD_DIM
    wide = values.shape[1] // heads
    return jnp.concatenate(
        [
            values[h * HEAD_DIM : (h + 1) * HEAD_DIM, h * wide : (h + 1) * wide]
            for h in range(heads)
        ],
        axis=0,
    )


def exp_parts(parts):
    high = functools.reduce(jnp.maximum, [jnp.max(part, axis=0, keepdims=True) for part in parts])
    parts = [jnp.exp2(part - high) for part in parts]
    total = sum(jnp.sum(part, axis=0, keepdims=True) for part in parts)
    return parts, 1.0 / total


def row_forward(sites, haps, idx, link, *refs):
    pieces = refs[:sites]
    cot, gain, w_t, row_out, x_out, n_out = refs[sites:]
    me = idx[0]
    rows, width = cot.shape
    for k in range(sites):
        xhat, _ = norm_parts(pieces[k][...].astype(F32))
        n_out[k * rows : (k + 1) * rows, :] = (xhat * gain[:1, :]).astype(BF16)
    normed = n_out[...]
    q = mm_nt(normed[:rows], w_t[:width, :]).astype(BF16)
    key = mm_nt(normed, w_t[width : 2 * width, :]).astype(BF16)
    v_t = mm_nt(w_t[2 * width :, :], normed).astype(BF16)
    scores = mm_nt(key, head_stack(q)) * (SCALE * LOG2E)
    bias = [jnp.where(link[me, me ^ a] > 0, 0.0, -jnp.inf) for a in range(sites)]
    parts = [scores[a * rows : (a + 1) * rows] + bias[a] for a in range(sites)]
    parts, inverse = exp_parts(parts)
    exps = jnp.concatenate([part.astype(BF16) for part in parts], axis=0)
    att_t = head_blocks(mm(v_t, exps) * inverse)
    att = jnp.transpose(att_t).astype(BF16)
    hid = pieces[0][...].astype(F32) + mm(att, row_out[...])
    joined = jnp.concatenate([hid, cot[...].astype(F32), att.astype(F32)], axis=1)
    x_out[...] = joined.reshape(haps, rows // haps, 3 * width).astype(BF16)


def row_probs(sites, idx, link, normed_ref, w_t, p_out, q_out, v_out, kt_out):
    me = idx[0]
    normed = normed_ref[...]
    total, width = q_out.shape
    full = normed.shape[1]
    rows = total // sites

    def weights(part):
        return w_t[pl.ds(pl.multiple_of(part * full + me * width, width), width), :]

    q = mm_nt(normed, weights(0)).astype(BF16)
    key = mm_nt(normed, weights(1)).astype(BF16)
    q_out[...] = q
    v_out[...] = mm_nt(normed, weights(2)).astype(BF16)
    kt_out[...] = mm_nt(weights(1), normed).astype(BF16)
    scores = mm_nt(key, head_stack(q)) * (SCALE * LOG2E)
    parts = []
    for a in range(sites):
        bias = [
            jnp.full((1, rows), jnp.where(link[me ^ b, me ^ a] > 0, 0.0, -jnp.inf), F32)
            for b in range(sites)
        ]
        bias = jnp.concatenate(bias * (width // HEAD_DIM), axis=1)
        parts.append(scores[a * rows : (a + 1) * rows] + bias)
    parts, inverse = exp_parts(parts)
    for a in range(sites):
        p_out[a * rows : (a + 1) * rows, :] = (parts[a] * inverse).astype(BF16)


def column_step(sites, haps, hap, x_in, row_out, gain, col_proj, kv_t_w, col_out, *refs):
    ga_out, send, keep, og_out, og, w_all, sems = refs
    core = hap[0] % 2
    half = row_out.shape[0] // 2
    mine = pl.ds(pl.multiple_of(core * half, half), half)
    other = pl.ds(pl.multiple_of((1 - core) * half, half), half)

    def save(j, cols):
        return pltpu.make_async_copy(w_all.at[mine, cols], keep.at[:, cols], sems.at[j])

    def save_outputs(j, cols):
        return pltpu.make_async_copy(og.at[:, :, cols], og_out.at[:, :, cols], sems.at[j])

    width = row_out.shape[0]
    group = width // sites
    x_all = flat_rows(x_in[...], F32)
    rows = x_all.shape[0]
    per = rows // haps
    hid = x_all[:, :width]
    cot_f = x_all[:, width : 2 * width]
    cot = cot_f.astype(BF16)
    row_att = x_all[:, 2 * width :].astype(BF16)
    grad_att = mm_nt(cot, col_out[...]).astype(BF16)
    xhat, rstd = norm_parts(hid)
    normed = (xhat * gain[1:2, :]).astype(BF16)
    packed = mm(normed, col_proj[...]).astype(BF16)
    q = packed[:, :width]
    key = packed[:, width : 2 * width]
    val = packed[:, 2 * width :]
    kv_t = mm_nt(kv_t_w[...], normed).astype(BF16)
    q_st = head_stack(q)
    g_st = head_stack(grad_att)
    scores = mm_nt(key, q_st) * (SCALE * LOG2E)
    dprob = mm_nt(val, g_st)
    same = (
        lax.broadcasted_iota(jnp.int32, scores.shape, 0) % per
        == lax.broadcasted_iota(jnp.int32, scores.shape, 1) % per
    )
    scores = jnp.where(same, scores, -jnp.inf)
    exps = jnp.exp2(scores - jnp.max(scores, axis=0, keepdims=True))
    inverse = 1.0 / jnp.sum(exps, axis=0, keepdims=True)
    att_t = head_blocks(mm(kv_t[width:, :], exps.astype(BF16)) * inverse)
    probs = exps * inverse
    delta = jnp.sum(probs * dprob, axis=0, keepdims=True)
    dscore = (probs * (dprob - delta)).astype(BF16)
    dv = mm(probs.astype(BF16), g_st)
    dk = mm(dscore, q_st)
    dq = jnp.transpose(head_blocks(mm(kv_t[:width, :], dscore)))
    w_all[:, 3 * width : 4 * width] = mm(att_t.astype(BF16), cot).astype(BF16)
    att = jnp.transpose(att_t).astype(BF16)
    out = hid + mm(att, col_out[...])
    og[:, :, :width] = out.reshape(haps, per, width).astype(BF16)
    third = save_outputs(2, slice(0, width))
    third.start()
    packed_grad = jnp.concatenate([dq * SCALE, dk * SCALE, dv], axis=1).astype(BF16)
    w_all[:, : 3 * width] = mm_tn(normed, packed_grad).astype(BF16)
    first = save(0, slice(0, 4 * width))
    first.start()
    grad_normed = mm_nt(packed_grad, col_proj[...])
    grad_hidden = (cot_f + norm_back(xhat, rstd, gain[1:2, :], grad_normed)).astype(BF16)
    og[:, :, width:] = grad_hidden.astype(F32).reshape(haps, per, width).astype(BF16)
    fourth = save_outputs(3, slice(width, 2 * width))
    fourth.start()
    w_all[:, 4 * width :] = mm_tn(row_att, grad_hidden).astype(BF16)
    second = save(1, slice(4 * width, 5 * width))
    second.start()
    for i in range(sites):
        g_i = mm_nt(grad_hidden, row_out[i * group : (i + 1) * group, :])
        ga_out[i * haps : (i + 1) * haps] = pack_block(g_i, haps)
    send[...] = w_all[other, :]
    for copy in (first, second, third, fourth):
        copy.wait()


def split_outputs(hap, og, keep, send):
    for m in range(keep.shape[0]):
        keep[m] = og[hap[0] ^ (2 * m)]
        send[m] = og[hap[0] ^ (2 * m + 1)]


def column_split(sites, idx, keep, *refs):
    outs, both, gots = refs[-sites - 1 : -1], refs[-1], refs[: -sites - 1]
    got = jnp.concatenate([g[...].astype(F32) for g in gots], axis=0)
    both[...] = (keep[...].astype(F32) + got).astype(BF16)
    part = keep.shape[0] // sites
    for k in range(sites):
        outs[k][...] = both[pl.ds(pl.multiple_of((idx[0] ^ k) * part, part), part), :]


def row_backward(sites, haps, idx, core, g_in, prob, q, val, key_t, normed, *refs):
    gp_outs = refs[:sites]
    keep, send, g_all, w_out = refs[sites:]
    me = idx[0]
    total, width = q.shape
    rows = total // sites
    for b in range(sites):
        g_all[b * rows : (b + 1) * rows, :] = unpack_block(
            g_in[pl.ds((me ^ b) * haps, haps)], width
        )
    g_st = head_stack(g_all[...])
    p_all = prob[...].astype(F32)
    dprob = mm_nt(val[...], g_st)
    delta = jnp.sum(p_all * dprob, axis=0, keepdims=True)
    dscore = (p_all * (dprob - delta)).astype(BF16)
    dv = mm(prob[...], g_st)
    dk = mm(dscore, head_stack(q[...]))
    dq_t = head_blocks(mm(key_t[...], dscore)) * SCALE
    dk16 = (dk * SCALE).astype(BF16)
    dv16 = dv.astype(BF16)
    w_out[:width, :] = mm(dq_t.astype(BF16), normed[...]).astype(BF16)
    w_out[width : 2 * width, :] = mm_tn(dk16, normed[...]).astype(BF16)
    w_out[2 * width :, :] = mm_tn(dv16, normed[...]).astype(BF16)
    half = 3 * width // 2
    keep[...] = w_out[pl.ds(pl.multiple_of(core[0] * half, half), half), :]
    send[...] = w_out[pl.ds(pl.multiple_of((1 - core[0]) * half, half), half), :]
    dq = jnp.transpose(dq_t).astype(BF16)
    joined = jnp.concatenate([dq, dk16, dv16], axis=1)
    for b in range(sites):
        gp_outs[b][...] = joined[b * rows : (b + 1) * rows]


def row_finish(sites, haps, final, idx, hap, feats, gain, w_t, gp, *refs):
    gps, (kept, last, out_ref, gf_ref, og) = refs[: sites - 1], refs[sites - 1 :]
    me = idx[0]
    rows, width = feats.shape
    group = width // sites
    per = rows // haps
    inner = len(final) // 2
    for place, (m, _) in enumerate(final):
        source, base = kept, 4 * per * place
        if place >= inner:
            source, base = last, last.shape[0] - 4 * per * (len(final) - place)
        for j in range(2):
            for side in range(2):
                start = base + (2 * j + side) * per
                og[side, hap[0] ^ (2 * m + j)] = source[start : start + per, :].astype(F32)
    grads = [gp[...]] + [g[g.shape[0] - rows :, : 3 * group] for g in gps]
    grad_normed = 0.0
    for k in range(sites):
        place = [pl.multiple_of(p * width + (me ^ k) * group, group) for p in range(3)]
        weights = jnp.concatenate([w_t[pl.ds(p, group), :] for p in place], axis=0)
        grad_normed = grad_normed + mm(grads[k], weights)
    xhat, rstd = norm_parts(feats[...].astype(F32))
    grad = og[1].reshape(rows, width) + norm_back(xhat, rstd, gain[:1, :], grad_normed)
    out_ref[...] = og[0].reshape(rows, width).astype(BF16)
    gf_ref[...] = grad.astype(BF16)


def outputs_pair(keep, got, m, width):
    both = [keep[m].astype(F32), got[m].astype(F32)]
    both = [x[:, j * width : (j + 1) * width] for x in both for j in range(2)]
    return jnp.concatenate(both, axis=0).astype(BF16)


def outputs_plan(count):
    hold, steps, bit = [(0, d) for d in range(count)], [], 1
    while bit < count:
        send = [h for h in hold if h[1] & bit]
        keep = [h for h in hold if not h[1] & bit]
        steps.append((hold, send, keep))
        hold = keep + [(s ^ bit, d ^ bit) for s, d in send]
        bit *= 2
    return steps, hold


def weights_join(sites, step, row_keep, row_got, og_keep, og_got, *refs):
    cols, (out, kept) = refs[:sites], refs[sites:]
    _, send, keep = step
    half, width = row_keep.shape
    depth = half + 5 * cols[0].shape[0]
    tall = 4 * og_keep.shape[1]
    total = sum(c[...].astype(F32) for c in cols)
    tiles = [total[:, t * width : (t + 1) * width] for t in range(5)]
    rows = row_keep[...].astype(F32) + row_got[...].astype(F32)
    out[:depth, :] = jnp.concatenate([rows] + tiles, axis=0).astype(BF16)
    for j, (_, d) in enumerate(send):
        start = depth + j * tall
        out[start : start + tall, :] = outputs_pair(og_keep, og_got, d, width)
    for j, (_, d) in enumerate(keep):
        kept[j * tall : (j + 1) * tall, :] = outputs_pair(og_keep, og_got, d, width)


def weights_step(step, mine, got, kept, out, kept_out):
    hold, send, keep = step
    tall = 2 * kept.shape[0] // len(hold)
    depth = mine.shape[0] - kept.shape[0]
    out[:depth, :] = (mine[:depth, :].astype(F32) + got[:depth, :].astype(F32)).astype(BF16)

    def block(item):
        place = hold.index(item)
        inner = len(hold) // 2
        if place < inner:
            return kept[place * tall : (place + 1) * tall, :]
        start = depth + (place - inner) * tall
        return got[start : start + tall, :]

    for j, item in enumerate(send):
        out[depth + j * tall : depth + (j + 1) * tall, :] = block(item)
    for j, item in enumerate(keep):
        kept_out[j * tall : (j + 1) * tall, :] = block(item)


def weights_last(left, right, *refs):
    gps, mine, outs = refs[: len(refs) // 2], refs[len(refs) // 2], refs[len(refs) // 2 + 1 :]
    depth, width = mine.shape
    mine[...] = (left[:depth, :].astype(F32) + right[:depth, :].astype(F32)).astype(BF16)
    for gp, out in zip(gps, outs):
        out[:depth, :] = mine[...]
        out[depth:, : gp.shape[1]] = gp[...]
        out[depth:, gp.shape[1] :] = jnp.zeros((gp.shape[0], width - gp.shape[1]), BF16)


def weights_finish(sites, idx, core, *refs):
    pieces = refs[: 2 * sites]
    rp, ro, cp, co, rows_t = refs[2 * sites :]
    width = ro.shape[0]
    group = width // sites
    unit = group // 2
    part = width // 2 // sites
    for j in range(2 * sites):
        k = j // 2
        cc = core[0] ^ (j % 2)
        g = idx[0] ^ k
        piece = pieces[j][...].astype(F32)
        for u in range(3):
            place = 3 * cc + u
            dest = (place // 2) * width + g * group + (place % 2) * unit
            rows_t[pl.ds(pl.multiple_of(dest, unit), unit), :] = piece[u * unit : (u + 1) * unit]
        here = pl.ds(pl.multiple_of(cc * (width // 2) + g * part, part), part)
        tiles = [piece[3 * unit + t * part : 3 * unit + (t + 1) * part] for t in range(5)]
        for t in range(3):
            cp[here, t * width : (t + 1) * width] = tiles[t]
        co[here, :] = tiles[3]
        ro[here, :] = tiles[4]
    rp[...] = jnp.transpose(rows_t[...])


def exchange(value, axis):
    return lax.all_to_all(value, axis, 0, 0, tiled=True)


def swapped(value, axis, by):
    length = lax.axis_size(axis)
    return lax.ppermute(value, axis, [(i, i ^ by) for i in range(length)])


def on_device(
    features,
    link_pattern,
    row_gain,
    row_proj,
    row_out,
    column_norm_gain,
    col_proj,
    col_out,
    cotangent,
):
    rows, _, width = features.shape
    sites, haps = lax.axis_size("site"), lax.axis_size("hap")
    count = sites * haps
    per = rows // haps
    group = width // sites
    heads = group // HEAD_DIM
    total = rows * sites
    both_axes = ("site", "hap")
    me = lax.axis_index("site")
    idx = me.reshape(1).astype(jnp.int32)
    hap = lax.axis_index("hap").reshape(1).astype(jnp.int32)
    core = hap % 2
    factor = lane_factor(per, group)
    block = ((count, per // factor, group * factor), BF16)
    feats = features.reshape(rows, width)
    cot = cotangent.reshape(rows, width)

    pieces = [feats] + [swapped(feats, "site", k) for k in range(1, sites)]
    link_pattern = jnp.where(link_pattern > 0, 1, 0)
    gains = jnp.stack([row_gain, column_norm_gain])
    w_t = jnp.transpose(row_proj)
    kv_t_w = jnp.transpose(col_proj[:, width:])

    x_out, normed = call(
        functools.partial(row_forward, sites, haps),
        [((haps, per, 3 * width), BF16), ((total, width), BF16)],
        idx, link_pattern, *pieces, cot, gains, w_t, row_out, scalars=2,
    )
    x_in = exchange(x_out, "hap")
    prob, q, val, key_t = call(
        functools.partial(row_probs, sites),
        [
            ((total, heads * total), BF16),
            ((total, group), BF16),
            ((total, group), BF16),
            ((group, total), BF16),
        ],
        idx, link_pattern, normed, w_t, scalars=2, us=20,
    )
    x_in, _ = lax.optimization_barrier((x_in, prob))
    half = width // 2
    ga, col_send, col_keep, og = call(
        functools.partial(column_step, sites, haps),
        [
            block,
            ((half, 5 * width), BF16),
            ((half, 5 * width), BF16),
            ((haps, per, 2 * width), BF16),
        ],
        hap, x_in, row_out, gains, col_proj, kv_t_w, col_out, scalars=1, far=2,
        scratch=[
            pltpu.VMEM((haps, per, 2 * width), BF16),
            pltpu.VMEM((width, 5 * width), BF16),
            pltpu.SemaphoreType.DMA((4,)),
        ],
    )
    g_in = exchange(ga, both_axes)
    col_got = [swapped(col_send, "hap", 1)]
    cols = call(
        functools.partial(column_split, sites),
        [((half // sites, 5 * width), BF16)] * sites,
        idx, col_keep, *col_got, scalars=1, us=0,
        scratch=[pltpu.VMEM((half, 5 * width), BF16)],
    )
    og_keep, og_send = call(
        split_outputs, [((haps // 2, per, 2 * width), BF16)] * 2, hap, og, scalars=1
    )
    og_got = swapped(og_send, "hap", 1)
    g_in, _ = lax.optimization_barrier((g_in, (cols, og_got)))
    cols = [cols[0]] + [swapped(cols[k], "site", k) for k in range(1, sites)]
    *gps, row_keep, row_send = call(
        functools.partial(row_backward, sites, haps),
        [((rows, 3 * group), BF16)] * sites + [((3 * group // 2, width), BF16)] * 2,
        idx, core, g_in, prob, q, val, key_t, normed, scalars=2,
        scratch=[
            pltpu.VMEM((total, group), BF16),
            pltpu.VMEM((3 * group, width), BF16),
        ],
    )
    row_got = swapped(row_send, "hap", 1)
    depth = 3 * group // 2 + 5 * half // sites
    steps, final = outputs_plan(haps // 2)
    moving, staying = 2 * per * (haps // 2), 2 * per * (haps // 2)
    left, kept = call(
        functools.partial(weights_join, sites, steps[0]),
        [((depth + moving, width), BF16), ((staying, width), BF16)],
        row_keep, row_got, og_keep, og_got, *cols,
    )
    right = swapped(left, "hap", 2)
    for j, step in enumerate(steps[1:]):
        left, kept = call(
            functools.partial(weights_step, step),
            [((depth + moving, width), BF16), ((staying, width), BF16)],
            left, right, kept,
        )
        right = swapped(left, "hap", 4 * 2**j)
    mine, *sends = call(
        weights_last,
        [((depth, width), BF16)] + [((depth + rows, width), BF16)] * (sites - 1),
        left, right, *gps[1:],
    )
    got = [swapped(sends[k - 1], "site", k) for k in range(1, sites)]
    mine_swapped = swapped(mine, "hap", 1)
    got[0], mine_swapped = lax.optimization_barrier((got[0], mine_swapped))
    full = [mine, mine_swapped] + [x for p in got for x in (p, swapped(p, "hap", 1))]
    out, grad = call(
        functools.partial(row_finish, sites, haps, final),
        [((rows, width), BF16)] * 2,
        idx, hap, feats, gains, w_t, gps[0], *got, kept, right, scalars=2,
        scratch=[pltpu.VMEM((2, haps, per, width), F32)],
    )
    rp, ro, cp, co = call(
        functools.partial(weights_finish, sites),
        [((width, 3 * width), F32), ((width, width), F32)] * 2,
        idx, core, *full, scalars=2,
        scratch=[pltpu.VMEM((3 * width, width), F32)],
    )
    shape = (rows, 1, width)
    return (out.reshape(shape), grad.reshape(shape), rp, ro, cp, co)


def solution(mesh):
    data = P("site", "hap", None)
    return jax.shard_map(
        on_device,
        mesh=mesh,
        in_specs=(data, P(), P(), P(), P(), P(), P(), P(), data),
        out_specs=(data, data, P(), P(), P(), P()),
        check_vma=False,
    )
```

```python
import functools

import jax
import jax.numpy as jnp
from jax import lax
from jax.experimental import pallas as pl
from jax.experimental.pallas import tpu as pltpu
from jax.sharding import PartitionSpec as P

HEAD_DIM = 32
EPSILON = 1e-05
LOG2E = 1.4426950408889634
SCALE = HEAD_DIM ** (-0.5)
F32 = jnp.float32
BF16 = jnp.bfloat16
VMEM = pl.BlockSpec(memory_space=pltpu.VMEM)
HBM = pl.BlockSpec(memory_space=pltpu.HBM)
SMEM = pl.BlockSpec(memory_space=pltpu.SMEM)
PARAMS = pltpu.CompilerParams(vmem_limit_bytes=24 << 20)


def mm(a, b):
    return lax.dot_general(a, b, (((1,), (0,)), ((), ())), preferred_element_type=F32)


def mm_nt(a, b):
    return lax.dot_general(a, b, (((1,), (1,)), ((), ())), preferred_element_type=F32)


def mm_tn(a, b):
    return lax.dot_general(a, b, (((0,), (0,)), ((), ())), preferred_element_type=F32)


def norm_parts(x):
    centred = x - jnp.mean(x, axis=-1, keepdims=True)
    rstd = lax.rsqrt(jnp.mean(centred * centred, axis=-1, keepdims=True) + EPSILON)
    return centred * rstd, rstd


def norm_back(xhat, rstd, gain, grad):
    scaled = grad * gain
    first = jnp.mean(scaled, axis=-1, keepdims=True)
    second = jnp.mean(scaled * xhat, axis=-1, keepdims=True)
    return rstd * (scaled - first - xhat * second)


def head_lanes(width, head):
    return lax.broadcasted_iota(jnp.int32, (1, width), 1) // HEAD_DIM == head


def only_head(values, head):
    return jnp.where(head_lanes(values.shape[1], head), values, jnp.zeros_like(values))


def flat_rows(values, dtype=BF16):
    wide = values.astype(F32)
    return wide.reshape(wide.shape[0] * wide.shape[1], wide.shape[2]).astype(dtype)


def lane_factor(rows, width):
    factor = 128 // width
    return factor if (rows // factor) % 8 == 0 else 1


def pack_block(values, outer):
    rows, width = values.shape[0] // outer, values.shape[1]
    factor = lane_factor(rows, width)
    split = values.reshape(outer, factor, rows // factor, width)
    return jnp.concatenate([split[:, j] for j in range(factor)], axis=2).astype(BF16)


def unpack_block(values, width):
    wide = values.astype(F32)
    factor = wide.shape[2] // width
    split = [wide[:, None, :, j * width : (j + 1) * width] for j in range(factor)]
    joined = jnp.concatenate(split, axis=1)
    return joined.reshape(-1, width).astype(BF16)


def call(body, outs, *operands, scalars=0, scratch=(), us=0, far=0):
    cost = pl.CostEstimate(flops=us * 10**9 + 1, bytes_accessed=us * 3_600_000 + 1, transcendentals=0)
    return pl.pallas_call(
        body,
        out_shape=[jax.ShapeDtypeStruct(s, d) for s, d in outs[: len(outs) - far]]
        + [pltpu.HBM(s, d) for s, d in outs[len(outs) - far :]],
        in_specs=[SMEM] * scalars + [VMEM] * (len(operands) - scalars),
        out_specs=[VMEM] * (len(outs) - far) + [HBM] * far,
        scratch_shapes=list(scratch),
        compiler_params=PARAMS,
        cost_estimate=cost,
    )(*operands)


def head_stack(values):
    heads = values.shape[1] // HEAD_DIM
    return jnp.concatenate([only_head(values, h) for h in range(heads)], axis=0)


def head_blocks(values):
    heads = values.shape[0] // HEAD_DIM
    wide = values.shape[1] // heads
    return jnp.concatenate(
        [
            values[h * HEAD_DIM : (h + 1) * HEAD_DIM, h * wide : (h + 1) * wide]
            for h in range(heads)
        ],
        axis=0,
    )


def exp_parts(parts):
    high = functools.reduce(jnp.maximum, [jnp.max(part, axis=0, keepdims=True) for part in parts])
    parts = [jnp.exp2(part - high) for part in parts]
    total = sum(jnp.sum(part, axis=0, keepdims=True) for part in parts)
    return parts, 1.0 / total


def row_forward(sites, haps, idx, link, *refs):
    pieces = refs[:sites]
    cot, gain, w_t, row_out, x_out, n_out = refs[sites:]
    me = idx[0]
    rows, width = cot.shape
    for k in range(sites):
        xhat, _ = norm_parts(pieces[k][...].astype(F32))
        n_out[k * rows : (k + 1) * rows, :] = (xhat * gain[:1, :]).astype(BF16)
    normed = n_out[...]
    q = mm_nt(normed[:rows], w_t[:width, :]).astype(BF16)
    key = mm_nt(normed, w_t[width : 2 * width, :]).astype(BF16)
    v_t = mm_nt(w_t[2 * width :, :], normed).astype(BF16)
    scores = mm_nt(key, head_stack(q)) * (SCALE * LOG2E)
    bias = [jnp.where(link[me, me ^ a] > 0, 0.0, -jnp.inf) for a in range(sites)]
    parts = [scores[a * rows : (a + 1) * rows] + bias[a] for a in range(sites)]
    parts, inverse = exp_parts(parts)
    exps = jnp.concatenate([part.astype(BF16) for part in parts], axis=0)
    att_t = head_blocks(mm(v_t, exps) * inverse)
    att = jnp.transpose(att_t).astype(BF16)
    hid = pieces[0][...].astype(F32) + mm(att, row_out[...])
    joined = jnp.concatenate([hid, cot[...].astype(F32), att.astype(F32)], axis=1)
    x_out[...] = joined.reshape(haps, rows // haps, 3 * width).astype(BF16)


def row_probs(sites, idx, link, normed_ref, w_t, p_out, q_out, v_out, kt_out):
    me = idx[0]
    normed = normed_ref[...]
    total, width = q_out.shape
    full = normed.shape[1]
    rows = total // sites

    def weights(part):
        return w_t[pl.ds(pl.multiple_of(part * full + me * width, width), width), :]

    q = mm_nt(normed, weights(0)).astype(BF16)
    key = mm_nt(normed, weights(1)).astype(BF16)
    q_out[...] = q
    v_out[...] = mm_nt(normed, weights(2)).astype(BF16)
    kt_out[...] = mm_nt(weights(1), normed).astype(BF16)
    scores = mm_nt(key, head_stack(q)) * (SCALE * LOG2E)
    parts = []
    for a in range(sites):
        bias = [
            jnp.full((1, rows), jnp.where(link[me ^ b, me ^ a] > 0, 0.0, -jnp.inf), F32)
            for b in range(sites)
        ]
        bias = jnp.concatenate(bias * (width // HEAD_DIM), axis=1)
        parts.append(scores[a * rows : (a + 1) * rows] + bias)
    parts, inverse = exp_parts(parts)
    for a in range(sites):
        p_out[a * rows : (a + 1) * rows, :] = (parts[a] * inverse).astype(BF16)


def column_step(sites, haps, hap, x_in, row_out, gain, col_proj, kv_t_w, col_out, *refs):
    ga_out, send, keep, og_out, og, w_all, sems = refs
    core = hap[0] % 2
    half = row_out.shape[0] // 2
    mine = pl.ds(pl.multiple_of(core * half, half), half)
    other = pl.ds(pl.multiple_of((1 - core) * half, half), half)

    def save(j, cols):
        return pltpu.make_async_copy(w_all.at[mine, cols], keep.at[:, cols], sems.at[j])

    def save_outputs(j, cols):
        return pltpu.make_async_copy(og.at[:, :, cols], og_out.at[:, :, cols], sems.at[j])

    width = row_out.shape[0]
    group = width // sites
    x_all = flat_rows(x_in[...], F32)
    rows = x_all.shape[0]
    per = rows // haps
    hid = x_all[:, :width]
    cot_f = x_all[:, width : 2 * width]
    cot = cot_f.astype(BF16)
    row_att = x_all[:, 2 * width :].astype(BF16)
    grad_att = mm_nt(cot, col_out[...]).astype(BF16)
    xhat, rstd = norm_parts(hid)
    normed = (xhat * gain[1:2, :]).astype(BF16)
    packed = mm(normed, col_proj[...]).astype(BF16)
    q = packed[:, :width]
    key = packed[:, width : 2 * width]
    val = packed[:, 2 * width :]
    kv_t = mm_nt(kv_t_w[...], normed).astype(BF16)
    q_st = head_stack(q)
    g_st = head_stack(grad_att)
    scores = mm_nt(key, q_st) * (SCALE * LOG2E)
    dprob = mm_nt(val, g_st)
    same = (
        lax.broadcasted_iota(jnp.int32, scores.shape, 0) % per
        == lax.broadcasted_iota(jnp.int32, scores.shape, 1) % per
    )
    scores = jnp.where(same, scores, -jnp.inf)
    exps = jnp.exp2(scores - jnp.max(scores, axis=0, keepdims=True))
    inverse = 1.0 / jnp.sum(exps, axis=0, keepdims=True)
    att_t = head_blocks(mm(kv_t[width:, :], exps.astype(BF16)) * inverse)
    probs = exps * inverse
    delta = jnp.sum(probs * dprob, axis=0, keepdims=True)
    dscore = (probs * (dprob - delta)).astype(BF16)
    dv = mm(probs.astype(BF16), g_st)
    dk = mm(dscore, q_st)
    dq = jnp.transpose(head_blocks(mm(kv_t[:width, :], dscore)))
    w_all[:, 3 * width : 4 * width] = mm(att_t.astype(BF16), cot).astype(BF16)
    att = jnp.transpose(att_t).astype(BF16)
    out = hid + mm(att, col_out[...])
    og[:, :, :width] = out.reshape(haps, per, width).astype(BF16)
    third = save_outputs(2, slice(0, width))
    third.start()
    packed_grad = jnp.concatenate([dq * SCALE, dk * SCALE, dv], axis=1).astype(BF16)
    w_all[:, : 3 * width] = mm_tn(normed, packed_grad).astype(BF16)
    first = save(0, slice(0, 4 * width))
    first.start()
    grad_normed = mm_nt(packed_grad, col_proj[...])
    grad_hidden = (cot_f + norm_back(xhat, rstd, gain[1:2, :], grad_normed)).astype(BF16)
    og[:, :, width:] = grad_hidden.astype(F32).reshape(haps, per, width).astype(BF16)
    fourth = save_outputs(3, slice(width, 2 * width))
    fourth.start()
    w_all[:, 4 * width :] = mm_tn(row_att, grad_hidden).astype(BF16)
    second = save(1, slice(4 * width, 5 * width))
    second.start()
    for i in range(sites):
        g_i = mm_nt(grad_hidden, row_out[i * group : (i + 1) * group, :])
        ga_out[i * haps : (i + 1) * haps] = pack_block(g_i, haps)
    send[...] = w_all[other, :]
    for copy in (first, second, third, fourth):
        copy.wait()


def split_outputs(hap, og, keep, send):
    for m in range(keep.shape[0]):
        keep[m] = og[hap[0] ^ (2 * m)]
        send[m] = og[hap[0] ^ (2 * m + 1)]


def column_split(sites, idx, keep, *refs):
    outs, both, gots = refs[-sites - 1 : -1], refs[-1], refs[: -sites - 1]
    got = jnp.concatenate([g[...].astype(F32) for g in gots], axis=0)
    both[...] = (keep[...].astype(F32) + got).astype(BF16)
    part = keep.shape[0] // sites
    for k in range(sites):
        outs[k][...] = both[pl.ds(pl.multiple_of((idx[0] ^ k) * part, part), part), :]


def row_backward(sites, haps, idx, core, g_in, prob, q, val, key_t, normed, *refs):
    gp_outs = refs[:sites]
    keep, send, g_all, w_out = refs[sites:]
    me = idx[0]
    total, width = q.shape
    rows = total // sites
    for b in range(sites):
        g_all[b * rows : (b + 1) * rows, :] = unpack_block(
            g_in[pl.ds((me ^ b) * haps, haps)], width
        )
    g_st = head_stack(g_all[...])
    p_all = prob[...].astype(F32)
    dprob = mm_nt(val[...], g_st)
    delta = jnp.sum(p_all * dprob, axis=0, keepdims=True)
    dscore = (p_all * (dprob - delta)).astype(BF16)
    dv = mm(prob[...], g_st)
    dk = mm(dscore, head_stack(q[...]))
    dq_t = head_blocks(mm(key_t[...], dscore)) * SCALE
    dk16 = (dk * SCALE).astype(BF16)
    dv16 = dv.astype(BF16)
    w_out[:width, :] = mm(dq_t.astype(BF16), normed[...]).astype(BF16)
    w_out[width : 2 * width, :] = mm_tn(dk16, normed[...]).astype(BF16)
    w_out[2 * width :, :] = mm_tn(dv16, normed[...]).astype(BF16)
    half = 3 * width // 2
    keep[...] = w_out[pl.ds(pl.multiple_of(core[0] * half, half), half), :]
    send[...] = w_out[pl.ds(pl.multiple_of((1 - core[0]) * half, half), half), :]
    dq = jnp.transpose(dq_t).astype(BF16)
    joined = jnp.concatenate([dq, dk16, dv16], axis=1)
    for b in range(sites):
        gp_outs[b][...] = joined[b * rows : (b + 1) * rows]


def row_finish(sites, haps, idx, hap, feats, gain, w_t, gp, *refs):
    gps, parts = refs[: sites - 1], refs[sites - 1 : sites - 1 + haps // 2]
    out_ref, gf_ref, og = refs[sites - 1 + haps // 2 :]
    me = idx[0]
    rows, width = feats.shape
    group = width // sites
    per = rows // haps
    for m in range(haps // 2):
        base = parts[m].shape[0] - 4 * per
        for j in range(2):
            for side in range(2):
                start = base + (2 * j + side) * per
                og[side, hap[0] ^ (2 * m + j)] = parts[m][start : start + per, :].astype(F32)
    grads = [gp[...]] + [g[g.shape[0] - rows :, : 3 * group] for g in gps]
    grad_normed = 0.0
    for k in range(sites):
        place = [pl.multiple_of(p * width + (me ^ k) * group, group) for p in range(3)]
        weights = jnp.concatenate([w_t[pl.ds(p, group), :] for p in place], axis=0)
        grad_normed = grad_normed + mm(grads[k], weights)
    xhat, rstd = norm_parts(feats[...].astype(F32))
    grad = og[1].reshape(rows, width) + norm_back(xhat, rstd, gain[:1, :], grad_normed)
    out_ref[...] = og[0].reshape(rows, width).astype(BF16)
    gf_ref[...] = grad.astype(BF16)


def outputs_pair(keep, got, m, width):
    both = [keep[m].astype(F32), got[m].astype(F32)]
    both = [x[:, j * width : (j + 1) * width] for x in both for j in range(2)]
    return jnp.concatenate(both, axis=0).astype(BF16)


def weights_join(sites, row_keep, row_got, og_keep, og_got, *refs):
    cols, (near, own, *far) = refs[:sites], refs[sites:]
    half, width = row_keep.shape
    depth = half + 5 * cols[0].shape[0]
    total = sum(c[...].astype(F32) for c in cols)
    tiles = [total[:, t * width : (t + 1) * width] for t in range(5)]
    rows = row_keep[...].astype(F32) + row_got[...].astype(F32)
    near[:depth, :] = jnp.concatenate([rows] + tiles, axis=0).astype(BF16)
    near[depth:, :] = outputs_pair(og_keep, og_got, 1, width)
    own[...] = outputs_pair(og_keep, og_got, 0, width)
    for j, out in enumerate(far):
        out[...] = outputs_pair(og_keep, og_got, j + 2, width)


def weights_add(mine, got, out):
    depth = out.shape[0]
    out[...] = (mine[:depth, :].astype(F32) + got[:depth, :].astype(F32)).astype(BF16)


def weights_finish(sites, idx, core, *refs):
    pieces = refs[: 2 * sites]
    rp, ro, cp, co, rows_t = refs[2 * sites :]
    width = ro.shape[0]
    group = width // sites
    unit = group // 2
    part = width // 2 // sites
    for j in range(2 * sites):
        k = j // 2
        cc = core[0] ^ (j % 2)
        g = idx[0] ^ k
        piece = pieces[j][...].astype(F32)
        for u in range(3):
            place = 3 * cc + u
            dest = (place // 2) * width + g * group + (place % 2) * unit
            rows_t[pl.ds(pl.multiple_of(dest, unit), unit), :] = piece[u * unit : (u + 1) * unit]
        here = pl.ds(pl.multiple_of(cc * (width // 2) + g * part, part), part)
        tiles = [piece[3 * unit + t * part : 3 * unit + (t + 1) * part] for t in range(5)]
        for t in range(3):
            cp[here, t * width : (t + 1) * width] = tiles[t]
        co[here, :] = tiles[3]
        ro[here, :] = tiles[4]
    rp[...] = jnp.transpose(rows_t[...])


def exchange(value, axis):
    return lax.all_to_all(value, axis, 0, 0, tiled=True)


def swapped(value, axis, by):
    length = lax.axis_size(axis)
    return lax.ppermute(value, axis, [(i, i ^ by) for i in range(length)])


def on_device(
    features,
    link_pattern,
    row_gain,
    row_proj,
    row_out,
    column_norm_gain,
    col_proj,
    col_out,
    cotangent,
):
    rows, _, width = features.shape
    sites, haps = lax.axis_size("site"), lax.axis_size("hap")
    count = sites * haps
    per = rows // haps
    group = width // sites
    heads = group // HEAD_DIM
    total = rows * sites
    both_axes = ("site", "hap")
    me = lax.axis_index("site")
    idx = me.reshape(1).astype(jnp.int32)
    hap = lax.axis_index("hap").reshape(1).astype(jnp.int32)
    core = hap % 2
    factor = lane_factor(per, group)
    block = ((count, per // factor, group * factor), BF16)
    feats = features.reshape(rows, width)
    cot = cotangent.reshape(rows, width)

    pieces = [feats] + [swapped(feats, "site", k) for k in range(1, sites)]
    link_pattern = jnp.where(link_pattern > 0, 1, 0)
    gains = jnp.stack([row_gain, column_norm_gain])
    w_t = jnp.transpose(row_proj)
    kv_t_w = jnp.transpose(col_proj[:, width:])

    x_out, normed = call(
        functools.partial(row_forward, sites, haps),
        [((haps, per, 3 * width), BF16), ((total, width), BF16)],
        idx, link_pattern, *pieces, cot, gains, w_t, row_out, scalars=2,
    )
    x_in = exchange(x_out, "hap")
    prob, q, val, key_t = call(
        functools.partial(row_probs, sites),
        [
            ((total, heads * total), BF16),
            ((total, group), BF16),
            ((total, group), BF16),
            ((group, total), BF16),
        ],
        idx, link_pattern, normed, w_t, scalars=2, us=20,
    )
    x_in, _ = lax.optimization_barrier((x_in, prob))
    half = width // 2
    ga, col_send, col_keep, og = call(
        functools.partial(column_step, sites, haps),
        [
            block,
            ((half, 5 * width), BF16),
            ((half, 5 * width), BF16),
            ((haps, per, 2 * width), BF16),
        ],
        hap, x_in, row_out, gains, col_proj, kv_t_w, col_out, scalars=1, far=2,
        scratch=[
            pltpu.VMEM((haps, per, 2 * width), BF16),
            pltpu.VMEM((width, 5 * width), BF16),
            pltpu.SemaphoreType.DMA((4,)),
        ],
    )
    g_in = exchange(ga, both_axes)
    col_got = [swapped(col_send, "hap", 1)]
    cols = call(
        functools.partial(column_split, sites),
        [((half // sites, 5 * width), BF16)] * sites,
        idx, col_keep, *col_got, scalars=1, us=0,
        scratch=[pltpu.VMEM((half, 5 * width), BF16)],
    )
    og_keep, og_send = call(
        split_outputs, [((haps // 2, per, 2 * width), BF16)] * 2, hap, og, scalars=1
    )
    og_got = swapped(og_send, "hap", 1)
    g_in, _ = lax.optimization_barrier((g_in, (cols, og_got)))
    cols = [cols[0]] + [swapped(cols[k], "site", k) for k in range(1, sites)]
    *gps, row_keep, row_send = call(
        functools.partial(row_backward, sites, haps),
        [((rows, 3 * group), BF16)] * sites + [((3 * group // 2, width), BF16)] * 2,
        idx, core, g_in, prob, q, val, key_t, normed, scalars=2,
        scratch=[
            pltpu.VMEM((total, group), BF16),
            pltpu.VMEM((3 * group, width), BF16),
        ],
    )
    row_got = swapped(row_send, "hap", 1)
    depth = 3 * group // 2 + 5 * half // sites
    near, own, *far = call(
        functools.partial(weights_join, sites),
        [((depth + 4 * per, width), BF16)] + [((4 * per, width), BF16)] * (haps // 2 - 1),
        row_keep, row_got, og_keep, og_got, *cols,
    )
    near_got = swapped(near, "hap", 2)
    far = [swapped(x, "hap", 2 * (j + 2)) for j, x in enumerate(far)]
    near_got, far = lax.optimization_barrier((near_got, far))
    parts = [own, near_got] + list(far)
    left, right, step = near, near_got, 2
    while 2 * step < haps:
        (left,) = call(weights_add, [((depth, width), BF16)], left, right)
        right, step = swapped(left, "hap", 2 * step), 2 * step
    gps, _ = lax.optimization_barrier((gps, left))
    gps = [gps[0]] + [swapped(gps[k], "site", k) for k in range(1, sites)]
    right, gps = lax.optimization_barrier((right, gps))
    (mine,) = call(weights_add, [((depth, width), BF16)], left, right)
    got = [swapped(mine, "site", k) for k in range(1, sites)]
    mine_swapped = swapped(mine, "hap", 1)
    out, grad = call(
        functools.partial(row_finish, sites, haps),
        [((rows, width), BF16)] * 2,
        idx, hap, feats, gains, w_t, *gps, *parts, scalars=2,
        scratch=[pltpu.VMEM((2, haps, per, width), F32)],
    )
    got, mine_swapped, out = lax.optimization_barrier((got, mine_swapped, out))
    full = [mine, mine_swapped] + [x for p in got for x in (p, swapped(p, "hap", 1))]
    rp, ro, cp, co = call(
        functools.partial(weights_finish, sites),
        [((width, 3 * width), F32), ((width, width), F32)] * 2,
        idx, core, *full, scalars=2,
        scratch=[pltpu.VMEM((3 * width, width), F32)],
    )
    shape = (rows, 1, width)
    return (out.reshape(shape), grad.reshape(shape), rp, ro, cp, co)


def solution(mesh):
    data = P("site", "hap", None)
    return jax.shard_map(
        on_device,
        mesh=mesh,
        in_specs=(data, P(), P(), P(), P(), P(), P(), P(), data),
        out_specs=(data, data, P(), P(), P(), P()),
        check_vma=False,
    )
```

```python
import functools

import jax
import jax.numpy as jnp
from jax import lax
from jax.experimental import pallas as pl
from jax.experimental.pallas import tpu as pltpu
from jax.sharding import PartitionSpec as P

HEAD_DIM = 32
EPSILON = 1e-05
LOG2E = 1.4426950408889634
SCALE = HEAD_DIM ** (-0.5)
F32 = jnp.float32
BF16 = jnp.bfloat16
VMEM = pl.BlockSpec(memory_space=pltpu.VMEM)
HBM = pl.BlockSpec(memory_space=pltpu.HBM)
SMEM = pl.BlockSpec(memory_space=pltpu.SMEM)
PARAMS = pltpu.CompilerParams(vmem_limit_bytes=24 << 20)


def mm(a, b):
    return lax.dot_general(a, b, (((1,), (0,)), ((), ())), preferred_element_type=F32)


def mm_nt(a, b):
    return lax.dot_general(a, b, (((1,), (1,)), ((), ())), preferred_element_type=F32)


def mm_tn(a, b):
    return lax.dot_general(a, b, (((0,), (0,)), ((), ())), preferred_element_type=F32)


def norm_parts(x):
    centred = x - jnp.mean(x, axis=-1, keepdims=True)
    rstd = lax.rsqrt(jnp.mean(centred * centred, axis=-1, keepdims=True) + EPSILON)
    return centred * rstd, rstd


def norm_back(xhat, rstd, gain, grad):
    scaled = grad * gain
    first = jnp.mean(scaled, axis=-1, keepdims=True)
    second = jnp.mean(scaled * xhat, axis=-1, keepdims=True)
    return rstd * (scaled - first - xhat * second)


def head_lanes(width, head):
    return lax.broadcasted_iota(jnp.int32, (1, width), 1) // HEAD_DIM == head


def only_head(values, head):
    return jnp.where(head_lanes(values.shape[1], head), values, jnp.zeros_like(values))


def flat_rows(values, dtype=BF16):
    wide = values.astype(F32)
    return wide.reshape(wide.shape[0] * wide.shape[1], wide.shape[2]).astype(dtype)


def lane_factor(rows, width):
    factor = 128 // width
    return factor if (rows // factor) % 8 == 0 else 1


def pack_block(values, outer):
    rows, width = values.shape[0] // outer, values.shape[1]
    factor = lane_factor(rows, width)
    split = values.reshape(outer, factor, rows // factor, width)
    return jnp.concatenate([split[:, j] for j in range(factor)], axis=2).astype(BF16)


def unpack_block(values, width):
    wide = values.astype(F32)
    factor = wide.shape[2] // width
    split = [wide[:, None, :, j * width : (j + 1) * width] for j in range(factor)]
    joined = jnp.concatenate(split, axis=1)
    return joined.reshape(-1, width).astype(BF16)


def call(body, outs, *operands, scalars=0, scratch=(), us=0, far=0):
    cost = pl.CostEstimate(flops=us * 10**9 + 1, bytes_accessed=us * 3_600_000 + 1, transcendentals=0)
    return pl.pallas_call(
        body,
        out_shape=[jax.ShapeDtypeStruct(s, d) for s, d in outs[: len(outs) - far]]
        + [pltpu.HBM(s, d) for s, d in outs[len(outs) - far :]],
        in_specs=[SMEM] * scalars + [VMEM] * (len(operands) - scalars),
        out_specs=[VMEM] * (len(outs) - far) + [HBM] * far,
        scratch_shapes=list(scratch),
        compiler_params=PARAMS,
        cost_estimate=cost,
    )(*operands)


def head_stack(values):
    heads = values.shape[1] // HEAD_DIM
    return jnp.concatenate([only_head(values, h) for h in range(heads)], axis=0)


def head_blocks(values):
    heads = values.shape[0] // HEAD_DIM
    wide = values.shape[1] // heads
    return jnp.concatenate(
        [
            values[h * HEAD_DIM : (h + 1) * HEAD_DIM, h * wide : (h + 1) * wide]
            for h in range(heads)
        ],
        axis=0,
    )


def exp_parts(parts):
    high = functools.reduce(jnp.maximum, [jnp.max(part, axis=0, keepdims=True) for part in parts])
    parts = [jnp.exp2(part - high) for part in parts]
    total = sum(jnp.sum(part, axis=0, keepdims=True) for part in parts)
    return parts, 1.0 / total


def row_forward(sites, haps, idx, link, *refs):
    pieces = refs[:1] + refs[sites - 1 : 0 : -1]
    cot, gain, w_t, row_out, x_out, n_out = refs[sites:]
    me = idx[0]
    rows, width = cot.shape
    for k in range(sites):
        xhat, _ = norm_parts(pieces[k][...].astype(F32))
        n_out[k * rows : (k + 1) * rows, :] = (xhat * gain[:1, :]).astype(BF16)
    normed = n_out[...]
    q = mm_nt(normed[:rows], w_t[:width, :]).astype(BF16)
    key = mm_nt(normed, w_t[width : 2 * width, :]).astype(BF16)
    v_t = mm_nt(w_t[2 * width :, :], normed).astype(BF16)
    scores = mm_nt(key, head_stack(q)) * (SCALE * LOG2E)
    bias = [jnp.where(link[me, me ^ a] > 0, 0.0, -jnp.inf) for a in range(sites)]
    parts = [scores[a * rows : (a + 1) * rows] + bias[a] for a in range(sites)]
    parts, inverse = exp_parts(parts)
    exps = jnp.concatenate([part.astype(BF16) for part in parts], axis=0)
    att_t = head_blocks(mm(v_t, exps) * inverse)
    att = jnp.transpose(att_t).astype(BF16)
    hid = pieces[0][...].astype(F32) + mm(att, row_out[...])
    joined = jnp.concatenate([hid, cot[...].astype(F32), att.astype(F32)], axis=1)
    x_out[...] = joined.reshape(haps, rows // haps, 3 * width).astype(BF16)


def row_probs(sites, idx, link, normed_ref, w_t, p_out, q_out, v_out, kt_out):
    me = idx[0]
    normed = normed_ref[...]
    total, width = q_out.shape
    full = normed.shape[1]
    rows = total // sites

    def weights(part):
        return w_t[pl.ds(pl.multiple_of(part * full + me * width, width), width), :]

    q = mm_nt(normed, weights(0)).astype(BF16)
    key = mm_nt(normed, weights(1)).astype(BF16)
    q_out[...] = q
    v_out[...] = mm_nt(normed, weights(2)).astype(BF16)
    kt_out[...] = mm_nt(weights(1), normed).astype(BF16)
    scores = mm_nt(key, head_stack(q)) * (SCALE * LOG2E)
    parts = []
    for a in range(sites):
        bias = [
            jnp.full((1, rows), jnp.where(link[me ^ b, me ^ a] > 0, 0.0, -jnp.inf), F32)
            for b in range(sites)
        ]
        bias = jnp.concatenate(bias * (width // HEAD_DIM), axis=1)
        parts.append(scores[a * rows : (a + 1) * rows] + bias)
    parts, inverse = exp_parts(parts)
    for a in range(sites):
        p_out[a * rows : (a + 1) * rows, :] = (parts[a] * inverse).astype(BF16)


def column_step(sites, haps, hap, x_in, row_out, gain, col_proj, kv_t_w, col_out, *refs):
    ga_out, send, keep, og_out, og, w_all, sems = refs
    core = hap[0] % 2
    half = row_out.shape[0] // 2
    mine = pl.ds(pl.multiple_of(core * half, half), half)
    other = pl.ds(pl.multiple_of((1 - core) * half, half), half)

    def save(j, cols):
        return pltpu.make_async_copy(w_all.at[mine, cols], keep.at[:, cols], sems.at[j])

    def save_outputs(j, cols):
        return pltpu.make_async_copy(og.at[:, :, cols], og_out.at[:, :, cols], sems.at[j])

    width = row_out.shape[0]
    group = width // sites
    x_all = flat_rows(x_in[...], F32)
    rows = x_all.shape[0]
    per = rows // haps
    hid = x_all[:, :width]
    cot_f = x_all[:, width : 2 * width]
    cot = cot_f.astype(BF16)
    row_att = x_all[:, 2 * width :].astype(BF16)
    grad_att = mm_nt(cot, col_out[...]).astype(BF16)
    xhat, rstd = norm_parts(hid)
    normed = (xhat * gain[1:2, :]).astype(BF16)
    packed = mm(normed, col_proj[...]).astype(BF16)
    q = packed[:, :width]
    key = packed[:, width : 2 * width]
    val = packed[:, 2 * width :]
    kv_t = mm_nt(kv_t_w[...], normed).astype(BF16)
    q_st = head_stack(q)
    g_st = head_stack(grad_att)
    scores = mm_nt(key, q_st) * (SCALE * LOG2E)
    dprob = mm_nt(val, g_st)
    same = (
        lax.broadcasted_iota(jnp.int32, scores.shape, 0) % per
        == lax.broadcasted_iota(jnp.int32, scores.shape, 1) % per
    )
    scores = jnp.where(same, scores, -jnp.inf)
    exps = jnp.exp2(scores - jnp.max(scores, axis=0, keepdims=True))
    inverse = 1.0 / jnp.sum(exps, axis=0, keepdims=True)
    att_t = head_blocks(mm(kv_t[width:, :], exps.astype(BF16)) * inverse)
    probs = exps * inverse
    delta = jnp.sum(probs * dprob, axis=0, keepdims=True)
    dscore = (probs * (dprob - delta)).astype(BF16)
    dv = mm(probs.astype(BF16), g_st)
    dk = mm(dscore, q_st)
    dq = jnp.transpose(head_blocks(mm(kv_t[:width, :], dscore)))
    w_all[:, 3 * width : 4 * width] = mm(att_t.astype(BF16), cot).astype(BF16)
    att = jnp.transpose(att_t).astype(BF16)
    out = hid + mm(att, col_out[...])
    og[:, :, :width] = out.reshape(haps, per, width).astype(BF16)
    third = save_outputs(2, slice(0, width))
    third.start()
    packed_grad = jnp.concatenate([dq * SCALE, dk * SCALE, dv], axis=1).astype(BF16)
    w_all[:, : 3 * width] = mm_tn(normed, packed_grad).astype(BF16)
    first = save(0, slice(0, 4 * width))
    first.start()
    grad_normed = mm_nt(packed_grad, col_proj[...])
    grad_hidden = (cot_f + norm_back(xhat, rstd, gain[1:2, :], grad_normed)).astype(BF16)
    og[:, :, width:] = grad_hidden.astype(F32).reshape(haps, per, width).astype(BF16)
    fourth = save_outputs(3, slice(width, 2 * width))
    fourth.start()
    w_all[:, 4 * width :] = mm_tn(row_att, grad_hidden).astype(BF16)
    second = save(1, slice(4 * width, 5 * width))
    second.start()
    for i in range(sites):
        g_i = mm_nt(grad_hidden, row_out[i * group : (i + 1) * group, :])
        ga_out[i * haps : (i + 1) * haps] = pack_block(g_i, haps)
    send[...] = w_all[other, :]
    for copy in (first, second, third, fourth):
        copy.wait()


def split_outputs(hap, og, keep, send):
    for m in range(keep.shape[0]):
        keep[m] = og[hap[0] ^ (2 * m)]
        send[m] = og[hap[0] ^ (2 * m + 1)]


def column_split(sites, idx, keep, *refs):
    outs, both, gots = refs[-sites - 1 : -1], refs[-1], refs[: -sites - 1]
    got = jnp.concatenate([g[...].astype(F32) for g in gots], axis=0)
    both[...] = (keep[...].astype(F32) + got).astype(BF16)
    part = keep.shape[0] // sites
    for k in range(sites):
        outs[k][...] = both[pl.ds(pl.multiple_of((idx[0] ^ k) * part, part), part), :]


def row_backward(sites, haps, idx, core, g_in, prob, q, val, key_t, normed, *refs):
    gp_outs = refs[:sites]
    keep, send, g_all, w_out = refs[sites:]
    me = idx[0]
    total, width = q.shape
    rows = total // sites
    for b in range(sites):
        g_all[b * rows : (b + 1) * rows, :] = unpack_block(
            g_in[pl.ds((me ^ b) * haps, haps)], width
        )
    g_st = head_stack(g_all[...])
    p_all = prob[...].astype(F32)
    dprob = mm_nt(val[...], g_st)
    delta = jnp.sum(p_all * dprob, axis=0, keepdims=True)
    dscore = (p_all * (dprob - delta)).astype(BF16)
    dv = mm(prob[...], g_st)
    dk = mm(dscore, head_stack(q[...]))
    dq_t = head_blocks(mm(key_t[...], dscore)) * SCALE
    dk16 = (dk * SCALE).astype(BF16)
    dv16 = dv.astype(BF16)
    w_out[:width, :] = mm(dq_t.astype(BF16), normed[...]).astype(BF16)
    w_out[width : 2 * width, :] = mm_tn(dk16, normed[...]).astype(BF16)
    w_out[2 * width :, :] = mm_tn(dv16, normed[...]).astype(BF16)
    half = 3 * width // 2
    keep[...] = w_out[pl.ds(pl.multiple_of(core[0] * half, half), half), :]
    send[...] = w_out[pl.ds(pl.multiple_of((1 - core[0]) * half, half), half), :]
    dq = jnp.transpose(dq_t).astype(BF16)
    joined = jnp.concatenate([dq, dk16, dv16], axis=1)
    for b in range(sites):
        gp_outs[b][...] = joined[b * rows : (b + 1) * rows]


def row_finish(sites, haps, idx, hap, feats, gain, w_t, gp, *refs):
    gps, parts = refs[: sites - 1], refs[sites - 1 : sites - 1 + haps // 2]
    out_ref, gf_ref, og = refs[sites - 1 + haps // 2 :]
    me = idx[0]
    rows, width = feats.shape
    group = width // sites
    per = rows // haps
    for m in range(haps // 2):
        base = parts[m].shape[0] - 4 * per
        for j in range(2):
            for side in range(2):
                start = base + (2 * j + side) * per
                og[side, hap[0] ^ (2 * m + j)] = parts[m][start : start + per, :].astype(F32)
    grads = [gp[...]] + [g[g.shape[0] - rows :, : 3 * group] for g in gps]
    grad_normed = 0.0
    for k in range(sites):
        place = [pl.multiple_of(p * width + (me ^ k) * group, group) for p in range(3)]
        weights = jnp.concatenate([w_t[pl.ds(p, group), :] for p in place], axis=0)
        grad_normed = grad_normed + mm(grads[k], weights)
    xhat, rstd = norm_parts(feats[...].astype(F32))
    grad = og[1].reshape(rows, width) + norm_back(xhat, rstd, gain[:1, :], grad_normed)
    out_ref[...] = og[0].reshape(rows, width).astype(BF16)
    gf_ref[...] = grad.astype(BF16)


def outputs_pair(keep, got, m, width):
    both = [keep[m].astype(F32), got[m].astype(F32)]
    both = [x[:, j * width : (j + 1) * width] for x in both for j in range(2)]
    return jnp.concatenate(both, axis=0).astype(BF16)


def weights_join(sites, row_keep, row_got, og_keep, og_got, *refs):
    cols, (near, own, *far) = refs[:sites], refs[sites:]
    half, width = row_keep.shape
    depth = half + 5 * cols[0].shape[0]
    total = sum(c[...].astype(F32) for c in cols)
    tiles = [total[:, t * width : (t + 1) * width] for t in range(5)]
    rows = row_keep[...].astype(F32) + row_got[...].astype(F32)
    near[:depth, :] = jnp.concatenate([rows] + tiles, axis=0).astype(BF16)
    near[depth:, :] = outputs_pair(og_keep, og_got, 1, width)
    own[...] = outputs_pair(og_keep, og_got, 0, width)
    for j, out in enumerate(far):
        out[...] = outputs_pair(og_keep, og_got, j + 2, width)


def weights_add(mine, got, out):
    depth = out.shape[0]
    out[...] = (mine[:depth, :].astype(F32) + got[:depth, :].astype(F32)).astype(BF16)


def weights_finish(sites, idx, core, *refs):
    pieces = refs[: 2 * sites]
    rp, ro, cp, co, rows_t = refs[2 * sites :]
    width = ro.shape[0]
    group = width // sites
    unit = group // 2
    part = width // 2 // sites
    for j in range(2 * sites):
        k = j // 2
        cc = core[0] ^ (j % 2)
        g = idx[0] ^ k
        piece = pieces[j][...].astype(F32)
        for u in range(3):
            place = 3 * cc + u
            dest = (place // 2) * width + g * group + (place % 2) * unit
            rows_t[pl.ds(pl.multiple_of(dest, unit), unit), :] = piece[u * unit : (u + 1) * unit]
        here = pl.ds(pl.multiple_of(cc * (width // 2) + g * part, part), part)
        tiles = [piece[3 * unit + t * part : 3 * unit + (t + 1) * part] for t in range(5)]
        for t in range(3):
            cp[here, t * width : (t + 1) * width] = tiles[t]
        co[here, :] = tiles[3]
        ro[here, :] = tiles[4]
    rp[...] = jnp.transpose(rows_t[...])


def exchange(value, axis):
    return lax.all_to_all(value, axis, 0, 0, tiled=True)


def swapped(value, axis, by):
    length = lax.axis_size(axis)
    return lax.ppermute(value, axis, [(i, i ^ by) for i in range(length)])


def on_device(
    features,
    link_pattern,
    row_gain,
    row_proj,
    row_out,
    column_norm_gain,
    col_proj,
    col_out,
    cotangent,
):
    rows, _, width = features.shape
    sites, haps = lax.axis_size("site"), lax.axis_size("hap")
    count = sites * haps
    per = rows // haps
    group = width // sites
    heads = group // HEAD_DIM
    total = rows * sites
    both_axes = ("site", "hap")
    me = lax.axis_index("site")
    idx = me.reshape(1).astype(jnp.int32)
    hap = lax.axis_index("hap").reshape(1).astype(jnp.int32)
    core = hap % 2
    factor = lane_factor(per, group)
    block = ((count, per // factor, group * factor), BF16)
    feats = features.reshape(rows, width)
    cot = cotangent.reshape(rows, width)

    pieces = [feats] + [swapped(feats, "site", k) for k in range(1, sites)]
    link_pattern = jnp.where(link_pattern > 0, 1, 0)
    gains = jnp.stack([row_gain, column_norm_gain])
    w_t = jnp.transpose(row_proj)
    kv_t_w = jnp.transpose(col_proj[:, width:])

    x_out, normed = call(
        functools.partial(row_forward, sites, haps),
        [((haps, per, 3 * width), BF16), ((total, width), BF16)],
        idx, link_pattern, pieces[0], *pieces[:0:-1], cot, gains, w_t, row_out, scalars=2,
    )
    x_in = exchange(x_out, "hap")
    prob, q, val, key_t = call(
        functools.partial(row_probs, sites),
        [
            ((total, heads * total), BF16),
            ((total, group), BF16),
            ((total, group), BF16),
            ((group, total), BF16),
        ],
        idx, link_pattern, normed, w_t, scalars=2, us=20,
    )
    x_in, _ = lax.optimization_barrier((x_in, prob))
    half = width // 2
    ga, col_send, col_keep, og = call(
        functools.partial(column_step, sites, haps),
        [
            block,
            ((half, 5 * width), BF16),
            ((half, 5 * width), BF16),
            ((haps, per, 2 * width), BF16),
        ],
        hap, x_in, row_out, gains, col_proj, kv_t_w, col_out, scalars=1, far=2,
        scratch=[
            pltpu.VMEM((haps, per, 2 * width), BF16),
            pltpu.VMEM((width, 5 * width), BF16),
            pltpu.SemaphoreType.DMA((4,)),
        ],
    )
    g_in = exchange(ga, both_axes)
    col_got = [swapped(col_send, "hap", 1)]
    cols = call(
        functools.partial(column_split, sites),
        [((half // sites, 5 * width), BF16)] * sites,
        idx, col_keep, *col_got, scalars=1, us=0,
        scratch=[pltpu.VMEM((half, 5 * width), BF16)],
    )
    og_keep, og_send = call(
        split_outputs, [((haps // 2, per, 2 * width), BF16)] * 2, hap, og, scalars=1
    )
    og_got = swapped(og_send, "hap", 1)
    g_in, _ = lax.optimization_barrier((g_in, (cols, og_got)))
    cols = [cols[0]] + [swapped(cols[k], "site", k) for k in range(1, sites)]
    *gps, row_keep, row_send = call(
        functools.partial(row_backward, sites, haps),
        [((rows, 3 * group), BF16)] * sites + [((3 * group // 2, width), BF16)] * 2,
        idx, core, g_in, prob, q, val, key_t, normed, scalars=2,
        scratch=[
            pltpu.VMEM((total, group), BF16),
            pltpu.VMEM((3 * group, width), BF16),
        ],
    )
    row_got = swapped(row_send, "hap", 1)
    depth = 3 * group // 2 + 5 * half // sites
    near, own, *far = call(
        functools.partial(weights_join, sites),
        [((depth + 4 * per, width), BF16)] + [((4 * per, width), BF16)] * (haps // 2 - 1),
        row_keep, row_got, og_keep, og_got, *cols,
    )
    near_got = swapped(near, "hap", 2)
    far = [swapped(x, "hap", 2 * (j + 2)) for j, x in enumerate(far)]
    near_got, far = lax.optimization_barrier((near_got, far))
    parts = [own, near_got] + list(far)
    left, right, step = near, near_got, 2
    while 2 * step < haps:
        (left,) = call(weights_add, [((depth, width), BF16)], left, right)
        right, step = swapped(left, "hap", 2 * step), 2 * step
    gps, _ = lax.optimization_barrier((gps, left))
    gps = [gps[0]] + [swapped(gps[k], "site", k) for k in range(1, sites)]
    right, gps = lax.optimization_barrier((right, gps))
    (mine,) = call(weights_add, [((depth, width), BF16)], left, right)
    got = [swapped(mine, "site", k) for k in range(1, sites)]
    mine_swapped = swapped(mine, "hap", 1)
    out, grad = call(
        functools.partial(row_finish, sites, haps),
        [((rows, width), BF16)] * 2,
        idx, hap, feats, gains, w_t, *gps, *parts, scalars=2,
        scratch=[pltpu.VMEM((2, haps, per, width), F32)],
    )
    got, mine_swapped, out = lax.optimization_barrier((got, mine_swapped, out))
    full = [mine, mine_swapped] + [x for p in got for x in (p, swapped(p, "hap", 1))]
    rp, ro, cp, co = call(
        functools.partial(weights_finish, sites),
        [((width, 3 * width), F32), ((width, width), F32)] * 2,
        idx, core, *full, scalars=2,
        scratch=[pltpu.VMEM((3 * width, width), F32)],
    )
    shape = (rows, 1, width)
    return (out.reshape(shape), grad.reshape(shape), rp, ro, cp, co)


def solution(mesh):
    data = P("site", "hap", None)
    return jax.shard_map(
        on_device,
        mesh=mesh,
        in_specs=(data, P(), P(), P(), P(), P(), P(), P(), data),
        out_specs=(data, data, P(), P(), P(), P()),
        check_vma=False,
    )
```

```python
import functools

import jax
import jax.numpy as jnp
from jax import lax
from jax.experimental import pallas as pl
from jax.experimental.pallas import tpu as pltpu
from jax.sharding import PartitionSpec as P

HEAD_DIM = 32
EPSILON = 1e-05
LOG2E = 1.4426950408889634
SCALE = HEAD_DIM ** (-0.5)
F32 = jnp.float32
BF16 = jnp.bfloat16
VMEM = pl.BlockSpec(memory_space=pltpu.VMEM)
HBM = pl.BlockSpec(memory_space=pltpu.HBM)
SMEM = pl.BlockSpec(memory_space=pltpu.SMEM)
PARAMS = pltpu.CompilerParams(vmem_limit_bytes=24 << 20)


def mm(a, b):
    return lax.dot_general(a, b, (((1,), (0,)), ((), ())), preferred_element_type=F32)


def mm_nt(a, b):
    return lax.dot_general(a, b, (((1,), (1,)), ((), ())), preferred_element_type=F32)


def mm_tn(a, b):
    return lax.dot_general(a, b, (((0,), (0,)), ((), ())), preferred_element_type=F32)


def norm_parts(x):
    centred = x - jnp.mean(x, axis=-1, keepdims=True)
    rstd = lax.rsqrt(jnp.mean(centred * centred, axis=-1, keepdims=True) + EPSILON)
    return centred * rstd, rstd


def norm_back(xhat, rstd, gain, grad):
    scaled = grad * gain
    first = jnp.mean(scaled, axis=-1, keepdims=True)
    second = jnp.mean(scaled * xhat, axis=-1, keepdims=True)
    return rstd * (scaled - first - xhat * second)


def head_lanes(width, head):
    return lax.broadcasted_iota(jnp.int32, (1, width), 1) // HEAD_DIM == head


def only_head(values, head):
    return jnp.where(head_lanes(values.shape[1], head), values, jnp.zeros_like(values))


def flat_rows(values, dtype=BF16):
    wide = values.astype(F32)
    return wide.reshape(wide.shape[0] * wide.shape[1], wide.shape[2]).astype(dtype)


def lane_factor(rows, width):
    factor = 128 // width
    return factor if (rows // factor) % 8 == 0 else 1


def pack_block(values, outer):
    rows, width = values.shape[0] // outer, values.shape[1]
    factor = lane_factor(rows, width)
    split = values.reshape(outer, factor, rows // factor, width)
    return jnp.concatenate([split[:, j] for j in range(factor)], axis=2).astype(BF16)


def unpack_block(values, width):
    wide = values.astype(F32)
    factor = wide.shape[2] // width
    split = [wide[:, None, :, j * width : (j + 1) * width] for j in range(factor)]
    joined = jnp.concatenate(split, axis=1)
    return joined.reshape(-1, width).astype(BF16)


def call(body, outs, *operands, scalars=0, scratch=(), us=0, far=0):
    cost = pl.CostEstimate(flops=us * 10**9 + 1, bytes_accessed=us * 3_600_000 + 1, transcendentals=0)
    return pl.pallas_call(
        body,
        out_shape=[jax.ShapeDtypeStruct(s, d) for s, d in outs[: len(outs) - far]]
        + [pltpu.HBM(s, d) for s, d in outs[len(outs) - far :]],
        in_specs=[SMEM] * scalars + [VMEM] * (len(operands) - scalars),
        out_specs=[VMEM] * (len(outs) - far) + [HBM] * far,
        scratch_shapes=list(scratch),
        compiler_params=PARAMS,
        cost_estimate=cost,
    )(*operands)


def head_stack(values):
    heads = values.shape[1] // HEAD_DIM
    return jnp.concatenate([only_head(values, h) for h in range(heads)], axis=0)


def head_blocks(values):
    heads = values.shape[0] // HEAD_DIM
    wide = values.shape[1] // heads
    return jnp.concatenate(
        [
            values[h * HEAD_DIM : (h + 1) * HEAD_DIM, h * wide : (h + 1) * wide]
            for h in range(heads)
        ],
        axis=0,
    )


def exp_parts(parts):
    high = functools.reduce(jnp.maximum, [jnp.max(part, axis=0, keepdims=True) for part in parts])
    parts = [jnp.exp2(part - high) for part in parts]
    total = sum(jnp.sum(part, axis=0, keepdims=True) for part in parts)
    return parts, 1.0 / total


def row_forward(sites, haps, idx, link, *refs):
    pieces = refs[:1] + refs[sites - 1 : 0 : -1]
    cot, gain, w_t, row_out, x_out, n_out = refs[sites:]
    me = idx[0]
    rows, width = cot.shape
    for k in range(sites):
        xhat, _ = norm_parts(pieces[k][...].astype(F32))
        n_out[k * rows : (k + 1) * rows, :] = (xhat * gain[:1, :]).astype(BF16)
    normed = n_out[...]
    q = mm_nt(normed[:rows], w_t[:width, :]).astype(BF16)
    key = mm_nt(normed, w_t[width : 2 * width, :]).astype(BF16)
    v_t = mm_nt(w_t[2 * width :, :], normed).astype(BF16)
    scores = mm_nt(key, head_stack(q)) * (SCALE * LOG2E)
    bias = [jnp.where(link[me, me ^ a] > 0, 0.0, -jnp.inf) for a in range(sites)]
    parts = [scores[a * rows : (a + 1) * rows] + bias[a] for a in range(sites)]
    parts, inverse = exp_parts(parts)
    exps = jnp.concatenate([part.astype(BF16) for part in parts], axis=0)
    att_t = head_blocks(mm(v_t, exps) * inverse)
    att = jnp.transpose(att_t).astype(BF16)
    hid = pieces[0][...].astype(F32) + mm(att, row_out[...])
    joined = jnp.concatenate([hid, cot[...].astype(F32), att.astype(F32)], axis=1)
    x_out[...] = joined.reshape(haps, rows // haps, 3 * width).astype(BF16)


def row_probs(sites, idx, link, normed_ref, w_t, p_out, q_out, v_out, kt_out):
    me = idx[0]
    normed = normed_ref[...]
    total, width = q_out.shape
    full = normed.shape[1]
    rows = total // sites

    def weights(part):
        return w_t[pl.ds(pl.multiple_of(part * full + me * width, width), width), :]

    q = mm_nt(normed, weights(0)).astype(BF16)
    key = mm_nt(normed, weights(1)).astype(BF16)
    q_out[...] = q
    v_out[...] = mm_nt(normed, weights(2)).astype(BF16)
    kt_out[...] = mm_nt(weights(1), normed).astype(BF16)
    scores = mm_nt(key, head_stack(q)) * (SCALE * LOG2E)
    parts = []
    for a in range(sites):
        bias = [
            jnp.full((1, rows), jnp.where(link[me ^ b, me ^ a] > 0, 0.0, -jnp.inf), F32)
            for b in range(sites)
        ]
        bias = jnp.concatenate(bias * (width // HEAD_DIM), axis=1)
        parts.append(scores[a * rows : (a + 1) * rows] + bias)
    parts, inverse = exp_parts(parts)
    for a in range(sites):
        p_out[a * rows : (a + 1) * rows, :] = (parts[a] * inverse).astype(BF16)


def column_step(sites, haps, hap, x_in, row_out, gain, col_proj, kv_t_w, col_out, *refs):
    ga_out, send, keep, og_out, og, w_all, sems = refs
    core = hap[0] % 2
    half = row_out.shape[0] // 2
    mine = pl.ds(pl.multiple_of(core * half, half), half)
    other = pl.ds(pl.multiple_of((1 - core) * half, half), half)

    def save(j, cols):
        return pltpu.make_async_copy(w_all.at[mine, cols], keep.at[:, cols], sems.at[j])

    def save_outputs(j, cols):
        return pltpu.make_async_copy(og.at[:, :, cols], og_out.at[:, :, cols], sems.at[j])

    width = row_out.shape[0]
    group = width // sites
    x_all = flat_rows(x_in[...], F32)
    rows = x_all.shape[0]
    per = rows // haps
    hid = x_all[:, :width]
    cot_f = x_all[:, width : 2 * width]
    cot = cot_f.astype(BF16)
    row_att = x_all[:, 2 * width :].astype(BF16)
    grad_att = mm_nt(cot, col_out[...]).astype(BF16)
    xhat, rstd = norm_parts(hid)
    normed = (xhat * gain[1:2, :]).astype(BF16)
    packed = mm(normed, col_proj[...]).astype(BF16)
    q = packed[:, :width]
    key = packed[:, width : 2 * width]
    val = packed[:, 2 * width :]
    kv_t = mm_nt(kv_t_w[...], normed).astype(BF16)
    q_st = head_stack(q)
    g_st = head_stack(grad_att)
    scores = mm_nt(key, q_st) * (SCALE * LOG2E)
    dprob = mm_nt(val, g_st)
    same = (
        lax.broadcasted_iota(jnp.int32, scores.shape, 0) % per
        == lax.broadcasted_iota(jnp.int32, scores.shape, 1) % per
    )
    scores = jnp.where(same, scores, -jnp.inf)
    exps = jnp.exp2(scores - jnp.max(scores, axis=0, keepdims=True))
    inverse = 1.0 / jnp.sum(exps, axis=0, keepdims=True)
    att_t = head_blocks(mm(kv_t[width:, :], exps.astype(BF16)) * inverse)
    probs = exps * inverse
    delta = jnp.sum(probs * dprob, axis=0, keepdims=True)
    dscore = (probs * (dprob - delta)).astype(BF16)
    dv = mm(probs.astype(BF16), g_st)
    dk = mm(dscore, q_st)
    dq = jnp.transpose(head_blocks(mm(kv_t[:width, :], dscore)))
    w_all[:, 3 * width : 4 * width] = mm(att_t.astype(BF16), cot).astype(BF16)
    att = jnp.transpose(att_t).astype(BF16)
    out = hid + mm(att, col_out[...])
    og[:, :, :width] = out.reshape(haps, per, width).astype(BF16)
    third = save_outputs(2, slice(0, width))
    third.start()
    packed_grad = jnp.concatenate([dq * SCALE, dk * SCALE, dv], axis=1).astype(BF16)
    w_all[:, : 3 * width] = mm_tn(normed, packed_grad).astype(BF16)
    first = save(0, slice(0, 4 * width))
    first.start()
    grad_normed = mm_nt(packed_grad, col_proj[...])
    grad_hidden = (cot_f + norm_back(xhat, rstd, gain[1:2, :], grad_normed)).astype(BF16)
    og[:, :, width:] = grad_hidden.astype(F32).reshape(haps, per, width).astype(BF16)
    fourth = save_outputs(3, slice(width, 2 * width))
    fourth.start()
    w_all[:, 4 * width :] = mm_tn(row_att, grad_hidden).astype(BF16)
    second = save(1, slice(4 * width, 5 * width))
    second.start()
    for i in range(sites):
        g_i = mm_nt(grad_hidden, row_out[i * group : (i + 1) * group, :])
        ga_out[i * haps : (i + 1) * haps] = pack_block(g_i, haps)
    send[...] = w_all[other, :]
    for copy in (first, second, third, fourth):
        copy.wait()


def split_outputs(hap, og, keep, send):
    for m in range(keep.shape[0]):
        keep[m] = og[hap[0] ^ (2 * m)]
        send[m] = og[hap[0] ^ (2 * m + 1)]


def column_split(sites, idx, keep, *refs):
    outs, both, gots = refs[-sites - 1 : -1], refs[-1], refs[: -sites - 1]
    got = jnp.concatenate([g[...].astype(F32) for g in gots], axis=0)
    both[...] = (keep[...].astype(F32) + got).astype(BF16)
    part = keep.shape[0] // sites
    for k in range(sites):
        outs[k][...] = both[pl.ds(pl.multiple_of((idx[0] ^ k) * part, part), part), :]


def row_backward(sites, haps, idx, core, g_in, prob, q, val, key_t, normed, *refs):
    gp_outs = refs[:sites]
    keep, send, g_all, w_out = refs[sites:]
    me = idx[0]
    total, width = q.shape
    rows = total // sites
    for b in range(sites):
        g_all[b * rows : (b + 1) * rows, :] = unpack_block(
            g_in[pl.ds((me ^ b) * haps, haps)], width
        )
    g_st = head_stack(g_all[...])
    p_all = prob[...].astype(F32)
    dprob = mm_nt(val[...], g_st)
    delta = jnp.sum(p_all * dprob, axis=0, keepdims=True)
    dscore = (p_all * (dprob - delta)).astype(BF16)
    dv = mm(prob[...], g_st)
    dk = mm(dscore, head_stack(q[...]))
    dq_t = head_blocks(mm(key_t[...], dscore)) * SCALE
    dk16 = (dk * SCALE).astype(BF16)
    dv16 = dv.astype(BF16)
    w_out[:width, :] = mm(dq_t.astype(BF16), normed[...]).astype(BF16)
    w_out[width : 2 * width, :] = mm_tn(dk16, normed[...]).astype(BF16)
    w_out[2 * width :, :] = mm_tn(dv16, normed[...]).astype(BF16)
    half = 3 * width // 2
    keep[...] = w_out[pl.ds(pl.multiple_of(core[0] * half, half), half), :]
    send[...] = w_out[pl.ds(pl.multiple_of((1 - core[0]) * half, half), half), :]
    dq = jnp.transpose(dq_t).astype(BF16)
    joined = jnp.concatenate([dq, dk16, dv16], axis=1)
    for b in range(sites):
        gp_outs[b][...] = joined[b * rows : (b + 1) * rows]


def row_finish(sites, haps, idx, hap, feats, gain, w_t, gp, *refs):
    gps, parts = refs[: sites - 1], refs[sites - 1 : sites - 1 + haps // 2]
    out_ref, gf_ref, og = refs[sites - 1 + haps // 2 :]
    me = idx[0]
    rows, width = feats.shape
    group = width // sites
    per = rows // haps
    for m in range(haps // 2):
        base = parts[m].shape[0] - 4 * per
        for j in range(2):
            for side in range(2):
                start = base + (2 * j + side) * per
                og[side, hap[0] ^ (2 * m + j)] = parts[m][start : start + per, :].astype(F32)
    grads = [gp[...]] + [g[g.shape[0] - rows :, : 3 * group] for g in gps]
    grad_normed = 0.0
    for k in range(sites):
        place = [pl.multiple_of(p * width + (me ^ k) * group, group) for p in range(3)]
        weights = jnp.concatenate([w_t[pl.ds(p, group), :] for p in place], axis=0)
        grad_normed = grad_normed + mm(grads[k], weights)
    xhat, rstd = norm_parts(feats[...].astype(F32))
    grad = og[1].reshape(rows, width) + norm_back(xhat, rstd, gain[:1, :], grad_normed)
    out_ref[...] = og[0].reshape(rows, width).astype(BF16)
    gf_ref[...] = grad.astype(BF16)


def outputs_pair(keep, got, m, width):
    both = [keep[m].astype(F32), got[m].astype(F32)]
    both = [x[:, j * width : (j + 1) * width] for x in both for j in range(2)]
    return jnp.concatenate(both, axis=0).astype(BF16)


def weights_join(sites, row_keep, row_got, og_keep, og_got, *refs):
    cols, (near, own, *far) = refs[:sites], refs[sites:]
    half, width = row_keep.shape
    depth = half + 5 * cols[0].shape[0]
    total = sum(c[...].astype(F32) for c in cols)
    tiles = [total[:, t * width : (t + 1) * width] for t in range(5)]
    rows = row_keep[...].astype(F32) + row_got[...].astype(F32)
    near[:depth, :] = jnp.concatenate([rows] + tiles, axis=0).astype(BF16)
    near[depth:, :] = outputs_pair(og_keep, og_got, 1, width)
    own[...] = outputs_pair(og_keep, og_got, 0, width)
    for j, out in enumerate(far):
        out[...] = outputs_pair(og_keep, og_got, j + 2, width)


def weights_add(mine, got, out):
    depth = out.shape[0]
    out[...] = (mine[:depth, :].astype(F32) + got[:depth, :].astype(F32)).astype(BF16)


def weights_finish(sites, idx, core, *refs):
    pieces = refs[: 2 * sites]
    rp, ro, cp, co, rows_t = refs[2 * sites :]
    width = ro.shape[0]
    group = width // sites
    unit = group // 2
    part = width // 2 // sites
    for j in range(2 * sites):
        k = j // 2
        cc = core[0] ^ (j % 2)
        g = idx[0] ^ k
        piece = pieces[j][...].astype(F32)
        for u in range(3):
            place = 3 * cc + u
            dest = (place // 2) * width + g * group + (place % 2) * unit
            rows_t[pl.ds(pl.multiple_of(dest, unit), unit), :] = piece[u * unit : (u + 1) * unit]
        here = pl.ds(pl.multiple_of(cc * (width // 2) + g * part, part), part)
        tiles = [piece[3 * unit + t * part : 3 * unit + (t + 1) * part] for t in range(5)]
        for t in range(3):
            cp[here, t * width : (t + 1) * width] = tiles[t]
        co[here, :] = tiles[3]
        ro[here, :] = tiles[4]
    rp[...] = jnp.transpose(rows_t[...])


def exchange(value, axis):
    return lax.all_to_all(value, axis, 0, 0, tiled=True)


def swapped(value, axis, by):
    length = lax.axis_size(axis)
    return lax.ppermute(value, axis, [(i, i ^ by) for i in range(length)])


def on_device(
    features,
    link_pattern,
    row_gain,
    row_proj,
    row_out,
    column_norm_gain,
    col_proj,
    col_out,
    cotangent,
):
    rows, _, width = features.shape
    sites, haps = lax.axis_size("site"), lax.axis_size("hap")
    count = sites * haps
    per = rows // haps
    group = width // sites
    heads = group // HEAD_DIM
    total = rows * sites
    both_axes = ("site", "hap")
    me = lax.axis_index("site")
    idx = me.reshape(1).astype(jnp.int32)
    hap = lax.axis_index("hap").reshape(1).astype(jnp.int32)
    core = hap % 2
    factor = lane_factor(per, group)
    block = ((count, per // factor, group * factor), BF16)
    feats = features.reshape(rows, width)
    cot = cotangent.reshape(rows, width)

    pieces = [feats] + [swapped(feats, "site", k) for k in range(1, sites)]
    link_pattern = jnp.where(link_pattern > 0, 1, 0)
    gains = jnp.stack([row_gain, column_norm_gain])
    w_t = jnp.transpose(row_proj)
    kv_t_w = jnp.transpose(col_proj[:, width:])

    x_out, normed = call(
        functools.partial(row_forward, sites, haps),
        [((haps, per, 3 * width), BF16), ((total, width), BF16)],
        idx, link_pattern, pieces[0], *pieces[:0:-1], cot, gains, w_t, row_out, scalars=2,
    )
    x_in = exchange(x_out, "hap")
    prob, q, val, key_t = call(
        functools.partial(row_probs, sites),
        [
            ((total, heads * total), BF16),
            ((total, group), BF16),
            ((total, group), BF16),
            ((group, total), BF16),
        ],
        idx, link_pattern, normed, w_t, scalars=2, us=20,
    )
    x_in, _ = lax.optimization_barrier((x_in, prob))
    half = width // 2
    ga, col_send, col_keep, og = call(
        functools.partial(column_step, sites, haps),
        [
            block,
            ((half, 5 * width), BF16),
            ((half, 5 * width), BF16),
            ((haps, per, 2 * width), BF16),
        ],
        hap, x_in, row_out, gains, col_proj, kv_t_w, col_out, scalars=1, far=2,
        scratch=[
            pltpu.VMEM((haps, per, 2 * width), BF16),
            pltpu.VMEM((width, 5 * width), BF16),
            pltpu.SemaphoreType.DMA((4,)),
        ],
    )
    g_in = exchange(ga, both_axes)
    col_got = [swapped(col_send, "hap", 1)]
    cols = call(
        functools.partial(column_split, sites),
        [((half // sites, 5 * width), BF16)] * sites,
        idx, col_keep, *col_got, scalars=1, us=0,
        scratch=[pltpu.VMEM((half, 5 * width), BF16)],
    )
    og_keep, og_send = call(
        split_outputs, [((haps // 2, per, 2 * width), BF16)] * 2, hap, og, scalars=1
    )
    og_got = swapped(og_send, "hap", 1)
    g_in, _ = lax.optimization_barrier((g_in, (cols, og_got)))
    cols = [cols[0]] + [swapped(cols[k], "site", k) for k in range(1, sites)]
    *gps, row_keep, row_send = call(
        functools.partial(row_backward, sites, haps),
        [((rows, 3 * group), BF16)] * sites + [((3 * group // 2, width), BF16)] * 2,
        idx, core, g_in, prob, q, val, key_t, normed, scalars=2,
        scratch=[
            pltpu.VMEM((total, group), BF16),
            pltpu.VMEM((3 * group, width), BF16),
        ],
    )
    row_got = swapped(row_send, "hap", 1)
    depth = 3 * group // 2 + 5 * half // sites
    near, own, *far = call(
        functools.partial(weights_join, sites),
        [((depth + 4 * per, width), BF16)] + [((4 * per, width), BF16)] * (haps // 2 - 1),
        row_keep, row_got, og_keep, og_got, *cols,
    )
    near_got = swapped(near, "hap", 2)
    far = [swapped(x, "hap", 2 * (j + 2)) for j, x in enumerate(far)]
    near_got, far = lax.optimization_barrier((near_got, far))
    parts = [own, near_got] + list(far)
    left, right, step = near, near_got, 2
    while 2 * step < haps:
        (left,) = call(weights_add, [((depth, width), BF16)], left, right)
        right, step = swapped(left, "hap", 2 * step), 2 * step
    gps, _ = lax.optimization_barrier((gps, left))
    gps = [gps[0]] + [swapped(gps[k], "site", k) for k in range(1, sites)]
    right, gps = lax.optimization_barrier((right, gps))
    (mine,) = call(weights_add, [((depth, width), BF16)], left, right)
    got = [swapped(mine, "site", k) for k in range(1, sites)]
    mine_swapped = swapped(mine, "hap", 1)
    out, grad = call(
        functools.partial(row_finish, sites, haps),
        [((rows, width), BF16)] * 2,
        idx, hap, feats, gains, w_t, *gps, *parts, scalars=2,
        scratch=[pltpu.VMEM((2, haps, per, width), F32)],
    )
    got[0], mine_swapped, out = lax.optimization_barrier((got[0], mine_swapped, out))
    full = [mine, mine_swapped] + [x for p in got for x in (p, swapped(p, "hap", 1))]
    rp, ro, cp, co = call(
        functools.partial(weights_finish, sites),
        [((width, 3 * width), F32), ((width, width), F32)] * 2,
        idx, core, *full, scalars=2,
        scratch=[pltpu.VMEM((3 * width, width), F32)],
    )
    shape = (rows, 1, width)
    return (out.reshape(shape), grad.reshape(shape), rp, ro, cp, co)


def solution(mesh):
    data = P("site", "hap", None)
    return jax.shard_map(
        on_device,
        mesh=mesh,
        in_specs=(data, P(), P(), P(), P(), P(), P(), P(), data),
        out_specs=(data, data, P(), P(), P(), P()),
        check_vma=False,
    )
```

```python
import functools

import jax
import jax.numpy as jnp
from jax import lax
from jax.experimental import pallas as pl
from jax.experimental.pallas import tpu as pltpu
from jax.sharding import PartitionSpec as P

HEAD_DIM = 32
EPSILON = 1e-05
LOG2E = 1.4426950408889634
SCALE = HEAD_DIM ** (-0.5)
F32 = jnp.float32
BF16 = jnp.bfloat16
VMEM = pl.BlockSpec(memory_space=pltpu.VMEM)
HBM = pl.BlockSpec(memory_space=pltpu.HBM)
SMEM = pl.BlockSpec(memory_space=pltpu.SMEM)
PARAMS = pltpu.CompilerParams(vmem_limit_bytes=24 << 20)


def mm(a, b):
    return lax.dot_general(a, b, (((1,), (0,)), ((), ())), preferred_element_type=F32)


def mm_nt(a, b):
    return lax.dot_general(a, b, (((1,), (1,)), ((), ())), preferred_element_type=F32)


def mm_tn(a, b):
    return lax.dot_general(a, b, (((0,), (0,)), ((), ())), preferred_element_type=F32)


def norm_parts(x):
    centred = x - jnp.mean(x, axis=-1, keepdims=True)
    rstd = lax.rsqrt(jnp.mean(centred * centred, axis=-1, keepdims=True) + EPSILON)
    return centred * rstd, rstd


def norm_back(xhat, rstd, gain, grad):
    scaled = grad * gain
    first = jnp.mean(scaled, axis=-1, keepdims=True)
    second = jnp.mean(scaled * xhat, axis=-1, keepdims=True)
    return rstd * (scaled - first - xhat * second)


def head_lanes(width, head):
    return lax.broadcasted_iota(jnp.int32, (1, width), 1) // HEAD_DIM == head


def only_head(values, head):
    return jnp.where(head_lanes(values.shape[1], head), values, jnp.zeros_like(values))


def flat_rows(values, dtype=BF16):
    wide = values.astype(F32)
    return wide.reshape(wide.shape[0] * wide.shape[1], wide.shape[2]).astype(dtype)


def lane_factor(rows, width):
    factor = 128 // width
    return factor if (rows // factor) % 8 == 0 else 1


def pack_block(values, outer):
    rows, width = values.shape[0] // outer, values.shape[1]
    factor = lane_factor(rows, width)
    split = values.reshape(outer, factor, rows // factor, width)
    return jnp.concatenate([split[:, j] for j in range(factor)], axis=2).astype(BF16)


def unpack_block(values, width):
    wide = values.astype(F32)
    factor = wide.shape[2] // width
    split = [wide[:, None, :, j * width : (j + 1) * width] for j in range(factor)]
    joined = jnp.concatenate(split, axis=1)
    return joined.reshape(-1, width).astype(BF16)


def call(body, outs, *operands, scalars=0, scratch=(), us=0, far=0):
    cost = pl.CostEstimate(flops=us * 10**9 + 1, bytes_accessed=us * 3_600_000 + 1, transcendentals=0)
    return pl.pallas_call(
        body,
        out_shape=[jax.ShapeDtypeStruct(s, d) for s, d in outs[: len(outs) - far]]
        + [pltpu.HBM(s, d) for s, d in outs[len(outs) - far :]],
        in_specs=[SMEM] * scalars + [VMEM] * (len(operands) - scalars),
        out_specs=[VMEM] * (len(outs) - far) + [HBM] * far,
        scratch_shapes=list(scratch),
        compiler_params=PARAMS,
        cost_estimate=cost,
    )(*operands)


def head_stack(values):
    heads = values.shape[1] // HEAD_DIM
    return jnp.concatenate([only_head(values, h) for h in range(heads)], axis=0)


def head_blocks(values):
    heads = values.shape[0] // HEAD_DIM
    wide = values.shape[1] // heads
    return jnp.concatenate(
        [
            values[h * HEAD_DIM : (h + 1) * HEAD_DIM, h * wide : (h + 1) * wide]
            for h in range(heads)
        ],
        axis=0,
    )


def exp_parts(parts):
    high = functools.reduce(jnp.maximum, [jnp.max(part, axis=0, keepdims=True) for part in parts])
    parts = [jnp.exp2(part - high) for part in parts]
    total = sum(jnp.sum(part, axis=0, keepdims=True) for part in parts)
    return parts, 1.0 / total


def row_forward(sites, haps, idx, link, *refs):
    pieces = refs[:1] + refs[sites - 1 : 0 : -1]
    cot, gain, w_t, row_out, x_out, n_out = refs[sites:]
    me = idx[0]
    rows, width = cot.shape
    for k in range(sites):
        xhat, _ = norm_parts(pieces[k][...].astype(F32))
        n_out[k * rows : (k + 1) * rows, :] = (xhat * gain[:1, :]).astype(BF16)
    normed = n_out[...]
    q = mm_nt(normed[:rows], w_t[:width, :]).astype(BF16)
    key = mm_nt(normed, w_t[width : 2 * width, :]).astype(BF16)
    v_t = mm_nt(w_t[2 * width :, :], normed).astype(BF16)
    scores = mm_nt(key, head_stack(q)) * (SCALE * LOG2E)
    bias = [jnp.where(link[me, me ^ a] > 0, 0.0, -jnp.inf) for a in range(sites)]
    parts = [scores[a * rows : (a + 1) * rows] + bias[a] for a in range(sites)]
    parts, inverse = exp_parts(parts)
    exps = jnp.concatenate([part.astype(BF16) for part in parts], axis=0)
    att_t = head_blocks(mm(v_t, exps) * inverse)
    att = jnp.transpose(att_t).astype(BF16)
    hid = pieces[0][...].astype(F32) + mm(att, row_out[...])
    joined = jnp.concatenate([hid, cot[...].astype(F32), att.astype(F32)], axis=1)
    x_out[...] = joined.reshape(haps, rows // haps, 3 * width).astype(BF16)


def row_probs(sites, idx, link, normed_ref, w_t, p_out, q_out, v_out, kt_out):
    me = idx[0]
    normed = normed_ref[...]
    total, width = q_out.shape
    full = normed.shape[1]
    rows = total // sites

    def weights(part):
        return w_t[pl.ds(pl.multiple_of(part * full + me * width, width), width), :]

    q = mm_nt(normed, weights(0)).astype(BF16)
    key = mm_nt(normed, weights(1)).astype(BF16)
    q_out[...] = q
    v_out[...] = mm_nt(normed, weights(2)).astype(BF16)
    kt_out[...] = mm_nt(weights(1), normed).astype(BF16)
    scores = mm_nt(key, head_stack(q)) * (SCALE * LOG2E)
    parts = []
    for a in range(sites):
        bias = [
            jnp.full((1, rows), jnp.where(link[me ^ b, me ^ a] > 0, 0.0, -jnp.inf), F32)
            for b in range(sites)
        ]
        bias = jnp.concatenate(bias * (width // HEAD_DIM), axis=1)
        parts.append(scores[a * rows : (a + 1) * rows] + bias)
    parts, inverse = exp_parts(parts)
    for a in range(sites):
        p_out[a * rows : (a + 1) * rows, :] = (parts[a] * inverse).astype(BF16)


def column_step(sites, haps, hap, x_in, row_out, gain, col_proj, kv_t_w, col_out, *refs):
    ga_out, send, keep, og_out, og, w_all, sems = refs
    core = hap[0] % 2
    half = row_out.shape[0] // 2
    mine = pl.ds(pl.multiple_of(core * half, half), half)
    other = pl.ds(pl.multiple_of((1 - core) * half, half), half)

    def save(j, cols):
        return pltpu.make_async_copy(w_all.at[mine, cols], keep.at[:, cols], sems.at[j])

    def save_outputs(j, cols):
        return pltpu.make_async_copy(og.at[:, :, cols], og_out.at[:, :, cols], sems.at[j])

    width = row_out.shape[0]
    group = width // sites
    x_all = flat_rows(x_in[...], F32)
    rows = x_all.shape[0]
    per = rows // haps
    hid = x_all[:, :width]
    cot_f = x_all[:, width : 2 * width]
    cot = cot_f.astype(BF16)
    row_att = x_all[:, 2 * width :].astype(BF16)
    grad_att = mm_nt(cot, col_out[...]).astype(BF16)
    xhat, rstd = norm_parts(hid)
    normed = (xhat * gain[1:2, :]).astype(BF16)
    packed = mm(normed, col_proj[...]).astype(BF16)
    q = packed[:, :width]
    key = packed[:, width : 2 * width]
    val = packed[:, 2 * width :]
    kv_t = mm_nt(kv_t_w[...], normed).astype(BF16)
    q_st = head_stack(q)
    g_st = head_stack(grad_att)
    scores = mm_nt(key, q_st) * (SCALE * LOG2E)
    dprob = mm_nt(val, g_st)
    same = (
        lax.broadcasted_iota(jnp.int32, scores.shape, 0) % per
        == lax.broadcasted_iota(jnp.int32, scores.shape, 1) % per
    )
    scores = jnp.where(same, scores, -jnp.inf)
    exps = jnp.exp2(scores - jnp.max(scores, axis=0, keepdims=True))
    inverse = 1.0 / jnp.sum(exps, axis=0, keepdims=True)
    att_t = head_blocks(mm(kv_t[width:, :], exps.astype(BF16)) * inverse)
    probs = exps * inverse
    delta = jnp.sum(probs * dprob, axis=0, keepdims=True)
    dscore = (probs * (dprob - delta)).astype(BF16)
    dv = mm(probs.astype(BF16), g_st)
    dk = mm(dscore, q_st)
    dq = jnp.transpose(head_blocks(mm(kv_t[:width, :], dscore)))
    w_all[:, 3 * width : 4 * width] = mm(att_t.astype(BF16), cot).astype(BF16)
    att = jnp.transpose(att_t).astype(BF16)
    out = hid + mm(att, col_out[...])
    og[:, :, :width] = out.reshape(haps, per, width).astype(BF16)
    third = save_outputs(2, slice(0, width))
    third.start()
    packed_grad = jnp.concatenate([dq * SCALE, dk * SCALE, dv], axis=1).astype(BF16)
    w_all[:, : 3 * width] = mm_tn(normed, packed_grad).astype(BF16)
    first = save(0, slice(0, 4 * width))
    first.start()
    grad_normed = mm_nt(packed_grad, col_proj[...])
    grad_hidden = (cot_f + norm_back(xhat, rstd, gain[1:2, :], grad_normed)).astype(BF16)
    og[:, :, width:] = grad_hidden.astype(F32).reshape(haps, per, width).astype(BF16)
    fourth = save_outputs(3, slice(width, 2 * width))
    fourth.start()
    w_all[:, 4 * width :] = mm_tn(row_att, grad_hidden).astype(BF16)
    second = save(1, slice(4 * width, 5 * width))
    second.start()
    for i in range(sites):
        g_i = mm_nt(grad_hidden, row_out[i * group : (i + 1) * group, :])
        ga_out[i * haps : (i + 1) * haps] = pack_block(g_i, haps)
    send[...] = w_all[other, :]
    for copy in (first, second, third, fourth):
        copy.wait()


def split_outputs(hap, og, keep, send):
    for m in range(keep.shape[0]):
        keep[m] = og[hap[0] ^ (2 * m)]
        send[m] = og[hap[0] ^ (2 * m + 1)]


def column_split(sites, idx, keep, *refs):
    outs, both, gots = refs[-sites - 1 : -1], refs[-1], refs[: -sites - 1]
    got = jnp.concatenate([g[...].astype(F32) for g in gots], axis=0)
    both[...] = (keep[...].astype(F32) + got).astype(BF16)
    part = keep.shape[0] // sites
    for k in range(sites):
        outs[k][...] = both[pl.ds(pl.multiple_of((idx[0] ^ k) * part, part), part), :]


def row_backward(sites, haps, idx, core, g_in, prob, q, val, key_t, normed, *refs):
    gp_outs = refs[:sites]
    keep, send, g_all, w_out = refs[sites:]
    me = idx[0]
    total, width = q.shape
    rows = total // sites
    for b in range(sites):
        g_all[b * rows : (b + 1) * rows, :] = unpack_block(
            g_in[pl.ds((me ^ b) * haps, haps)], width
        )
    g_st = head_stack(g_all[...])
    p_all = prob[...].astype(F32)
    dprob = mm_nt(val[...], g_st)
    delta = jnp.sum(p_all * dprob, axis=0, keepdims=True)
    dscore = (p_all * (dprob - delta)).astype(BF16)
    dv = mm(prob[...], g_st)
    dk = mm(dscore, head_stack(q[...]))
    dq_t = head_blocks(mm(key_t[...], dscore)) * SCALE
    dk16 = (dk * SCALE).astype(BF16)
    dv16 = dv.astype(BF16)
    w_out[:width, :] = mm(dq_t.astype(BF16), normed[...]).astype(BF16)
    w_out[width : 2 * width, :] = mm_tn(dk16, normed[...]).astype(BF16)
    w_out[2 * width :, :] = mm_tn(dv16, normed[...]).astype(BF16)
    half = 3 * width // 2
    keep[...] = w_out[pl.ds(pl.multiple_of(core[0] * half, half), half), :]
    send[...] = w_out[pl.ds(pl.multiple_of((1 - core[0]) * half, half), half), :]
    dq = jnp.transpose(dq_t).astype(BF16)
    joined = jnp.concatenate([dq, dk16, dv16], axis=1)
    for b in range(sites):
        gp_outs[b][...] = joined[b * rows : (b + 1) * rows]


def row_finish(sites, haps, idx, hap, feats, gain, w_t, gp, *refs):
    gps, parts = refs[: sites - 1], refs[sites - 1 : sites - 1 + haps // 2]
    out_ref, gf_ref, og = refs[sites - 1 + haps // 2 :]
    me = idx[0]
    rows, width = feats.shape
    group = width // sites
    per = rows // haps
    for m in range(haps // 2):
        base = parts[m].shape[0] - 4 * per
        for j in range(2):
            for side in range(2):
                start = base + (2 * j + side) * per
                og[side, hap[0] ^ (2 * m + j)] = parts[m][start : start + per, :].astype(F32)
    grads = [gp[...]] + [g[g.shape[0] - rows :, : 3 * group] for g in gps]
    grad_normed = 0.0
    for k in range(sites):
        place = [pl.multiple_of(p * width + (me ^ k) * group, group) for p in range(3)]
        weights = jnp.concatenate([w_t[pl.ds(p, group), :] for p in place], axis=0)
        grad_normed = grad_normed + mm(grads[k], weights)
    xhat, rstd = norm_parts(feats[...].astype(F32))
    grad = og[1].reshape(rows, width) + norm_back(xhat, rstd, gain[:1, :], grad_normed)
    out_ref[...] = og[0].reshape(rows, width).astype(BF16)
    gf_ref[...] = grad.astype(BF16)


def outputs_pair(keep, got, m, width):
    both = [keep[m].astype(F32), got[m].astype(F32)]
    both = [x[:, j * width : (j + 1) * width] for x in both for j in range(2)]
    return jnp.concatenate(both, axis=0).astype(BF16)


def weights_join(sites, row_keep, row_got, og_keep, og_got, *refs):
    cols, (near, own, *far) = refs[:sites], refs[sites:]
    half, width = row_keep.shape
    depth = half + 5 * cols[0].shape[0]
    total = sum(c[...].astype(F32) for c in cols)
    tiles = [total[:, t * width : (t + 1) * width] for t in range(5)]
    rows = row_keep[...].astype(F32) + row_got[...].astype(F32)
    near[:depth, :] = jnp.concatenate([rows] + tiles, axis=0).astype(BF16)
    near[depth:, :] = outputs_pair(og_keep, og_got, 1, width)
    own[...] = outputs_pair(og_keep, og_got, 0, width)
    for j, out in enumerate(far):
        out[...] = outputs_pair(og_keep, og_got, j + 2, width)


def weights_add(mine, got, out):
    depth = out.shape[0]
    out[...] = (mine[:depth, :].astype(F32) + got[:depth, :].astype(F32)).astype(BF16)


def weights_finish(sites, idx, core, *refs):
    pieces = refs[: 2 * sites]
    rp, ro, cp, co, rows_t = refs[2 * sites :]
    width = ro.shape[0]
    group = width // sites
    unit = group // 2
    part = width // 2 // sites
    for j in range(2 * sites):
        k = j // 2
        cc = core[0] ^ (j % 2)
        g = idx[0] ^ k
        piece = pieces[j][...].astype(F32)
        for u in range(3):
            place = 3 * cc + u
            dest = (place // 2) * width + g * group + (place % 2) * unit
            rows_t[pl.ds(pl.multiple_of(dest, unit), unit), :] = piece[u * unit : (u + 1) * unit]
        here = pl.ds(pl.multiple_of(cc * (width // 2) + g * part, part), part)
        tiles = [piece[3 * unit + t * part : 3 * unit + (t + 1) * part] for t in range(5)]
        for t in range(3):
            cp[here, t * width : (t + 1) * width] = tiles[t]
        co[here, :] = tiles[3]
        ro[here, :] = tiles[4]
    rp[...] = jnp.transpose(rows_t[...])


def exchange(value, axis):
    return lax.all_to_all(value, axis, 0, 0, tiled=True)


def swapped(value, axis, by):
    length = lax.axis_size(axis)
    return lax.ppermute(value, axis, [(i, i ^ by) for i in range(length)])


def on_device(
    features,
    link_pattern,
    row_gain,
    row_proj,
    row_out,
    column_norm_gain,
    col_proj,
    col_out,
    cotangent,
):
    rows, _, width = features.shape
    sites, haps = lax.axis_size("site"), lax.axis_size("hap")
    count = sites * haps
    per = rows // haps
    group = width // sites
    heads = group // HEAD_DIM
    total = rows * sites
    both_axes = ("site", "hap")
    me = lax.axis_index("site")
    idx = me.reshape(1).astype(jnp.int32)
    hap = lax.axis_index("hap").reshape(1).astype(jnp.int32)
    core = hap % 2
    factor = lane_factor(per, group)
    block = ((count, per // factor, group * factor), BF16)
    feats = features.reshape(rows, width)
    cot = cotangent.reshape(rows, width)

    pieces = [feats] + [swapped(feats, "site", k) for k in range(1, sites)]
    link_pattern = jnp.where(link_pattern > 0, 1, 0)
    gains = jnp.stack([row_gain, column_norm_gain])
    w_t = jnp.transpose(row_proj)
    kv_t_w = jnp.transpose(col_proj[:, width:])

    x_out, normed = call(
        functools.partial(row_forward, sites, haps),
        [((haps, per, 3 * width), BF16), ((total, width), BF16)],
        idx, link_pattern, pieces[0], *pieces[:0:-1], cot, gains, w_t, row_out, scalars=2,
    )
    x_in = exchange(x_out, "hap")
    prob, q, val, key_t = call(
        functools.partial(row_probs, sites),
        [
            ((total, heads * total), BF16),
            ((total, group), BF16),
            ((total, group), BF16),
            ((group, total), BF16),
        ],
        idx, link_pattern, normed, w_t, scalars=2, us=20,
    )
    x_in, _ = lax.optimization_barrier((x_in, prob))
    half = width // 2
    ga, col_send, col_keep, og = call(
        functools.partial(column_step, sites, haps),
        [
            block,
            ((half, 5 * width), BF16),
            ((half, 5 * width), BF16),
            ((haps, per, 2 * width), BF16),
        ],
        hap, x_in, row_out, gains, col_proj, kv_t_w, col_out, scalars=1, far=2,
        scratch=[
            pltpu.VMEM((haps, per, 2 * width), BF16),
            pltpu.VMEM((width, 5 * width), BF16),
            pltpu.SemaphoreType.DMA((4,)),
        ],
    )
    g_in = exchange(ga, both_axes)
    col_got = [swapped(col_send, "hap", 1)]
    cols = call(
        functools.partial(column_split, sites),
        [((half // sites, 5 * width), BF16)] * sites,
        idx, col_keep, *col_got, scalars=1, us=0,
        scratch=[pltpu.VMEM((half, 5 * width), BF16)],
    )
    og_keep, og_send = call(
        split_outputs, [((haps // 2, per, 2 * width), BF16)] * 2, hap, og, scalars=1
    )
    og_got = swapped(og_send, "hap", 1)
    g_in, _ = lax.optimization_barrier((g_in, (cols, og_got)))
    cols = [cols[0]] + [swapped(cols[k], "site", k) for k in range(1, sites)]
    *gps, row_keep, row_send = call(
        functools.partial(row_backward, sites, haps),
        [((rows, 3 * group), BF16)] * sites + [((3 * group // 2, width), BF16)] * 2,
        idx, core, g_in, prob, q, val, key_t, normed, scalars=2,
        scratch=[
            pltpu.VMEM((total, group), BF16),
            pltpu.VMEM((3 * group, width), BF16),
        ],
    )
    row_got = swapped(row_send, "hap", 1)
    depth = 3 * group // 2 + 5 * half // sites
    near, own, *far = call(
        functools.partial(weights_join, sites),
        [((depth + 4 * per, width), BF16)] + [((4 * per, width), BF16)] * (haps // 2 - 1),
        row_keep, row_got, og_keep, og_got, *cols,
    )
    near_got = swapped(near, "hap", 2)
    far = [swapped(x, "hap", 2 * (j + 2)) for j, x in enumerate(far)]
    near_got, far = lax.optimization_barrier((near_got, far[::-1]))
    far = far[::-1]
    parts = [own, near_got] + list(far)
    left, right, step = near, near_got, 2
    while 2 * step < haps:
        (left,) = call(weights_add, [((depth, width), BF16)], left, right)
        right, step = swapped(left, "hap", 2 * step), 2 * step
    gps, _ = lax.optimization_barrier((gps, left))
    gps = [gps[0]] + [swapped(gps[k], "site", k) for k in range(1, sites)]
    right, gps = lax.optimization_barrier((right, gps))
    (mine,) = call(weights_add, [((depth, width), BF16)], left, right)
    got = [swapped(mine, "site", k) for k in range(1, sites)]
    mine_swapped = swapped(mine, "hap", 1)
    out, grad = call(
        functools.partial(row_finish, sites, haps),
        [((rows, width), BF16)] * 2,
        idx, hap, feats, gains, w_t, *gps, *parts, scalars=2,
        scratch=[pltpu.VMEM((2, haps, per, width), F32)],
    )
    got, mine_swapped, out = lax.optimization_barrier((got, mine_swapped, out))
    full = [mine, mine_swapped] + [x for p in got for x in (p, swapped(p, "hap", 1))]
    rp, ro, cp, co = call(
        functools.partial(weights_finish, sites),
        [((width, 3 * width), F32), ((width, width), F32)] * 2,
        idx, core, *full, scalars=2,
        scratch=[pltpu.VMEM((3 * width, width), F32)],
    )
    shape = (rows, 1, width)
    return (out.reshape(shape), grad.reshape(shape), rp, ro, cp, co)


def solution(mesh):
    data = P("site", "hap", None)
    return jax.shard_map(
        on_device,
        mesh=mesh,
        in_specs=(data, P(), P(), P(), P(), P(), P(), P(), data),
        out_specs=(data, data, P(), P(), P(), P()),
        check_vma=False,
    )
```
